256 devices in a mesh: prow: 4 (over z_hi, core), pcol: 4 (over y), pl: 16 (over z_lo, x).
Axes of the slice: x: 4, y: 4, z: 8 (z_hi: 2, z_lo: 4; z = z_hi * 4 + z_lo), core: 2. Of those that a mesh axis runs over, the one named last changes fastest.
Arguments:
- factor_cols: bfloat16 [32768, 4096], P(('prow', 'pcol'), 'pl'), may hold values from -0.09375 to 0.09375
- modal_at_loads: bfloat16 [2048, 32768], P(None, ('prow', 'pcol')), may hold values from -0.03125 to 0.03125
- mode_shapes: bfloat16 [8192, 2048], P(('prow', 'pl')), may hold values from -0.125 to 0.125
- natural_freq: float32 [2048], replicated, may hold values from 0.5 to 2
- damping: float32 [2048], replicated, may hold values from 0.05 to 0.2
Outputs:
- cospectrum: float32 [8192, 8192], P(('prow', 'pl'), 'pcol')
The draws below stay inside these ranges and needn't reach their ends.
All inputs are finite; a program needn't handle non-finite values.
Results may differ from the reference program's by a relative error of at most 0.022.
Values may be sent and summed in bfloat16 or wider, within the bound.
A program may use at most 128 MiB of HBM per device.

```python
import math
import jax
import jax.numpy as jnp

NLOAD = 32768
MODES = 2048
RESP = 8192
PSEUDO = 4096


def block_scale(own_key, dims, split, low, high):
    level, own = 1.0, jax.random.fold_in(own_key, 6)
    for axis_at, shards_of in split:
        heights = jnp.exp(jax.random.uniform(jax.random.fold_in(own, axis_at), (shards_of,), jnp.float32, low / len(split), high / len(split)))
        level = level * jnp.repeat(heights, dims[axis_at] // shards_of).reshape([-1 if axis == axis_at else 1 for axis in range(len(dims))])
    return level


def centred(own_key, extent, scale, most, split=(), dtype=jnp.bfloat16):
    level = block_scale(own_key, extent, split, -0.22, 0.18) if split else 1.0
    entries = jax.random.normal(own_key, extent, jnp.float32) * scale * level
    return jnp.minimum(jnp.maximum(entries, -most), most).astype(dtype)


def setup_inputs(seed: int = 0) -> dict:
    streams_of = jax.random.split(jax.random.key(seed), 6)
    return {
        "factor_cols": centred(streams_of[0], (NLOAD, PSEUDO), PSEUDO ** -0.5, 0.09375, ((0, 16), (1, 16))),
        "modal_at_loads": centred(streams_of[1], (MODES, NLOAD), NLOAD ** -0.5, 0.03125, ((1, 16),)),
        "mode_shapes": centred(streams_of[2], (RESP, MODES), MODES ** -0.5, 0.125, ((0, 64),)),
        "natural_freq": jnp.clip(jnp.exp(jax.random.uniform(streams_of[3], (MODES,), jnp.float32, math.log(0.5), math.log(2.0))), 0.5, 2.0),
        "damping": jnp.clip(jnp.exp(jax.random.uniform(streams_of[4], (MODES,), jnp.float32, math.log(0.05), math.log(0.2))), 0.05, 0.2),
    }


def transfer_pair(natural_freq, damping):
    detuning = natural_freq * natural_freq - 1.0
    damper = 2.0 * damping * natural_freq
    modulus = detuning * detuning + damper * damper
    return detuning / modulus, -damper / modulus


def reference(factor_cols, modal_at_loads, mode_shapes, natural_freq, damping):
    in_phase, quadrature = transfer_pair(natural_freq, damping)
    modal_load = jnp.dot(modal_at_loads, factor_cols, preferred_element_type=jnp.float32).astype(jnp.bfloat16)
    modal_wide = modal_load.astype(jnp.float32)
    pseudo_real = (in_phase[:, None] * modal_wide).astype(jnp.bfloat16)
    pseudo_imag = (quadrature[:, None] * modal_wide).astype(jnp.bfloat16)
    stacked = jnp.concatenate([pseudo_real, pseudo_imag], axis=1)
    modal_gram = jnp.dot(stacked, stacked.T, preferred_element_type=jnp.float32).astype(jnp.bfloat16)
    weighted = jnp.dot(mode_shapes, modal_gram, preferred_element_type=jnp.float32).astype(jnp.bfloat16)
    return jnp.dot(weighted, mode_shapes.T, preferred_element_type=jnp.float32)
```

```python
import jax
import jax.numpy as jnp
from jax import lax
from jax.sharding import PartitionSpec as P


def transfer_pair(natural_freq, damping):
    detuning = natural_freq * natural_freq - 1.0
    damper = 2.0 * damping * natural_freq
    modulus = detuning * detuning + damper * damper
    return (detuning / modulus, -damper / modulus)


def outer_rows(left_rows, right_rows):
    return lax.dot_general(
        left_rows, right_rows, (((1,), (1,)), ((), ())), preferred_element_type=jnp.float32
    )


def make_body(n_row, n_col):
    swap = [(c * n_col + r, r * n_col + c) for r in range(n_row) for c in range(n_col)]

    def body(factor_cols, modal_at_loads, mode_shapes, natural_freq, damping):
        in_phase, quadrature = transfer_pair(natural_freq, damping)
        own_rows = lax.psum_scatter(
            jnp.dot(modal_at_loads, factor_cols, preferred_element_type=jnp.float32),
            ("prow", "pcol"),
            scatter_dimension=0,
            tiled=True,
        )
        modal_load = lax.all_gather(own_rows.astype(jnp.bfloat16), ("prow", "pcol"), axis=0, tiled=True)
        modal_wide = modal_load.astype(jnp.float32)
        pseudo = jnp.concatenate(
            [
                (in_phase[:, None] * modal_wide).astype(jnp.bfloat16),
                (quadrature[:, None] * modal_wide).astype(jnp.bfloat16),
            ],
            axis=1,
        )
        block = pseudo.shape[0] // (n_row * n_col)
        row, col = lax.axis_index("prow"), lax.axis_index("pcol")
        first_row = (col * n_row + row) * block
        own_pseudo = lax.dynamic_slice_in_dim(pseudo, first_row, block, 0)
        partial_gram = outer_rows(own_pseudo, pseudo)
        gram_block = lax.psum(partial_gram.astype(jnp.bfloat16), "pl")
        gram_panel = lax.all_gather(gram_block, "prow", axis=0, tiled=True)
        weighted_part = outer_rows(mode_shapes, gram_panel).astype(jnp.bfloat16)
        weighted = lax.all_gather(weighted_part, "pcol", axis=1, tiled=True)
        panel_piece = lax.ppermute(mode_shapes, ("prow", "pcol"), swap)
        return outer_rows(weighted, lax.all_gather(panel_piece, "pl", axis=0, tiled=True))

    return body


def solution(mesh):
    in_specs = (
        P(("prow", "pcol"), "pl"),
        P(None, ("prow", "pcol")),
        P(("prow", "pl"), None),
        P(),
        P(),
    )
    out_specs = P(("prow", "pl"), "pcol")
    body = make_body(mesh.shape["prow"], mesh.shape["pcol"])
    return jax.shard_map(body, mesh=mesh, in_specs=in_specs, out_specs=out_specs, check_vma=False)
```

```python
import functools
import math

import jax
import jax.numpy as jnp
from jax import lax
from jax.experimental import pallas as pl
from jax.experimental.pallas import tpu as pltpu
from jax.sharding import PartitionSpec as P

MESH = pl.DeviceIdType.MESH


def transfer_pair(natural_freq, damping):
    detuning = natural_freq * natural_freq - 1.0
    damper = 2.0 * damping * natural_freq
    modulus = detuning * detuning + damper * damper
    return (detuning / modulus, -damper / modulus)


def outer_rows(left_rows, right_rows):
    return lax.dot_general(
        left_rows, right_rows, (((1,), (1,)), ((), ())), preferred_element_type=jnp.float32
    )


def exchange_kernel(x_ref, out_ref, send_sem, recv_sem, local_sem, *, axes, sizes, group, same):
    coords = {a: lax.axis_index(a) for a in axes}
    count = math.prod(sizes[a] for a in group)
    me = 0
    for a in group:
        me = me * sizes[a] + coords[a]

    def device(member):
        place = dict(coords)
        for a in reversed(group):
            place[a] = lax.rem(member, sizes[a])
            member = member // sizes[a]
        return tuple(place[a] for a in axes)

    def source(member):
        return x_ref if same else x_ref.at[member]

    def copy(offset):
        peer = lax.rem(me + offset, count)
        return pltpu.make_async_remote_copy(
            src_ref=source(peer),
            dst_ref=out_ref.at[me],
            send_sem=send_sem.at[offset],
            recv_sem=recv_sem.at[offset],
            device_id=device(peer),
            device_id_type=MESH,
        )

    def landing(offset):
        sender = lax.rem(me + count - offset, count)
        return pltpu.make_async_remote_copy(
            src_ref=source(me),
            dst_ref=out_ref.at[sender],
            send_sem=send_sem.at[offset],
            recv_sem=recv_sem.at[offset],
            device_id=device(sender),
            device_id_type=MESH,
        )

    local = pltpu.make_async_copy(source(me), out_ref.at[me], local_sem)
    local.start()
    for offset in range(1, count):
        copy(offset).start()
    local.wait()
    for offset in range(1, count):
        copy(offset).wait_send()
    for offset in range(1, count):
        landing(offset).wait_recv()


def exchange(x, group, axes, sizes, same):
    count = math.prod(sizes[a] for a in group)
    block = x.shape if same else x.shape[1:]
    kernel = functools.partial(exchange_kernel, axes=axes, sizes=sizes, group=group, same=same)
    return pl.pallas_call(
        kernel,
        out_shape=jax.ShapeDtypeStruct((count,) + tuple(block), x.dtype),
        in_specs=[pl.BlockSpec(memory_space=pl.ANY)],
        out_specs=pl.BlockSpec(memory_space=pl.ANY),
        scratch_shapes=[
            pltpu.SemaphoreType.DMA((count,)),
            pltpu.SemaphoreType.DMA((count,)),
            pltpu.SemaphoreType.DMA(()),
        ],
        compiler_params=pltpu.CompilerParams(has_side_effects=True),
    )(x)


def make_body(axes, sizes):
    n_row, n_col, n_pl = sizes["prow"], sizes["pcol"], sizes["pl"]
    swap = [(c * n_col + r, r * n_col + c) for r in range(n_row) for c in range(n_col)]
    ex = functools.partial(exchange, axes=axes, sizes=sizes)

    def body(factor_cols, modal_at_loads, mode_shapes, natural_freq, damping):
        in_phase, quadrature = transfer_pair(natural_freq, damping)
        modes = modal_at_loads.shape[0]
        block = modes // (n_row * n_col)
        partial_load = jnp.dot(modal_at_loads, factor_cols, preferred_element_type=jnp.float32)
        pieces = ex(partial_load.reshape(n_row * n_col, block, -1), ("prow", "pcol"), same=False)
        own_rows = jnp.sum(pieces, axis=0).astype(jnp.bfloat16)
        modal_load = ex(own_rows, ("prow", "pcol"), same=True).reshape(modes, -1)
        modal_wide = modal_load.astype(jnp.float32)
        pseudo = jnp.concatenate(
            [
                (in_phase[:, None] * modal_wide).astype(jnp.bfloat16),
                (quadrature[:, None] * modal_wide).astype(jnp.bfloat16),
            ],
            axis=1,
        )
        row, col = lax.axis_index("prow"), lax.axis_index("pcol")
        first_row = (col * n_row + row) * block
        own_pseudo = lax.dynamic_slice_in_dim(pseudo, first_row, block, 0)
        partial_gram = outer_rows(own_pseudo, pseudo)
        chunk = modes // n_pl
        by_chunk = partial_gram.reshape(block, n_pl, chunk).transpose(1, 0, 2)
        gram_sums = ex(by_chunk, ("pl",), same=False)
        gram_piece = jnp.sum(gram_sums, axis=0).astype(jnp.bfloat16)
        gram_all = ex(gram_piece, ("prow", "pl"), same=True)
        gram_panel = (
            gram_all.reshape(n_row, n_pl, block, chunk).transpose(0, 2, 1, 3).reshape(n_row * block, modes)
        )
        weighted_part = outer_rows(mode_shapes, gram_panel).astype(jnp.bfloat16)
        weighted_all = ex(weighted_part, ("pcol",), same=True)
        weighted = weighted_all.transpose(1, 0, 2).reshape(weighted_part.shape[0], modes)
        panel_piece = lax.ppermute(mode_shapes, ("prow", "pcol"), swap)
        panel = ex(panel_piece, ("pl",), same=True).reshape(-1, modes)
        return outer_rows(weighted, panel)

    return body


def solution(mesh):
    in_specs = (
        P(("prow", "pcol"), "pl"),
        P(None, ("prow", "pcol")),
        P(("prow", "pl"), None),
        P(),
        P(),
    )
    out_specs = P(("prow", "pl"), "pcol")
    axes = tuple(mesh.axis_names)
    body = make_body(axes, dict(mesh.shape))
    return jax.shard_map(body, mesh=mesh, in_specs=in_specs, out_specs=out_specs, check_vma=False)
```

```python
import functools
import math

import jax
import jax.numpy as jnp
from jax import lax
from jax.experimental import pallas as pl
from jax.experimental.pallas import tpu as pltpu
from jax.sharding import PartitionSpec as P

MESH = pl.DeviceIdType.MESH


def transfer_pair(natural_freq, damping):
    detuning = natural_freq * natural_freq - 1.0
    damper = 2.0 * damping * natural_freq
    modulus = detuning * detuning + damper * damper
    return (detuning / modulus, -damper / modulus)


def outer_rows(left_rows, right_rows):
    return lax.dot_general(
        left_rows, right_rows, (((1,), (1,)), ((), ())), preferred_element_type=jnp.float32
    )


def exchange_kernel(x_ref, out_ref, send_sem, recv_sem, local_sem, *, axes, sizes, group, same):
    coords = {a: lax.axis_index(a) for a in axes}
    count = math.prod(sizes[a] for a in group)
    me = 0
    for a in group:
        me = me * sizes[a] + coords[a]

    def device(member):
        place = dict(coords)
        for a in reversed(group):
            place[a] = lax.rem(member, sizes[a])
            member = member // sizes[a]
        return tuple(place[a] for a in axes)

    def source(member):
        return x_ref if same else x_ref.at[member]

    def copy(offset):
        peer = lax.rem(me + offset, count)
        return pltpu.make_async_remote_copy(
            src_ref=source(peer),
            dst_ref=out_ref.at[me],
            send_sem=send_sem.at[offset],
            recv_sem=recv_sem.at[offset],
            device_id=device(peer),
            device_id_type=MESH,
        )

    def landing(offset):
        sender = lax.rem(me + count - offset, count)
        return pltpu.make_async_remote_copy(
            src_ref=source(me),
            dst_ref=out_ref.at[sender],
            send_sem=send_sem.at[offset],
            recv_sem=recv_sem.at[offset],
            device_id=device(sender),
            device_id_type=MESH,
        )

    local = pltpu.make_async_copy(source(me), out_ref.at[me], local_sem)
    local.start()
    barrier = pltpu.get_barrier_semaphore()
    for offset in range(1, count):
        peer = lax.rem(me + offset, count)
        pl.semaphore_signal(barrier, inc=1, device_id=device(peer), device_id_type=MESH)
    pl.semaphore_wait(barrier, count - 1)
    for offset in range(1, count):
        copy(offset).start()
    local.wait()
    for offset in range(1, count):
        copy(offset).wait_send()
    for offset in range(1, count):
        landing(offset).wait_recv()


def exchange(x, group, axes, sizes, same, kernel_id):
    count = math.prod(sizes[a] for a in group)
    block = x.shape if same else x.shape[1:]
    kernel = functools.partial(exchange_kernel, axes=axes, sizes=sizes, group=group, same=same)
    return pl.pallas_call(
        kernel,
        out_shape=jax.ShapeDtypeStruct((count,) + tuple(block), x.dtype),
        in_specs=[pl.BlockSpec(memory_space=pl.ANY)],
        out_specs=pl.BlockSpec(memory_space=pl.ANY),
        scratch_shapes=[
            pltpu.SemaphoreType.DMA((count,)),
            pltpu.SemaphoreType.DMA((count,)),
            pltpu.SemaphoreType.DMA(()),
        ],
        compiler_params=pltpu.CompilerParams(collective_id=kernel_id, has_side_effects=True),
    )(x)


def make_body(axes, sizes):
    n_row, n_col, n_pl = sizes["prow"], sizes["pcol"], sizes["pl"]
    swap = [(c * n_col + r, r * n_col + c) for r in range(n_row) for c in range(n_col)]
    ex = functools.partial(exchange, axes=axes, sizes=sizes)

    def body(factor_cols, modal_at_loads, mode_shapes, natural_freq, damping):
        in_phase, quadrature = transfer_pair(natural_freq, damping)
        modes = modal_at_loads.shape[0]
        block = modes // (n_row * n_col)
        partial_load = jnp.dot(modal_at_loads, factor_cols, preferred_element_type=jnp.float32)
        pieces = ex(partial_load.reshape(n_row * n_col, block, -1), ("prow", "pcol"), same=False, kernel_id=0)
        own_rows = jnp.sum(pieces, axis=0).astype(jnp.bfloat16)
        modal_load = ex(own_rows, ("prow", "pcol"), same=True, kernel_id=1).reshape(modes, -1)
        modal_wide = modal_load.astype(jnp.float32)
        pseudo = jnp.concatenate(
            [
                (in_phase[:, None] * modal_wide).astype(jnp.bfloat16),
                (quadrature[:, None] * modal_wide).astype(jnp.bfloat16),
            ],
            axis=1,
        )
        row, col = lax.axis_index("prow"), lax.axis_index("pcol")
        first_row = (col * n_row + row) * block
        own_pseudo = lax.dynamic_slice_in_dim(pseudo, first_row, block, 0)
        partial_gram = outer_rows(own_pseudo, pseudo)
        chunk = modes // n_pl
        by_chunk = partial_gram.reshape(block, n_pl, chunk).transpose(1, 0, 2)
        gram_sums = ex(by_chunk, ("pl",), same=False, kernel_id=2)
        gram_piece = jnp.sum(gram_sums, axis=0).astype(jnp.bfloat16)
        gram_all = ex(gram_piece, ("prow", "pl"), same=True, kernel_id=3)
        gram_panel = (
            gram_all.reshape(n_row, n_pl, block, chunk).transpose(0, 2, 1, 3).reshape(n_row * block, modes)
        )
        weighted_part = outer_rows(mode_shapes, gram_panel).astype(jnp.bfloat16)
        weighted_all = ex(weighted_part, ("pcol",), same=True, kernel_id=4)
        weighted = weighted_all.transpose(1, 0, 2).reshape(weighted_part.shape[0], modes)
        panel_piece = lax.ppermute(mode_shapes, ("prow", "pcol"), swap)
        panel = lax.all_gather(panel_piece, "pl", axis=0, tiled=True)
        return outer_rows(weighted, panel)

    return body


def solution(mesh):
    in_specs = (
        P(("prow", "pcol"), "pl"),
        P(None, ("prow", "pcol")),
        P(("prow", "pl"), None),
        P(),
        P(),
    )
    out_specs = P(("prow", "pl"), "pcol")
    axes = tuple(mesh.axis_names)
    body = make_body(axes, dict(mesh.shape))
    return jax.shard_map(body, mesh=mesh, in_specs=in_specs, out_specs=out_specs, check_vma=False)
```

```python
import functools
import math

import jax
import jax.numpy as jnp
from jax import lax
from jax.experimental import pallas as pl
from jax.experimental.pallas import tpu as pltpu
from jax.sharding import PartitionSpec as P

MESH = pl.DeviceIdType.MESH


def transfer_pair(natural_freq, damping):
    detuning = natural_freq * natural_freq - 1.0
    damper = 2.0 * damping * natural_freq
    modulus = detuning * detuning + damper * damper
    return (detuning / modulus, -damper / modulus)


def outer_rows(left_rows, right_rows):
    return lax.dot_general(
        left_rows, right_rows, (((1,), (1,)), ((), ())), preferred_element_type=jnp.float32
    )


def exchange_kernel(x_ref, out_ref, send_sem, recv_sem, local_sem, *, axes, sizes, group, same):
    coords = {a: lax.axis_index(a) for a in axes}
    count = math.prod(sizes[a] for a in group)
    me = 0
    for a in group:
        me = me * sizes[a] + coords[a]

    def device(member):
        place = dict(coords)
        for a in reversed(group):
            place[a] = lax.rem(member, sizes[a])
            member = member // sizes[a]
        return tuple(place[a] for a in axes)

    def source(member):
        return x_ref if same else x_ref.at[member]

    def copy(offset):
        peer = lax.rem(me + offset, count)
        return pltpu.make_async_remote_copy(
            src_ref=source(peer),
            dst_ref=out_ref.at[me],
            send_sem=send_sem.at[offset],
            recv_sem=recv_sem.at[offset],
            device_id=device(peer),
            device_id_type=MESH,
        )

    def landing(offset):
        sender = lax.rem(me + count - offset, count)
        return pltpu.make_async_remote_copy(
            src_ref=source(me),
            dst_ref=out_ref.at[sender],
            send_sem=send_sem.at[offset],
            recv_sem=recv_sem.at[offset],
            device_id=device(sender),
            device_id_type=MESH,
        )

    local = pltpu.make_async_copy(source(me), out_ref.at[me], local_sem)
    local.start()
    barrier = pltpu.get_barrier_semaphore()
    for offset in range(1, count):
        peer = lax.rem(me + offset, count)
        pl.semaphore_signal(barrier, inc=1, device_id=device(peer), device_id_type=MESH)
    pl.semaphore_wait(barrier, count - 1)
    for offset in range(1, count):
        copy(offset).start()
    local.wait()
    for offset in range(1, count):
        copy(offset).wait_send()
    for offset in range(1, count):
        landing(offset).wait_recv()


def exchange(x, group, axes, sizes, same, kernel_id):
    count = math.prod(sizes[a] for a in group)
    block = x.shape if same else x.shape[1:]
    kernel = functools.partial(exchange_kernel, axes=axes, sizes=sizes, group=group, same=same)
    return pl.pallas_call(
        kernel,
        out_shape=jax.ShapeDtypeStruct((count,) + tuple(block), x.dtype),
        in_specs=[pl.BlockSpec(memory_space=pl.ANY)],
        out_specs=pl.BlockSpec(memory_space=pl.ANY),
        scratch_shapes=[
            pltpu.SemaphoreType.DMA((count,)),
            pltpu.SemaphoreType.DMA((count,)),
            pltpu.SemaphoreType.DMA(()),
        ],
        compiler_params=pltpu.CompilerParams(collective_id=kernel_id, has_side_effects=True),
    )(x)


def make_body(axes, sizes):
    n_row, n_col, n_pl = sizes["prow"], sizes["pcol"], sizes["pl"]
    swap = [(c * n_col + r, r * n_col + c) for r in range(n_row) for c in range(n_col)]
    sibling = [(r, r ^ 1) for r in range(n_row)]
    ex = functools.partial(exchange, axes=axes, sizes=sizes)

    def body(factor_cols, modal_at_loads, mode_shapes, natural_freq, damping):
        in_phase, quadrature = transfer_pair(natural_freq, damping)
        modes = modal_at_loads.shape[0]
        block = modes // (n_row * n_col)
        partial_load = jnp.dot(modal_at_loads, factor_cols, preferred_element_type=jnp.float32)
        pieces = ex(partial_load.reshape(n_row * n_col, block, -1), ("prow", "pcol"), same=False, kernel_id=0)
        own_rows = jnp.sum(pieces, axis=0).astype(jnp.bfloat16)
        modal_load = ex(own_rows, ("prow", "pcol"), same=True, kernel_id=1).reshape(modes, -1)
        modal_wide = modal_load.astype(jnp.float32)
        pseudo = jnp.concatenate(
            [
                (in_phase[:, None] * modal_wide).astype(jnp.bfloat16),
                (quadrature[:, None] * modal_wide).astype(jnp.bfloat16),
            ],
            axis=1,
        )
        row, col = lax.axis_index("prow"), lax.axis_index("pcol")
        first_row = (col * n_row + row) * block
        own_pseudo = lax.dynamic_slice_in_dim(pseudo, first_row, block, 0)
        partial_gram = outer_rows(own_pseudo, pseudo).astype(jnp.bfloat16)
        chunk = modes // n_pl
        by_chunk = partial_gram.reshape(block, n_pl, chunk).transpose(1, 0, 2)
        gram_sums = ex(by_chunk, ("pl",), same=False, kernel_id=2)
        gram_piece = jnp.sum(gram_sums.astype(jnp.float32), axis=0).astype(jnp.bfloat16)
        gram_all = ex(gram_piece, ("prow", "pl"), same=True, kernel_id=3)
        gram_panel = (
            gram_all.reshape(n_row, n_pl, block, chunk).transpose(0, 2, 1, 3).reshape(n_row * block, modes)
        )
        weighted_part = outer_rows(mode_shapes, gram_panel).astype(jnp.bfloat16)
        weighted_all = ex(weighted_part, ("pcol",), same=True, kernel_id=4)
        weighted = weighted_all.transpose(1, 0, 2).reshape(weighted_part.shape[0], modes)
        half = modes // 2
        send_half = lax.dynamic_slice_in_dim(mode_shapes, (col % 2) * half, half, 1)
        panel_piece = lax.ppermute(send_half, ("prow", "pcol"), swap)
        panel_mine = lax.all_gather(panel_piece, "pl", axis=0, tiled=True)
        panel_mine, weighted = lax.optimization_barrier((panel_mine, weighted))
        panel_other = lax.ppermute(panel_mine, "prow", sibling)
        core = row % 2
        weighted_mine = lax.dynamic_slice_in_dim(weighted, core * half, half, 1)
        weighted_other = lax.dynamic_slice_in_dim(weighted, (1 - core) * half, half, 1)
        return outer_rows(weighted_mine, panel_mine) + outer_rows(weighted_other, panel_other)

    return body


def solution(mesh):
    in_specs = (
        P(("prow", "pcol"), "pl"),
        P(None, ("prow", "pcol")),
        P(("prow", "pl"), None),
        P(),
        P(),
    )
    out_specs = P(("prow", "pl"), "pcol")
    axes = tuple(mesh.axis_names)
    body = make_body(axes, dict(mesh.shape))
    return jax.shard_map(body, mesh=mesh, in_specs=in_specs, out_specs=out_specs, check_vma=False)
```

```python
import functools
import math

import jax
import jax.numpy as jnp
from jax import lax
from jax.experimental import pallas as pl
from jax.experimental.pallas import tpu as pltpu
from jax.sharding import PartitionSpec as P

MESH = pl.DeviceIdType.MESH


def transfer_pair(natural_freq, damping):
    detuning = natural_freq * natural_freq - 1.0
    damper = 2.0 * damping * natural_freq
    modulus = detuning * detuning + damper * damper
    return (detuning / modulus, -damper / modulus)


def outer_rows(left_rows, right_rows):
    return lax.dot_general(
        left_rows, right_rows, (((1,), (1,)), ((), ())), preferred_element_type=jnp.float32
    )


def factor_table(sizes):
    return {
        "zh": ("prow", sizes["prow"] // 2, 2),
        "core": ("prow", 2, 1),
        "pcol": ("pcol", sizes["pcol"], 1),
        "pl": ("pl", sizes["pl"], 1),
    }


def exchange_kernel(x_ref, out_ref, send_sem, recv_sem, local_sem, *, axes, factors, group, same):
    coords = {a: lax.axis_index(a) for a in axes}

    def value(f):
        axis, size, stride = factors[f]
        return lax.rem(coords[axis] // stride, size)

    count = math.prod(factors[f][1] for f in group)
    me = 0
    for f in group:
        me = me * factors[f][1] + value(f)

    def device(member):
        place = dict(coords)
        for f in reversed(group):
            axis, size, stride = factors[f]
            place[axis] = place[axis] + (lax.rem(member, size) - value(f)) * stride
            member = member // size
        return tuple(place[a] for a in axes)

    def source(member):
        return x_ref if same else x_ref.at[member]

    def copy(offset):
        peer = lax.rem(me + offset, count)
        return pltpu.make_async_remote_copy(
            src_ref=source(peer),
            dst_ref=out_ref.at[me],
            send_sem=send_sem.at[offset],
            recv_sem=recv_sem.at[offset],
            device_id=device(peer),
            device_id_type=MESH,
        )

    def landing(offset):
        sender = lax.rem(me + count - offset, count)
        return pltpu.make_async_remote_copy(
            src_ref=source(me),
            dst_ref=out_ref.at[sender],
            send_sem=send_sem.at[offset],
            recv_sem=recv_sem.at[offset],
            device_id=device(sender),
            device_id_type=MESH,
        )

    local = pltpu.make_async_copy(source(me), out_ref.at[me], local_sem)
    local.start()
    barrier = pltpu.get_barrier_semaphore()
    for offset in range(1, count):
        peer = lax.rem(me + offset, count)
        pl.semaphore_signal(barrier, inc=1, device_id=device(peer), device_id_type=MESH)
    pl.semaphore_wait(barrier, count - 1)
    for offset in range(1, count):
        copy(offset).start()
    local.wait()
    for offset in range(1, count):
        copy(offset).wait_send()
    for offset in range(1, count):
        landing(offset).wait_recv()


class Exchanger:
    def __init__(self, axes, sizes):
        self.axes, self.factors, self.calls = axes, factor_table(sizes), 0

    def __call__(self, x, group, same):
        count = math.prod(self.factors[f][1] for f in group)
        block = x.shape if same else x.shape[1:]
        if count == 1:
            return x[None] if same else x
        kernel = functools.partial(
            exchange_kernel, axes=self.axes, factors=self.factors, group=group, same=same
        )
        self.calls += 1
        return pl.pallas_call(
            kernel,
            out_shape=jax.ShapeDtypeStruct((count,) + tuple(block), x.dtype),
            in_specs=[pl.BlockSpec(memory_space=pl.ANY)],
            out_specs=pl.BlockSpec(memory_space=pl.ANY),
            scratch_shapes=[
                pltpu.SemaphoreType.DMA((count,)),
                pltpu.SemaphoreType.DMA((count,)),
                pltpu.SemaphoreType.DMA(()),
            ],
            compiler_params=pltpu.CompilerParams(collective_id=self.calls, has_side_effects=True),
        )(x)


def make_body(axes, sizes):
    n_row, n_col, n_pl = sizes["prow"], sizes["pcol"], sizes["pl"]
    swap = [(c * n_col + r, r * n_col + c) for r in range(n_row) for c in range(n_col)]
    sibling = [(r, r ^ 1) for r in range(n_row)]
    n_zh = n_row // 2

    def body(factor_cols, modal_at_loads, mode_shapes, natural_freq, damping):
        ex = Exchanger(axes, sizes)
        in_phase, quadrature = transfer_pair(natural_freq, damping)
        modes = modal_at_loads.shape[0]
        block = modes // (n_row * n_col)
        partial_load = jnp.dot(modal_at_loads, factor_cols, preferred_element_type=jnp.float32)
        width = partial_load.shape[1]
        sums = jnp.sum(ex(partial_load.reshape(2, modes // 2, width), ("core",), same=False), axis=0)
        sums = jnp.sum(ex(sums.reshape(n_col, -1, width), ("pcol",), same=False), axis=0)
        sums = jnp.sum(ex(sums.reshape(n_zh, -1, width), ("zh",), same=False), axis=0)
        gathered = ex(sums.astype(jnp.bfloat16), ("zh",), same=True).reshape(-1, width)
        gathered = ex(gathered, ("pcol",), same=True).reshape(-1, width)
        modal_load = ex(gathered, ("core",), same=True).reshape(modes, width)
        modal_wide = modal_load.astype(jnp.float32)
        pseudo = jnp.concatenate(
            [
                (in_phase[:, None] * modal_wide).astype(jnp.bfloat16),
                (quadrature[:, None] * modal_wide).astype(jnp.bfloat16),
            ],
            axis=1,
        )
        row, col = lax.axis_index("prow"), lax.axis_index("pcol")
        first_row = (col * n_row + row) * block
        own_pseudo = lax.dynamic_slice_in_dim(pseudo, first_row, block, 0)
        partial_gram = outer_rows(own_pseudo, pseudo).astype(jnp.bfloat16)
        chunk = modes // n_pl
        by_chunk = partial_gram.reshape(block, n_pl, chunk).transpose(1, 0, 2)
        gram_sums = ex(by_chunk, ("pl",), same=False)
        gram_piece = jnp.sum(gram_sums.astype(jnp.float32), axis=0).astype(jnp.bfloat16)
        gram_all = ex(ex(ex(gram_piece, ("zh",), same=True), ("pl",), same=True), ("core",), same=True)
        gram_panel = gram_all.transpose(2, 0, 3, 1, 4).reshape(n_row * block, modes)
        weighted_part = outer_rows(mode_shapes, gram_panel).astype(jnp.bfloat16)
        weighted_all = ex(weighted_part, ("pcol",), same=True)
        weighted = weighted_all.transpose(1, 0, 2).reshape(weighted_part.shape[0], modes)
        half = modes // 2
        send_half = lax.dynamic_slice_in_dim(mode_shapes, (col % 2) * half, half, 1)
        panel_piece = lax.ppermute(send_half, ("prow", "pcol"), swap)
        panel_mine = lax.all_gather(panel_piece, "pl", axis=0, tiled=True)
        panel_mine, weighted = lax.optimization_barrier((panel_mine, weighted))
        panel_other = lax.ppermute(panel_mine, "prow", sibling)
        core = row % 2
        weighted_mine = lax.dynamic_slice_in_dim(weighted, core * half, half, 1)
        weighted_other = lax.dynamic_slice_in_dim(weighted, (1 - core) * half, half, 1)
        return outer_rows(weighted_mine, panel_mine) + outer_rows(weighted_other, panel_other)

    return body


def solution(mesh):
    in_specs = (
        P(("prow", "pcol"), "pl"),
        P(None, ("prow", "pcol")),
        P(("prow", "pl"), None),
        P(),
        P(),
    )
    out_specs = P(("prow", "pl"), "pcol")
    axes = tuple(mesh.axis_names)
    body = make_body(axes, dict(mesh.shape))
    return jax.shard_map(body, mesh=mesh, in_specs=in_specs, out_specs=out_specs, check_vma=False)
```

```python
import functools
import math

import jax
import jax.numpy as jnp
from jax import lax
from jax.experimental import pallas as pl
from jax.experimental.pallas import tpu as pltpu
from jax.sharding import PartitionSpec as P

MESH = pl.DeviceIdType.MESH


def transfer_pair(natural_freq, damping):
    detuning = natural_freq * natural_freq - 1.0
    damper = 2.0 * damping * natural_freq
    modulus = detuning * detuning + damper * damper
    return (detuning / modulus, -damper / modulus)


def outer_rows(left_rows, right_rows):
    return lax.dot_general(
        left_rows, right_rows, (((1,), (1,)), ((), ())), preferred_element_type=jnp.float32
    )


def factor_table(sizes):
    return {
        "zh": ("prow", sizes["prow"] // 2, 2),
        "core": ("prow", 2, 1),
        "pcol": ("pcol", sizes["pcol"], 1),
        "pl": ("pl", sizes["pl"], 1),
    }


def exchange_kernel(x_ref, out_ref, send_sem, recv_sem, local_sem, *, axes, factors, group, same):
    coords = {a: lax.axis_index(a) for a in axes}

    def value(f):
        axis, size, stride = factors[f]
        return lax.rem(coords[axis] // stride, size)

    count = math.prod(factors[f][1] for f in group)
    me = 0
    for f in group:
        me = me * factors[f][1] + value(f)

    def device(member):
        place = dict(coords)
        for f in reversed(group):
            axis, size, stride = factors[f]
            place[axis] = place[axis] + (lax.rem(member, size) - value(f)) * stride
            member = member // size
        return tuple(place[a] for a in axes)

    def source(member):
        return x_ref if same else x_ref.at[member]

    def copy(offset):
        peer = lax.rem(me + offset, count)
        return pltpu.make_async_remote_copy(
            src_ref=source(peer),
            dst_ref=out_ref.at[me],
            send_sem=send_sem.at[offset],
            recv_sem=recv_sem.at[offset],
            device_id=device(peer),
            device_id_type=MESH,
        )

    def landing(offset):
        sender = lax.rem(me + count - offset, count)
        return pltpu.make_async_remote_copy(
            src_ref=source(me),
            dst_ref=out_ref.at[sender],
            send_sem=send_sem.at[offset],
            recv_sem=recv_sem.at[offset],
            device_id=device(sender),
            device_id_type=MESH,
        )

    local = pltpu.make_async_copy(source(me), out_ref.at[me], local_sem)
    local.start()
    barrier = pltpu.get_barrier_semaphore()
    for offset in range(1, count):
        peer = lax.rem(me + offset, count)
        pl.semaphore_signal(barrier, inc=1, device_id=device(peer), device_id_type=MESH)
    pl.semaphore_wait(barrier, count - 1)
    for offset in range(1, count):
        copy(offset).start()
    local.wait()
    for offset in range(1, count):
        copy(offset).wait_send()
    for offset in range(1, count):
        landing(offset).wait_recv()


class Exchanger:
    def __init__(self, axes, sizes):
        self.axes, self.factors, self.calls = axes, factor_table(sizes), 0

    def __call__(self, x, group, same):
        count = math.prod(self.factors[f][1] for f in group)
        block = x.shape if same else x.shape[1:]
        if count == 1:
            return x[None] if same else x
        kernel = functools.partial(
            exchange_kernel, axes=self.axes, factors=self.factors, group=group, same=same
        )
        self.calls += 1
        return pl.pallas_call(
            kernel,
            out_shape=jax.ShapeDtypeStruct((count,) + tuple(block), x.dtype),
            in_specs=[pl.BlockSpec(memory_space=pl.ANY)],
            out_specs=pl.BlockSpec(memory_space=pl.ANY),
            scratch_shapes=[
                pltpu.SemaphoreType.DMA((count,)),
                pltpu.SemaphoreType.DMA((count,)),
                pltpu.SemaphoreType.DMA(()),
            ],
            compiler_params=pltpu.CompilerParams(collective_id=self.calls, has_side_effects=True),
        )(x)


def make_body(axes, sizes):
    n_row, n_col, n_pl = sizes["prow"], sizes["pcol"], sizes["pl"]
    swap = [(c * n_col + r, r * n_col + c) for r in range(n_row) for c in range(n_col)]
    sibling = [(r, r ^ 1) for r in range(n_row)]
    n_zh = n_row // 2

    def beside_sibling(part, core):
        other = lax.ppermute(part, "prow", sibling)
        first, second = jnp.where(core == 0, part, other), jnp.where(core == 0, other, part)
        return jnp.concatenate([first, second], axis=0)

    def body(factor_cols, modal_at_loads, mode_shapes, natural_freq, damping):
        ex = Exchanger(axes, sizes)
        in_phase, quadrature = transfer_pair(natural_freq, damping)
        modes = modal_at_loads.shape[0]
        block = modes // (n_row * n_col)
        row, col = lax.axis_index("prow"), lax.axis_index("pcol")
        partial_load = jnp.dot(modal_at_loads, factor_cols, preferred_element_type=jnp.float32)
        width = partial_load.shape[1]
        core = row % 2
        mine = lax.dynamic_slice_in_dim(partial_load, core * (modes // 2), modes // 2, 0)
        theirs = lax.dynamic_slice_in_dim(partial_load, (1 - core) * (modes // 2), modes // 2, 0)
        sums = mine + lax.ppermute(theirs, "prow", sibling)
        sums = jnp.sum(ex(sums.reshape(n_col, -1, width), ("pcol",), same=False), axis=0)
        sums = jnp.sum(ex(sums.reshape(n_zh, -1, width), ("zh",), same=False), axis=0)
        gathered = ex(sums.astype(jnp.bfloat16), ("zh",), same=True).reshape(-1, width)
        gathered = ex(gathered, ("pcol",), same=True).reshape(-1, width)
        modal_load = beside_sibling(gathered, core)
        modal_wide = modal_load.astype(jnp.float32)
        pseudo = jnp.concatenate(
            [
                (in_phase[:, None] * modal_wide).astype(jnp.bfloat16),
                (quadrature[:, None] * modal_wide).astype(jnp.bfloat16),
            ],
            axis=1,
        )
        first_row = (col * n_row + row) * block
        own_pseudo = lax.dynamic_slice_in_dim(pseudo, first_row, block, 0)
        partial_gram = outer_rows(own_pseudo, pseudo).astype(jnp.bfloat16)
        chunk = modes // n_pl
        by_chunk = partial_gram.reshape(block, n_pl, chunk).transpose(1, 0, 2)
        gram_sums = ex(by_chunk, ("pl",), same=False)
        gram_piece = jnp.sum(gram_sums.astype(jnp.float32), axis=0).astype(jnp.bfloat16)
        gram_all = ex(ex(gram_piece, ("zh",), same=True), ("pl",), same=True)
        gram_all = beside_sibling(gram_all[None], core)
        gram_panel = gram_all.transpose(2, 0, 3, 1, 4).reshape(n_row * block, modes)
        weighted_part = outer_rows(mode_shapes, gram_panel).astype(jnp.bfloat16)
        weighted_all = ex(weighted_part, ("pcol",), same=True)
        weighted = weighted_all.transpose(1, 0, 2).reshape(weighted_part.shape[0], modes)
        half = modes // 2
        send_half = lax.dynamic_slice_in_dim(mode_shapes, (col % 2) * half, half, 1)
        panel_piece = lax.ppermute(send_half, ("prow", "pcol"), swap)
        panel_mine = lax.all_gather(panel_piece, "pl", axis=0, tiled=True)
        panel_mine, weighted = lax.optimization_barrier((panel_mine, weighted))
        panel_other = lax.ppermute(panel_mine, "prow", sibling)
        weighted_mine = lax.dynamic_slice_in_dim(weighted, core * half, half, 1)
        weighted_other = lax.dynamic_slice_in_dim(weighted, (1 - core) * half, half, 1)
        return outer_rows(weighted_mine, panel_mine) + outer_rows(weighted_other, panel_other)

    return body


def solution(mesh):
    in_specs = (
        P(("prow", "pcol"), "pl"),
        P(None, ("prow", "pcol")),
        P(("prow", "pl"), None),
        P(),
        P(),
    )
    out_specs = P(("prow", "pl"), "pcol")
    axes = tuple(mesh.axis_names)
    body = make_body(axes, dict(mesh.shape))
    return jax.shard_map(body, mesh=mesh, in_specs=in_specs, out_specs=out_specs, check_vma=False)
```

```python
import functools
import math

import jax
import jax.numpy as jnp
from jax import lax
from jax.experimental import pallas as pl
from jax.experimental.pallas import tpu as pltpu
from jax.sharding import PartitionSpec as P

MESH = pl.DeviceIdType.MESH


def transfer_pair(natural_freq, damping):
    detuning = natural_freq * natural_freq - 1.0
    damper = 2.0 * damping * natural_freq
    modulus = detuning * detuning + damper * damper
    return (detuning / modulus, -damper / modulus)


def outer_rows(left_rows, right_rows):
    return lax.dot_general(
        left_rows, right_rows, (((1,), (1,)), ((), ())), preferred_element_type=jnp.float32
    )


def factor_table(sizes):
    return {
        "zh": ("prow", sizes["prow"] // 2, 2),
        "core": ("prow", 2, 1),
        "pcol": ("pcol", sizes["pcol"], 1),
        "pl": ("pl", sizes["pl"], 1),
    }


def exchange_kernel(x_ref, out_ref, send_sem, recv_sem, local_sem, *, axes, factors, group, same):
    coords = {a: lax.axis_index(a) for a in axes}

    def value(f):
        axis, size, stride = factors[f]
        return lax.rem(coords[axis] // stride, size)

    count = math.prod(factors[f][1] for f in group)
    me = 0
    for f in group:
        me = me * factors[f][1] + value(f)

    def device(member):
        place = dict(coords)
        for f in reversed(group):
            axis, size, stride = factors[f]
            place[axis] = place[axis] + (lax.rem(member, size) - value(f)) * stride
            member = member // size
        return tuple(place[a] for a in axes)

    def source(member):
        return x_ref if same else x_ref.at[member]

    def copy(offset):
        peer = lax.rem(me + offset, count)
        return pltpu.make_async_remote_copy(
            src_ref=source(peer),
            dst_ref=out_ref.at[me],
            send_sem=send_sem.at[offset],
            recv_sem=recv_sem.at[offset],
            device_id=device(peer),
            device_id_type=MESH,
        )

    def landing(offset):
        sender = lax.rem(me + count - offset, count)
        return pltpu.make_async_remote_copy(
            src_ref=source(me),
            dst_ref=out_ref.at[sender],
            send_sem=send_sem.at[offset],
            recv_sem=recv_sem.at[offset],
            device_id=device(sender),
            device_id_type=MESH,
        )

    local = pltpu.make_async_copy(source(me), out_ref.at[me], local_sem)
    local.start()
    barrier = pltpu.get_barrier_semaphore()
    for offset in range(1, count):
        peer = lax.rem(me + offset, count)
        pl.semaphore_signal(barrier, inc=1, device_id=device(peer), device_id_type=MESH)
    pl.semaphore_wait(barrier, count - 1)
    for offset in range(1, count):
        copy(offset).start()
    local.wait()
    for offset in range(1, count):
        copy(offset).wait_send()
    for offset in range(1, count):
        landing(offset).wait_recv()


class Exchanger:
    def __init__(self, axes, sizes):
        self.axes, self.factors, self.calls = axes, factor_table(sizes), 0

    def __call__(self, x, group, same):
        count = math.prod(self.factors[f][1] for f in group)
        block = x.shape if same else x.shape[1:]
        if count == 1:
            return x[None] if same else x
        kernel = functools.partial(
            exchange_kernel, axes=self.axes, factors=self.factors, group=group, same=same
        )
        self.calls += 1
        return pl.pallas_call(
            kernel,
            out_shape=jax.ShapeDtypeStruct((count,) + tuple(block), x.dtype),
            in_specs=[pl.BlockSpec(memory_space=pl.ANY)],
            out_specs=pl.BlockSpec(memory_space=pl.ANY),
            scratch_shapes=[
                pltpu.SemaphoreType.DMA((count,)),
                pltpu.SemaphoreType.DMA((count,)),
                pltpu.SemaphoreType.DMA(()),
            ],
            compiler_params=pltpu.CompilerParams(collective_id=self.calls, has_side_effects=True),
        )(x)


def make_body(axes, sizes):
    n_row, n_col, n_pl = sizes["prow"], sizes["pcol"], sizes["pl"]
    swap = [(c * n_col + r, r * n_col + c) for r in range(n_row) for c in range(n_col)]
    sibling = [(r, r ^ 1) for r in range(n_row)]
    n_zh = n_row // 2

    def beside_sibling(part, core):
        other = lax.ppermute(part, "prow", sibling)
        first, second = jnp.where(core == 0, part, other), jnp.where(core == 0, other, part)
        return jnp.concatenate([first, second], axis=0)

    def body(factor_cols, modal_at_loads, mode_shapes, natural_freq, damping):
        ex = Exchanger(axes, sizes)
        in_phase, quadrature = transfer_pair(natural_freq, damping)
        modes = modal_at_loads.shape[0]
        block = modes // (n_row * n_col)
        row, col = lax.axis_index("prow"), lax.axis_index("pcol")
        partial_load = jnp.dot(modal_at_loads, factor_cols, preferred_element_type=jnp.float32)
        width = partial_load.shape[1]
        core = row % 2
        mine = lax.dynamic_slice_in_dim(partial_load, core * (modes // 2), modes // 2, 0)
        theirs = lax.dynamic_slice_in_dim(partial_load, (1 - core) * (modes // 2), modes // 2, 0)
        sums = mine + lax.ppermute(theirs, "prow", sibling)
        sums = jnp.sum(ex(sums.reshape(n_col, -1, width), ("pcol",), same=False), axis=0)
        gathered = jnp.sum(ex(sums, ("zh",), same=True), axis=0).astype(jnp.bfloat16)
        gathered = ex(gathered, ("pcol",), same=True).reshape(-1, width)
        modal_load = beside_sibling(gathered, core)
        modal_wide = modal_load.astype(jnp.float32)
        pseudo = jnp.concatenate(
            [
                (in_phase[:, None] * modal_wide).astype(jnp.bfloat16),
                (quadrature[:, None] * modal_wide).astype(jnp.bfloat16),
            ],
            axis=1,
        )
        first_row = (col * n_row + row) * block
        own_pseudo = lax.dynamic_slice_in_dim(pseudo, first_row, block, 0)
        partial_gram = outer_rows(own_pseudo, pseudo).astype(jnp.bfloat16)
        chunk = modes // n_pl
        by_chunk = partial_gram.reshape(block, n_pl, chunk).transpose(1, 0, 2)
        gram_sums = ex(by_chunk, ("pl",), same=False)
        gram_piece = jnp.sum(gram_sums.astype(jnp.float32), axis=0).astype(jnp.bfloat16)
        gram_all = ex(ex(gram_piece, ("zh",), same=True), ("pl",), same=True)
        gram_all = beside_sibling(gram_all[None], core)
        gram_panel = gram_all.transpose(2, 0, 3, 1, 4).reshape(n_row * block, modes)
        half = modes // 2
        send_half = lax.dynamic_slice_in_dim(mode_shapes, (col % 2) * half, half, 1)
        panel_piece = lax.ppermute(send_half, ("prow", "pcol"), swap)
        panel_mine = lax.all_gather(panel_piece, "pl", axis=0, tiled=True)
        panel_mine, gram_panel = lax.optimization_barrier((panel_mine, gram_panel))
        panel_other = lax.ppermute(panel_mine, "prow", sibling)
        weighted_part = outer_rows(mode_shapes, gram_panel).astype(jnp.bfloat16)
        weighted_all = ex(weighted_part, ("pcol",), same=True)
        weighted = weighted_all.transpose(1, 0, 2).reshape(weighted_part.shape[0], modes)
        weighted_mine = lax.dynamic_slice_in_dim(weighted, core * half, half, 1)
        weighted_other = lax.dynamic_slice_in_dim(weighted, (1 - core) * half, half, 1)
        return outer_rows(weighted_mine, panel_mine) + outer_rows(weighted_other, panel_other)

    return body


def solution(mesh):
    in_specs = (
        P(("prow", "pcol"), "pl"),
        P(None, ("prow", "pcol")),
        P(("prow", "pl"), None),
        P(),
        P(),
    )
    out_specs = P(("prow", "pl"), "pcol")
    axes = tuple(mesh.axis_names)
    body = make_body(axes, dict(mesh.shape))
    return jax.shard_map(body, mesh=mesh, in_specs=in_specs, out_specs=out_specs, check_vma=False)
```

```python
import functools
import math

import jax
import jax.numpy as jnp
from jax import lax
from jax.experimental import pallas as pl
from jax.experimental.pallas import tpu as pltpu
from jax.sharding import PartitionSpec as P

MESH = pl.DeviceIdType.MESH


def transfer_pair(natural_freq, damping):
    detuning = natural_freq * natural_freq - 1.0
    damper = 2.0 * damping * natural_freq
    modulus = detuning * detuning + damper * damper
    return (detuning / modulus, -damper / modulus)


def outer_rows(left_rows, right_rows):
    return lax.dot_general(
        left_rows, right_rows, (((1,), (1,)), ((), ())), preferred_element_type=jnp.float32
    )


def factor_table(sizes):
    return {
        "zh": ("prow", sizes["prow"] // 2, 2),
        "core": ("prow", 2, 1),
        "pcol": ("pcol", sizes["pcol"], 1),
        "pl": ("pl", sizes["pl"], 1),
    }


def exchange_kernel(x_ref, out_ref, send_sem, recv_sem, local_sem, *, axes, factors, group, same):
    coords = {a: lax.axis_index(a) for a in axes}

    def value(f):
        axis, size, stride = factors[f]
        return lax.rem(coords[axis] // stride, size)

    count = math.prod(factors[f][1] for f in group)
    me = 0
    for f in group:
        me = me * factors[f][1] + value(f)

    def device(member):
        place = dict(coords)
        for f in reversed(group):
            axis, size, stride = factors[f]
            place[axis] = place[axis] + (lax.rem(member, size) - value(f)) * stride
            member = member // size
        return tuple(place[a] for a in axes)

    def source(member):
        return x_ref if same else x_ref.at[member]

    def copy(offset):
        peer = lax.rem(me + offset, count)
        return pltpu.make_async_remote_copy(
            src_ref=source(peer),
            dst_ref=out_ref.at[me],
            send_sem=send_sem.at[offset],
            recv_sem=recv_sem.at[offset],
            device_id=device(peer),
            device_id_type=MESH,
        )

    def landing(offset):
        sender = lax.rem(me + count - offset, count)
        return pltpu.make_async_remote_copy(
            src_ref=source(me),
            dst_ref=out_ref.at[sender],
            send_sem=send_sem.at[offset],
            recv_sem=recv_sem.at[offset],
            device_id=device(sender),
            device_id_type=MESH,
        )

    local = pltpu.make_async_copy(source(me), out_ref.at[me], local_sem)
    local.start()
    barrier = pltpu.get_barrier_semaphore()
    for offset in range(1, count):
        peer = lax.rem(me + offset, count)
        pl.semaphore_signal(barrier, inc=1, device_id=device(peer), device_id_type=MESH)
    pl.semaphore_wait(barrier, count - 1)
    for offset in range(1, count):
        copy(offset).start()
    local.wait()
    for offset in range(1, count):
        copy(offset).wait_send()
    for offset in range(1, count):
        landing(offset).wait_recv()


class Exchanger:
    def __init__(self, axes, sizes):
        self.axes, self.factors, self.calls = axes, factor_table(sizes), 0

    def __call__(self, x, group, same):
        count = math.prod(self.factors[f][1] for f in group)
        block = x.shape if same else x.shape[1:]
        if count == 1:
            return x[None] if same else x
        kernel = functools.partial(
            exchange_kernel, axes=self.axes, factors=self.factors, group=group, same=same
        )
        self.calls += 1
        return pl.pallas_call(
            kernel,
            out_shape=jax.ShapeDtypeStruct((count,) + tuple(block), x.dtype),
            in_specs=[pl.BlockSpec(memory_space=pl.ANY)],
            out_specs=pl.BlockSpec(memory_space=pl.ANY),
            scratch_shapes=[
                pltpu.SemaphoreType.DMA((count,)),
                pltpu.SemaphoreType.DMA((count,)),
                pltpu.SemaphoreType.DMA(()),
            ],
            compiler_params=pltpu.CompilerParams(collective_id=self.calls, has_side_effects=True),
        )(x)


def make_body(axes, sizes):
    n_row, n_col, n_pl = sizes["prow"], sizes["pcol"], sizes["pl"]
    swap = [(c * n_col + r, r * n_col + c) for r in range(n_row) for c in range(n_col)]
    sibling = [(r, r ^ 1) for r in range(n_row)]
    n_zh = n_row // 2

    def beside_sibling(part, core):
        other = lax.ppermute(part, "prow", sibling)
        first, second = jnp.where(core == 0, part, other), jnp.where(core == 0, other, part)
        return jnp.concatenate([first, second], axis=0)

    def body(factor_cols, modal_at_loads, mode_shapes, natural_freq, damping):
        ex = Exchanger(axes, sizes)
        in_phase, quadrature = transfer_pair(natural_freq, damping)
        modes = modal_at_loads.shape[0]
        block = modes // (n_row * n_col)
        row, col = lax.axis_index("prow"), lax.axis_index("pcol")
        partial_load = jnp.dot(modal_at_loads, factor_cols, preferred_element_type=jnp.float32)
        width = partial_load.shape[1]
        core = row % 2
        mine = lax.dynamic_slice_in_dim(partial_load, core * (modes // 2), modes // 2, 0)
        theirs = lax.dynamic_slice_in_dim(partial_load, (1 - core) * (modes // 2), modes // 2, 0)
        wide = lambda part: part.astype(jnp.float32)
        sums = mine + wide(lax.ppermute(theirs.astype(jnp.bfloat16), "prow", sibling))
        pieces = ex(sums.astype(jnp.bfloat16).reshape(n_col, -1, width), ("pcol",), same=False)
        sums = jnp.sum(wide(pieces), axis=0)
        pieces = ex(sums.astype(jnp.bfloat16), ("zh",), same=True)
        gathered = jnp.sum(wide(pieces), axis=0).astype(jnp.bfloat16)
        gathered = ex(gathered, ("pcol",), same=True).reshape(-1, width)
        modal_load = beside_sibling(gathered, core)
        modal_wide = modal_load.astype(jnp.float32)
        pseudo = jnp.concatenate(
            [
                (in_phase[:, None] * modal_wide).astype(jnp.bfloat16),
                (quadrature[:, None] * modal_wide).astype(jnp.bfloat16),
            ],
            axis=1,
        )
        first_row = (col * n_row + row) * block
        own_pseudo = lax.dynamic_slice_in_dim(pseudo, first_row, block, 0)
        partial_gram = outer_rows(own_pseudo, pseudo).astype(jnp.bfloat16)
        chunk = modes // n_pl
        by_chunk = partial_gram.reshape(block, n_pl, chunk).transpose(1, 0, 2)
        gram_sums = ex(by_chunk, ("pl",), same=False)
        gram_piece = jnp.sum(gram_sums.astype(jnp.float32), axis=0).astype(jnp.bfloat16)
        gram_all = ex(ex(gram_piece, ("zh",), same=True), ("pl",), same=True)
        gram_all = beside_sibling(gram_all[None], core)
        gram_panel = gram_all.transpose(2, 0, 3, 1, 4).reshape(n_row * block, modes)
        half = modes // 2
        send_half = lax.dynamic_slice_in_dim(mode_shapes, (col % 2) * half, half, 1)
        panel_piece = lax.ppermute(send_half, ("prow", "pcol"), swap)
        panel_mine = lax.all_gather(panel_piece, "pl", axis=0, tiled=True)
        panel_mine, gram_panel = lax.optimization_barrier((panel_mine, gram_panel))
        panel_other = lax.ppermute(panel_mine, "prow", sibling)
        weighted_part = outer_rows(mode_shapes, gram_panel).astype(jnp.bfloat16)
        weighted_all = ex(weighted_part, ("pcol",), same=True)
        weighted = weighted_all.transpose(1, 0, 2).reshape(weighted_part.shape[0], modes)
        weighted_mine = lax.dynamic_slice_in_dim(weighted, core * half, half, 1)
        weighted_other = lax.dynamic_slice_in_dim(weighted, (1 - core) * half, half, 1)
        return outer_rows(weighted_mine, panel_mine) + outer_rows(weighted_other, panel_other)

    return body


def solution(mesh):
    in_specs = (
        P(("prow", "pcol"), "pl"),
        P(None, ("prow", "pcol")),
        P(("prow", "pl"), None),
        P(),
        P(),
    )
    out_specs = P(("prow", "pl"), "pcol")
    axes = tuple(mesh.axis_names)
    body = make_body(axes, dict(mesh.shape))
    return jax.shard_map(body, mesh=mesh, in_specs=in_specs, out_specs=out_specs, check_vma=False)
```

```python
import functools
import math

import jax
import jax.numpy as jnp
from jax import lax
from jax.experimental import pallas as pl
from jax.experimental.pallas import tpu as pltpu
from jax.sharding import PartitionSpec as P

MESH = pl.DeviceIdType.MESH


def transfer_pair(natural_freq, damping):
    detuning = natural_freq * natural_freq - 1.0
    damper = 2.0 * damping * natural_freq
    modulus = detuning * detuning + damper * damper
    return (detuning / modulus, -damper / modulus)


def outer_rows(left_rows, right_rows):
    return lax.dot_general(
        left_rows, right_rows, (((1,), (1,)), ((), ())), preferred_element_type=jnp.float32
    )


def factor_table(sizes):
    return {
        "zh": ("prow", sizes["prow"] // 2, 2),
        "core": ("prow", 2, 1),
        "pcol": ("pcol", sizes["pcol"], 1),
        "pl": ("pl", sizes["pl"], 1),
        "plz": ("pl", sizes["pl"] // 4, 4),
        "plx": ("pl", 4, 1),
    }


def exchange_kernel(x_ref, out_ref, send_sem, recv_sem, local_sem, *, axes, factors, group, same):
    coords = {a: lax.axis_index(a) for a in axes}

    def value(f):
        axis, size, stride = factors[f]
        return lax.rem(coords[axis] // stride, size)

    count = math.prod(factors[f][1] for f in group)
    me = 0
    for f in group:
        me = me * factors[f][1] + value(f)

    def device(member):
        place = dict(coords)
        for f in reversed(group):
            axis, size, stride = factors[f]
            place[axis] = place[axis] + (lax.rem(member, size) - value(f)) * stride
            member = member // size
        return tuple(place[a] for a in axes)

    def source(member):
        return x_ref if same else x_ref.at[member]

    def copy(offset):
        peer = lax.rem(me + offset, count)
        return pltpu.make_async_remote_copy(
            src_ref=source(peer),
            dst_ref=out_ref.at[me],
            send_sem=send_sem.at[offset],
            recv_sem=recv_sem.at[offset],
            device_id=device(peer),
            device_id_type=MESH,
        )

    def landing(offset):
        sender = lax.rem(me + count - offset, count)
        return pltpu.make_async_remote_copy(
            src_ref=source(me),
            dst_ref=out_ref.at[sender],
            send_sem=send_sem.at[offset],
            recv_sem=recv_sem.at[offset],
            device_id=device(sender),
            device_id_type=MESH,
        )

    local = pltpu.make_async_copy(source(me), out_ref.at[me], local_sem)
    local.start()
    barrier = pltpu.get_barrier_semaphore()
    for offset in range(1, count):
        peer = lax.rem(me + offset, count)
        pl.semaphore_signal(barrier, inc=1, device_id=device(peer), device_id_type=MESH)
    pl.semaphore_wait(barrier, count - 1)
    for offset in range(1, count):
        copy(offset).start()
    local.wait()
    for offset in range(1, count):
        copy(offset).wait_send()
    for offset in range(1, count):
        landing(offset).wait_recv()


class Exchanger:
    def __init__(self, axes, sizes):
        self.axes, self.factors, self.calls = axes, factor_table(sizes), 0

    def __call__(self, x, group, same):
        count = math.prod(self.factors[f][1] for f in group)
        block = x.shape if same else x.shape[1:]
        if count == 1:
            return x[None] if same else x
        kernel = functools.partial(
            exchange_kernel, axes=self.axes, factors=self.factors, group=group, same=same
        )
        self.calls += 1
        return pl.pallas_call(
            kernel,
            out_shape=jax.ShapeDtypeStruct((count,) + tuple(block), x.dtype),
            in_specs=[pl.BlockSpec(memory_space=pl.ANY)],
            out_specs=pl.BlockSpec(memory_space=pl.ANY),
            scratch_shapes=[
                pltpu.SemaphoreType.DMA((count,)),
                pltpu.SemaphoreType.DMA((count,)),
                pltpu.SemaphoreType.DMA(()),
            ],
            compiler_params=pltpu.CompilerParams(collective_id=self.calls, has_side_effects=True),
        )(x)


def make_body(axes, sizes):
    n_row, n_col, n_pl = sizes["prow"], sizes["pcol"], sizes["pl"]
    swap = [(c * n_col + r, r * n_col + c) for r in range(n_row) for c in range(n_col)]
    sibling = [(r, r ^ 1) for r in range(n_row)]
    n_zh = n_row // 2

    def beside_sibling(part, core):
        other = lax.ppermute(part, "prow", sibling)
        first, second = jnp.where(core == 0, part, other), jnp.where(core == 0, other, part)
        return jnp.concatenate([first, second], axis=0)

    def body(factor_cols, modal_at_loads, mode_shapes, natural_freq, damping):
        ex = Exchanger(axes, sizes)
        in_phase, quadrature = transfer_pair(natural_freq, damping)
        modes = modal_at_loads.shape[0]
        block = modes // (n_row * n_col)
        row, col = lax.axis_index("prow"), lax.axis_index("pcol")
        partial_load = jnp.dot(modal_at_loads, factor_cols, preferred_element_type=jnp.float32)
        width = partial_load.shape[1]
        core = row % 2
        mine = lax.dynamic_slice_in_dim(partial_load, core * (modes // 2), modes // 2, 0)
        theirs = lax.dynamic_slice_in_dim(partial_load, (1 - core) * (modes // 2), modes // 2, 0)
        wide = lambda part: part.astype(jnp.float32)
        sums = mine + wide(lax.ppermute(theirs.astype(jnp.bfloat16), "prow", sibling))
        pieces = ex(sums.astype(jnp.bfloat16).reshape(n_col, -1, width), ("pcol",), same=False)
        sums = jnp.sum(wide(pieces), axis=0)
        pieces = ex(sums.astype(jnp.bfloat16), ("zh",), same=True)
        gathered = jnp.sum(wide(pieces), axis=0).astype(jnp.bfloat16)
        gathered = ex(gathered, ("pcol",), same=True).reshape(-1, width)
        modal_load = beside_sibling(gathered, core)
        modal_wide = modal_load.astype(jnp.float32)
        pseudo = jnp.concatenate(
            [
                (in_phase[:, None] * modal_wide).astype(jnp.bfloat16),
                (quadrature[:, None] * modal_wide).astype(jnp.bfloat16),
            ],
            axis=1,
        )
        first_row = (col * n_row + row) * block
        own_pseudo = lax.dynamic_slice_in_dim(pseudo, first_row, block, 0)
        partial_gram = outer_rows(own_pseudo, pseudo).astype(jnp.bfloat16)
        chunk = modes // n_pl
        n_z = n_pl // 4
        by_x = partial_gram.reshape(block, n_z, 4, chunk).transpose(2, 1, 0, 3)
        sums = jnp.sum(ex(by_x, ("plx",), same=False).astype(jnp.float32), axis=0)
        gram_piece = jnp.sum(ex(sums, ("plz",), same=False), axis=0).astype(jnp.bfloat16)
        gram_all = ex(ex(ex(gram_piece, ("zh",), same=True), ("plz",), same=True), ("plx",), same=True)
        gram_all = beside_sibling(gram_all[None], core)
        gram_panel = gram_all.transpose(3, 0, 4, 2, 1, 5).reshape(n_row * block, modes)
        half = modes // 2
        send_half = lax.dynamic_slice_in_dim(mode_shapes, (col % 2) * half, half, 1)
        panel_piece = lax.ppermute(send_half, ("prow", "pcol"), swap)
        panel_mine = lax.all_gather(panel_piece, "pl", axis=0, tiled=True)
        panel_mine, gram_panel = lax.optimization_barrier((panel_mine, gram_panel))
        panel_other = lax.ppermute(panel_mine, "prow", sibling)
        weighted_part = outer_rows(mode_shapes, gram_panel).astype(jnp.bfloat16)
        weighted_all = ex(weighted_part, ("pcol",), same=True)
        weighted = weighted_all.transpose(1, 0, 2).reshape(weighted_part.shape[0], modes)
        weighted_mine = lax.dynamic_slice_in_dim(weighted, core * half, half, 1)
        weighted_other = lax.dynamic_slice_in_dim(weighted, (1 - core) * half, half, 1)
        return outer_rows(weighted_mine, panel_mine) + outer_rows(weighted_other, panel_other)

    return body


def solution(mesh):
    in_specs = (
        P(("prow", "pcol"), "pl"),
        P(None, ("prow", "pcol")),
        P(("prow", "pl"), None),
        P(),
        P(),
    )
    out_specs = P(("prow", "pl"), "pcol")
    axes = tuple(mesh.axis_names)
    body = make_body(axes, dict(mesh.shape))
    return jax.shard_map(body, mesh=mesh, in_specs=in_specs, out_specs=out_specs, check_vma=False)
```

```python
import functools
import math

import jax
import jax.numpy as jnp
from jax import lax
from jax.experimental import pallas as pl
from jax.experimental.pallas import tpu as pltpu
from jax.sharding import PartitionSpec as P

MESH = pl.DeviceIdType.MESH


def transfer_pair(natural_freq, damping):
    detuning = natural_freq * natural_freq - 1.0
    damper = 2.0 * damping * natural_freq
    modulus = detuning * detuning + damper * damper
    return (detuning / modulus, -damper / modulus)


def outer_rows(left_rows, right_rows):
    return lax.dot_general(
        left_rows, right_rows, (((1,), (1,)), ((), ())), preferred_element_type=jnp.float32
    )


def factor_table(sizes):
    return {
        "zh": ("prow", sizes["prow"] // 2, 2),
        "core": ("prow", 2, 1),
        "pcol": ("pcol", sizes["pcol"], 1),
        "pl": ("pl", sizes["pl"], 1),
    }


def exchange_kernel(x_ref, out_ref, send_sem, recv_sem, local_sem, *, axes, factors, group, same):
    coords = {a: lax.axis_index(a) for a in axes}

    def value(f):
        axis, size, stride = factors[f]
        return lax.rem(coords[axis] // stride, size)

    count = math.prod(factors[f][1] for f in group)
    me = 0
    for f in group:
        me = me * factors[f][1] + value(f)

    def device(member):
        place = dict(coords)
        for f in reversed(group):
            axis, size, stride = factors[f]
            place[axis] = place[axis] + (lax.rem(member, size) - value(f)) * stride
            member = member // size
        return tuple(place[a] for a in axes)

    def source(member):
        return x_ref if same else x_ref.at[member]

    def copy(offset):
        peer = lax.rem(me + offset, count)
        return pltpu.make_async_remote_copy(
            src_ref=source(peer),
            dst_ref=out_ref.at[me],
            send_sem=send_sem.at[offset],
            recv_sem=recv_sem.at[offset],
            device_id=device(peer),
            device_id_type=MESH,
        )

    def landing(offset):
        sender = lax.rem(me + count - offset, count)
        return pltpu.make_async_remote_copy(
            src_ref=source(me),
            dst_ref=out_ref.at[sender],
            send_sem=send_sem.at[offset],
            recv_sem=recv_sem.at[offset],
            device_id=device(sender),
            device_id_type=MESH,
        )

    local = pltpu.make_async_copy(source(me), out_ref.at[me], local_sem)
    local.start()
    barrier = pltpu.get_barrier_semaphore()
    for offset in range(1, count):
        peer = lax.rem(me + offset, count)
        pl.semaphore_signal(barrier, inc=1, device_id=device(peer), device_id_type=MESH)
    pl.semaphore_wait(barrier, count - 1)
    for offset in range(1, count):
        copy(offset).start()
    local.wait()
    for offset in range(1, count):
        copy(offset).wait_send()
    for offset in range(1, count):
        landing(offset).wait_recv()


def modal_sum_kernel(x_ref, out_ref, got, coll, part_out, part_in, send_a, recv_a, send_b, recv_b,
                     send_c, recv_c, *, axes, factors):
    coords = {a: lax.axis_index(a) for a in axes}

    def value(f):
        axis, size, stride = factors[f]
        return lax.rem(coords[axis] // stride, size)

    def device(f, v):
        place = dict(coords)
        axis, size, stride = factors[f]
        place[axis] = place[axis] + (v - value(f)) * stride
        return tuple(place[a] for a in axes)

    n = factors["pcol"][1]
    me, half = value("pcol"), value("zh")
    partner = device("zh", 1 - half)
    peer = lambda k: lax.rem(me + k, n)
    sender = lambda k: lax.rem(me + n - k, n)

    def step(src, dst_at, k, to, sems):
        return pltpu.make_async_remote_copy(
            src_ref=src, dst_ref=dst_at, send_sem=sems[0].at[k], recv_sem=sems[1].at[k],
            device_id=to, device_id_type=MESH,
        )

    barrier = pltpu.get_barrier_semaphore()
    for k in range(1, n):
        pl.semaphore_signal(barrier, inc=1, device_id=device("pcol", peer(k)), device_id_type=MESH)
    pl.semaphore_signal(barrier, inc=1, device_id=partner, device_id_type=MESH)
    pl.semaphore_wait(barrier, n)

    for k in range(1, n):
        step(x_ref.at[peer(k)], got.at[me], k, device("pcol", peer(k)), (send_a, recv_a)).start()
    for k in range(1, n):
        step(x_ref.at[peer(k)], got.at[me], k, device("pcol", peer(k)), (send_a, recv_a)).wait_send()
    for k in range(1, n):
        step(x_ref.at[me], got.at[sender(k)], k, device("pcol", sender(k)), (send_a, recv_a)).wait_recv()
    total = x_ref[me].astype(jnp.float32)
    for k in range(1, n):
        total = total + got[sender(k)].astype(jnp.float32)
    part_out[...] = total.astype(part_out.dtype)

    across = pltpu.make_async_remote_copy(
        src_ref=part_out, dst_ref=part_in, send_sem=send_b, recv_sem=recv_b,
        device_id=partner, device_id_type=MESH,
    )
    across.start()
    across.wait_send()
    across.wait_recv()
    coll[me] = (part_out[...].astype(jnp.float32) + part_in[...].astype(jnp.float32)).astype(coll.dtype)

    for k in range(1, n):
        step(coll.at[me], coll.at[me], k, device("pcol", peer(k)), (send_c, recv_c)).start()
    for k in range(1, n):
        step(coll.at[me], coll.at[me], k, device("pcol", peer(k)), (send_c, recv_c)).wait_send()
    for k in range(1, n):
        step(coll.at[me], coll.at[sender(k)], k, device("pcol", sender(k)), (send_c, recv_c)).wait_recv()
    out_ref[...] = coll[...]


def modal_sum(x, axes, sizes):
    n, rows, width = x.shape
    kernel = functools.partial(modal_sum_kernel, axes=axes, factors=factor_table(sizes))
    return pl.pallas_call(
        kernel,
        out_shape=jax.ShapeDtypeStruct(x.shape, x.dtype),
        in_specs=[pl.BlockSpec(memory_space=pltpu.VMEM)],
        out_specs=pl.BlockSpec(memory_space=pltpu.VMEM),
        scratch_shapes=[
            pltpu.VMEM(x.shape, x.dtype),
            pltpu.VMEM(x.shape, x.dtype),
            pltpu.VMEM((rows, width), x.dtype),
            pltpu.VMEM((rows, width), x.dtype),
            pltpu.SemaphoreType.DMA((n,)),
            pltpu.SemaphoreType.DMA((n,)),
            pltpu.SemaphoreType.DMA(()),
            pltpu.SemaphoreType.DMA(()),
            pltpu.SemaphoreType.DMA((n,)),
            pltpu.SemaphoreType.DMA((n,)),
        ],
        compiler_params=pltpu.CompilerParams(collective_id=0, has_side_effects=True),
    )(x)


class Exchanger:
    def __init__(self, axes, sizes):
        self.axes, self.factors, self.calls = axes, factor_table(sizes), 0

    def __call__(self, x, group, same):
        count = math.prod(self.factors[f][1] for f in group)
        block = x.shape if same else x.shape[1:]
        if count == 1:
            return x[None] if same else x
        kernel = functools.partial(
            exchange_kernel, axes=self.axes, factors=self.factors, group=group, same=same
        )
        self.calls += 1
        return pl.pallas_call(
            kernel,
            out_shape=jax.ShapeDtypeStruct((count,) + tuple(block), x.dtype),
            in_specs=[pl.BlockSpec(memory_space=pl.ANY)],
            out_specs=pl.BlockSpec(memory_space=pl.ANY),
            scratch_shapes=[
                pltpu.SemaphoreType.DMA((count,)),
                pltpu.SemaphoreType.DMA((count,)),
                pltpu.SemaphoreType.DMA(()),
            ],
            compiler_params=pltpu.CompilerParams(collective_id=self.calls, has_side_effects=True),
        )(x)


def make_body(axes, sizes):
    n_row, n_col, n_pl = sizes["prow"], sizes["pcol"], sizes["pl"]
    swap = [(c * n_col + r, r * n_col + c) for r in range(n_row) for c in range(n_col)]
    sibling = [(r, r ^ 1) for r in range(n_row)]
    n_zh = n_row // 2

    def beside_sibling(part, core):
        other = lax.ppermute(part, "prow", sibling)
        first, second = jnp.where(core == 0, part, other), jnp.where(core == 0, other, part)
        return jnp.concatenate([first, second], axis=0)

    def body(factor_cols, modal_at_loads, mode_shapes, natural_freq, damping):
        ex = Exchanger(axes, sizes)
        in_phase, quadrature = transfer_pair(natural_freq, damping)
        modes = modal_at_loads.shape[0]
        block = modes // (n_row * n_col)
        row, col = lax.axis_index("prow"), lax.axis_index("pcol")
        partial_load = jnp.dot(modal_at_loads, factor_cols, preferred_element_type=jnp.float32)
        width = partial_load.shape[1]
        core = row % 2
        mine = lax.dynamic_slice_in_dim(partial_load, core * (modes // 2), modes // 2, 0)
        theirs = lax.dynamic_slice_in_dim(partial_load, (1 - core) * (modes // 2), modes // 2, 0)
        wide = lambda part: part.astype(jnp.float32)
        sums = mine + wide(lax.ppermute(theirs.astype(jnp.bfloat16), "prow", sibling))
        pieces = sums.astype(jnp.bfloat16).reshape(n_col, -1, width)
        gathered = modal_sum(pieces, axes, sizes).reshape(-1, width)
        modal_load = beside_sibling(gathered, core)
        modal_wide = modal_load.astype(jnp.float32)
        pseudo = jnp.concatenate(
            [
                (in_phase[:, None] * modal_wide).astype(jnp.bfloat16),
                (quadrature[:, None] * modal_wide).astype(jnp.bfloat16),
            ],
            axis=1,
        )
        first_row = (col * n_row + row) * block
        own_pseudo = lax.dynamic_slice_in_dim(pseudo, first_row, block, 0)
        partial_gram = outer_rows(own_pseudo, pseudo).astype(jnp.bfloat16)
        chunk = modes // n_pl
        by_chunk = partial_gram.reshape(block, n_pl, chunk).transpose(1, 0, 2)
        gram_sums = ex(by_chunk, ("pl",), same=False)
        gram_piece = jnp.sum(gram_sums.astype(jnp.float32), axis=0).astype(jnp.bfloat16)
        gram_all = ex(ex(gram_piece, ("zh",), same=True), ("pl",), same=True)
        gram_all = beside_sibling(gram_all[None], core)
        gram_panel = gram_all.transpose(2, 0, 3, 1, 4).reshape(n_row * block, modes)
        half = modes // 2
        send_half = lax.dynamic_slice_in_dim(mode_shapes, (col % 2) * half, half, 1)
        panel_piece = lax.ppermute(send_half, ("prow", "pcol"), swap)
        panel_mine = lax.all_gather(panel_piece, "pl", axis=0, tiled=True)
        panel_mine, gram_panel = lax.optimization_barrier((panel_mine, gram_panel))
        panel_other = lax.ppermute(panel_mine, "prow", sibling)
        weighted_part = outer_rows(mode_shapes, gram_panel).astype(jnp.bfloat16)
        weighted_all = ex(weighted_part, ("pcol",), same=True)
        weighted = weighted_all.transpose(1, 0, 2).reshape(weighted_part.shape[0], modes)
        weighted_mine = lax.dynamic_slice_in_dim(weighted, core * half, half, 1)
        weighted_other = lax.dynamic_slice_in_dim(weighted, (1 - core) * half, half, 1)
        return outer_rows(weighted_mine, panel_mine) + outer_rows(weighted_other, panel_other)

    return body


def solution(mesh):
    in_specs = (
        P(("prow", "pcol"), "pl"),
        P(None, ("prow", "pcol")),
        P(("prow", "pl"), None),
        P(),
        P(),
    )
    out_specs = P(("prow", "pl"), "pcol")
    axes = tuple(mesh.axis_names)
    body = make_body(axes, dict(mesh.shape))
    return jax.shard_map(body, mesh=mesh, in_specs=in_specs, out_specs=out_specs, check_vma=False)
```

```python
import functools
import math

import jax
import jax.numpy as jnp
from jax import lax
from jax.experimental import pallas as pl
from jax.experimental.pallas import tpu as pltpu
from jax.sharding import PartitionSpec as P

MESH = pl.DeviceIdType.MESH


def transfer_pair(natural_freq, damping):
    detuning = natural_freq * natural_freq - 1.0
    damper = 2.0 * damping * natural_freq
    modulus = detuning * detuning + damper * damper
    return (detuning / modulus, -damper / modulus)


def outer_rows(left_rows, right_rows):
    return lax.dot_general(
        left_rows, right_rows, (((1,), (1,)), ((), ())), preferred_element_type=jnp.float32
    )


def factor_table(sizes):
    return {
        "zh": ("prow", sizes["prow"] // 2, 2),
        "core": ("prow", 2, 1),
        "pcol": ("pcol", sizes["pcol"], 1),
        "pl": ("pl", sizes["pl"], 1),
    }


def exchange_kernel(x_ref, out_ref, send_sem, recv_sem, local_sem, *, axes, factors, group, same):
    coords = {a: lax.axis_index(a) for a in axes}

    def value(f):
        axis, size, stride = factors[f]
        return lax.rem(coords[axis] // stride, size)

    count = math.prod(factors[f][1] for f in group)
    me = 0
    for f in group:
        me = me * factors[f][1] + value(f)

    def device(member):
        place = dict(coords)
        for f in reversed(group):
            axis, size, stride = factors[f]
            place[axis] = place[axis] + (lax.rem(member, size) - value(f)) * stride
            member = member // size
        return tuple(place[a] for a in axes)

    def source(member):
        return x_ref if same else x_ref.at[member]

    def copy(offset):
        peer = lax.rem(me + offset, count)
        return pltpu.make_async_remote_copy(
            src_ref=source(peer),
            dst_ref=out_ref.at[me],
            send_sem=send_sem.at[offset],
            recv_sem=recv_sem.at[offset],
            device_id=device(peer),
            device_id_type=MESH,
        )

    def landing(offset):
        sender = lax.rem(me + count - offset, count)
        return pltpu.make_async_remote_copy(
            src_ref=source(me),
            dst_ref=out_ref.at[sender],
            send_sem=send_sem.at[offset],
            recv_sem=recv_sem.at[offset],
            device_id=device(sender),
            device_id_type=MESH,
        )

    local = pltpu.make_async_copy(source(me), out_ref.at[me], local_sem)
    local.start()
    barrier = pltpu.get_barrier_semaphore()
    for offset in range(1, count):
        peer = lax.rem(me + offset, count)
        pl.semaphore_signal(barrier, inc=1, device_id=device(peer), device_id_type=MESH)
    pl.semaphore_wait(barrier, count - 1)
    for offset in range(1, count):
        copy(offset).start()
    local.wait()
    for offset in range(1, count):
        copy(offset).wait_send()
    for offset in range(1, count):
        landing(offset).wait_recv()


def fused_sum_kernel(x_ref, out_ref, got, coll, part_out, part_in, send_a, recv_a, send_b, recv_b,
                     send_c, recv_c, *, axes, factors, over, add_across):
    coords = {a: lax.axis_index(a) for a in axes}

    def value(f):
        axis, size, stride = factors[f]
        return lax.rem(coords[axis] // stride, size)

    def device(f, v):
        place = dict(coords)
        axis, size, stride = factors[f]
        place[axis] = place[axis] + (v - value(f)) * stride
        return tuple(place[a] for a in axes)

    n = factors[over][1]
    me, half = value(over), value("zh")
    partner = device("zh", 1 - half)
    peer = lambda k: lax.rem(me + k, n)
    sender = lambda k: lax.rem(me + n - k, n)

    def step(src, dst_at, k, to, sems):
        return pltpu.make_async_remote_copy(
            src_ref=src, dst_ref=dst_at, send_sem=sems[0].at[k], recv_sem=sems[1].at[k],
            device_id=to, device_id_type=MESH,
        )

    barrier = pltpu.get_barrier_semaphore()
    for k in range(1, n):
        pl.semaphore_signal(barrier, inc=1, device_id=device(over, peer(k)), device_id_type=MESH)
    pl.semaphore_signal(barrier, inc=1, device_id=partner, device_id_type=MESH)
    pl.semaphore_wait(barrier, n)

    for k in range(1, n):
        step(x_ref.at[peer(k)], got.at[me], k, device(over, peer(k)), (send_a, recv_a)).start()
    for k in range(1, n):
        step(x_ref.at[peer(k)], got.at[me], k, device(over, peer(k)), (send_a, recv_a)).wait_send()
    for k in range(1, n):
        step(x_ref.at[me], got.at[sender(k)], k, device(over, sender(k)), (send_a, recv_a)).wait_recv()
    total = x_ref[me].astype(jnp.float32)
    for k in range(1, n):
        total = total + got[sender(k)].astype(jnp.float32)
    part_out[...] = total.astype(part_out.dtype)

    across = pltpu.make_async_remote_copy(
        src_ref=part_out, dst_ref=part_in, send_sem=send_b, recv_sem=recv_b,
        device_id=partner, device_id_type=MESH,
    )
    across.start()
    across.wait_send()
    across.wait_recv()
    if add_across:
        mine, theirs = part_out[...].astype(jnp.float32), part_in[...].astype(jnp.float32)
        coll[me] = (mine + theirs).astype(coll.dtype)
    else:
        mine, theirs = part_out[...], part_in[...]
        first = jnp.where(half == 0, mine, theirs)
        second = jnp.where(half == 0, theirs, mine)
        coll[me] = jnp.stack([first, second])

    for k in range(1, n):
        step(coll.at[me], coll.at[me], k, device(over, peer(k)), (send_c, recv_c)).start()
    for k in range(1, n):
        step(coll.at[me], coll.at[me], k, device(over, peer(k)), (send_c, recv_c)).wait_send()
    for k in range(1, n):
        step(coll.at[me], coll.at[sender(k)], k, device(over, sender(k)), (send_c, recv_c)).wait_recv()
    out_ref[...] = coll[...]


def fused_sum(x, axes, sizes, over, add_across, kernel_id):
    n, rows, width = x.shape
    block = (rows, width) if add_across else (2, rows, width)
    kernel = functools.partial(
        fused_sum_kernel, axes=axes, factors=factor_table(sizes), over=over, add_across=add_across
    )
    return pl.pallas_call(
        kernel,
        out_shape=jax.ShapeDtypeStruct((n,) + block, x.dtype),
        in_specs=[pl.BlockSpec(memory_space=pltpu.VMEM)],
        out_specs=pl.BlockSpec(memory_space=pltpu.VMEM),
        scratch_shapes=[
            pltpu.VMEM(x.shape, x.dtype),
            pltpu.VMEM((n,) + block, x.dtype),
            pltpu.VMEM((rows, width), x.dtype),
            pltpu.VMEM((rows, width), x.dtype),
            pltpu.SemaphoreType.DMA((n,)),
            pltpu.SemaphoreType.DMA((n,)),
            pltpu.SemaphoreType.DMA(()),
            pltpu.SemaphoreType.DMA(()),
            pltpu.SemaphoreType.DMA((n,)),
            pltpu.SemaphoreType.DMA((n,)),
        ],
        compiler_params=pltpu.CompilerParams(collective_id=kernel_id, has_side_effects=True),
    )(x)


class Exchanger:
    def __init__(self, axes, sizes):
        self.axes, self.factors, self.calls = axes, factor_table(sizes), 0

    def __call__(self, x, group, same):
        count = math.prod(self.factors[f][1] for f in group)
        block = x.shape if same else x.shape[1:]
        if count == 1:
            return x[None] if same else x
        kernel = functools.partial(
            exchange_kernel, axes=self.axes, factors=self.factors, group=group, same=same
        )
        self.calls += 1
        return pl.pallas_call(
            kernel,
            out_shape=jax.ShapeDtypeStruct((count,) + tuple(block), x.dtype),
            in_specs=[pl.BlockSpec(memory_space=pl.ANY)],
            out_specs=pl.BlockSpec(memory_space=pl.ANY),
            scratch_shapes=[
                pltpu.SemaphoreType.DMA((count,)),
                pltpu.SemaphoreType.DMA((count,)),
                pltpu.SemaphoreType.DMA(()),
            ],
            compiler_params=pltpu.CompilerParams(collective_id=self.calls, has_side_effects=True),
        )(x)


def make_body(axes, sizes):
    n_row, n_col, n_pl = sizes["prow"], sizes["pcol"], sizes["pl"]
    swap = [(c * n_col + r, r * n_col + c) for r in range(n_row) for c in range(n_col)]
    sibling = [(r, r ^ 1) for r in range(n_row)]
    n_zh = n_row // 2

    def beside_sibling(part, core):
        other = lax.ppermute(part, "prow", sibling)
        first, second = jnp.where(core == 0, part, other), jnp.where(core == 0, other, part)
        return jnp.concatenate([first, second], axis=0)

    def body(factor_cols, modal_at_loads, mode_shapes, natural_freq, damping):
        ex = Exchanger(axes, sizes)
        in_phase, quadrature = transfer_pair(natural_freq, damping)
        modes = modal_at_loads.shape[0]
        block = modes // (n_row * n_col)
        row, col = lax.axis_index("prow"), lax.axis_index("pcol")
        partial_load = jnp.dot(modal_at_loads, factor_cols, preferred_element_type=jnp.float32)
        width = partial_load.shape[1]
        core = row % 2
        mine = lax.dynamic_slice_in_dim(partial_load, core * (modes // 2), modes // 2, 0)
        theirs = lax.dynamic_slice_in_dim(partial_load, (1 - core) * (modes // 2), modes // 2, 0)
        wide = lambda part: part.astype(jnp.float32)
        sums = mine + wide(lax.ppermute(theirs.astype(jnp.bfloat16), "prow", sibling))
        pieces = sums.astype(jnp.bfloat16).reshape(n_col, -1, width)
        gathered = fused_sum(pieces, axes, sizes, "pcol", True, 100).reshape(-1, width)
        modal_load = beside_sibling(gathered, core)
        modal_wide = modal_load.astype(jnp.float32)
        pseudo = jnp.concatenate(
            [
                (in_phase[:, None] * modal_wide).astype(jnp.bfloat16),
                (quadrature[:, None] * modal_wide).astype(jnp.bfloat16),
            ],
            axis=1,
        )
        first_row = (col * n_row + row) * block
        own_pseudo = lax.dynamic_slice_in_dim(pseudo, first_row, block, 0)
        partial_gram = outer_rows(own_pseudo, pseudo).astype(jnp.bfloat16)
        chunk = modes // n_pl
        by_chunk = partial_gram.reshape(block, n_pl, chunk).transpose(1, 0, 2)
        gram_all = fused_sum(by_chunk, axes, sizes, "pl", False, 101)
        gram_all = beside_sibling(gram_all[None], core)
        gram_panel = gram_all.transpose(2, 0, 3, 1, 4).reshape(n_row * block, modes)
        half = modes // 2
        send_half = lax.dynamic_slice_in_dim(mode_shapes, (col % 2) * half, half, 1)
        panel_piece = lax.ppermute(send_half, ("prow", "pcol"), swap)
        panel_mine = lax.all_gather(panel_piece, "pl", axis=0, tiled=True)
        panel_mine, gram_panel = lax.optimization_barrier((panel_mine, gram_panel))
        panel_other = lax.ppermute(panel_mine, "prow", sibling)
        weighted_part = outer_rows(mode_shapes, gram_panel).astype(jnp.bfloat16)
        weighted_all = ex(weighted_part, ("pcol",), same=True)
        weighted = weighted_all.transpose(1, 0, 2).reshape(weighted_part.shape[0], modes)
        weighted_mine = lax.dynamic_slice_in_dim(weighted, core * half, half, 1)
        weighted_other = lax.dynamic_slice_in_dim(weighted, (1 - core) * half, half, 1)
        return outer_rows(weighted_mine, panel_mine) + outer_rows(weighted_other, panel_other)

    return body


def solution(mesh):
    in_specs = (
        P(("prow", "pcol"), "pl"),
        P(None, ("prow", "pcol")),
        P(("prow", "pl"), None),
        P(),
        P(),
    )
    out_specs = P(("prow", "pl"), "pcol")
    axes = tuple(mesh.axis_names)
    body = make_body(axes, dict(mesh.shape))
    return jax.shard_map(body, mesh=mesh, in_specs=in_specs, out_specs=out_specs, check_vma=False)
```

```python
import functools
import math

import jax
import jax.numpy as jnp
from jax import lax
from jax.experimental import pallas as pl
from jax.experimental.pallas import tpu as pltpu
from jax.sharding import PartitionSpec as P

MESH = pl.DeviceIdType.MESH


def transfer_pair(natural_freq, damping):
    detuning = natural_freq * natural_freq - 1.0
    damper = 2.0 * damping * natural_freq
    modulus = detuning * detuning + damper * damper
    return (detuning / modulus, -damper / modulus)


def outer_rows(left_rows, right_rows):
    return lax.dot_general(
        left_rows, right_rows, (((1,), (1,)), ((), ())), preferred_element_type=jnp.float32
    )


def factor_table(sizes):
    return {
        "zh": ("prow", sizes["prow"] // 2, 2),
        "core": ("prow", 2, 1),
        "pcol": ("pcol", sizes["pcol"], 1),
        "pl": ("pl", sizes["pl"], 1),
    }


def exchange_kernel(x_ref, out_ref, send_sem, recv_sem, local_sem, *, axes, factors, group, same):
    coords = {a: lax.axis_index(a) for a in axes}

    def value(f):
        axis, size, stride = factors[f]
        return lax.rem(coords[axis] // stride, size)

    count = math.prod(factors[f][1] for f in group)
    me = 0
    for f in group:
        me = me * factors[f][1] + value(f)

    def device(member):
        place = dict(coords)
        for f in reversed(group):
            axis, size, stride = factors[f]
            place[axis] = place[axis] + (lax.rem(member, size) - value(f)) * stride
            member = member // size
        return tuple(place[a] for a in axes)

    def source(member):
        return x_ref if same else x_ref.at[member]

    def copy(offset):
        peer = lax.rem(me + offset, count)
        return pltpu.make_async_remote_copy(
            src_ref=source(peer),
            dst_ref=out_ref.at[me],
            send_sem=send_sem.at[offset],
            recv_sem=recv_sem.at[offset],
            device_id=device(peer),
            device_id_type=MESH,
        )

    def landing(offset):
        sender = lax.rem(me + count - offset, count)
        return pltpu.make_async_remote_copy(
            src_ref=source(me),
            dst_ref=out_ref.at[sender],
            send_sem=send_sem.at[offset],
            recv_sem=recv_sem.at[offset],
            device_id=device(sender),
            device_id_type=MESH,
        )

    local = pltpu.make_async_copy(source(me), out_ref.at[me], local_sem)
    local.start()
    barrier = pltpu.get_barrier_semaphore()
    for offset in range(1, count):
        peer = lax.rem(me + offset, count)
        pl.semaphore_signal(barrier, inc=1, device_id=device(peer), device_id_type=MESH)
    pl.semaphore_wait(barrier, count - 1)
    for offset in range(1, count):
        copy(offset).start()
    local.wait()
    for offset in range(1, count):
        copy(offset).wait_send()
    for offset in range(1, count):
        landing(offset).wait_recv()


def fused_sum_kernel(x_ref, out_ref, got, coll, part_out, part_in, send_a, recv_a, send_b, recv_b,
                     send_c, recv_c, *, axes, factors, over, add_across):
    coords = {a: lax.axis_index(a) for a in axes}

    def value(f):
        axis, size, stride = factors[f]
        return lax.rem(coords[axis] // stride, size)

    def device(f, v):
        place = dict(coords)
        axis, size, stride = factors[f]
        place[axis] = place[axis] + (v - value(f)) * stride
        return tuple(place[a] for a in axes)

    n = factors[over][1]
    me, half = value(over), value("zh")
    partner = device("zh", 1 - half)
    peer = lambda k: lax.rem(me + k, n)
    sender = lambda k: lax.rem(me + n - k, n)

    def step(src, dst_at, k, to, sems):
        return pltpu.make_async_remote_copy(
            src_ref=src, dst_ref=dst_at, send_sem=sems[0].at[k], recv_sem=sems[1].at[k],
            device_id=to, device_id_type=MESH,
        )

    barrier = pltpu.get_barrier_semaphore()
    for k in range(1, n):
        pl.semaphore_signal(barrier, inc=1, device_id=device(over, peer(k)), device_id_type=MESH)
    pl.semaphore_signal(barrier, inc=1, device_id=partner, device_id_type=MESH)
    pl.semaphore_wait(barrier, n)

    for k in range(1, n):
        step(x_ref.at[peer(k)], got.at[me], k, device(over, peer(k)), (send_a, recv_a)).start()
    for k in range(1, n):
        step(x_ref.at[peer(k)], got.at[me], k, device(over, peer(k)), (send_a, recv_a)).wait_send()
    for k in range(1, n):
        step(x_ref.at[me], got.at[sender(k)], k, device(over, sender(k)), (send_a, recv_a)).wait_recv()
    total = x_ref[me].astype(jnp.float32)
    for k in range(1, n):
        total = total + got[sender(k)].astype(jnp.float32)
    part_out[...] = total.astype(part_out.dtype)

    across = pltpu.make_async_remote_copy(
        src_ref=part_out, dst_ref=part_in, send_sem=send_b, recv_sem=recv_b,
        device_id=partner, device_id_type=MESH,
    )
    across.start()
    across.wait_send()
    across.wait_recv()
    if add_across:
        mine, theirs = part_out[...].astype(jnp.float32), part_in[...].astype(jnp.float32)
        coll[me] = (mine + theirs).astype(coll.dtype)
    else:
        mine, theirs = part_out[...], part_in[...]
        first = jnp.where(half == 0, mine, theirs)
        second = jnp.where(half == 0, theirs, mine)
        coll[me] = jnp.stack([first, second])

    for k in range(1, n):
        step(coll.at[me], coll.at[me], k, device(over, peer(k)), (send_c, recv_c)).start()
    for k in range(1, n):
        step(coll.at[me], coll.at[me], k, device(over, peer(k)), (send_c, recv_c)).wait_send()
    for k in range(1, n):
        step(coll.at[me], coll.at[sender(k)], k, device(over, sender(k)), (send_c, recv_c)).wait_recv()
    out_ref[...] = coll[...]


def modal_sum_kernel(mine_ref, theirs_ref, out_ref, sib_in, pieces, got, coll, part_out, part_in,
                     sib_out, send_s, recv_s, send_a, recv_a, send_b, recv_b, send_c, recv_c,
                     send_d, recv_d, *, axes, factors):
    coords = {a: lax.axis_index(a) for a in axes}

    def value(f):
        axis, size, stride = factors[f]
        return lax.rem(coords[axis] // stride, size)

    def device(f, v):
        place = dict(coords)
        axis, size, stride = factors[f]
        place[axis] = place[axis] + (v - value(f)) * stride
        return tuple(place[a] for a in axes)

    n = factors["pcol"][1]
    me, half, core = value("pcol"), value("zh"), value("core")
    partner, sibling = device("zh", 1 - half), device("core", 1 - core)
    peer = lambda k: lax.rem(me + k, n)
    sender = lambda k: lax.rem(me + n - k, n)

    def step(src, dst_at, k, to, sems):
        return pltpu.make_async_remote_copy(
            src_ref=src, dst_ref=dst_at, send_sem=sems[0].at[k], recv_sem=sems[1].at[k],
            device_id=to, device_id_type=MESH,
        )

    def one(src, dst, to, send_sem, recv_sem):
        return pltpu.make_async_remote_copy(
            src_ref=src, dst_ref=dst, send_sem=send_sem, recv_sem=recv_sem,
            device_id=to, device_id_type=MESH,
        )

    barrier = pltpu.get_barrier_semaphore()
    for k in range(1, n):
        pl.semaphore_signal(barrier, inc=1, device_id=device("pcol", peer(k)), device_id_type=MESH)
    pl.semaphore_signal(barrier, inc=1, device_id=partner, device_id_type=MESH)
    pl.semaphore_signal(barrier, inc=1, device_id=sibling, device_id_type=MESH)
    pl.semaphore_wait(barrier, n + 1)

    chip = one(theirs_ref, sib_in, sibling, send_s, recv_s)
    chip.start()
    chip.wait_send()
    chip.wait_recv()
    summed = mine_ref[...] + sib_in[...].astype(jnp.float32)
    pieces[...] = summed.astype(pieces.dtype).reshape(pieces.shape)

    for k in range(1, n):
        step(pieces.at[peer(k)], got.at[me], k, device("pcol", peer(k)), (send_a, recv_a)).start()
    for k in range(1, n):
        step(pieces.at[peer(k)], got.at[me], k, device("pcol", peer(k)), (send_a, recv_a)).wait_send()
    for k in range(1, n):
        step(pieces.at[me], got.at[sender(k)], k, device("pcol", sender(k)), (send_a, recv_a)).wait_recv()
    total = pieces[me].astype(jnp.float32)
    for k in range(1, n):
        total = total + got[sender(k)].astype(jnp.float32)
    part_out[...] = total.astype(part_out.dtype)

    across = one(part_out, part_in, partner, send_b, recv_b)
    across.start()
    across.wait_send()
    across.wait_recv()
    coll[me] = (part_out[...].astype(jnp.float32) + part_in[...].astype(jnp.float32)).astype(coll.dtype)

    for k in range(1, n):
        step(coll.at[me], coll.at[me], k, device("pcol", peer(k)), (send_c, recv_c)).start()
    for k in range(1, n):
        step(coll.at[me], coll.at[me], k, device("pcol", peer(k)), (send_c, recv_c)).wait_send()
    for k in range(1, n):
        step(coll.at[me], coll.at[sender(k)], k, device("pcol", sender(k)), (send_c, recv_c)).wait_recv()

    join = one(coll, sib_out, sibling, send_d, recv_d)
    join.start()
    join.wait_send()
    join.wait_recv()
    out_ref[core] = coll[...]
    out_ref[1 - core] = sib_out[...]


def modal_sum(mine, theirs, axes, sizes):
    n = sizes["pcol"]
    rows, width = mine.shape
    block = (n, rows // n, width)
    kernel = functools.partial(modal_sum_kernel, axes=axes, factors=factor_table(sizes))
    return pl.pallas_call(
        kernel,
        out_shape=jax.ShapeDtypeStruct((2,) + block, jnp.bfloat16),
        in_specs=[pl.BlockSpec(memory_space=pltpu.VMEM)] * 2,
        out_specs=pl.BlockSpec(memory_space=pltpu.VMEM),
        scratch_shapes=[
            pltpu.VMEM((rows, width), jnp.bfloat16),
            pltpu.VMEM(block, jnp.bfloat16),
            pltpu.VMEM(block, jnp.bfloat16),
            pltpu.VMEM(block, jnp.bfloat16),
            pltpu.VMEM(block[1:], jnp.bfloat16),
            pltpu.VMEM(block[1:], jnp.bfloat16),
            pltpu.VMEM(block, jnp.bfloat16),
            pltpu.SemaphoreType.DMA(()),
            pltpu.SemaphoreType.DMA(()),
            pltpu.SemaphoreType.DMA((n,)),
            pltpu.SemaphoreType.DMA((n,)),
            pltpu.SemaphoreType.DMA(()),
            pltpu.SemaphoreType.DMA(()),
            pltpu.SemaphoreType.DMA((n,)),
            pltpu.SemaphoreType.DMA((n,)),
            pltpu.SemaphoreType.DMA(()),
            pltpu.SemaphoreType.DMA(()),
        ],
        compiler_params=pltpu.CompilerParams(collective_id=102, has_side_effects=True),
    )(mine, theirs)


def fused_sum(x, axes, sizes, over, add_across, kernel_id):
    n, rows, width = x.shape
    block = (rows, width) if add_across else (2, rows, width)
    kernel = functools.partial(
        fused_sum_kernel, axes=axes, factors=factor_table(sizes), over=over, add_across=add_across
    )
    return pl.pallas_call(
        kernel,
        out_shape=jax.ShapeDtypeStruct((n,) + block, x.dtype),
        in_specs=[pl.BlockSpec(memory_space=pltpu.VMEM)],
        out_specs=pl.BlockSpec(memory_space=pltpu.VMEM),
        scratch_shapes=[
            pltpu.VMEM(x.shape, x.dtype),
            pltpu.VMEM((n,) + block, x.dtype),
            pltpu.VMEM((rows, width), x.dtype),
            pltpu.VMEM((rows, width), x.dtype),
            pltpu.SemaphoreType.DMA((n,)),
            pltpu.SemaphoreType.DMA((n,)),
            pltpu.SemaphoreType.DMA(()),
            pltpu.SemaphoreType.DMA(()),
            pltpu.SemaphoreType.DMA((n,)),
            pltpu.SemaphoreType.DMA((n,)),
        ],
        compiler_params=pltpu.CompilerParams(collective_id=kernel_id, has_side_effects=True),
    )(x)


class Exchanger:
    def __init__(self, axes, sizes):
        self.axes, self.factors, self.calls = axes, factor_table(sizes), 0

    def __call__(self, x, group, same):
        count = math.prod(self.factors[f][1] for f in group)
        block = x.shape if same else x.shape[1:]
        if count == 1:
            return x[None] if same else x
        kernel = functools.partial(
            exchange_kernel, axes=self.axes, factors=self.factors, group=group, same=same
        )
        self.calls += 1
        return pl.pallas_call(
            kernel,
            out_shape=jax.ShapeDtypeStruct((count,) + tuple(block), x.dtype),
            in_specs=[pl.BlockSpec(memory_space=pl.ANY)],
            out_specs=pl.BlockSpec(memory_space=pl.ANY),
            scratch_shapes=[
                pltpu.SemaphoreType.DMA((count,)),
                pltpu.SemaphoreType.DMA((count,)),
                pltpu.SemaphoreType.DMA(()),
            ],
            compiler_params=pltpu.CompilerParams(collective_id=self.calls, has_side_effects=True),
        )(x)


def make_body(axes, sizes):
    n_row, n_col, n_pl = sizes["prow"], sizes["pcol"], sizes["pl"]
    swap = [(c * n_col + r, r * n_col + c) for r in range(n_row) for c in range(n_col)]
    sibling = [(r, r ^ 1) for r in range(n_row)]
    n_zh = n_row // 2

    def beside_sibling(part, core):
        other = lax.ppermute(part, "prow", sibling)
        first, second = jnp.where(core == 0, part, other), jnp.where(core == 0, other, part)
        return jnp.concatenate([first, second], axis=0)

    def body(factor_cols, modal_at_loads, mode_shapes, natural_freq, damping):
        ex = Exchanger(axes, sizes)
        in_phase, quadrature = transfer_pair(natural_freq, damping)
        modes = modal_at_loads.shape[0]
        block = modes // (n_row * n_col)
        row, col = lax.axis_index("prow"), lax.axis_index("pcol")
        partial_load = jnp.dot(modal_at_loads, factor_cols, preferred_element_type=jnp.float32)
        width = partial_load.shape[1]
        core = row % 2
        mine = lax.dynamic_slice_in_dim(partial_load, core * (modes // 2), modes // 2, 0)
        theirs = lax.dynamic_slice_in_dim(partial_load, (1 - core) * (modes // 2), modes // 2, 0)
        modal_load = modal_sum(mine, theirs.astype(jnp.bfloat16), axes, sizes).reshape(modes, width)
        modal_wide = modal_load.astype(jnp.float32)
        pseudo = jnp.concatenate(
            [
                (in_phase[:, None] * modal_wide).astype(jnp.bfloat16),
                (quadrature[:, None] * modal_wide).astype(jnp.bfloat16),
            ],
            axis=1,
        )
        first_row = (col * n_row + row) * block
        own_pseudo = lax.dynamic_slice_in_dim(pseudo, first_row, block, 0)
        partial_gram = outer_rows(own_pseudo, pseudo).astype(jnp.bfloat16)
        chunk = modes // n_pl
        by_chunk = partial_gram.reshape(block, n_pl, chunk).transpose(1, 0, 2)
        gram_all = fused_sum(by_chunk, axes, sizes, "pl", False, 101)
        gram_all = beside_sibling(gram_all[None], core)
        gram_panel = gram_all.transpose(2, 0, 3, 1, 4).reshape(n_row * block, modes)
        half = modes // 2
        send_half = lax.dynamic_slice_in_dim(mode_shapes, (col % 2) * half, half, 1)
        panel_piece = lax.ppermute(send_half, ("prow", "pcol"), swap)
        panel_mine = lax.all_gather(panel_piece, "pl", axis=0, tiled=True)
        panel_mine, gram_panel = lax.optimization_barrier((panel_mine, gram_panel))
        panel_other = lax.ppermute(panel_mine, "prow", sibling)
        weighted_part = outer_rows(mode_shapes, gram_panel).astype(jnp.bfloat16)
        weighted_all = ex(weighted_part, ("pcol",), same=True)
        weighted = weighted_all.transpose(1, 0, 2).reshape(weighted_part.shape[0], modes)
        weighted_mine = lax.dynamic_slice_in_dim(weighted, core * half, half, 1)
        weighted_other = lax.dynamic_slice_in_dim(weighted, (1 - core) * half, half, 1)
        return outer_rows(weighted_mine, panel_mine) + outer_rows(weighted_other, panel_other)

    return body


def solution(mesh):
    in_specs = (
        P(("prow", "pcol"), "pl"),
        P(None, ("prow", "pcol")),
        P(("prow", "pl"), None),
        P(),
        P(),
    )
    out_specs = P(("prow", "pl"), "pcol")
    axes = tuple(mesh.axis_names)
    body = make_body(axes, dict(mesh.shape))
    return jax.shard_map(body, mesh=mesh, in_specs=in_specs, out_specs=out_specs, check_vma=False)
```

```python
import functools
import math

import jax
import jax.numpy as jnp
from jax import lax
from jax.experimental import pallas as pl
from jax.experimental.pallas import tpu as pltpu
from jax.sharding import PartitionSpec as P

MESH = pl.DeviceIdType.MESH


def transfer_pair(natural_freq, damping):
    detuning = natural_freq * natural_freq - 1.0
    damper = 2.0 * damping * natural_freq
    modulus = detuning * detuning + damper * damper
    return (detuning / modulus, -damper / modulus)


def outer_rows(left_rows, right_rows):
    return lax.dot_general(
        left_rows, right_rows, (((1,), (1,)), ((), ())), preferred_element_type=jnp.float32
    )


def factor_table(sizes):
    return {
        "zh": ("prow", sizes["prow"] // 2, 2),
        "core": ("prow", 2, 1),
        "pcol": ("pcol", sizes["pcol"], 1),
        "pl": ("pl", sizes["pl"], 1),
    }


def exchange_kernel(x_ref, out_ref, send_sem, recv_sem, local_sem, *, axes, factors, group, same):
    coords = {a: lax.axis_index(a) for a in axes}

    def value(f):
        axis, size, stride = factors[f]
        return lax.rem(coords[axis] // stride, size)

    count = math.prod(factors[f][1] for f in group)
    me = 0
    for f in group:
        me = me * factors[f][1] + value(f)

    def device(member):
        place = dict(coords)
        for f in reversed(group):
            axis, size, stride = factors[f]
            place[axis] = place[axis] + (lax.rem(member, size) - value(f)) * stride
            member = member // size
        return tuple(place[a] for a in axes)

    def source(member):
        return x_ref if same else x_ref.at[member]

    def copy(offset):
        peer = lax.rem(me + offset, count)
        return pltpu.make_async_remote_copy(
            src_ref=source(peer),
            dst_ref=out_ref.at[me],
            send_sem=send_sem.at[offset],
            recv_sem=recv_sem.at[offset],
            device_id=device(peer),
            device_id_type=MESH,
        )

    def landing(offset):
        sender = lax.rem(me + count - offset, count)
        return pltpu.make_async_remote_copy(
            src_ref=source(me),
            dst_ref=out_ref.at[sender],
            send_sem=send_sem.at[offset],
            recv_sem=recv_sem.at[offset],
            device_id=device(sender),
            device_id_type=MESH,
        )

    local = pltpu.make_async_copy(source(me), out_ref.at[me], local_sem)
    local.start()
    barrier = pltpu.get_barrier_semaphore()
    for offset in range(1, count):
        peer = lax.rem(me + offset, count)
        pl.semaphore_signal(barrier, inc=1, device_id=device(peer), device_id_type=MESH)
    pl.semaphore_wait(barrier, count - 1)
    for offset in range(1, count):
        copy(offset).start()
    local.wait()
    for offset in range(1, count):
        copy(offset).wait_send()
    for offset in range(1, count):
        landing(offset).wait_recv()


def fused_sum_kernel(x_ref, out_ref, got, coll, part_out, part_in, send_a, recv_a, send_b, recv_b,
                     send_c, recv_c, *, axes, factors, over, add_across):
    coords = {a: lax.axis_index(a) for a in axes}

    def value(f):
        axis, size, stride = factors[f]
        return lax.rem(coords[axis] // stride, size)

    def device(f, v):
        place = dict(coords)
        axis, size, stride = factors[f]
        place[axis] = place[axis] + (v - value(f)) * stride
        return tuple(place[a] for a in axes)

    n = factors[over][1]
    me, half = value(over), value("zh")
    partner = device("zh", 1 - half)
    peer = lambda k: lax.rem(me + k, n)
    sender = lambda k: lax.rem(me + n - k, n)

    def step(src, dst_at, k, to, sems):
        return pltpu.make_async_remote_copy(
            src_ref=src, dst_ref=dst_at, send_sem=sems[0].at[k], recv_sem=sems[1].at[k],
            device_id=to, device_id_type=MESH,
        )

    barrier = pltpu.get_barrier_semaphore()
    for k in range(1, n):
        pl.semaphore_signal(barrier, inc=1, device_id=device(over, peer(k)), device_id_type=MESH)
    pl.semaphore_signal(barrier, inc=1, device_id=partner, device_id_type=MESH)
    pl.semaphore_wait(barrier, n)

    for k in range(1, n):
        step(x_ref.at[peer(k)], got.at[me], k, device(over, peer(k)), (send_a, recv_a)).start()
    for k in range(1, n):
        step(x_ref.at[peer(k)], got.at[me], k, device(over, peer(k)), (send_a, recv_a)).wait_send()
    for k in range(1, n):
        step(x_ref.at[me], got.at[sender(k)], k, device(over, sender(k)), (send_a, recv_a)).wait_recv()
    total = x_ref[me].astype(jnp.float32)
    for k in range(1, n):
        total = total + got[sender(k)].astype(jnp.float32)
    part_out[...] = total.astype(part_out.dtype)

    across = pltpu.make_async_remote_copy(
        src_ref=part_out, dst_ref=part_in, send_sem=send_b, recv_sem=recv_b,
        device_id=partner, device_id_type=MESH,
    )
    across.start()
    across.wait_send()
    across.wait_recv()
    if add_across:
        mine, theirs = part_out[...].astype(jnp.float32), part_in[...].astype(jnp.float32)
        coll[me] = (mine + theirs).astype(coll.dtype)
    else:
        mine, theirs = part_out[...], part_in[...]
        first = jnp.where(half == 0, mine, theirs)
        second = jnp.where(half == 0, theirs, mine)
        coll[me] = jnp.stack([first, second])

    for k in range(1, n):
        step(coll.at[me], coll.at[me], k, device(over, peer(k)), (send_c, recv_c)).start()
    for k in range(1, n):
        step(coll.at[me], coll.at[me], k, device(over, peer(k)), (send_c, recv_c)).wait_send()
    for k in range(1, n):
        step(coll.at[me], coll.at[sender(k)], k, device(over, sender(k)), (send_c, recv_c)).wait_recv()
    out_ref[...] = coll[...]


def modal_sum_kernel(mine_ref, theirs_ref, out_ref, sib_in, pieces, got, coll, part_out, part_in,
                     sib_out, send_s, recv_s, send_a, recv_a, send_b, recv_b, send_c, recv_c,
                     send_d, recv_d, *, axes, factors):
    coords = {a: lax.axis_index(a) for a in axes}

    def value(f):
        axis, size, stride = factors[f]
        return lax.rem(coords[axis] // stride, size)

    def device(f, v):
        place = dict(coords)
        axis, size, stride = factors[f]
        place[axis] = place[axis] + (v - value(f)) * stride
        return tuple(place[a] for a in axes)

    n = factors["pcol"][1]
    me, half, core = value("pcol"), value("zh"), value("core")
    partner, sibling = device("zh", 1 - half), device("core", 1 - core)
    peer = lambda k: lax.rem(me + k, n)
    sender = lambda k: lax.rem(me + n - k, n)

    def step(src, dst_at, k, to, sems):
        return pltpu.make_async_remote_copy(
            src_ref=src, dst_ref=dst_at, send_sem=sems[0].at[k], recv_sem=sems[1].at[k],
            device_id=to, device_id_type=MESH,
        )

    def one(src, dst, to, send_sem, recv_sem):
        return pltpu.make_async_remote_copy(
            src_ref=src, dst_ref=dst, send_sem=send_sem, recv_sem=recv_sem,
            device_id=to, device_id_type=MESH,
        )

    barrier = pltpu.get_barrier_semaphore()
    for k in range(1, n):
        pl.semaphore_signal(barrier, inc=1, device_id=device("pcol", peer(k)), device_id_type=MESH)
    pl.semaphore_signal(barrier, inc=1, device_id=partner, device_id_type=MESH)
    pl.semaphore_signal(barrier, inc=1, device_id=sibling, device_id_type=MESH)
    pl.semaphore_wait(barrier, n + 1)

    chip = one(theirs_ref, sib_in, sibling, send_s, recv_s)
    chip.start()
    chip.wait_send()
    chip.wait_recv()
    summed = mine_ref[...] + sib_in[...].astype(jnp.float32)
    pieces[...] = summed.astype(pieces.dtype).reshape(pieces.shape)

    for k in range(1, n):
        step(pieces.at[peer(k)], got.at[me], k, device("pcol", peer(k)), (send_a, recv_a)).start()
    for k in range(1, n):
        step(pieces.at[peer(k)], got.at[me], k, device("pcol", peer(k)), (send_a, recv_a)).wait_send()
    for k in range(1, n):
        step(pieces.at[me], got.at[sender(k)], k, device("pcol", sender(k)), (send_a, recv_a)).wait_recv()
    total = pieces[me].astype(jnp.float32)
    for k in range(1, n):
        total = total + got[sender(k)].astype(jnp.float32)
    part_out[...] = total.astype(part_out.dtype)

    across = one(part_out, part_in, partner, send_b, recv_b)
    across.start()
    across.wait_send()
    across.wait_recv()
    coll[me] = (part_out[...].astype(jnp.float32) + part_in[...].astype(jnp.float32)).astype(coll.dtype)

    for k in range(1, n):
        step(coll.at[me], coll.at[me], k, device("pcol", peer(k)), (send_c, recv_c)).start()
    for k in range(1, n):
        step(coll.at[me], coll.at[me], k, device("pcol", peer(k)), (send_c, recv_c)).wait_send()
    for k in range(1, n):
        step(coll.at[me], coll.at[sender(k)], k, device("pcol", sender(k)), (send_c, recv_c)).wait_recv()

    join = one(coll, sib_out, sibling, send_d, recv_d)
    join.start()
    join.wait_send()
    join.wait_recv()
    out_ref[core] = coll[...]
    out_ref[1 - core] = sib_out[...]


def modal_sum(mine, theirs, axes, sizes):
    n = sizes["pcol"]
    rows, width = mine.shape
    block = (n, rows // n, width)
    kernel = functools.partial(modal_sum_kernel, axes=axes, factors=factor_table(sizes))
    return pl.pallas_call(
        kernel,
        out_shape=jax.ShapeDtypeStruct((2,) + block, jnp.bfloat16),
        in_specs=[pl.BlockSpec(memory_space=pltpu.VMEM)] * 2,
        out_specs=pl.BlockSpec(memory_space=pltpu.VMEM),
        scratch_shapes=[
            pltpu.VMEM((rows, width), jnp.bfloat16),
            pltpu.VMEM(block, jnp.bfloat16),
            pltpu.VMEM(block, jnp.bfloat16),
            pltpu.VMEM(block, jnp.bfloat16),
            pltpu.VMEM(block[1:], jnp.bfloat16),
            pltpu.VMEM(block[1:], jnp.bfloat16),
            pltpu.VMEM(block, jnp.bfloat16),
            pltpu.SemaphoreType.DMA(()),
            pltpu.SemaphoreType.DMA(()),
            pltpu.SemaphoreType.DMA((n,)),
            pltpu.SemaphoreType.DMA((n,)),
            pltpu.SemaphoreType.DMA(()),
            pltpu.SemaphoreType.DMA(()),
            pltpu.SemaphoreType.DMA((n,)),
            pltpu.SemaphoreType.DMA((n,)),
            pltpu.SemaphoreType.DMA(()),
            pltpu.SemaphoreType.DMA(()),
        ],
        compiler_params=pltpu.CompilerParams(collective_id=102, has_side_effects=True),
    )(mine, theirs)


def gram_weighted_kernel(x_ref, shapes_ref, out_ref, got, coll, sib_coll, part_out, part_in, wbuf,
                         send_a, recv_a, send_b, recv_b, send_c, recv_c, send_d, recv_d, send_e,
                         recv_e, *, axes, factors):
    coords = {a: lax.axis_index(a) for a in axes}

    def value(f):
        axis, size, stride = factors[f]
        return lax.rem(coords[axis] // stride, size)

    def device(f, v):
        place = dict(coords)
        axis, size, stride = factors[f]
        place[axis] = place[axis] + (v - value(f)) * stride
        return tuple(place[a] for a in axes)

    n, n_col = factors["pl"][1], factors["pcol"][1]
    me, half, core, col = value("pl"), value("zh"), value("core"), value("pcol")
    partner, sibling = device("zh", 1 - half), device("core", 1 - core)

    def step(src, dst_at, k, to, sems):
        return pltpu.make_async_remote_copy(
            src_ref=src, dst_ref=dst_at, send_sem=sems[0].at[k], recv_sem=sems[1].at[k],
            device_id=to, device_id_type=MESH,
        )

    def one(src, dst, to, send_sem, recv_sem):
        return pltpu.make_async_remote_copy(
            src_ref=src, dst_ref=dst, send_sem=send_sem, recv_sem=recv_sem,
            device_id=to, device_id_type=MESH,
        )

    barrier = pltpu.get_barrier_semaphore()
    for k in range(1, n):
        pl.semaphore_signal(barrier, inc=1, device_id=device("pl", lax.rem(me + k, n)), device_id_type=MESH)
    for k in range(1, n_col):
        pl.semaphore_signal(
            barrier, inc=1, device_id=device("pcol", lax.rem(col + k, n_col)), device_id_type=MESH
        )
    pl.semaphore_signal(barrier, inc=1, device_id=partner, device_id_type=MESH)
    pl.semaphore_signal(barrier, inc=1, device_id=sibling, device_id_type=MESH)
    pl.semaphore_wait(barrier, n + n_col)

    peer = lambda k: lax.rem(me + k, n)
    sender = lambda k: lax.rem(me + n - k, n)
    for k in range(1, n):
        step(x_ref.at[peer(k)], got.at[me], k, device("pl", peer(k)), (send_a, recv_a)).start()
    for k in range(1, n):
        step(x_ref.at[peer(k)], got.at[me], k, device("pl", peer(k)), (send_a, recv_a)).wait_send()
    for k in range(1, n):
        step(x_ref.at[me], got.at[sender(k)], k, device("pl", sender(k)), (send_a, recv_a)).wait_recv()
    total = x_ref[me].astype(jnp.float32)
    for k in range(1, n):
        total = total + got[sender(k)].astype(jnp.float32)
    part_out[...] = total.astype(part_out.dtype)

    across = one(part_out, part_in, partner, send_b, recv_b)
    across.start()
    across.wait_send()
    across.wait_recv()
    mine, theirs = part_out[...], part_in[...]
    coll[me] = jnp.stack([jnp.where(half == 0, mine, theirs), jnp.where(half == 0, theirs, mine)])

    for k in range(1, n):
        step(coll.at[me], coll.at[me], k, device("pl", peer(k)), (send_c, recv_c)).start()
    for k in range(1, n):
        step(coll.at[me], coll.at[me], k, device("pl", peer(k)), (send_c, recv_c)).wait_send()
    for k in range(1, n):
        step(coll.at[me], coll.at[sender(k)], k, device("pl", sender(k)), (send_c, recv_c)).wait_recv()

    join = one(coll, sib_coll, sibling, send_d, recv_d)
    join.start()
    join.wait_send()
    join.wait_recv()

    chunk = coll.shape[-1]
    parts = []
    for h in range(2):
        for k in range(2):
            acc = jnp.zeros((shapes_ref.shape[0], coll.shape[2]), jnp.float32)
            for l in range(n):
                block = jnp.where(core == k, coll[l, h], sib_coll[l, h])
                acc = acc + lax.dot_general(
                    shapes_ref[:, l * chunk:(l + 1) * chunk], block,
                    (((1,), (1,)), ((), ())), preferred_element_type=jnp.float32,
                )
            parts.append(acc)
    wbuf[col] = jnp.concatenate(parts, axis=1).astype(wbuf.dtype)

    wpeer = lambda k: lax.rem(col + k, n_col)
    wsender = lambda k: lax.rem(col + n_col - k, n_col)
    for k in range(1, n_col):
        step(wbuf.at[col], wbuf.at[col], k, device("pcol", wpeer(k)), (send_e, recv_e)).start()
    for k in range(1, n_col):
        step(wbuf.at[col], wbuf.at[col], k, device("pcol", wpeer(k)), (send_e, recv_e)).wait_send()
    for k in range(1, n_col):
        step(wbuf.at[col], wbuf.at[wsender(k)], k, device("pcol", wsender(k)), (send_e, recv_e)).wait_recv()
    out_ref[...] = wbuf[...]


def gram_weighted(x, mode_shapes, axes, sizes):
    n, rows, width = x.shape
    n_col = sizes["pcol"]
    wshape = (n_col, mode_shapes.shape[0], 4 * rows)
    kernel = functools.partial(gram_weighted_kernel, axes=axes, factors=factor_table(sizes))
    return pl.pallas_call(
        kernel,
        out_shape=jax.ShapeDtypeStruct(wshape, jnp.bfloat16),
        in_specs=[pl.BlockSpec(memory_space=pltpu.VMEM)] * 2,
        out_specs=pl.BlockSpec(memory_space=pltpu.VMEM),
        scratch_shapes=[
            pltpu.VMEM(x.shape, x.dtype),
            pltpu.VMEM((n, 2, rows, width), x.dtype),
            pltpu.VMEM((n, 2, rows, width), x.dtype),
            pltpu.VMEM((rows, width), x.dtype),
            pltpu.VMEM((rows, width), x.dtype),
            pltpu.VMEM(wshape, jnp.bfloat16),
            pltpu.SemaphoreType.DMA((n,)),
            pltpu.SemaphoreType.DMA((n,)),
            pltpu.SemaphoreType.DMA(()),
            pltpu.SemaphoreType.DMA(()),
            pltpu.SemaphoreType.DMA((n,)),
            pltpu.SemaphoreType.DMA((n,)),
            pltpu.SemaphoreType.DMA(()),
            pltpu.SemaphoreType.DMA(()),
            pltpu.SemaphoreType.DMA((n_col,)),
            pltpu.SemaphoreType.DMA((n_col,)),
        ],
        compiler_params=pltpu.CompilerParams(collective_id=103, has_side_effects=True),
    )(x, mode_shapes)


def fused_sum(x, axes, sizes, over, add_across, kernel_id):
    n, rows, width = x.shape
    block = (rows, width) if add_across else (2, rows, width)
    kernel = functools.partial(
        fused_sum_kernel, axes=axes, factors=factor_table(sizes), over=over, add_across=add_across
    )
    return pl.pallas_call(
        kernel,
        out_shape=jax.ShapeDtypeStruct((n,) + block, x.dtype),
        in_specs=[pl.BlockSpec(memory_space=pltpu.VMEM)],
        out_specs=pl.BlockSpec(memory_space=pltpu.VMEM),
        scratch_shapes=[
            pltpu.VMEM(x.shape, x.dtype),
            pltpu.VMEM((n,) + block, x.dtype),
            pltpu.VMEM((rows, width), x.dtype),
            pltpu.VMEM((rows, width), x.dtype),
            pltpu.SemaphoreType.DMA((n,)),
            pltpu.SemaphoreType.DMA((n,)),
            pltpu.SemaphoreType.DMA(()),
            pltpu.SemaphoreType.DMA(()),
            pltpu.SemaphoreType.DMA((n,)),
            pltpu.SemaphoreType.DMA((n,)),
        ],
        compiler_params=pltpu.CompilerParams(collective_id=kernel_id, has_side_effects=True),
    )(x)


class Exchanger:
    def __init__(self, axes, sizes):
        self.axes, self.factors, self.calls = axes, factor_table(sizes), 0

    def __call__(self, x, group, same):
        count = math.prod(self.factors[f][1] for f in group)
        block = x.shape if same else x.shape[1:]
        if count == 1:
            return x[None] if same else x
        kernel = functools.partial(
            exchange_kernel, axes=self.axes, factors=self.factors, group=group, same=same
        )
        self.calls += 1
        return pl.pallas_call(
            kernel,
            out_shape=jax.ShapeDtypeStruct((count,) + tuple(block), x.dtype),
            in_specs=[pl.BlockSpec(memory_space=pl.ANY)],
            out_specs=pl.BlockSpec(memory_space=pl.ANY),
            scratch_shapes=[
                pltpu.SemaphoreType.DMA((count,)),
                pltpu.SemaphoreType.DMA((count,)),
                pltpu.SemaphoreType.DMA(()),
            ],
            compiler_params=pltpu.CompilerParams(collective_id=self.calls, has_side_effects=True),
        )(x)


def make_body(axes, sizes):
    n_row, n_col, n_pl = sizes["prow"], sizes["pcol"], sizes["pl"]
    swap = [(c * n_col + r, r * n_col + c) for r in range(n_row) for c in range(n_col)]
    sibling = [(r, r ^ 1) for r in range(n_row)]
    n_zh = n_row // 2

    def beside_sibling(part, core):
        other = lax.ppermute(part, "prow", sibling)
        first, second = jnp.where(core == 0, part, other), jnp.where(core == 0, other, part)
        return jnp.concatenate([first, second], axis=0)

    def body(factor_cols, modal_at_loads, mode_shapes, natural_freq, damping):
        ex = Exchanger(axes, sizes)
        in_phase, quadrature = transfer_pair(natural_freq, damping)
        modes = modal_at_loads.shape[0]
        block = modes // (n_row * n_col)
        row, col = lax.axis_index("prow"), lax.axis_index("pcol")
        partial_load = jnp.dot(modal_at_loads, factor_cols, preferred_element_type=jnp.float32)
        width = partial_load.shape[1]
        core = row % 2
        mine = lax.dynamic_slice_in_dim(partial_load, core * (modes // 2), modes // 2, 0)
        theirs = lax.dynamic_slice_in_dim(partial_load, (1 - core) * (modes // 2), modes // 2, 0)
        modal_load = modal_sum(mine, theirs.astype(jnp.bfloat16), axes, sizes).reshape(modes, width)
        modal_wide = modal_load.astype(jnp.float32)
        pseudo = jnp.concatenate(
            [
                (in_phase[:, None] * modal_wide).astype(jnp.bfloat16),
                (quadrature[:, None] * modal_wide).astype(jnp.bfloat16),
            ],
            axis=1,
        )
        first_row = (col * n_row + row) * block
        own_pseudo = lax.dynamic_slice_in_dim(pseudo, first_row, block, 0)
        partial_gram = outer_rows(own_pseudo, pseudo).astype(jnp.bfloat16)
        chunk = modes // n_pl
        by_chunk = partial_gram.reshape(block, n_pl, chunk).transpose(1, 0, 2)
        half = modes // 2
        send_half = lax.dynamic_slice_in_dim(mode_shapes, (col % 2) * half, half, 1)
        panel_piece = lax.ppermute(send_half, ("prow", "pcol"), swap)
        panel_mine = lax.all_gather(panel_piece, "pl", axis=0, tiled=True)
        weighted_all = gram_weighted(by_chunk, mode_shapes, axes, sizes)
        panel_mine, weighted_all = lax.optimization_barrier((panel_mine, weighted_all))
        panel_other = lax.ppermute(panel_mine, "prow", sibling)
        weighted = weighted_all.transpose(1, 0, 2).reshape(mode_shapes.shape[0], modes)
        weighted_mine = lax.dynamic_slice_in_dim(weighted, core * half, half, 1)
        weighted_other = lax.dynamic_slice_in_dim(weighted, (1 - core) * half, half, 1)
        return outer_rows(weighted_mine, panel_mine) + outer_rows(weighted_other, panel_other)

    return body


def solution(mesh):
    in_specs = (
        P(("prow", "pcol"), "pl"),
        P(None, ("prow", "pcol")),
        P(("prow", "pl"), None),
        P(),
        P(),
    )
    out_specs = P(("prow", "pl"), "pcol")
    axes = tuple(mesh.axis_names)
    body = make_body(axes, dict(mesh.shape))
    return jax.shard_map(body, mesh=mesh, in_specs=in_specs, out_specs=out_specs, check_vma=False)
```

```python
import functools
import math

import jax
import jax.numpy as jnp
from jax import lax
from jax.experimental import pallas as pl
from jax.experimental.pallas import tpu as pltpu
from jax.sharding import PartitionSpec as P

MESH = pl.DeviceIdType.MESH


def transfer_pair(natural_freq, damping):
    detuning = natural_freq * natural_freq - 1.0
    damper = 2.0 * damping * natural_freq
    modulus = detuning * detuning + damper * damper
    return (detuning / modulus, -damper / modulus)


def outer_rows(left_rows, right_rows):
    return lax.dot_general(
        left_rows, right_rows, (((1,), (1,)), ((), ())), preferred_element_type=jnp.float32
    )


def factor_table(sizes):
    return {
        "zh": ("prow", sizes["prow"] // 2, 2),
        "core": ("prow", 2, 1),
        "pcol": ("pcol", sizes["pcol"], 1),
        "pl": ("pl", sizes["pl"], 1),
    }


def exchange_kernel(x_ref, out_ref, send_sem, recv_sem, local_sem, *, axes, factors, group, same):
    coords = {a: lax.axis_index(a) for a in axes}

    def value(f):
        axis, size, stride = factors[f]
        return lax.rem(coords[axis] // stride, size)

    count = math.prod(factors[f][1] for f in group)
    me = 0
    for f in group:
        me = me * factors[f][1] + value(f)

    def device(member):
        place = dict(coords)
        for f in reversed(group):
            axis, size, stride = factors[f]
            place[axis] = place[axis] + (lax.rem(member, size) - value(f)) * stride
            member = member // size
        return tuple(place[a] for a in axes)

    def source(member):
        return x_ref if same else x_ref.at[member]

    def copy(offset):
        peer = lax.rem(me + offset, count)
        return pltpu.make_async_remote_copy(
            src_ref=source(peer),
            dst_ref=out_ref.at[me],
            send_sem=send_sem.at[offset],
            recv_sem=recv_sem.at[offset],
            device_id=device(peer),
            device_id_type=MESH,
        )

    def landing(offset):
        sender = lax.rem(me + count - offset, count)
        return pltpu.make_async_remote_copy(
            src_ref=source(me),
            dst_ref=out_ref.at[sender],
            send_sem=send_sem.at[offset],
            recv_sem=recv_sem.at[offset],
            device_id=device(sender),
            device_id_type=MESH,
        )

    local = pltpu.make_async_copy(source(me), out_ref.at[me], local_sem)
    local.start()
    barrier = pltpu.get_barrier_semaphore()
    for offset in range(1, count):
        peer = lax.rem(me + offset, count)
        pl.semaphore_signal(barrier, inc=1, device_id=device(peer), device_id_type=MESH)
    pl.semaphore_wait(barrier, count - 1)
    for offset in range(1, count):
        copy(offset).start()
    local.wait()
    for offset in range(1, count):
        copy(offset).wait_send()
    for offset in range(1, count):
        landing(offset).wait_recv()


def fused_sum_kernel(x_ref, out_ref, got, coll, part_out, part_in, send_a, recv_a, send_b, recv_b,
                     send_c, recv_c, *, axes, factors, over, add_across):
    coords = {a: lax.axis_index(a) for a in axes}

    def value(f):
        axis, size, stride = factors[f]
        return lax.rem(coords[axis] // stride, size)

    def device(f, v):
        place = dict(coords)
        axis, size, stride = factors[f]
        place[axis] = place[axis] + (v - value(f)) * stride
        return tuple(place[a] for a in axes)

    n = factors[over][1]
    me, half = value(over), value("zh")
    partner = device("zh", 1 - half)
    peer = lambda k: lax.rem(me + k, n)
    sender = lambda k: lax.rem(me + n - k, n)

    def step(src, dst_at, k, to, sems):
        return pltpu.make_async_remote_copy(
            src_ref=src, dst_ref=dst_at, send_sem=sems[0].at[k], recv_sem=sems[1].at[k],
            device_id=to, device_id_type=MESH,
        )

    barrier = pltpu.get_barrier_semaphore()
    for k in range(1, n):
        pl.semaphore_signal(barrier, inc=1, device_id=device(over, peer(k)), device_id_type=MESH)
    pl.semaphore_signal(barrier, inc=1, device_id=partner, device_id_type=MESH)
    pl.semaphore_wait(barrier, n)

    for k in range(1, n):
        step(x_ref.at[peer(k)], got.at[me], k, device(over, peer(k)), (send_a, recv_a)).start()
    for k in range(1, n):
        step(x_ref.at[peer(k)], got.at[me], k, device(over, peer(k)), (send_a, recv_a)).wait_send()
    for k in range(1, n):
        step(x_ref.at[me], got.at[sender(k)], k, device(over, sender(k)), (send_a, recv_a)).wait_recv()
    total = x_ref[me].astype(jnp.float32)
    for k in range(1, n):
        total = total + got[sender(k)].astype(jnp.float32)
    part_out[...] = total.astype(part_out.dtype)

    across = pltpu.make_async_remote_copy(
        src_ref=part_out, dst_ref=part_in, send_sem=send_b, recv_sem=recv_b,
        device_id=partner, device_id_type=MESH,
    )
    across.start()
    across.wait_send()
    across.wait_recv()
    if add_across:
        mine, theirs = part_out[...].astype(jnp.float32), part_in[...].astype(jnp.float32)
        coll[me] = (mine + theirs).astype(coll.dtype)
    else:
        mine, theirs = part_out[...], part_in[...]
        first = jnp.where(half == 0, mine, theirs)
        second = jnp.where(half == 0, theirs, mine)
        coll[me] = jnp.stack([first, second])

    for k in range(1, n):
        step(coll.at[me], coll.at[me], k, device(over, peer(k)), (send_c, recv_c)).start()
    for k in range(1, n):
        step(coll.at[me], coll.at[me], k, device(over, peer(k)), (send_c, recv_c)).wait_send()
    for k in range(1, n):
        step(coll.at[me], coll.at[sender(k)], k, device(over, sender(k)), (send_c, recv_c)).wait_recv()
    out_ref[...] = coll[...]


def modal_sum_kernel(mine_ref, theirs_ref, out_ref, sib_in, pieces, got, coll, part_out, part_in,
                     sib_out, send_s, recv_s, send_a, recv_a, send_b, recv_b, send_c, recv_c,
                     send_d, recv_d, *, axes, factors):
    coords = {a: lax.axis_index(a) for a in axes}

    def value(f):
        axis, size, stride = factors[f]
        return lax.rem(coords[axis] // stride, size)

    def device(f, v):
        place = dict(coords)
        axis, size, stride = factors[f]
        place[axis] = place[axis] + (v - value(f)) * stride
        return tuple(place[a] for a in axes)

    n = factors["pcol"][1]
    me, half, core = value("pcol"), value("zh"), value("core")
    partner, sibling = device("zh", 1 - half), device("core", 1 - core)
    peer = lambda k: lax.rem(me + k, n)
    sender = lambda k: lax.rem(me + n - k, n)

    def step(src, dst_at, k, to, sems):
        return pltpu.make_async_remote_copy(
            src_ref=src, dst_ref=dst_at, send_sem=sems[0].at[k], recv_sem=sems[1].at[k],
            device_id=to, device_id_type=MESH,
        )

    def one(src, dst, to, send_sem, recv_sem):
        return pltpu.make_async_remote_copy(
            src_ref=src, dst_ref=dst, send_sem=send_sem, recv_sem=recv_sem,
            device_id=to, device_id_type=MESH,
        )

    barrier = pltpu.get_barrier_semaphore()
    for k in range(1, n):
        pl.semaphore_signal(barrier, inc=1, device_id=device("pcol", peer(k)), device_id_type=MESH)
    pl.semaphore_signal(barrier, inc=1, device_id=partner, device_id_type=MESH)
    pl.semaphore_signal(barrier, inc=1, device_id=sibling, device_id_type=MESH)
    pl.semaphore_wait(barrier, n + 1)

    chip = one(theirs_ref, sib_in, sibling, send_s, recv_s)
    chip.start()
    chip.wait_send()
    chip.wait_recv()
    summed = mine_ref[...] + sib_in[...].astype(jnp.float32)
    pieces[...] = summed.astype(pieces.dtype).reshape(pieces.shape)

    for k in range(1, n):
        step(pieces.at[peer(k)], got.at[me], k, device("pcol", peer(k)), (send_a, recv_a)).start()
    for k in range(1, n):
        step(pieces.at[peer(k)], got.at[me], k, device("pcol", peer(k)), (send_a, recv_a)).wait_send()
    for k in range(1, n):
        step(pieces.at[me], got.at[sender(k)], k, device("pcol", sender(k)), (send_a, recv_a)).wait_recv()
    total = pieces[me].astype(jnp.float32)
    for k in range(1, n):
        total = total + got[sender(k)].astype(jnp.float32)
    part_out[...] = total.astype(part_out.dtype)

    across = one(part_out, part_in, partner, send_b, recv_b)
    across.start()
    across.wait_send()
    across.wait_recv()
    coll[me] = (part_out[...].astype(jnp.float32) + part_in[...].astype(jnp.float32)).astype(coll.dtype)

    for k in range(1, n):
        step(coll.at[me], coll.at[me], k, device("pcol", peer(k)), (send_c, recv_c)).start()
    for k in range(1, n):
        step(coll.at[me], coll.at[me], k, device("pcol", peer(k)), (send_c, recv_c)).wait_send()
    for k in range(1, n):
        step(coll.at[me], coll.at[sender(k)], k, device("pcol", sender(k)), (send_c, recv_c)).wait_recv()

    join = one(coll, sib_out, sibling, send_d, recv_d)
    join.start()
    join.wait_send()
    join.wait_recv()
    out_ref[core] = coll[...]
    out_ref[1 - core] = sib_out[...]


def modal_sum(mine, theirs, axes, sizes):
    n = sizes["pcol"]
    rows, width = mine.shape
    block = (n, rows // n, width)
    kernel = functools.partial(modal_sum_kernel, axes=axes, factors=factor_table(sizes))
    return pl.pallas_call(
        kernel,
        out_shape=jax.ShapeDtypeStruct((2,) + block, jnp.bfloat16),
        in_specs=[pl.BlockSpec(memory_space=pltpu.VMEM)] * 2,
        out_specs=pl.BlockSpec(memory_space=pltpu.VMEM),
        scratch_shapes=[
            pltpu.VMEM((rows, width), jnp.bfloat16),
            pltpu.VMEM(block, jnp.bfloat16),
            pltpu.VMEM(block, jnp.bfloat16),
            pltpu.VMEM(block, jnp.bfloat16),
            pltpu.VMEM(block[1:], jnp.bfloat16),
            pltpu.VMEM(block[1:], jnp.bfloat16),
            pltpu.VMEM(block, jnp.bfloat16),
            pltpu.SemaphoreType.DMA(()),
            pltpu.SemaphoreType.DMA(()),
            pltpu.SemaphoreType.DMA((n,)),
            pltpu.SemaphoreType.DMA((n,)),
            pltpu.SemaphoreType.DMA(()),
            pltpu.SemaphoreType.DMA(()),
            pltpu.SemaphoreType.DMA((n,)),
            pltpu.SemaphoreType.DMA((n,)),
            pltpu.SemaphoreType.DMA(()),
            pltpu.SemaphoreType.DMA(()),
        ],
        compiler_params=pltpu.CompilerParams(collective_id=102, has_side_effects=True),
    )(mine, theirs)


def gram_weighted_kernel(x_ref, shapes_ref, out_ref, got, coll, sib_coll, part_out, part_in, wbuf,
                         send_a, recv_a, send_b, recv_b, send_c, recv_c, send_d, recv_d, send_e,
                         recv_e, *, axes, factors):
    coords = {a: lax.axis_index(a) for a in axes}

    def value(f):
        axis, size, stride = factors[f]
        return lax.rem(coords[axis] // stride, size)

    def device(f, v):
        place = dict(coords)
        axis, size, stride = factors[f]
        place[axis] = place[axis] + (v - value(f)) * stride
        return tuple(place[a] for a in axes)

    n, n_col = factors["pl"][1], factors["pcol"][1]
    me, half, core, col = value("pl"), value("zh"), value("core"), value("pcol")
    partner, sibling = device("zh", 1 - half), device("core", 1 - core)

    def step(src, dst_at, k, to, sems):
        return pltpu.make_async_remote_copy(
            src_ref=src, dst_ref=dst_at, send_sem=sems[0].at[k], recv_sem=sems[1].at[k],
            device_id=to, device_id_type=MESH,
        )

    def one(src, dst, to, send_sem, recv_sem):
        return pltpu.make_async_remote_copy(
            src_ref=src, dst_ref=dst, send_sem=send_sem, recv_sem=recv_sem,
            device_id=to, device_id_type=MESH,
        )

    barrier = pltpu.get_barrier_semaphore()
    for k in range(1, n):
        pl.semaphore_signal(barrier, inc=1, device_id=device("pl", lax.rem(me + k, n)), device_id_type=MESH)
    for k in range(1, n_col):
        pl.semaphore_signal(
            barrier, inc=1, device_id=device("pcol", lax.rem(col + k, n_col)), device_id_type=MESH
        )
    pl.semaphore_signal(barrier, inc=1, device_id=partner, device_id_type=MESH)
    pl.semaphore_signal(barrier, inc=1, device_id=sibling, device_id_type=MESH)
    pl.semaphore_wait(barrier, n + n_col)

    peer = lambda k: lax.rem(me + k, n)
    sender = lambda k: lax.rem(me + n - k, n)
    for k in range(1, n):
        step(x_ref.at[peer(k)], got.at[me], k, device("pl", peer(k)), (send_a, recv_a)).start()
    for k in range(1, n):
        step(x_ref.at[peer(k)], got.at[me], k, device("pl", peer(k)), (send_a, recv_a)).wait_send()
    for k in range(1, n):
        step(x_ref.at[me], got.at[sender(k)], k, device("pl", sender(k)), (send_a, recv_a)).wait_recv()
    total = x_ref[me].astype(jnp.float32)
    for k in range(1, n):
        total = total + got[sender(k)].astype(jnp.float32)
    part_out[...] = total.astype(part_out.dtype)

    across = one(part_out, part_in, partner, send_b, recv_b)
    across.start()
    across.wait_send()
    across.wait_recv()
    mine, theirs = part_out[...], part_in[...]
    coll[me] = jnp.stack([jnp.where(half == 0, mine, theirs), jnp.where(half == 0, theirs, mine)])

    for k in range(1, n):
        step(coll.at[me], coll.at[me], k, device("pl", peer(k)), (send_c, recv_c)).start()
    for k in range(1, n):
        step(coll.at[me], coll.at[me], k, device("pl", peer(k)), (send_c, recv_c)).wait_send()
    for k in range(1, n):
        step(coll.at[me], coll.at[sender(k)], k, device("pl", sender(k)), (send_c, recv_c)).wait_recv()

    join = one(coll, sib_coll, sibling, send_d, recv_d)
    join.start()
    join.wait_send()
    join.wait_recv()

    chunk = coll.shape[-1]
    parts = []
    for h in range(2):
        for k in range(2):
            acc = jnp.zeros((shapes_ref.shape[0], coll.shape[2]), jnp.float32)
            for l in range(n):
                block = jnp.where(core == k, coll[l, h], sib_coll[l, h])
                acc = acc + lax.dot_general(
                    shapes_ref[:, l * chunk:(l + 1) * chunk], block,
                    (((1,), (1,)), ((), ())), preferred_element_type=jnp.float32,
                )
            parts.append(acc)
    wbuf[col] = jnp.concatenate(parts, axis=1).astype(wbuf.dtype)

    wpeer = lambda k: lax.rem(col + k, n_col)
    wsender = lambda k: lax.rem(col + n_col - k, n_col)
    for k in range(1, n_col):
        step(wbuf.at[col], wbuf.at[col], k, device("pcol", wpeer(k)), (send_e, recv_e)).start()
    for k in range(1, n_col):
        step(wbuf.at[col], wbuf.at[col], k, device("pcol", wpeer(k)), (send_e, recv_e)).wait_send()
    for k in range(1, n_col):
        step(wbuf.at[col], wbuf.at[wsender(k)], k, device("pcol", wsender(k)), (send_e, recv_e)).wait_recv()
    out_ref[...] = wbuf[...]


def gram_weighted(x, mode_shapes, axes, sizes):
    n, rows, width = x.shape
    n_col = sizes["pcol"]
    wshape = (n_col, mode_shapes.shape[0], 4 * rows)
    kernel = functools.partial(gram_weighted_kernel, axes=axes, factors=factor_table(sizes))
    return pl.pallas_call(
        kernel,
        out_shape=jax.ShapeDtypeStruct(wshape, jnp.bfloat16),
        in_specs=[pl.BlockSpec(memory_space=pltpu.VMEM)] * 2,
        out_specs=pl.BlockSpec(memory_space=pltpu.VMEM),
        scratch_shapes=[
            pltpu.VMEM(x.shape, x.dtype),
            pltpu.VMEM((n, 2, rows, width), x.dtype),
            pltpu.VMEM((n, 2, rows, width), x.dtype),
            pltpu.VMEM((rows, width), x.dtype),
            pltpu.VMEM((rows, width), x.dtype),
            pltpu.VMEM(wshape, jnp.bfloat16),
            pltpu.SemaphoreType.DMA((n,)),
            pltpu.SemaphoreType.DMA((n,)),
            pltpu.SemaphoreType.DMA(()),
            pltpu.SemaphoreType.DMA(()),
            pltpu.SemaphoreType.DMA((n,)),
            pltpu.SemaphoreType.DMA((n,)),
            pltpu.SemaphoreType.DMA(()),
            pltpu.SemaphoreType.DMA(()),
            pltpu.SemaphoreType.DMA((n_col,)),
            pltpu.SemaphoreType.DMA((n_col,)),
        ],
        compiler_params=pltpu.CompilerParams(collective_id=103, has_side_effects=True),
    )(x, mode_shapes)


def fused_sum(x, axes, sizes, over, add_across, kernel_id):
    n, rows, width = x.shape
    block = (rows, width) if add_across else (2, rows, width)
    kernel = functools.partial(
        fused_sum_kernel, axes=axes, factors=factor_table(sizes), over=over, add_across=add_across
    )
    return pl.pallas_call(
        kernel,
        out_shape=jax.ShapeDtypeStruct((n,) + block, x.dtype),
        in_specs=[pl.BlockSpec(memory_space=pltpu.VMEM)],
        out_specs=pl.BlockSpec(memory_space=pltpu.VMEM),
        scratch_shapes=[
            pltpu.VMEM(x.shape, x.dtype),
            pltpu.VMEM((n,) + block, x.dtype),
            pltpu.VMEM((rows, width), x.dtype),
            pltpu.VMEM((rows, width), x.dtype),
            pltpu.SemaphoreType.DMA((n,)),
            pltpu.SemaphoreType.DMA((n,)),
            pltpu.SemaphoreType.DMA(()),
            pltpu.SemaphoreType.DMA(()),
            pltpu.SemaphoreType.DMA((n,)),
            pltpu.SemaphoreType.DMA((n,)),
        ],
        compiler_params=pltpu.CompilerParams(collective_id=kernel_id, has_side_effects=True),
    )(x)


class Exchanger:
    def __init__(self, axes, sizes):
        self.axes, self.factors, self.calls = axes, factor_table(sizes), 0

    def __call__(self, x, group, same):
        count = math.prod(self.factors[f][1] for f in group)
        block = x.shape if same else x.shape[1:]
        if count == 1:
            return x[None] if same else x
        kernel = functools.partial(
            exchange_kernel, axes=self.axes, factors=self.factors, group=group, same=same
        )
        self.calls += 1
        return pl.pallas_call(
            kernel,
            out_shape=jax.ShapeDtypeStruct((count,) + tuple(block), x.dtype),
            in_specs=[pl.BlockSpec(memory_space=pl.ANY)],
            out_specs=pl.BlockSpec(memory_space=pl.ANY),
            scratch_shapes=[
                pltpu.SemaphoreType.DMA((count,)),
                pltpu.SemaphoreType.DMA((count,)),
                pltpu.SemaphoreType.DMA(()),
            ],
            compiler_params=pltpu.CompilerParams(collective_id=self.calls, has_side_effects=True),
        )(x)


def make_body(axes, sizes):
    n_row, n_col, n_pl = sizes["prow"], sizes["pcol"], sizes["pl"]
    swap = [(c * n_col + r, r * n_col + c) for r in range(n_row) for c in range(n_col)]
    sibling = [(r, r ^ 1) for r in range(n_row)]
    n_zh = n_row // 2

    def beside_sibling(part, core):
        other = lax.ppermute(part, "prow", sibling)
        first, second = jnp.where(core == 0, part, other), jnp.where(core == 0, other, part)
        return jnp.concatenate([first, second], axis=0)

    def body(factor_cols, modal_at_loads, mode_shapes, natural_freq, damping):
        ex = Exchanger(axes, sizes)
        in_phase, quadrature = transfer_pair(natural_freq, damping)
        modes = modal_at_loads.shape[0]
        block = modes // (n_row * n_col)
        row, col = lax.axis_index("prow"), lax.axis_index("pcol")
        partial_load = jnp.dot(modal_at_loads, factor_cols, preferred_element_type=jnp.float32)
        width = partial_load.shape[1]
        core = row % 2
        mine = lax.dynamic_slice_in_dim(partial_load, core * (modes // 2), modes // 2, 0)
        theirs = lax.dynamic_slice_in_dim(partial_load, (1 - core) * (modes // 2), modes // 2, 0)
        modal_load = modal_sum(mine, theirs.astype(jnp.bfloat16), axes, sizes).reshape(modes, width)
        modal_wide = modal_load.astype(jnp.float32)
        pseudo = jnp.concatenate(
            [
                (in_phase[:, None] * modal_wide).astype(jnp.bfloat16),
                (quadrature[:, None] * modal_wide).astype(jnp.bfloat16),
            ],
            axis=1,
        )
        first_row = (col * n_row + row) * block
        own_pseudo = lax.dynamic_slice_in_dim(pseudo, first_row, block, 0)
        partial_gram = outer_rows(own_pseudo, pseudo).astype(jnp.bfloat16)
        chunk = modes // n_pl
        by_chunk = partial_gram.reshape(block, n_pl, chunk).transpose(1, 0, 2)
        half = modes // 2
        send_half = lax.dynamic_slice_in_dim(mode_shapes, (col % 2) * half, half, 1)
        panel_piece = lax.ppermute(send_half, ("prow", "pcol"), swap)
        panel_mine = lax.all_gather(panel_piece, "pl", axis=0, tiled=True)
        weighted_all = gram_weighted(by_chunk, mode_shapes, axes, sizes)
        panel_mine, weighted_all = lax.optimization_barrier((panel_mine, weighted_all))
        panel_other = lax.ppermute(panel_mine, "prow", sibling)
        weighted = weighted_all.transpose(1, 0, 2).reshape(mode_shapes.shape[0], modes)
        weighted_mine = lax.dynamic_slice_in_dim(weighted, core * half, half, 1)
        weighted_other = lax.dynamic_slice_in_dim(weighted, (1 - core) * half, half, 1)
        return outer_rows(weighted_other, panel_other) + outer_rows(weighted_mine, panel_mine)

    return body


def solution(mesh):
    in_specs = (
        P(("prow", "pcol"), "pl"),
        P(None, ("prow", "pcol")),
        P(("prow", "pl"), None),
        P(),
        P(),
    )
    out_specs = P(("prow", "pl"), "pcol")
    axes = tuple(mesh.axis_names)
    body = make_body(axes, dict(mesh.shape))
    return jax.shard_map(body, mesh=mesh, in_specs=in_specs, out_specs=out_specs, check_vma=False)
```

```python
import functools
import math

import jax
import jax.numpy as jnp
from jax import lax
from jax.experimental import pallas as pl
from jax.experimental.pallas import tpu as pltpu
from jax.sharding import PartitionSpec as P

MESH = pl.DeviceIdType.MESH


def transfer_pair(natural_freq, damping):
    detuning = natural_freq * natural_freq - 1.0
    damper = 2.0 * damping * natural_freq
    modulus = detuning * detuning + damper * damper
    return (detuning / modulus, -damper / modulus)


def outer_rows(left_rows, right_rows):
    return lax.dot_general(
        left_rows, right_rows, (((1,), (1,)), ((), ())), preferred_element_type=jnp.float32
    )


def factor_table(sizes):
    return {
        "zh": ("prow", sizes["prow"] // 2, 2),
        "core": ("prow", 2, 1),
        "pcol": ("pcol", sizes["pcol"], 1),
        "pl": ("pl", sizes["pl"], 1),
    }


def exchange_kernel(x_ref, out_ref, send_sem, recv_sem, local_sem, *, axes, factors, group, same):
    coords = {a: lax.axis_index(a) for a in axes}

    def value(f):
        axis, size, stride = factors[f]
        return lax.rem(coords[axis] // stride, size)

    count = math.prod(factors[f][1] for f in group)
    me = 0
    for f in group:
        me = me * factors[f][1] + value(f)

    def device(member):
        place = dict(coords)
        for f in reversed(group):
            axis, size, stride = factors[f]
            place[axis] = place[axis] + (lax.rem(member, size) - value(f)) * stride
            member = member // size
        return tuple(place[a] for a in axes)

    def source(member):
        return x_ref if same else x_ref.at[member]

    def copy(offset):
        peer = lax.rem(me + offset, count)
        return pltpu.make_async_remote_copy(
            src_ref=source(peer),
            dst_ref=out_ref.at[me],
            send_sem=send_sem.at[offset],
            recv_sem=recv_sem.at[offset],
            device_id=device(peer),
            device_id_type=MESH,
        )

    def landing(offset):
        sender = lax.rem(me + count - offset, count)
        return pltpu.make_async_remote_copy(
            src_ref=source(me),
            dst_ref=out_ref.at[sender],
            send_sem=send_sem.at[offset],
            recv_sem=recv_sem.at[offset],
            device_id=device(sender),
            device_id_type=MESH,
        )

    local = pltpu.make_async_copy(source(me), out_ref.at[me], local_sem)
    local.start()
    barrier = pltpu.get_barrier_semaphore()
    for offset in range(1, count):
        peer = lax.rem(me + offset, count)
        pl.semaphore_signal(barrier, inc=1, device_id=device(peer), device_id_type=MESH)
    pl.semaphore_wait(barrier, count - 1)
    for offset in range(1, count):
        copy(offset).start()
    local.wait()
    for offset in range(1, count):
        copy(offset).wait_send()
    for offset in range(1, count):
        landing(offset).wait_recv()


def fused_sum_kernel(x_ref, out_ref, got, coll, part_out, part_in, send_a, recv_a, send_b, recv_b,
                     send_c, recv_c, *, axes, factors, over, add_across):
    coords = {a: lax.axis_index(a) for a in axes}

    def value(f):
        axis, size, stride = factors[f]
        return lax.rem(coords[axis] // stride, size)

    def device(f, v):
        place = dict(coords)
        axis, size, stride = factors[f]
        place[axis] = place[axis] + (v - value(f)) * stride
        return tuple(place[a] for a in axes)

    n = factors[over][1]
    me, half = value(over), value("zh")
    partner = device("zh", 1 - half)
    peer = lambda k: lax.rem(me + k, n)
    sender = lambda k: lax.rem(me + n - k, n)

    def step(src, dst_at, k, to, sems):
        return pltpu.make_async_remote_copy(
            src_ref=src, dst_ref=dst_at, send_sem=sems[0].at[k], recv_sem=sems[1].at[k],
            device_id=to, device_id_type=MESH,
        )

    barrier = pltpu.get_barrier_semaphore()
    for k in range(1, n):
        pl.semaphore_signal(barrier, inc=1, device_id=device(over, peer(k)), device_id_type=MESH)
    pl.semaphore_signal(barrier, inc=1, device_id=partner, device_id_type=MESH)
    pl.semaphore_wait(barrier, n)

    for k in range(1, n):
        step(x_ref.at[peer(k)], got.at[me], k, device(over, peer(k)), (send_a, recv_a)).start()
    for k in range(1, n):
        step(x_ref.at[peer(k)], got.at[me], k, device(over, peer(k)), (send_a, recv_a)).wait_send()
    for k in range(1, n):
        step(x_ref.at[me], got.at[sender(k)], k, device(over, sender(k)), (send_a, recv_a)).wait_recv()
    total = x_ref[me].astype(jnp.float32)
    for k in range(1, n):
        total = total + got[sender(k)].astype(jnp.float32)
    part_out[...] = total.astype(part_out.dtype)

    across = pltpu.make_async_remote_copy(
        src_ref=part_out, dst_ref=part_in, send_sem=send_b, recv_sem=recv_b,
        device_id=partner, device_id_type=MESH,
    )
    across.start()
    across.wait_send()
    across.wait_recv()
    if add_across:
        mine, theirs = part_out[...].astype(jnp.float32), part_in[...].astype(jnp.float32)
        coll[me] = (mine + theirs).astype(coll.dtype)
    else:
        mine, theirs = part_out[...], part_in[...]
        first = jnp.where(half == 0, mine, theirs)
        second = jnp.where(half == 0, theirs, mine)
        coll[me] = jnp.stack([first, second])

    for k in range(1, n):
        step(coll.at[me], coll.at[me], k, device(over, peer(k)), (send_c, recv_c)).start()
    for k in range(1, n):
        step(coll.at[me], coll.at[me], k, device(over, peer(k)), (send_c, recv_c)).wait_send()
    for k in range(1, n):
        step(coll.at[me], coll.at[sender(k)], k, device(over, sender(k)), (send_c, recv_c)).wait_recv()
    out_ref[...] = coll[...]


def modal_sum_kernel(mine_ref, theirs_ref, out_ref, sib_in, pieces, got, coll, part_out, part_in,
                     sib_out, send_s, recv_s, send_a, recv_a, send_b, recv_b, send_c, recv_c,
                     send_d, recv_d, *, axes, factors):
    coords = {a: lax.axis_index(a) for a in axes}

    def value(f):
        axis, size, stride = factors[f]
        return lax.rem(coords[axis] // stride, size)

    def device(f, v):
        place = dict(coords)
        axis, size, stride = factors[f]
        place[axis] = place[axis] + (v - value(f)) * stride
        return tuple(place[a] for a in axes)

    n = factors["pcol"][1]
    me, half, core = value("pcol"), value("zh"), value("core")
    partner, sibling = device("zh", 1 - half), device("core", 1 - core)
    peer = lambda k: lax.rem(me + k, n)
    sender = lambda k: lax.rem(me + n - k, n)

    def step(src, dst_at, k, to, sems):
        return pltpu.make_async_remote_copy(
            src_ref=src, dst_ref=dst_at, send_sem=sems[0].at[k], recv_sem=sems[1].at[k],
            device_id=to, device_id_type=MESH,
        )

    def one(src, dst, to, send_sem, recv_sem):
        return pltpu.make_async_remote_copy(
            src_ref=src, dst_ref=dst, send_sem=send_sem, recv_sem=recv_sem,
            device_id=to, device_id_type=MESH,
        )

    barrier = pltpu.get_barrier_semaphore()
    for k in range(1, n):
        pl.semaphore_signal(barrier, inc=1, device_id=device("pcol", peer(k)), device_id_type=MESH)
    pl.semaphore_signal(barrier, inc=1, device_id=partner, device_id_type=MESH)
    pl.semaphore_signal(barrier, inc=1, device_id=sibling, device_id_type=MESH)
    pl.semaphore_wait(barrier, n + 1)

    chip = one(theirs_ref, sib_in, sibling, send_s, recv_s)
    chip.start()
    chip.wait_send()
    chip.wait_recv()
    summed = mine_ref[...] + sib_in[...].astype(jnp.float32)
    pieces[...] = summed.astype(pieces.dtype).reshape(pieces.shape)

    for k in range(1, n):
        step(pieces.at[peer(k)], got.at[me], k, device("pcol", peer(k)), (send_a, recv_a)).start()
    for k in range(1, n):
        step(pieces.at[peer(k)], got.at[me], k, device("pcol", peer(k)), (send_a, recv_a)).wait_send()
    for k in range(1, n):
        step(pieces.at[me], got.at[sender(k)], k, device("pcol", sender(k)), (send_a, recv_a)).wait_recv()
    total = pieces[me].astype(jnp.float32)
    for k in range(1, n):
        total = total + got[sender(k)].astype(jnp.float32)
    part_out[...] = total.astype(part_out.dtype)

    across = one(part_out, part_in, partner, send_b, recv_b)
    across.start()
    across.wait_send()
    across.wait_recv()
    coll[me] = (part_out[...].astype(jnp.float32) + part_in[...].astype(jnp.float32)).astype(coll.dtype)

    for k in range(1, n):
        step(coll.at[me], coll.at[me], k, device("pcol", peer(k)), (send_c, recv_c)).start()
    for k in range(1, n):
        step(coll.at[me], coll.at[me], k, device("pcol", peer(k)), (send_c, recv_c)).wait_send()
    for k in range(1, n):
        step(coll.at[me], coll.at[sender(k)], k, device("pcol", sender(k)), (send_c, recv_c)).wait_recv()

    join = one(coll, sib_out, sibling, send_d, recv_d)
    join.start()
    join.wait_send()
    join.wait_recv()
    out_ref[core] = coll[...]
    out_ref[1 - core] = sib_out[...]


def modal_sum(mine, theirs, axes, sizes):
    n = sizes["pcol"]
    rows, width = mine.shape
    block = (n, rows // n, width)
    kernel = functools.partial(modal_sum_kernel, axes=axes, factors=factor_table(sizes))
    return pl.pallas_call(
        kernel,
        out_shape=jax.ShapeDtypeStruct((2,) + block, jnp.bfloat16),
        in_specs=[pl.BlockSpec(memory_space=pltpu.VMEM)] * 2,
        out_specs=pl.BlockSpec(memory_space=pltpu.VMEM),
        scratch_shapes=[
            pltpu.VMEM((rows, width), jnp.bfloat16),
            pltpu.VMEM(block, jnp.bfloat16),
            pltpu.VMEM(block, jnp.bfloat16),
            pltpu.VMEM(block, jnp.bfloat16),
            pltpu.VMEM(block[1:], jnp.bfloat16),
            pltpu.VMEM(block[1:], jnp.bfloat16),
            pltpu.VMEM(block, jnp.bfloat16),
            pltpu.SemaphoreType.DMA(()),
            pltpu.SemaphoreType.DMA(()),
            pltpu.SemaphoreType.DMA((n,)),
            pltpu.SemaphoreType.DMA((n,)),
            pltpu.SemaphoreType.DMA(()),
            pltpu.SemaphoreType.DMA(()),
            pltpu.SemaphoreType.DMA((n,)),
            pltpu.SemaphoreType.DMA((n,)),
            pltpu.SemaphoreType.DMA(()),
            pltpu.SemaphoreType.DMA(()),
        ],
        compiler_params=pltpu.CompilerParams(collective_id=102, has_side_effects=True),
    )(mine, theirs)


def gram_weighted_kernel(x_ref, shapes_ref, out_ref, got, coll, sib_coll, part_out, part_in, wbuf,
                         send_a, recv_a, send_b, recv_b, send_c, recv_c, send_d, recv_d, send_e,
                         recv_e, *, axes, factors):
    coords = {a: lax.axis_index(a) for a in axes}

    def value(f):
        axis, size, stride = factors[f]
        return lax.rem(coords[axis] // stride, size)

    def device(f, v):
        place = dict(coords)
        axis, size, stride = factors[f]
        place[axis] = place[axis] + (v - value(f)) * stride
        return tuple(place[a] for a in axes)

    n, n_col = factors["pl"][1], factors["pcol"][1]
    me, half, core, col = value("pl"), value("zh"), value("core"), value("pcol")
    partner, sibling = device("zh", 1 - half), device("core", 1 - core)

    def step(src, dst_at, k, to, sems):
        return pltpu.make_async_remote_copy(
            src_ref=src, dst_ref=dst_at, send_sem=sems[0].at[k], recv_sem=sems[1].at[k],
            device_id=to, device_id_type=MESH,
        )

    def one(src, dst, to, send_sem, recv_sem):
        return pltpu.make_async_remote_copy(
            src_ref=src, dst_ref=dst, send_sem=send_sem, recv_sem=recv_sem,
            device_id=to, device_id_type=MESH,
        )

    barrier = pltpu.get_barrier_semaphore()
    for k in range(1, n):
        pl.semaphore_signal(barrier, inc=1, device_id=device("pl", lax.rem(me + k, n)), device_id_type=MESH)
    for k in range(1, n_col):
        pl.semaphore_signal(
            barrier, inc=1, device_id=device("pcol", lax.rem(col + k, n_col)), device_id_type=MESH
        )
    pl.semaphore_signal(barrier, inc=1, device_id=partner, device_id_type=MESH)
    pl.semaphore_signal(barrier, inc=1, device_id=sibling, device_id_type=MESH)
    pl.semaphore_wait(barrier, n + n_col)

    peer = lambda k: lax.rem(me + k, n)
    sender = lambda k: lax.rem(me + n - k, n)
    for k in range(1, n):
        step(x_ref.at[peer(k)], got.at[me], k, device("pl", peer(k)), (send_a, recv_a)).start()
    for k in range(1, n):
        step(x_ref.at[peer(k)], got.at[me], k, device("pl", peer(k)), (send_a, recv_a)).wait_send()
    for k in range(1, n):
        step(x_ref.at[me], got.at[sender(k)], k, device("pl", sender(k)), (send_a, recv_a)).wait_recv()
    total = x_ref[me].astype(jnp.float32)
    for k in range(1, n):
        total = total + got[sender(k)].astype(jnp.float32)
    part_out[...] = total.astype(part_out.dtype)

    across = one(part_out, part_in, partner, send_b, recv_b)
    across.start()
    across.wait_send()
    across.wait_recv()
    mine, theirs = part_out[...], part_in[...]
    coll[me] = jnp.stack([jnp.where(half == 0, mine, theirs), jnp.where(half == 0, theirs, mine)])

    for k in range(1, n):
        step(coll.at[me], coll.at[me], k, device("pl", peer(k)), (send_c, recv_c)).start()
    for k in range(1, n):
        step(coll.at[me], coll.at[me], k, device("pl", peer(k)), (send_c, recv_c)).wait_send()
    for k in range(1, n):
        step(coll.at[me], coll.at[sender(k)], k, device("pl", sender(k)), (send_c, recv_c)).wait_recv()

    join = one(coll, sib_coll, sibling, send_d, recv_d)
    join.start()
    join.wait_send()
    join.wait_recv()

    shapes = shapes_ref[...]
    parts = []
    for h in range(2):
        own, other = (
            jnp.einsum("laj,lij->lai", shapes, blocks[:, h], preferred_element_type=jnp.float32).sum(0)
            for blocks in (coll, sib_coll)
        )
        parts += [jnp.where(core == 0, own, other), jnp.where(core == 0, other, own)]
    wbuf[col] = jnp.concatenate(parts, axis=1).astype(wbuf.dtype)

    wpeer = lambda k: lax.rem(col + k, n_col)
    wsender = lambda k: lax.rem(col + n_col - k, n_col)
    for k in range(1, n_col):
        step(wbuf.at[col], wbuf.at[col], k, device("pcol", wpeer(k)), (send_e, recv_e)).start()
    for k in range(1, n_col):
        step(wbuf.at[col], wbuf.at[col], k, device("pcol", wpeer(k)), (send_e, recv_e)).wait_send()
    for k in range(1, n_col):
        step(wbuf.at[col], wbuf.at[wsender(k)], k, device("pcol", wsender(k)), (send_e, recv_e)).wait_recv()
    out_ref[...] = wbuf[...]


def gram_weighted(x, mode_shapes, axes, sizes):
    n, rows, width = x.shape
    n_col = sizes["pcol"]
    wshape = (n_col, mode_shapes.shape[0], 4 * rows)
    by_chunk = mode_shapes.reshape(mode_shapes.shape[0], n, width).transpose(1, 0, 2)
    kernel = functools.partial(gram_weighted_kernel, axes=axes, factors=factor_table(sizes))
    return pl.pallas_call(
        kernel,
        out_shape=jax.ShapeDtypeStruct(wshape, jnp.bfloat16),
        in_specs=[pl.BlockSpec(memory_space=pltpu.VMEM)] * 2,
        out_specs=pl.BlockSpec(memory_space=pltpu.VMEM),
        scratch_shapes=[
            pltpu.VMEM(x.shape, x.dtype),
            pltpu.VMEM((n, 2, rows, width), x.dtype),
            pltpu.VMEM((n, 2, rows, width), x.dtype),
            pltpu.VMEM((rows, width), x.dtype),
            pltpu.VMEM((rows, width), x.dtype),
            pltpu.VMEM(wshape, jnp.bfloat16),
            pltpu.SemaphoreType.DMA((n,)),
            pltpu.SemaphoreType.DMA((n,)),
            pltpu.SemaphoreType.DMA(()),
            pltpu.SemaphoreType.DMA(()),
            pltpu.SemaphoreType.DMA((n,)),
            pltpu.SemaphoreType.DMA((n,)),
            pltpu.SemaphoreType.DMA(()),
            pltpu.SemaphoreType.DMA(()),
            pltpu.SemaphoreType.DMA((n_col,)),
            pltpu.SemaphoreType.DMA((n_col,)),
        ],
        compiler_params=pltpu.CompilerParams(collective_id=103, has_side_effects=True),
    )(x, by_chunk)


def fused_sum(x, axes, sizes, over, add_across, kernel_id):
    n, rows, width = x.shape
    block = (rows, width) if add_across else (2, rows, width)
    kernel = functools.partial(
        fused_sum_kernel, axes=axes, factors=factor_table(sizes), over=over, add_across=add_across
    )
    return pl.pallas_call(
        kernel,
        out_shape=jax.ShapeDtypeStruct((n,) + block, x.dtype),
        in_specs=[pl.BlockSpec(memory_space=pltpu.VMEM)],
        out_specs=pl.BlockSpec(memory_space=pltpu.VMEM),
        scratch_shapes=[
            pltpu.VMEM(x.shape, x.dtype),
            pltpu.VMEM((n,) + block, x.dtype),
            pltpu.VMEM((rows, width), x.dtype),
            pltpu.VMEM((rows, width), x.dtype),
            pltpu.SemaphoreType.DMA((n,)),
            pltpu.SemaphoreType.DMA((n,)),
            pltpu.SemaphoreType.DMA(()),
            pltpu.SemaphoreType.DMA(()),
            pltpu.SemaphoreType.DMA((n,)),
            pltpu.SemaphoreType.DMA((n,)),
        ],
        compiler_params=pltpu.CompilerParams(collective_id=kernel_id, has_side_effects=True),
    )(x)


class Exchanger:
    def __init__(self, axes, sizes):
        self.axes, self.factors, self.calls = axes, factor_table(sizes), 0

    def __call__(self, x, group, same):
        count = math.prod(self.factors[f][1] for f in group)
        block = x.shape if same else x.shape[1:]
        if count == 1:
            return x[None] if same else x
        kernel = functools.partial(
            exchange_kernel, axes=self.axes, factors=self.factors, group=group, same=same
        )
        self.calls += 1
        return pl.pallas_call(
            kernel,
            out_shape=jax.ShapeDtypeStruct((count,) + tuple(block), x.dtype),
            in_specs=[pl.BlockSpec(memory_space=pl.ANY)],
            out_specs=pl.BlockSpec(memory_space=pl.ANY),
            scratch_shapes=[
                pltpu.SemaphoreType.DMA((count,)),
                pltpu.SemaphoreType.DMA((count,)),
                pltpu.SemaphoreType.DMA(()),
            ],
            compiler_params=pltpu.CompilerParams(collective_id=self.calls, has_side_effects=True),
        )(x)


def make_body(axes, sizes):
    n_row, n_col, n_pl = sizes["prow"], sizes["pcol"], sizes["pl"]
    swap = [(c * n_col + r, r * n_col + c) for r in range(n_row) for c in range(n_col)]
    sibling = [(r, r ^ 1) for r in range(n_row)]
    n_zh = n_row // 2

    def beside_sibling(part, core):
        other = lax.ppermute(part, "prow", sibling)
        first, second = jnp.where(core == 0, part, other), jnp.where(core == 0, other, part)
        return jnp.concatenate([first, second], axis=0)

    def body(factor_cols, modal_at_loads, mode_shapes, natural_freq, damping):
        ex = Exchanger(axes, sizes)
        in_phase, quadrature = transfer_pair(natural_freq, damping)
        modes = modal_at_loads.shape[0]
        block = modes // (n_row * n_col)
        row, col = lax.axis_index("prow"), lax.axis_index("pcol")
        partial_load = jnp.dot(modal_at_loads, factor_cols, preferred_element_type=jnp.float32)
        width = partial_load.shape[1]
        core = row % 2
        mine = lax.dynamic_slice_in_dim(partial_load, core * (modes // 2), modes // 2, 0)
        theirs = lax.dynamic_slice_in_dim(partial_load, (1 - core) * (modes // 2), modes // 2, 0)
        modal_load = modal_sum(mine, theirs.astype(jnp.bfloat16), axes, sizes).reshape(modes, width)
        modal_wide = modal_load.astype(jnp.float32)
        pseudo = jnp.concatenate(
            [
                (in_phase[:, None] * modal_wide).astype(jnp.bfloat16),
                (quadrature[:, None] * modal_wide).astype(jnp.bfloat16),
            ],
            axis=1,
        )
        first_row = (col * n_row + row) * block
        own_pseudo = lax.dynamic_slice_in_dim(pseudo, first_row, block, 0)
        partial_gram = outer_rows(own_pseudo, pseudo).astype(jnp.bfloat16)
        chunk = modes // n_pl
        by_chunk = partial_gram.reshape(block, n_pl, chunk).transpose(1, 0, 2)
        half = modes // 2
        send_half = lax.dynamic_slice_in_dim(mode_shapes, (col % 2) * half, half, 1)
        panel_piece = lax.ppermute(send_half, ("prow", "pcol"), swap)
        panel_mine = lax.all_gather(panel_piece, "pl", axis=0, tiled=True)
        weighted_all = gram_weighted(by_chunk, mode_shapes, axes, sizes)
        panel_mine, weighted_all = lax.optimization_barrier((panel_mine, weighted_all))
        panel_other = lax.ppermute(panel_mine, "prow", sibling)
        weighted = weighted_all.transpose(1, 0, 2).reshape(mode_shapes.shape[0], modes)
        weighted_mine = lax.dynamic_slice_in_dim(weighted, core * half, half, 1)
        weighted_other = lax.dynamic_slice_in_dim(weighted, (1 - core) * half, half, 1)
        return outer_rows(weighted_other, panel_other) + outer_rows(weighted_mine, panel_mine)

    return body


def solution(mesh):
    in_specs = (
        P(("prow", "pcol"), "pl"),
        P(None, ("prow", "pcol")),
        P(("prow", "pl"), None),
        P(),
        P(),
    )
    out_specs = P(("prow", "pl"), "pcol")
    axes = tuple(mesh.axis_names)
    body = make_body(axes, dict(mesh.shape))
    return jax.shard_map(body, mesh=mesh, in_specs=in_specs, out_specs=out_specs, check_vma=False)
```

```python
import functools
import math

import jax
import jax.numpy as jnp
from jax import lax
from jax.experimental import pallas as pl
from jax.experimental.pallas import tpu as pltpu
from jax.sharding import PartitionSpec as P

MESH = pl.DeviceIdType.MESH


def transfer_pair(natural_freq, damping):
    detuning = natural_freq * natural_freq - 1.0
    damper = 2.0 * damping * natural_freq
    modulus = detuning * detuning + damper * damper
    return (detuning / modulus, -damper / modulus)


def outer_rows(left_rows, right_rows):
    return lax.dot_general(
        left_rows, right_rows, (((1,), (1,)), ((), ())), preferred_element_type=jnp.float32
    )


def factor_table(sizes):
    return {
        "zh": ("prow", sizes["prow"] // 2, 2),
        "core": ("prow", 2, 1),
        "pcol": ("pcol", sizes["pcol"], 1),
        "pl": ("pl", sizes["pl"], 1),
    }


def exchange_kernel(x_ref, out_ref, send_sem, recv_sem, local_sem, *, axes, factors, group, same):
    coords = {a: lax.axis_index(a) for a in axes}

    def value(f):
        axis, size, stride = factors[f]
        return lax.rem(coords[axis] // stride, size)

    count = math.prod(factors[f][1] for f in group)
    me = 0
    for f in group:
        me = me * factors[f][1] + value(f)

    def device(member):
        place = dict(coords)
        for f in reversed(group):
            axis, size, stride = factors[f]
            place[axis] = place[axis] + (lax.rem(member, size) - value(f)) * stride
            member = member // size
        return tuple(place[a] for a in axes)

    def source(member):
        return x_ref if same else x_ref.at[member]

    def copy(offset):
        peer = lax.rem(me + offset, count)
        return pltpu.make_async_remote_copy(
            src_ref=source(peer),
            dst_ref=out_ref.at[me],
            send_sem=send_sem.at[offset],
            recv_sem=recv_sem.at[offset],
            device_id=device(peer),
            device_id_type=MESH,
        )

    def landing(offset):
        sender = lax.rem(me + count - offset, count)
        return pltpu.make_async_remote_copy(
            src_ref=source(me),
            dst_ref=out_ref.at[sender],
            send_sem=send_sem.at[offset],
            recv_sem=recv_sem.at[offset],
            device_id=device(sender),
            device_id_type=MESH,
        )

    local = pltpu.make_async_copy(source(me), out_ref.at[me], local_sem)
    local.start()
    barrier = pltpu.get_barrier_semaphore()
    for offset in range(1, count):
        peer = lax.rem(me + offset, count)
        pl.semaphore_signal(barrier, inc=1, device_id=device(peer), device_id_type=MESH)
    pl.semaphore_wait(barrier, count - 1)
    for offset in range(1, count):
        copy(offset).start()
    local.wait()
    for offset in range(1, count):
        copy(offset).wait_send()
    for offset in range(1, count):
        landing(offset).wait_recv()


def fused_sum_kernel(x_ref, out_ref, got, coll, part_out, part_in, send_a, recv_a, send_b, recv_b,
                     send_c, recv_c, *, axes, factors, over, add_across):
    coords = {a: lax.axis_index(a) for a in axes}

    def value(f):
        axis, size, stride = factors[f]
        return lax.rem(coords[axis] // stride, size)

    def device(f, v):
        place = dict(coords)
        axis, size, stride = factors[f]
        place[axis] = place[axis] + (v - value(f)) * stride
        return tuple(place[a] for a in axes)

    n = factors[over][1]
    me, half = value(over), value("zh")
    partner = device("zh", 1 - half)
    peer = lambda k: lax.rem(me + k, n)
    sender = lambda k: lax.rem(me + n - k, n)

    def step(src, dst_at, k, to, sems):
        return pltpu.make_async_remote_copy(
            src_ref=src, dst_ref=dst_at, send_sem=sems[0].at[k], recv_sem=sems[1].at[k],
            device_id=to, device_id_type=MESH,
        )

    barrier = pltpu.get_barrier_semaphore()
    for k in range(1, n):
        pl.semaphore_signal(barrier, inc=1, device_id=device(over, peer(k)), device_id_type=MESH)
    pl.semaphore_signal(barrier, inc=1, device_id=partner, device_id_type=MESH)
    pl.semaphore_wait(barrier, n)

    for k in range(1, n):
        step(x_ref.at[peer(k)], got.at[me], k, device(over, peer(k)), (send_a, recv_a)).start()
    for k in range(1, n):
        step(x_ref.at[peer(k)], got.at[me], k, device(over, peer(k)), (send_a, recv_a)).wait_send()
    for k in range(1, n):
        step(x_ref.at[me], got.at[sender(k)], k, device(over, sender(k)), (send_a, recv_a)).wait_recv()
    total = x_ref[me].astype(jnp.float32)
    for k in range(1, n):
        total = total + got[sender(k)].astype(jnp.float32)
    part_out[...] = total.astype(part_out.dtype)

    across = pltpu.make_async_remote_copy(
        src_ref=part_out, dst_ref=part_in, send_sem=send_b, recv_sem=recv_b,
        device_id=partner, device_id_type=MESH,
    )
    across.start()
    across.wait_send()
    across.wait_recv()
    if add_across:
        mine, theirs = part_out[...].astype(jnp.float32), part_in[...].astype(jnp.float32)
        coll[me] = (mine + theirs).astype(coll.dtype)
    else:
        mine, theirs = part_out[...], part_in[...]
        first = jnp.where(half == 0, mine, theirs)
        second = jnp.where(half == 0, theirs, mine)
        coll[me] = jnp.stack([first, second])

    for k in range(1, n):
        step(coll.at[me], coll.at[me], k, device(over, peer(k)), (send_c, recv_c)).start()
    for k in range(1, n):
        step(coll.at[me], coll.at[me], k, device(over, peer(k)), (send_c, recv_c)).wait_send()
    for k in range(1, n):
        step(coll.at[me], coll.at[sender(k)], k, device(over, sender(k)), (send_c, recv_c)).wait_recv()
    out_ref[...] = coll[...]


def modal_sum_kernel(mine_ref, theirs_ref, out_ref, sib_in, pieces, got, coll, part_out, part_in,
                     sib_out, send_s, recv_s, send_a, recv_a, send_b, recv_b, send_c, recv_c,
                     send_d, recv_d, *, axes, factors):
    coords = {a: lax.axis_index(a) for a in axes}

    def value(f):
        axis, size, stride = factors[f]
        return lax.rem(coords[axis] // stride, size)

    def device(f, v):
        place = dict(coords)
        axis, size, stride = factors[f]
        place[axis] = place[axis] + (v - value(f)) * stride
        return tuple(place[a] for a in axes)

    n = factors["pcol"][1]
    me, half, core = value("pcol"), value("zh"), value("core")
    partner, sibling = device("zh", 1 - half), device("core", 1 - core)
    peer = lambda k: lax.rem(me + k, n)
    sender = lambda k: lax.rem(me + n - k, n)

    def step(src, dst_at, k, to, sems):
        return pltpu.make_async_remote_copy(
            src_ref=src, dst_ref=dst_at, send_sem=sems[0].at[k], recv_sem=sems[1].at[k],
            device_id=to, device_id_type=MESH,
        )

    def one(src, dst, to, send_sem, recv_sem):
        return pltpu.make_async_remote_copy(
            src_ref=src, dst_ref=dst, send_sem=send_sem, recv_sem=recv_sem,
            device_id=to, device_id_type=MESH,
        )

    barrier = pltpu.get_barrier_semaphore()
    for k in range(1, n):
        pl.semaphore_signal(barrier, inc=1, device_id=device("pcol", peer(k)), device_id_type=MESH)
    pl.semaphore_signal(barrier, inc=1, device_id=partner, device_id_type=MESH)
    pl.semaphore_signal(barrier, inc=1, device_id=sibling, device_id_type=MESH)
    pl.semaphore_wait(barrier, n + 1)

    chip = one(theirs_ref, sib_in, sibling, send_s, recv_s)
    chip.start()
    chip.wait_send()
    chip.wait_recv()
    summed = mine_ref[...] + sib_in[...].astype(jnp.float32)
    pieces[...] = summed.astype(pieces.dtype).reshape(pieces.shape)

    for k in range(1, n):
        step(pieces.at[peer(k)], got.at[me], k, device("pcol", peer(k)), (send_a, recv_a)).start()
    for k in range(1, n):
        step(pieces.at[peer(k)], got.at[me], k, device("pcol", peer(k)), (send_a, recv_a)).wait_send()
    for k in range(1, n):
        step(pieces.at[me], got.at[sender(k)], k, device("pcol", sender(k)), (send_a, recv_a)).wait_recv()
    total = pieces[me].astype(jnp.float32)
    for k in range(1, n):
        total = total + got[sender(k)].astype(jnp.float32)
    part_out[...] = total.astype(part_out.dtype)

    across = one(part_out, part_in, partner, send_b, recv_b)
    across.start()
    across.wait_send()
    across.wait_recv()
    coll[me] = (part_out[...].astype(jnp.float32) + part_in[...].astype(jnp.float32)).astype(coll.dtype)

    for k in range(1, n):
        step(coll.at[me], coll.at[me], k, device("pcol", peer(k)), (send_c, recv_c)).start()
    for k in range(1, n):
        step(coll.at[me], coll.at[me], k, device("pcol", peer(k)), (send_c, recv_c)).wait_send()
    for k in range(1, n):
        step(coll.at[me], coll.at[sender(k)], k, device("pcol", sender(k)), (send_c, recv_c)).wait_recv()

    join = one(coll, sib_out, sibling, send_d, recv_d)
    join.start()
    join.wait_send()
    join.wait_recv()
    out_ref[core] = coll[...]
    out_ref[1 - core] = sib_out[...]


def modal_sum(mine, theirs, axes, sizes):
    n = sizes["pcol"]
    rows, width = mine.shape
    block = (n, rows // n, width)
    kernel = functools.partial(modal_sum_kernel, axes=axes, factors=factor_table(sizes))
    return pl.pallas_call(
        kernel,
        out_shape=jax.ShapeDtypeStruct((2,) + block, jnp.bfloat16),
        in_specs=[pl.BlockSpec(memory_space=pltpu.VMEM)] * 2,
        out_specs=pl.BlockSpec(memory_space=pltpu.VMEM),
        scratch_shapes=[
            pltpu.VMEM((rows, width), jnp.bfloat16),
            pltpu.VMEM(block, jnp.bfloat16),
            pltpu.VMEM(block, jnp.bfloat16),
            pltpu.VMEM(block, jnp.bfloat16),
            pltpu.VMEM(block[1:], jnp.bfloat16),
            pltpu.VMEM(block[1:], jnp.bfloat16),
            pltpu.VMEM(block, jnp.bfloat16),
            pltpu.SemaphoreType.DMA(()),
            pltpu.SemaphoreType.DMA(()),
            pltpu.SemaphoreType.DMA((n,)),
            pltpu.SemaphoreType.DMA((n,)),
            pltpu.SemaphoreType.DMA(()),
            pltpu.SemaphoreType.DMA(()),
            pltpu.SemaphoreType.DMA((n,)),
            pltpu.SemaphoreType.DMA((n,)),
            pltpu.SemaphoreType.DMA(()),
            pltpu.SemaphoreType.DMA(()),
        ],
        compiler_params=pltpu.CompilerParams(collective_id=102, has_side_effects=True),
    )(mine, theirs)


def gram_weighted_kernel(x_ref, shapes_ref, out_ref, got, coll, sib_coll, part_out, part_in, wbuf,
                         send_a, recv_a, send_b, recv_b, send_c, recv_c, send_d, recv_d, send_e,
                         recv_e, *, axes, factors):
    coords = {a: lax.axis_index(a) for a in axes}

    def value(f):
        axis, size, stride = factors[f]
        return lax.rem(coords[axis] // stride, size)

    def device(f, v):
        place = dict(coords)
        axis, size, stride = factors[f]
        place[axis] = place[axis] + (v - value(f)) * stride
        return tuple(place[a] for a in axes)

    n, n_col = factors["pl"][1], factors["pcol"][1]
    me, half, core, col = value("pl"), value("zh"), value("core"), value("pcol")
    partner, sibling = device("zh", 1 - half), device("core", 1 - core)

    def step(src, dst_at, k, to, sems):
        return pltpu.make_async_remote_copy(
            src_ref=src, dst_ref=dst_at, send_sem=sems[0].at[k], recv_sem=sems[1].at[k],
            device_id=to, device_id_type=MESH,
        )

    def one(src, dst, to, send_sem, recv_sem):
        return pltpu.make_async_remote_copy(
            src_ref=src, dst_ref=dst, send_sem=send_sem, recv_sem=recv_sem,
            device_id=to, device_id_type=MESH,
        )

    barrier = pltpu.get_barrier_semaphore()
    for k in range(1, n):
        pl.semaphore_signal(barrier, inc=1, device_id=device("pl", lax.rem(me + k, n)), device_id_type=MESH)
    for k in range(1, n_col):
        pl.semaphore_signal(
            barrier, inc=1, device_id=device("pcol", lax.rem(col + k, n_col)), device_id_type=MESH
        )
    pl.semaphore_signal(barrier, inc=1, device_id=partner, device_id_type=MESH)
    pl.semaphore_signal(barrier, inc=1, device_id=sibling, device_id_type=MESH)
    pl.semaphore_wait(barrier, n + n_col)

    peer = lambda k: lax.rem(me + k, n)
    sender = lambda k: lax.rem(me + n - k, n)
    for k in range(1, n):
        step(x_ref.at[peer(k)], got.at[me], k, device("pl", peer(k)), (send_a, recv_a)).start()
    for k in range(1, n):
        step(x_ref.at[peer(k)], got.at[me], k, device("pl", peer(k)), (send_a, recv_a)).wait_send()
    for k in range(1, n):
        step(x_ref.at[me], got.at[sender(k)], k, device("pl", sender(k)), (send_a, recv_a)).wait_recv()
    total = x_ref[me].astype(jnp.float32)
    for k in range(1, n):
        total = total + got[sender(k)].astype(jnp.float32)
    part_out[...] = total.astype(part_out.dtype)

    across = one(part_out, part_in, partner, send_b, recv_b)
    across.start()
    across.wait_send()
    across.wait_recv()
    mine, theirs = part_out[...], part_in[...]
    coll[me] = jnp.stack([jnp.where(half == 0, mine, theirs), jnp.where(half == 0, theirs, mine)])

    for k in range(1, n):
        step(coll.at[me], coll.at[me], k, device("pl", peer(k)), (send_c, recv_c)).start()
    for k in range(1, n):
        step(coll.at[me], coll.at[me], k, device("pl", peer(k)), (send_c, recv_c)).wait_send()
    for k in range(1, n):
        step(coll.at[me], coll.at[sender(k)], k, device("pl", sender(k)), (send_c, recv_c)).wait_recv()

    join = one(coll, sib_coll, sibling, send_d, recv_d)
    join.start()
    join.wait_send()
    join.wait_recv()

    chunk = coll.shape[-1]
    parts = []
    for h in range(2):
        for k in range(2):
            acc = jnp.zeros((shapes_ref.shape[0], coll.shape[2]), jnp.float32)
            for l in range(n):
                block = jnp.where(core == k, coll[l, h], sib_coll[l, h])
                acc = acc + lax.dot_general(
                    shapes_ref[:, l * chunk:(l + 1) * chunk], block,
                    (((1,), (1,)), ((), ())), preferred_element_type=jnp.float32,
                )
            parts.append(acc)
    wbuf[col] = jnp.concatenate(parts, axis=1).astype(wbuf.dtype)

    wpeer = lambda k: lax.rem(col + k, n_col)
    wsender = lambda k: lax.rem(col + n_col - k, n_col)
    for k in range(1, n_col):
        step(wbuf.at[col], wbuf.at[col], k, device("pcol", wpeer(k)), (send_e, recv_e)).start()
    for k in range(1, n_col):
        step(wbuf.at[col], wbuf.at[col], k, device("pcol", wpeer(k)), (send_e, recv_e)).wait_send()
    for k in range(1, n_col):
        step(wbuf.at[col], wbuf.at[wsender(k)], k, device("pcol", wsender(k)), (send_e, recv_e)).wait_recv()
    width_w = wbuf.shape[2]
    for c in range(n_col):
        out_ref[:, c * width_w:(c + 1) * width_w] = wbuf[c]


def gram_weighted(x, mode_shapes, axes, sizes):
    n, rows, width = x.shape
    n_col = sizes["pcol"]
    wshape = (n_col, mode_shapes.shape[0], 4 * rows)
    kernel = functools.partial(gram_weighted_kernel, axes=axes, factors=factor_table(sizes))
    return pl.pallas_call(
        kernel,
        out_shape=jax.ShapeDtypeStruct((wshape[1], n_col * wshape[2]), jnp.bfloat16),
        in_specs=[pl.BlockSpec(memory_space=pltpu.VMEM)] * 2,
        out_specs=pl.BlockSpec(memory_space=pltpu.VMEM),
        scratch_shapes=[
            pltpu.VMEM(x.shape, x.dtype),
            pltpu.VMEM((n, 2, rows, width), x.dtype),
            pltpu.VMEM((n, 2, rows, width), x.dtype),
            pltpu.VMEM((rows, width), x.dtype),
            pltpu.VMEM((rows, width), x.dtype),
            pltpu.VMEM(wshape, jnp.bfloat16),
            pltpu.SemaphoreType.DMA((n,)),
            pltpu.SemaphoreType.DMA((n,)),
            pltpu.SemaphoreType.DMA(()),
            pltpu.SemaphoreType.DMA(()),
            pltpu.SemaphoreType.DMA((n,)),
            pltpu.SemaphoreType.DMA((n,)),
            pltpu.SemaphoreType.DMA(()),
            pltpu.SemaphoreType.DMA(()),
            pltpu.SemaphoreType.DMA((n_col,)),
            pltpu.SemaphoreType.DMA((n_col,)),
        ],
        compiler_params=pltpu.CompilerParams(collective_id=103, has_side_effects=True),
    )(x, mode_shapes)


def fused_sum(x, axes, sizes, over, add_across, kernel_id):
    n, rows, width = x.shape
    block = (rows, width) if add_across else (2, rows, width)
    kernel = functools.partial(
        fused_sum_kernel, axes=axes, factors=factor_table(sizes), over=over, add_across=add_across
    )
    return pl.pallas_call(
        kernel,
        out_shape=jax.ShapeDtypeStruct((n,) + block, x.dtype),
        in_specs=[pl.BlockSpec(memory_space=pltpu.VMEM)],
        out_specs=pl.BlockSpec(memory_space=pltpu.VMEM),
        scratch_shapes=[
            pltpu.VMEM(x.shape, x.dtype),
            pltpu.VMEM((n,) + block, x.dtype),
            pltpu.VMEM((rows, width), x.dtype),
            pltpu.VMEM((rows, width), x.dtype),
            pltpu.SemaphoreType.DMA((n,)),
            pltpu.SemaphoreType.DMA((n,)),
            pltpu.SemaphoreType.DMA(()),
            pltpu.SemaphoreType.DMA(()),
            pltpu.SemaphoreType.DMA((n,)),
            pltpu.SemaphoreType.DMA((n,)),
        ],
        compiler_params=pltpu.CompilerParams(collective_id=kernel_id, has_side_effects=True),
    )(x)


class Exchanger:
    def __init__(self, axes, sizes):
        self.axes, self.factors, self.calls = axes, factor_table(sizes), 0

    def __call__(self, x, group, same):
        count = math.prod(self.factors[f][1] for f in group)
        block = x.shape if same else x.shape[1:]
        if count == 1:
            return x[None] if same else x
        kernel = functools.partial(
            exchange_kernel, axes=self.axes, factors=self.factors, group=group, same=same
        )
        self.calls += 1
        return pl.pallas_call(
            kernel,
            out_shape=jax.ShapeDtypeStruct((count,) + tuple(block), x.dtype),
            in_specs=[pl.BlockSpec(memory_space=pl.ANY)],
            out_specs=pl.BlockSpec(memory_space=pl.ANY),
            scratch_shapes=[
                pltpu.SemaphoreType.DMA((count,)),
                pltpu.SemaphoreType.DMA((count,)),
                pltpu.SemaphoreType.DMA(()),
            ],
            compiler_params=pltpu.CompilerParams(collective_id=self.calls, has_side_effects=True),
        )(x)


def make_body(axes, sizes):
    n_row, n_col, n_pl = sizes["prow"], sizes["pcol"], sizes["pl"]
    swap = [(c * n_col + r, r * n_col + c) for r in range(n_row) for c in range(n_col)]
    sibling = [(r, r ^ 1) for r in range(n_row)]
    n_zh = n_row // 2

    def beside_sibling(part, core):
        other = lax.ppermute(part, "prow", sibling)
        first, second = jnp.where(core == 0, part, other), jnp.where(core == 0, other, part)
        return jnp.concatenate([first, second], axis=0)

    def body(factor_cols, modal_at_loads, mode_shapes, natural_freq, damping):
        ex = Exchanger(axes, sizes)
        in_phase, quadrature = transfer_pair(natural_freq, damping)
        modes = modal_at_loads.shape[0]
        block = modes // (n_row * n_col)
        row, col = lax.axis_index("prow"), lax.axis_index("pcol")
        width = factor_cols.shape[1]
        core = row % 2
        own_modes = lax.dynamic_slice_in_dim(modal_at_loads, core * (modes // 2), modes // 2, 0)
        sib_modes = lax.dynamic_slice_in_dim(modal_at_loads, (1 - core) * (modes // 2), modes // 2, 0)
        mine = jnp.dot(own_modes, factor_cols, preferred_element_type=jnp.float32)
        theirs = jnp.dot(sib_modes, factor_cols, preferred_element_type=jnp.float32)
        modal_load = modal_sum(mine, theirs.astype(jnp.bfloat16), axes, sizes).reshape(modes, width)
        modal_wide = modal_load.astype(jnp.float32)
        pseudo = jnp.concatenate(
            [
                (in_phase[:, None] * modal_wide).astype(jnp.bfloat16),
                (quadrature[:, None] * modal_wide).astype(jnp.bfloat16),
            ],
            axis=1,
        )
        first_row = (col * n_row + row) * block
        own_pseudo = lax.dynamic_slice_in_dim(pseudo, first_row, block, 0)
        partial_gram = outer_rows(own_pseudo, pseudo).astype(jnp.bfloat16)
        chunk = modes // n_pl
        by_chunk = partial_gram.reshape(block, n_pl, chunk).transpose(1, 0, 2)
        half = modes // 2
        send_half = lax.dynamic_slice_in_dim(mode_shapes, (col % 2) * half, half, 1)
        panel_piece = lax.ppermute(send_half, ("prow", "pcol"), swap)
        panel_mine = lax.all_gather(panel_piece, "pl", axis=0, tiled=True)
        weighted = gram_weighted(by_chunk, mode_shapes, axes, sizes)
        panel_mine, weighted = lax.optimization_barrier((panel_mine, weighted))
        panel_other = lax.ppermute(panel_mine, "prow", sibling)
        weighted_mine = lax.dynamic_slice_in_dim(weighted, core * half, half, 1)
        weighted_other = lax.dynamic_slice_in_dim(weighted, (1 - core) * half, half, 1)
        return outer_rows(weighted_other, panel_other) + outer_rows(weighted_mine, panel_mine)

    return body


def solution(mesh):
    in_specs = (
        P(("prow", "pcol"), "pl"),
        P(None, ("prow", "pcol")),
        P(("prow", "pl"), None),
        P(),
        P(),
    )
    out_specs = P(("prow", "pl"), "pcol")
    axes = tuple(mesh.axis_names)
    body = make_body(axes, dict(mesh.shape))
    return jax.shard_map(body, mesh=mesh, in_specs=in_specs, out_specs=out_specs, check_vma=False)
```

```python
import functools
import math

import jax
import jax.numpy as jnp
from jax import lax
from jax.experimental import pallas as pl
from jax.experimental.pallas import tpu as pltpu
from jax.sharding import PartitionSpec as P

MESH = pl.DeviceIdType.MESH


def transfer_pair(natural_freq, damping):
    detuning = natural_freq * natural_freq - 1.0
    damper = 2.0 * damping * natural_freq
    modulus = detuning * detuning + damper * damper
    return (detuning / modulus, -damper / modulus)


def outer_rows(left_rows, right_rows):
    return lax.dot_general(
        left_rows, right_rows, (((1,), (1,)), ((), ())), preferred_element_type=jnp.float32
    )


def factor_table(sizes):
    return {
        "zh": ("prow", sizes["prow"] // 2, 2),
        "core": ("prow", 2, 1),
        "pcol": ("pcol", sizes["pcol"], 1),
        "pl": ("pl", sizes["pl"], 1),
    }


def exchange_kernel(x_ref, out_ref, send_sem, recv_sem, local_sem, *, axes, factors, group, same):
    coords = {a: lax.axis_index(a) for a in axes}

    def value(f):
        axis, size, stride = factors[f]
        return lax.rem(coords[axis] // stride, size)

    count = math.prod(factors[f][1] for f in group)
    me = 0
    for f in group:
        me = me * factors[f][1] + value(f)

    def device(member):
        place = dict(coords)
        for f in reversed(group):
            axis, size, stride = factors[f]
            place[axis] = place[axis] + (lax.rem(member, size) - value(f)) * stride
            member = member // size
        return tuple(place[a] for a in axes)

    def source(member):
        return x_ref if same else x_ref.at[member]

    def copy(offset):
        peer = lax.rem(me + offset, count)
        return pltpu.make_async_remote_copy(
            src_ref=source(peer),
            dst_ref=out_ref.at[me],
            send_sem=send_sem.at[offset],
            recv_sem=recv_sem.at[offset],
            device_id=device(peer),
            device_id_type=MESH,
        )

    def landing(offset):
        sender = lax.rem(me + count - offset, count)
        return pltpu.make_async_remote_copy(
            src_ref=source(me),
            dst_ref=out_ref.at[sender],
            send_sem=send_sem.at[offset],
            recv_sem=recv_sem.at[offset],
            device_id=device(sender),
            device_id_type=MESH,
        )

    local = pltpu.make_async_copy(source(me), out_ref.at[me], local_sem)
    local.start()
    barrier = pltpu.get_barrier_semaphore()
    for offset in range(1, count):
        peer = lax.rem(me + offset, count)
        pl.semaphore_signal(barrier, inc=1, device_id=device(peer), device_id_type=MESH)
    pl.semaphore_wait(barrier, count - 1)
    for offset in range(1, count):
        copy(offset).start()
    local.wait()
    for offset in range(1, count):
        copy(offset).wait_send()
    for offset in range(1, count):
        landing(offset).wait_recv()


def fused_sum_kernel(x_ref, out_ref, got, coll, part_out, part_in, send_a, recv_a, send_b, recv_b,
                     send_c, recv_c, *, axes, factors, over, add_across):
    coords = {a: lax.axis_index(a) for a in axes}

    def value(f):
        axis, size, stride = factors[f]
        return lax.rem(coords[axis] // stride, size)

    def device(f, v):
        place = dict(coords)
        axis, size, stride = factors[f]
        place[axis] = place[axis] + (v - value(f)) * stride
        return tuple(place[a] for a in axes)

    n = factors[over][1]
    me, half = value(over), value("zh")
    partner = device("zh", 1 - half)
    peer = lambda k: lax.rem(me + k, n)
    sender = lambda k: lax.rem(me + n - k, n)

    def step(src, dst_at, k, to, sems):
        return pltpu.make_async_remote_copy(
            src_ref=src, dst_ref=dst_at, send_sem=sems[0].at[k], recv_sem=sems[1].at[k],
            device_id=to, device_id_type=MESH,
        )

    barrier = pltpu.get_barrier_semaphore()
    for k in range(1, n):
        pl.semaphore_signal(barrier, inc=1, device_id=device(over, peer(k)), device_id_type=MESH)
    pl.semaphore_signal(barrier, inc=1, device_id=partner, device_id_type=MESH)
    pl.semaphore_wait(barrier, n)

    for k in range(1, n):
        step(x_ref.at[peer(k)], got.at[me], k, device(over, peer(k)), (send_a, recv_a)).start()
    for k in range(1, n):
        step(x_ref.at[peer(k)], got.at[me], k, device(over, peer(k)), (send_a, recv_a)).wait_send()
    for k in range(1, n):
        step(x_ref.at[me], got.at[sender(k)], k, device(over, sender(k)), (send_a, recv_a)).wait_recv()
    total = x_ref[me].astype(jnp.float32)
    for k in range(1, n):
        total = total + got[sender(k)].astype(jnp.float32)
    part_out[...] = total.astype(part_out.dtype)

    across = pltpu.make_async_remote_copy(
        src_ref=part_out, dst_ref=part_in, send_sem=send_b, recv_sem=recv_b,
        device_id=partner, device_id_type=MESH,
    )
    across.start()
    across.wait_send()
    across.wait_recv()
    if add_across:
        mine, theirs = part_out[...].astype(jnp.float32), part_in[...].astype(jnp.float32)
        coll[me] = (mine + theirs).astype(coll.dtype)
    else:
        mine, theirs = part_out[...], part_in[...]
        first = jnp.where(half == 0, mine, theirs)
        second = jnp.where(half == 0, theirs, mine)
        coll[me] = jnp.stack([first, second])

    for k in range(1, n):
        step(coll.at[me], coll.at[me], k, device(over, peer(k)), (send_c, recv_c)).start()
    for k in range(1, n):
        step(coll.at[me], coll.at[me], k, device(over, peer(k)), (send_c, recv_c)).wait_send()
    for k in range(1, n):
        step(coll.at[me], coll.at[sender(k)], k, device(over, sender(k)), (send_c, recv_c)).wait_recv()
    out_ref[...] = coll[...]


def modal_sum_kernel(mine_ref, theirs_ref, out_ref, sib_in, pieces, got, coll, part_out, part_in,
                     sib_out, send_s, recv_s, send_a, recv_a, send_b, recv_b, send_c, recv_c,
                     send_d, recv_d, *, axes, factors):
    coords = {a: lax.axis_index(a) for a in axes}

    def value(f):
        axis, size, stride = factors[f]
        return lax.rem(coords[axis] // stride, size)

    def device(f, v):
        place = dict(coords)
        axis, size, stride = factors[f]
        place[axis] = place[axis] + (v - value(f)) * stride
        return tuple(place[a] for a in axes)

    n = factors["pcol"][1]
    me, half, core = value("pcol"), value("zh"), value("core")
    partner, sibling = device("zh", 1 - half), device("core", 1 - core)
    peer = lambda k: lax.rem(me + k, n)
    sender = lambda k: lax.rem(me + n - k, n)

    def step(src, dst_at, k, to, sems):
        return pltpu.make_async_remote_copy(
            src_ref=src, dst_ref=dst_at, send_sem=sems[0].at[k], recv_sem=sems[1].at[k],
            device_id=to, device_id_type=MESH,
        )

    def one(src, dst, to, send_sem, recv_sem):
        return pltpu.make_async_remote_copy(
            src_ref=src, dst_ref=dst, send_sem=send_sem, recv_sem=recv_sem,
            device_id=to, device_id_type=MESH,
        )

    barrier = pltpu.get_barrier_semaphore()
    for k in range(1, n):
        pl.semaphore_signal(barrier, inc=1, device_id=device("pcol", peer(k)), device_id_type=MESH)
    pl.semaphore_signal(barrier, inc=1, device_id=partner, device_id_type=MESH)
    pl.semaphore_signal(barrier, inc=1, device_id=sibling, device_id_type=MESH)
    pl.semaphore_wait(barrier, n + 1)

    chip = one(theirs_ref, sib_in, sibling, send_s, recv_s)
    chip.start()
    chip.wait_send()
    chip.wait_recv()
    summed = mine_ref[...] + sib_in[...].astype(jnp.float32)
    pieces[...] = summed.astype(pieces.dtype).reshape(pieces.shape)

    for k in range(1, n):
        step(pieces.at[peer(k)], got.at[me], k, device("pcol", peer(k)), (send_a, recv_a)).start()
    for k in range(1, n):
        step(pieces.at[peer(k)], got.at[me], k, device("pcol", peer(k)), (send_a, recv_a)).wait_send()
    for k in range(1, n):
        step(pieces.at[me], got.at[sender(k)], k, device("pcol", sender(k)), (send_a, recv_a)).wait_recv()
    total = pieces[me].astype(jnp.float32)
    for k in range(1, n):
        total = total + got[sender(k)].astype(jnp.float32)
    part_out[...] = total.astype(part_out.dtype)

    across = one(part_out, part_in, partner, send_b, recv_b)
    across.start()
    across.wait_send()
    across.wait_recv()
    coll[me] = (part_out[...].astype(jnp.float32) + part_in[...].astype(jnp.float32)).astype(coll.dtype)

    for k in range(1, n):
        step(coll.at[me], coll.at[me], k, device("pcol", peer(k)), (send_c, recv_c)).start()
    for k in range(1, n):
        step(coll.at[me], coll.at[me], k, device("pcol", peer(k)), (send_c, recv_c)).wait_send()
    for k in range(1, n):
        step(coll.at[me], coll.at[sender(k)], k, device("pcol", sender(k)), (send_c, recv_c)).wait_recv()

    join = one(coll, sib_out, sibling, send_d, recv_d)
    join.start()
    join.wait_send()
    join.wait_recv()
    out_ref[core] = coll[...]
    out_ref[1 - core] = sib_out[...]


def modal_sum(mine, theirs, axes, sizes):
    n = sizes["pcol"]
    rows, width = mine.shape
    block = (n, rows // n, width)
    kernel = functools.partial(modal_sum_kernel, axes=axes, factors=factor_table(sizes))
    return pl.pallas_call(
        kernel,
        out_shape=jax.ShapeDtypeStruct((2,) + block, jnp.bfloat16),
        in_specs=[pl.BlockSpec(memory_space=pltpu.VMEM)] * 2,
        out_specs=pl.BlockSpec(memory_space=pltpu.VMEM),
        scratch_shapes=[
            pltpu.VMEM((rows, width), jnp.bfloat16),
            pltpu.VMEM(block, jnp.bfloat16),
            pltpu.VMEM(block, jnp.bfloat16),
            pltpu.VMEM(block, jnp.bfloat16),
            pltpu.VMEM(block[1:], jnp.bfloat16),
            pltpu.VMEM(block[1:], jnp.bfloat16),
            pltpu.VMEM(block, jnp.bfloat16),
            pltpu.SemaphoreType.DMA(()),
            pltpu.SemaphoreType.DMA(()),
            pltpu.SemaphoreType.DMA((n,)),
            pltpu.SemaphoreType.DMA((n,)),
            pltpu.SemaphoreType.DMA(()),
            pltpu.SemaphoreType.DMA(()),
            pltpu.SemaphoreType.DMA((n,)),
            pltpu.SemaphoreType.DMA((n,)),
            pltpu.SemaphoreType.DMA(()),
            pltpu.SemaphoreType.DMA(()),
        ],
        compiler_params=pltpu.CompilerParams(collective_id=102, has_side_effects=True),
    )(mine, theirs)


def gram_weighted_kernel(x_ref, shapes_ref, out_ref, got, coll, sib_coll, part_out, part_in, wbuf,
                         send_a, recv_a, send_b, recv_b, send_c, recv_c, send_d, recv_d, send_e,
                         recv_e, *, axes, factors):
    coords = {a: lax.axis_index(a) for a in axes}

    def value(f):
        axis, size, stride = factors[f]
        return lax.rem(coords[axis] // stride, size)

    def device(f, v):
        place = dict(coords)
        axis, size, stride = factors[f]
        place[axis] = place[axis] + (v - value(f)) * stride
        return tuple(place[a] for a in axes)

    n, n_col = factors["pl"][1], factors["pcol"][1]
    me, half, core, col = value("pl"), value("zh"), value("core"), value("pcol")
    partner, sibling = device("zh", 1 - half), device("core", 1 - core)

    def step(src, dst_at, k, to, sems):
        return pltpu.make_async_remote_copy(
            src_ref=src, dst_ref=dst_at, send_sem=sems[0].at[k], recv_sem=sems[1].at[k],
            device_id=to, device_id_type=MESH,
        )

    def one(src, dst, to, send_sem, recv_sem):
        return pltpu.make_async_remote_copy(
            src_ref=src, dst_ref=dst, send_sem=send_sem, recv_sem=recv_sem,
            device_id=to, device_id_type=MESH,
        )

    barrier = pltpu.get_barrier_semaphore()
    for k in range(1, n):
        pl.semaphore_signal(barrier, inc=1, device_id=device("pl", lax.rem(me + k, n)), device_id_type=MESH)
    for k in range(1, n_col):
        pl.semaphore_signal(
            barrier, inc=1, device_id=device("pcol", lax.rem(col + k, n_col)), device_id_type=MESH
        )
    pl.semaphore_signal(barrier, inc=1, device_id=partner, device_id_type=MESH)
    pl.semaphore_signal(barrier, inc=1, device_id=sibling, device_id_type=MESH)
    pl.semaphore_wait(barrier, n + n_col)

    peer = lambda k: lax.rem(me + k, n)
    sender = lambda k: lax.rem(me + n - k, n)
    for k in range(1, n):
        step(x_ref.at[peer(k)], got.at[me], k, device("pl", peer(k)), (send_a, recv_a)).start()
    for k in range(1, n):
        step(x_ref.at[peer(k)], got.at[me], k, device("pl", peer(k)), (send_a, recv_a)).wait_send()
    for k in range(1, n):
        step(x_ref.at[me], got.at[sender(k)], k, device("pl", sender(k)), (send_a, recv_a)).wait_recv()
    total = x_ref[me].astype(jnp.float32)
    for k in range(1, n):
        total = total + got[sender(k)].astype(jnp.float32)
    part_out[...] = total.astype(part_out.dtype)

    across = one(part_out, part_in, partner, send_b, recv_b)
    across.start()
    across.wait_send()
    across.wait_recv()
    mine, theirs = part_out[...], part_in[...]
    coll[me] = jnp.stack([jnp.where(half == 0, mine, theirs), jnp.where(half == 0, theirs, mine)])

    for k in range(1, n):
        step(coll.at[me], coll.at[me], k, device("pl", peer(k)), (send_c, recv_c)).start()
    for k in range(1, n):
        step(coll.at[me], coll.at[me], k, device("pl", peer(k)), (send_c, recv_c)).wait_send()
    for k in range(1, n):
        step(coll.at[me], coll.at[sender(k)], k, device("pl", sender(k)), (send_c, recv_c)).wait_recv()

    chunk = coll.shape[-1]

    def weighted_block(blocks, h):
        acc = jnp.zeros((shapes_ref.shape[0], blocks.shape[2]), jnp.float32)
        for l in range(n):
            acc = acc + lax.dot_general(
                shapes_ref[:, l * chunk:(l + 1) * chunk], blocks[l, h],
                (((1,), (1,)), ((), ())), preferred_element_type=jnp.float32,
            )
        return acc

    join = one(coll, sib_coll, sibling, send_d, recv_d)
    join.start()
    own = [weighted_block(coll, h) for h in range(2)]
    join.wait_send()
    join.wait_recv()
    other = [weighted_block(sib_coll, h) for h in range(2)]
    parts = []
    for h in range(2):
        parts += [jnp.where(core == 0, own[h], other[h]), jnp.where(core == 0, other[h], own[h])]
    wbuf[col] = jnp.concatenate(parts, axis=1).astype(wbuf.dtype)

    wpeer = lambda k: lax.rem(col + k, n_col)
    wsender = lambda k: lax.rem(col + n_col - k, n_col)
    for k in range(1, n_col):
        step(wbuf.at[col], wbuf.at[col], k, device("pcol", wpeer(k)), (send_e, recv_e)).start()
    for k in range(1, n_col):
        step(wbuf.at[col], wbuf.at[col], k, device("pcol", wpeer(k)), (send_e, recv_e)).wait_send()
    for k in range(1, n_col):
        step(wbuf.at[col], wbuf.at[wsender(k)], k, device("pcol", wsender(k)), (send_e, recv_e)).wait_recv()
    width_w = wbuf.shape[2]
    for c in range(n_col):
        out_ref[:, c * width_w:(c + 1) * width_w] = wbuf[c]


def gram_weighted(x, mode_shapes, axes, sizes):
    n, rows, width = x.shape
    n_col = sizes["pcol"]
    wshape = (n_col, mode_shapes.shape[0], 4 * rows)
    kernel = functools.partial(gram_weighted_kernel, axes=axes, factors=factor_table(sizes))
    return pl.pallas_call(
        kernel,
        out_shape=jax.ShapeDtypeStruct((wshape[1], n_col * wshape[2]), jnp.bfloat16),
        in_specs=[pl.BlockSpec(memory_space=pltpu.VMEM)] * 2,
        out_specs=pl.BlockSpec(memory_space=pltpu.VMEM),
        scratch_shapes=[
            pltpu.VMEM(x.shape, x.dtype),
            pltpu.VMEM((n, 2, rows, width), x.dtype),
            pltpu.VMEM((n, 2, rows, width), x.dtype),
            pltpu.VMEM((rows, width), x.dtype),
            pltpu.VMEM((rows, width), x.dtype),
            pltpu.VMEM(wshape, jnp.bfloat16),
            pltpu.SemaphoreType.DMA((n,)),
            pltpu.SemaphoreType.DMA((n,)),
            pltpu.SemaphoreType.DMA(()),
            pltpu.SemaphoreType.DMA(()),
            pltpu.SemaphoreType.DMA((n,)),
            pltpu.SemaphoreType.DMA((n,)),
            pltpu.SemaphoreType.DMA(()),
            pltpu.SemaphoreType.DMA(()),
            pltpu.SemaphoreType.DMA((n_col,)),
            pltpu.SemaphoreType.DMA((n_col,)),
        ],
        compiler_params=pltpu.CompilerParams(collective_id=103, has_side_effects=True),
    )(x, mode_shapes)


def fused_sum(x, axes, sizes, over, add_across, kernel_id):
    n, rows, width = x.shape
    block = (rows, width) if add_across else (2, rows, width)
    kernel = functools.partial(
        fused_sum_kernel, axes=axes, factors=factor_table(sizes), over=over, add_across=add_across
    )
    return pl.pallas_call(
        kernel,
        out_shape=jax.ShapeDtypeStruct((n,) + block, x.dtype),
        in_specs=[pl.BlockSpec(memory_space=pltpu.VMEM)],
        out_specs=pl.BlockSpec(memory_space=pltpu.VMEM),
        scratch_shapes=[
            pltpu.VMEM(x.shape, x.dtype),
            pltpu.VMEM((n,) + block, x.dtype),
            pltpu.VMEM((rows, width), x.dtype),
            pltpu.VMEM((rows, width), x.dtype),
            pltpu.SemaphoreType.DMA((n,)),
            pltpu.SemaphoreType.DMA((n,)),
            pltpu.SemaphoreType.DMA(()),
            pltpu.SemaphoreType.DMA(()),
            pltpu.SemaphoreType.DMA((n,)),
            pltpu.SemaphoreType.DMA((n,)),
        ],
        compiler_params=pltpu.CompilerParams(collective_id=kernel_id, has_side_effects=True),
    )(x)


class Exchanger:
    def __init__(self, axes, sizes):
        self.axes, self.factors, self.calls = axes, factor_table(sizes), 0

    def __call__(self, x, group, same):
        count = math.prod(self.factors[f][1] for f in group)
        block = x.shape if same else x.shape[1:]
        if count == 1:
            return x[None] if same else x
        kernel = functools.partial(
            exchange_kernel, axes=self.axes, factors=self.factors, group=group, same=same
        )
        self.calls += 1
        return pl.pallas_call(
            kernel,
            out_shape=jax.ShapeDtypeStruct((count,) + tuple(block), x.dtype),
            in_specs=[pl.BlockSpec(memory_space=pl.ANY)],
            out_specs=pl.BlockSpec(memory_space=pl.ANY),
            scratch_shapes=[
                pltpu.SemaphoreType.DMA((count,)),
                pltpu.SemaphoreType.DMA((count,)),
                pltpu.SemaphoreType.DMA(()),
            ],
            compiler_params=pltpu.CompilerParams(collective_id=self.calls, has_side_effects=True),
        )(x)


def make_body(axes, sizes):
    n_row, n_col, n_pl = sizes["prow"], sizes["pcol"], sizes["pl"]
    swap = [(c * n_col + r, r * n_col + c) for r in range(n_row) for c in range(n_col)]
    sibling = [(r, r ^ 1) for r in range(n_row)]
    n_zh = n_row // 2

    def beside_sibling(part, core):
        other = lax.ppermute(part, "prow", sibling)
        first, second = jnp.where(core == 0, part, other), jnp.where(core == 0, other, part)
        return jnp.concatenate([first, second], axis=0)

    def body(factor_cols, modal_at_loads, mode_shapes, natural_freq, damping):
        ex = Exchanger(axes, sizes)
        in_phase, quadrature = transfer_pair(natural_freq, damping)
        modes = modal_at_loads.shape[0]
        block = modes // (n_row * n_col)
        row, col = lax.axis_index("prow"), lax.axis_index("pcol")
        width = factor_cols.shape[1]
        core = row % 2
        own_modes = lax.dynamic_slice_in_dim(modal_at_loads, core * (modes // 2), modes // 2, 0)
        sib_modes = lax.dynamic_slice_in_dim(modal_at_loads, (1 - core) * (modes // 2), modes // 2, 0)
        mine = jnp.dot(own_modes, factor_cols, preferred_element_type=jnp.float32)
        theirs = jnp.dot(sib_modes, factor_cols, preferred_element_type=jnp.float32)
        modal_load = modal_sum(mine, theirs.astype(jnp.bfloat16), axes, sizes).reshape(modes, width)
        modal_wide = modal_load.astype(jnp.float32)
        pseudo = jnp.concatenate(
            [
                (in_phase[:, None] * modal_wide).astype(jnp.bfloat16),
                (quadrature[:, None] * modal_wide).astype(jnp.bfloat16),
            ],
            axis=1,
        )
        first_row = (col * n_row + row) * block
        own_pseudo = lax.dynamic_slice_in_dim(pseudo, first_row, block, 0)
        partial_gram = outer_rows(own_pseudo, pseudo).astype(jnp.bfloat16)
        chunk = modes // n_pl
        by_chunk = partial_gram.reshape(block, n_pl, chunk).transpose(1, 0, 2)
        half = modes // 2
        send_half = lax.dynamic_slice_in_dim(mode_shapes, (col % 2) * half, half, 1)
        panel_piece = lax.ppermute(send_half, ("prow", "pcol"), swap)
        panel_mine = lax.all_gather(panel_piece, "pl", axis=0, tiled=True)
        weighted = gram_weighted(by_chunk, mode_shapes, axes, sizes)
        panel_mine, weighted = lax.optimization_barrier((panel_mine, weighted))
        panel_other = lax.ppermute(panel_mine, "prow", sibling)
        weighted_mine = lax.dynamic_slice_in_dim(weighted, core * half, half, 1)
        weighted_other = lax.dynamic_slice_in_dim(weighted, (1 - core) * half, half, 1)
        return outer_rows(weighted_other, panel_other) + outer_rows(weighted_mine, panel_mine)

    return body


def solution(mesh):
    in_specs = (
        P(("prow", "pcol"), "pl"),
        P(None, ("prow", "pcol")),
        P(("prow", "pl"), None),
        P(),
        P(),
    )
    out_specs = P(("prow", "pl"), "pcol")
    axes = tuple(mesh.axis_names)
    body = make_body(axes, dict(mesh.shape))
    return jax.shard_map(body, mesh=mesh, in_specs=in_specs, out_specs=out_specs, check_vma=False)
```

```python
import functools
import math

import jax
import jax.numpy as jnp
from jax import lax
from jax.experimental import pallas as pl
from jax.experimental.pallas import tpu as pltpu
from jax.sharding import PartitionSpec as P

MESH = pl.DeviceIdType.MESH


def transfer_pair(natural_freq, damping):
    detuning = natural_freq * natural_freq - 1.0
    damper = 2.0 * damping * natural_freq
    modulus = detuning * detuning + damper * damper
    return (detuning / modulus, -damper / modulus)


def outer_rows(left_rows, right_rows):
    return lax.dot_general(
        left_rows, right_rows, (((1,), (1,)), ((), ())), preferred_element_type=jnp.float32
    )


def factor_table(sizes):
    return {
        "zh": ("prow", sizes["prow"] // 2, 2),
        "core": ("prow", 2, 1),
        "pcol": ("pcol", sizes["pcol"], 1),
        "pl": ("pl", sizes["pl"], 1),
    }


def exchange_kernel(x_ref, out_ref, send_sem, recv_sem, local_sem, *, axes, factors, group, same):
    coords = {a: lax.axis_index(a) for a in axes}

    def value(f):
        axis, size, stride = factors[f]
        return lax.rem(coords[axis] // stride, size)

    count = math.prod(factors[f][1] for f in group)
    me = 0
    for f in group:
        me = me * factors[f][1] + value(f)

    def device(member):
        place = dict(coords)
        for f in reversed(group):
            axis, size, stride = factors[f]
            place[axis] = place[axis] + (lax.rem(member, size) - value(f)) * stride
            member = member // size
        return tuple(place[a] for a in axes)

    def source(member):
        return x_ref if same else x_ref.at[member]

    def copy(offset):
        peer = lax.rem(me + offset, count)
        return pltpu.make_async_remote_copy(
            src_ref=source(peer),
            dst_ref=out_ref.at[me],
            send_sem=send_sem.at[offset],
            recv_sem=recv_sem.at[offset],
            device_id=device(peer),
            device_id_type=MESH,
        )

    def landing(offset):
        sender = lax.rem(me + count - offset, count)
        return pltpu.make_async_remote_copy(
            src_ref=source(me),
            dst_ref=out_ref.at[sender],
            send_sem=send_sem.at[offset],
            recv_sem=recv_sem.at[offset],
            device_id=device(sender),
            device_id_type=MESH,
        )

    local = pltpu.make_async_copy(source(me), out_ref.at[me], local_sem)
    local.start()
    barrier = pltpu.get_barrier_semaphore()
    for offset in range(1, count):
        peer = lax.rem(me + offset, count)
        pl.semaphore_signal(barrier, inc=1, device_id=device(peer), device_id_type=MESH)
    pl.semaphore_wait(barrier, count - 1)
    for offset in range(1, count):
        copy(offset).start()
    local.wait()
    for offset in range(1, count):
        copy(offset).wait_send()
    for offset in range(1, count):
        landing(offset).wait_recv()


def fused_sum_kernel(x_ref, out_ref, got, coll, part_out, part_in, send_a, recv_a, send_b, recv_b,
                     send_c, recv_c, *, axes, factors, over, add_across):
    coords = {a: lax.axis_index(a) for a in axes}

    def value(f):
        axis, size, stride = factors[f]
        return lax.rem(coords[axis] // stride, size)

    def device(f, v):
        place = dict(coords)
        axis, size, stride = factors[f]
        place[axis] = place[axis] + (v - value(f)) * stride
        return tuple(place[a] for a in axes)

    n = factors[over][1]
    me, half = value(over), value("zh")
    partner = device("zh", 1 - half)
    peer = lambda k: lax.rem(me + k, n)
    sender = lambda k: lax.rem(me + n - k, n)

    def step(src, dst_at, k, to, sems):
        return pltpu.make_async_remote_copy(
            src_ref=src, dst_ref=dst_at, send_sem=sems[0].at[k], recv_sem=sems[1].at[k],
            device_id=to, device_id_type=MESH,
        )

    barrier = pltpu.get_barrier_semaphore()
    for k in range(1, n):
        pl.semaphore_signal(barrier, inc=1, device_id=device(over, peer(k)), device_id_type=MESH)
    pl.semaphore_signal(barrier, inc=1, device_id=partner, device_id_type=MESH)
    pl.semaphore_wait(barrier, n)

    for k in range(1, n):
        step(x_ref.at[peer(k)], got.at[me], k, device(over, peer(k)), (send_a, recv_a)).start()
    for k in range(1, n):
        step(x_ref.at[peer(k)], got.at[me], k, device(over, peer(k)), (send_a, recv_a)).wait_send()
    for k in range(1, n):
        step(x_ref.at[me], got.at[sender(k)], k, device(over, sender(k)), (send_a, recv_a)).wait_recv()
    total = x_ref[me].astype(jnp.float32)
    for k in range(1, n):
        total = total + got[sender(k)].astype(jnp.float32)
    part_out[...] = total.astype(part_out.dtype)

    across = pltpu.make_async_remote_copy(
        src_ref=part_out, dst_ref=part_in, send_sem=send_b, recv_sem=recv_b,
        device_id=partner, device_id_type=MESH,
    )
    across.start()
    across.wait_send()
    across.wait_recv()
    if add_across:
        mine, theirs = part_out[...].astype(jnp.float32), part_in[...].astype(jnp.float32)
        coll[me] = (mine + theirs).astype(coll.dtype)
    else:
        mine, theirs = part_out[...], part_in[...]
        first = jnp.where(half == 0, mine, theirs)
        second = jnp.where(half == 0, theirs, mine)
        coll[me] = jnp.stack([first, second])

    for k in range(1, n):
        step(coll.at[me], coll.at[me], k, device(over, peer(k)), (send_c, recv_c)).start()
    for k in range(1, n):
        step(coll.at[me], coll.at[me], k, device(over, peer(k)), (send_c, recv_c)).wait_send()
    for k in range(1, n):
        step(coll.at[me], coll.at[sender(k)], k, device(over, sender(k)), (send_c, recv_c)).wait_recv()
    out_ref[...] = coll[...]


def modal_sum_kernel(mine_ref, theirs_ref, out_ref, sib_in, pieces, got, coll, part_out, part_in,
                     sib_out, send_s, recv_s, send_a, recv_a, send_b, recv_b, send_c, recv_c,
                     send_d, recv_d, *, axes, factors):
    coords = {a: lax.axis_index(a) for a in axes}

    def value(f):
        axis, size, stride = factors[f]
        return lax.rem(coords[axis] // stride, size)

    def device(f, v):
        place = dict(coords)
        axis, size, stride = factors[f]
        place[axis] = place[axis] + (v - value(f)) * stride
        return tuple(place[a] for a in axes)

    n = factors["pcol"][1]
    me, half, core = value("pcol"), value("zh"), value("core")
    partner, sibling = device("zh", 1 - half), device("core", 1 - core)
    peer = lambda k: lax.rem(me + k, n)
    sender = lambda k: lax.rem(me + n - k, n)

    def step(src, dst_at, k, to, sems):
        return pltpu.make_async_remote_copy(
            src_ref=src, dst_ref=dst_at, send_sem=sems[0].at[k], recv_sem=sems[1].at[k],
            device_id=to, device_id_type=MESH,
        )

    def one(src, dst, to, send_sem, recv_sem):
        return pltpu.make_async_remote_copy(
            src_ref=src, dst_ref=dst, send_sem=send_sem, recv_sem=recv_sem,
            device_id=to, device_id_type=MESH,
        )

    barrier = pltpu.get_barrier_semaphore()
    for k in range(1, n):
        pl.semaphore_signal(barrier, inc=1, device_id=device("pcol", peer(k)), device_id_type=MESH)
    pl.semaphore_signal(barrier, inc=1, device_id=partner, device_id_type=MESH)
    pl.semaphore_signal(barrier, inc=1, device_id=sibling, device_id_type=MESH)
    pl.semaphore_wait(barrier, n + 1)

    chip = one(theirs_ref, sib_in, sibling, send_s, recv_s)
    chip.start()
    chip.wait_send()
    chip.wait_recv()
    summed = mine_ref[...] + sib_in[...].astype(jnp.float32)
    pieces[...] = summed.astype(pieces.dtype).reshape(pieces.shape)

    for k in range(1, n):
        step(pieces.at[peer(k)], got.at[me], k, device("pcol", peer(k)), (send_a, recv_a)).start()
    for k in range(1, n):
        step(pieces.at[peer(k)], got.at[me], k, device("pcol", peer(k)), (send_a, recv_a)).wait_send()
    for k in range(1, n):
        step(pieces.at[me], got.at[sender(k)], k, device("pcol", sender(k)), (send_a, recv_a)).wait_recv()
    total = pieces[me].astype(jnp.float32)
    for k in range(1, n):
        total = total + got[sender(k)].astype(jnp.float32)
    part_out[...] = total.astype(part_out.dtype)

    across = one(part_out, part_in, partner, send_b, recv_b)
    across.start()
    across.wait_send()
    across.wait_recv()
    coll[me] = (part_out[...].astype(jnp.float32) + part_in[...].astype(jnp.float32)).astype(coll.dtype)

    for k in range(1, n):
        step(coll.at[me], coll.at[me], k, device("pcol", peer(k)), (send_c, recv_c)).start()
    for k in range(1, n):
        step(coll.at[me], coll.at[me], k, device("pcol", peer(k)), (send_c, recv_c)).wait_send()
    for k in range(1, n):
        step(coll.at[me], coll.at[sender(k)], k, device("pcol", sender(k)), (send_c, recv_c)).wait_recv()

    join = one(coll, sib_out, sibling, send_d, recv_d)
    join.start()
    join.wait_send()
    join.wait_recv()
    out_ref[core] = coll[...]
    out_ref[1 - core] = sib_out[...]


def modal_sum(mine, theirs, axes, sizes):
    n = sizes["pcol"]
    rows, width = mine.shape
    block = (n, rows // n, width)
    kernel = functools.partial(modal_sum_kernel, axes=axes, factors=factor_table(sizes))
    return pl.pallas_call(
        kernel,
        out_shape=jax.ShapeDtypeStruct((2,) + block, jnp.bfloat16),
        in_specs=[pl.BlockSpec(memory_space=pltpu.VMEM)] * 2,
        out_specs=pl.BlockSpec(memory_space=pltpu.VMEM),
        scratch_shapes=[
            pltpu.VMEM((rows, width), jnp.bfloat16),
            pltpu.VMEM(block, jnp.bfloat16),
            pltpu.VMEM(block, jnp.bfloat16),
            pltpu.VMEM(block, jnp.bfloat16),
            pltpu.VMEM(block[1:], jnp.bfloat16),
            pltpu.VMEM(block[1:], jnp.bfloat16),
            pltpu.VMEM(block, jnp.bfloat16),
            pltpu.SemaphoreType.DMA(()),
            pltpu.SemaphoreType.DMA(()),
            pltpu.SemaphoreType.DMA((n,)),
            pltpu.SemaphoreType.DMA((n,)),
            pltpu.SemaphoreType.DMA(()),
            pltpu.SemaphoreType.DMA(()),
            pltpu.SemaphoreType.DMA((n,)),
            pltpu.SemaphoreType.DMA((n,)),
            pltpu.SemaphoreType.DMA(()),
            pltpu.SemaphoreType.DMA(()),
        ],
        compiler_params=pltpu.CompilerParams(collective_id=102, has_side_effects=True),
    )(mine, theirs)


def gram_weighted_kernel(own_ref, pseudo_ref, shapes_ref, out_ref, x_ref, got, coll, sib_coll,
                         part_out, part_in, wbuf, send_a, recv_a, send_b, recv_b, send_c, recv_c,
                         send_d, recv_d, send_e, recv_e, *, axes, factors):
    coords = {a: lax.axis_index(a) for a in axes}

    def value(f):
        axis, size, stride = factors[f]
        return lax.rem(coords[axis] // stride, size)

    def device(f, v):
        place = dict(coords)
        axis, size, stride = factors[f]
        place[axis] = place[axis] + (v - value(f)) * stride
        return tuple(place[a] for a in axes)

    n, n_col = factors["pl"][1], factors["pcol"][1]
    me, half, core, col = value("pl"), value("zh"), value("core"), value("pcol")
    partner, sibling = device("zh", 1 - half), device("core", 1 - core)

    def step(src, dst_at, k, to, sems):
        return pltpu.make_async_remote_copy(
            src_ref=src, dst_ref=dst_at, send_sem=sems[0].at[k], recv_sem=sems[1].at[k],
            device_id=to, device_id_type=MESH,
        )

    def one(src, dst, to, send_sem, recv_sem):
        return pltpu.make_async_remote_copy(
            src_ref=src, dst_ref=dst, send_sem=send_sem, recv_sem=recv_sem,
            device_id=to, device_id_type=MESH,
        )

    partial = lax.dot_general(
        own_ref[...], pseudo_ref[...], (((1,), (1,)), ((), ())), preferred_element_type=jnp.float32
    ).astype(x_ref.dtype)
    width_x = x_ref.shape[2]
    for l in range(n):
        x_ref[l] = partial[:, l * width_x:(l + 1) * width_x]

    barrier = pltpu.get_barrier_semaphore()
    for k in range(1, n):
        pl.semaphore_signal(barrier, inc=1, device_id=device("pl", lax.rem(me + k, n)), device_id_type=MESH)
    for k in range(1, n_col):
        pl.semaphore_signal(
            barrier, inc=1, device_id=device("pcol", lax.rem(col + k, n_col)), device_id_type=MESH
        )
    pl.semaphore_signal(barrier, inc=1, device_id=partner, device_id_type=MESH)
    pl.semaphore_signal(barrier, inc=1, device_id=sibling, device_id_type=MESH)
    pl.semaphore_wait(barrier, n + n_col)

    peer = lambda k: lax.rem(me + k, n)
    sender = lambda k: lax.rem(me + n - k, n)
    for k in range(1, n):
        step(x_ref.at[peer(k)], got.at[me], k, device("pl", peer(k)), (send_a, recv_a)).start()
    for k in range(1, n):
        step(x_ref.at[peer(k)], got.at[me], k, device("pl", peer(k)), (send_a, recv_a)).wait_send()
    for k in range(1, n):
        step(x_ref.at[me], got.at[sender(k)], k, device("pl", sender(k)), (send_a, recv_a)).wait_recv()
    total = x_ref[me].astype(jnp.float32)
    for k in range(1, n):
        total = total + got[sender(k)].astype(jnp.float32)
    part_out[...] = total.astype(part_out.dtype)

    across = one(part_out, part_in, partner, send_b, recv_b)
    across.start()
    across.wait_send()
    across.wait_recv()
    mine, theirs = part_out[...], part_in[...]
    coll[me] = jnp.stack([jnp.where(half == 0, mine, theirs), jnp.where(half == 0, theirs, mine)])

    for k in range(1, n):
        step(coll.at[me], coll.at[me], k, device("pl", peer(k)), (send_c, recv_c)).start()
    for k in range(1, n):
        step(coll.at[me], coll.at[me], k, device("pl", peer(k)), (send_c, recv_c)).wait_send()
    for k in range(1, n):
        step(coll.at[me], coll.at[sender(k)], k, device("pl", sender(k)), (send_c, recv_c)).wait_recv()

    chunk = coll.shape[-1]

    def weighted_block(blocks, h):
        acc = jnp.zeros((shapes_ref.shape[0], blocks.shape[2]), jnp.float32)
        for l in range(n):
            acc = acc + lax.dot_general(
                shapes_ref[:, l * chunk:(l + 1) * chunk], blocks[l, h],
                (((1,), (1,)), ((), ())), preferred_element_type=jnp.float32,
            )
        return acc

    join = one(coll, sib_coll, sibling, send_d, recv_d)
    join.start()
    own = [weighted_block(coll, h) for h in range(2)]
    join.wait_send()
    join.wait_recv()
    other = [weighted_block(sib_coll, h) for h in range(2)]
    parts = []
    for h in range(2):
        parts += [jnp.where(core == 0, own[h], other[h]), jnp.where(core == 0, other[h], own[h])]
    wbuf[col] = jnp.concatenate(parts, axis=1).astype(wbuf.dtype)

    wpeer = lambda k: lax.rem(col + k, n_col)
    wsender = lambda k: lax.rem(col + n_col - k, n_col)
    for k in range(1, n_col):
        step(wbuf.at[col], wbuf.at[col], k, device("pcol", wpeer(k)), (send_e, recv_e)).start()
    for k in range(1, n_col):
        step(wbuf.at[col], wbuf.at[col], k, device("pcol", wpeer(k)), (send_e, recv_e)).wait_send()
    for k in range(1, n_col):
        step(wbuf.at[col], wbuf.at[wsender(k)], k, device("pcol", wsender(k)), (send_e, recv_e)).wait_recv()
    width_w = wbuf.shape[2]
    for c in range(n_col):
        out_ref[:, c * width_w:(c + 1) * width_w] = wbuf[c]


def gram_weighted(own_pseudo, pseudo, mode_shapes, axes, sizes):
    n, rows = sizes["pl"], own_pseudo.shape[0]
    width = pseudo.shape[0] // n
    x = jax.ShapeDtypeStruct((n, rows, width), jnp.bfloat16)
    n_col = sizes["pcol"]
    wshape = (n_col, mode_shapes.shape[0], 4 * rows)
    kernel = functools.partial(gram_weighted_kernel, axes=axes, factors=factor_table(sizes))
    return pl.pallas_call(
        kernel,
        out_shape=jax.ShapeDtypeStruct((wshape[1], n_col * wshape[2]), jnp.bfloat16),
        in_specs=[pl.BlockSpec(memory_space=pltpu.VMEM)] * 3,
        out_specs=pl.BlockSpec(memory_space=pltpu.VMEM),
        scratch_shapes=[
            pltpu.VMEM(x.shape, x.dtype),
            pltpu.VMEM(x.shape, x.dtype),
            pltpu.VMEM((n, 2, rows, width), x.dtype),
            pltpu.VMEM((n, 2, rows, width), x.dtype),
            pltpu.VMEM((rows, width), x.dtype),
            pltpu.VMEM((rows, width), x.dtype),
            pltpu.VMEM(wshape, jnp.bfloat16),
            pltpu.SemaphoreType.DMA((n,)),
            pltpu.SemaphoreType.DMA((n,)),
            pltpu.SemaphoreType.DMA(()),
            pltpu.SemaphoreType.DMA(()),
            pltpu.SemaphoreType.DMA((n,)),
            pltpu.SemaphoreType.DMA((n,)),
            pltpu.SemaphoreType.DMA(()),
            pltpu.SemaphoreType.DMA(()),
            pltpu.SemaphoreType.DMA((n_col,)),
            pltpu.SemaphoreType.DMA((n_col,)),
        ],
        compiler_params=pltpu.CompilerParams(collective_id=103, has_side_effects=True),
    )(own_pseudo, pseudo, mode_shapes)


def fused_sum(x, axes, sizes, over, add_across, kernel_id):
    n, rows, width = x.shape
    block = (rows, width) if add_across else (2, rows, width)
    kernel = functools.partial(
        fused_sum_kernel, axes=axes, factors=factor_table(sizes), over=over, add_across=add_across
    )
    return pl.pallas_call(
        kernel,
        out_shape=jax.ShapeDtypeStruct((n,) + block, x.dtype),
        in_specs=[pl.BlockSpec(memory_space=pltpu.VMEM)],
        out_specs=pl.BlockSpec(memory_space=pltpu.VMEM),
        scratch_shapes=[
            pltpu.VMEM(x.shape, x.dtype),
            pltpu.VMEM((n,) + block, x.dtype),
            pltpu.VMEM((rows, width), x.dtype),
            pltpu.VMEM((rows, width), x.dtype),
            pltpu.SemaphoreType.DMA((n,)),
            pltpu.SemaphoreType.DMA((n,)),
            pltpu.SemaphoreType.DMA(()),
            pltpu.SemaphoreType.DMA(()),
            pltpu.SemaphoreType.DMA((n,)),
            pltpu.SemaphoreType.DMA((n,)),
        ],
        compiler_params=pltpu.CompilerParams(collective_id=kernel_id, has_side_effects=True),
    )(x)


class Exchanger:
    def __init__(self, axes, sizes):
        self.axes, self.factors, self.calls = axes, factor_table(sizes), 0

    def __call__(self, x, group, same):
        count = math.prod(self.factors[f][1] for f in group)
        block = x.shape if same else x.shape[1:]
        if count == 1:
            return x[None] if same else x
        kernel = functools.partial(
            exchange_kernel, axes=self.axes, factors=self.factors, group=group, same=same
        )
        self.calls += 1
        return pl.pallas_call(
            kernel,
            out_shape=jax.ShapeDtypeStruct((count,) + tuple(block), x.dtype),
            in_specs=[pl.BlockSpec(memory_space=pl.ANY)],
            out_specs=pl.BlockSpec(memory_space=pl.ANY),
            scratch_shapes=[
                pltpu.SemaphoreType.DMA((count,)),
                pltpu.SemaphoreType.DMA((count,)),
                pltpu.SemaphoreType.DMA(()),
            ],
            compiler_params=pltpu.CompilerParams(collective_id=self.calls, has_side_effects=True),
        )(x)


def make_body(axes, sizes):
    n_row, n_col, n_pl = sizes["prow"], sizes["pcol"], sizes["pl"]
    swap = [(c * n_col + r, r * n_col + c) for r in range(n_row) for c in range(n_col)]
    sibling = [(r, r ^ 1) for r in range(n_row)]
    n_zh = n_row // 2

    def beside_sibling(part, core):
        other = lax.ppermute(part, "prow", sibling)
        first, second = jnp.where(core == 0, part, other), jnp.where(core == 0, other, part)
        return jnp.concatenate([first, second], axis=0)

    def body(factor_cols, modal_at_loads, mode_shapes, natural_freq, damping):
        ex = Exchanger(axes, sizes)
        in_phase, quadrature = transfer_pair(natural_freq, damping)
        modes = modal_at_loads.shape[0]
        block = modes // (n_row * n_col)
        row, col = lax.axis_index("prow"), lax.axis_index("pcol")
        width = factor_cols.shape[1]
        core = row % 2
        own_modes = lax.dynamic_slice_in_dim(modal_at_loads, core * (modes // 2), modes // 2, 0)
        sib_modes = lax.dynamic_slice_in_dim(modal_at_loads, (1 - core) * (modes // 2), modes // 2, 0)
        mine = jnp.dot(own_modes, factor_cols, preferred_element_type=jnp.float32)
        theirs = jnp.dot(sib_modes, factor_cols, preferred_element_type=jnp.float32)
        modal_load = modal_sum(mine, theirs.astype(jnp.bfloat16), axes, sizes).reshape(modes, width)
        modal_wide = modal_load.astype(jnp.float32)
        pseudo = jnp.concatenate(
            [
                (in_phase[:, None] * modal_wide).astype(jnp.bfloat16),
                (quadrature[:, None] * modal_wide).astype(jnp.bfloat16),
            ],
            axis=1,
        )
        first_row = (col * n_row + row) * block
        own_pseudo = lax.dynamic_slice_in_dim(pseudo, first_row, block, 0)
        half = modes // 2
        send_half = lax.dynamic_slice_in_dim(mode_shapes, (col % 2) * half, half, 1)
        panel_piece = lax.ppermute(send_half, ("prow", "pcol"), swap)
        panel_mine = lax.all_gather(panel_piece, "pl", axis=0, tiled=True)
        weighted = gram_weighted(own_pseudo, pseudo, mode_shapes, axes, sizes)
        panel_mine, weighted = lax.optimization_barrier((panel_mine, weighted))
        panel_other = lax.ppermute(panel_mine, "prow", sibling)
        weighted_mine = lax.dynamic_slice_in_dim(weighted, core * half, half, 1)
        weighted_other = lax.dynamic_slice_in_dim(weighted, (1 - core) * half, half, 1)
        return outer_rows(weighted_other, panel_other) + outer_rows(weighted_mine, panel_mine)

    return body


def solution(mesh):
    in_specs = (
        P(("prow", "pcol"), "pl"),
        P(None, ("prow", "pcol")),
        P(("prow", "pl"), None),
        P(),
        P(),
    )
    out_specs = P(("prow", "pl"), "pcol")
    axes = tuple(mesh.axis_names)
    body = make_body(axes, dict(mesh.shape))
    return jax.shard_map(body, mesh=mesh, in_specs=in_specs, out_specs=out_specs, check_vma=False)
```

```python
import functools
import math

import jax
import jax.numpy as jnp
from jax import lax
from jax.experimental import pallas as pl
from jax.experimental.pallas import tpu as pltpu
from jax.sharding import PartitionSpec as P

MESH = pl.DeviceIdType.MESH


def transfer_pair(natural_freq, damping):
    detuning = natural_freq * natural_freq - 1.0
    damper = 2.0 * damping * natural_freq
    modulus = detuning * detuning + damper * damper
    return (detuning / modulus, -damper / modulus)


def outer_rows(left_rows, right_rows):
    return lax.dot_general(
        left_rows, right_rows, (((1,), (1,)), ((), ())), preferred_element_type=jnp.float32
    )


def factor_table(sizes):
    return {
        "zh": ("prow", sizes["prow"] // 2, 2),
        "core": ("prow", 2, 1),
        "pcol": ("pcol", sizes["pcol"], 1),
        "pl": ("pl", sizes["pl"], 1),
    }


def exchange_kernel(x_ref, out_ref, send_sem, recv_sem, local_sem, *, axes, factors, group, same):
    coords = {a: lax.axis_index(a) for a in axes}

    def value(f):
        axis, size, stride = factors[f]
        return lax.rem(coords[axis] // stride, size)

    count = math.prod(factors[f][1] for f in group)
    me = 0
    for f in group:
        me = me * factors[f][1] + value(f)

    def device(member):
        place = dict(coords)
        for f in reversed(group):
            axis, size, stride = factors[f]
            place[axis] = place[axis] + (lax.rem(member, size) - value(f)) * stride
            member = member // size
        return tuple(place[a] for a in axes)

    def source(member):
        return x_ref if same else x_ref.at[member]

    def copy(offset):
        peer = lax.rem(me + offset, count)
        return pltpu.make_async_remote_copy(
            src_ref=source(peer),
            dst_ref=out_ref.at[me],
            send_sem=send_sem.at[offset],
            recv_sem=recv_sem.at[offset],
            device_id=device(peer),
            device_id_type=MESH,
        )

    def landing(offset):
        sender = lax.rem(me + count - offset, count)
        return pltpu.make_async_remote_copy(
            src_ref=source(me),
            dst_ref=out_ref.at[sender],
            send_sem=send_sem.at[offset],
            recv_sem=recv_sem.at[offset],
            device_id=device(sender),
            device_id_type=MESH,
        )

    local = pltpu.make_async_copy(source(me), out_ref.at[me], local_sem)
    local.start()
    barrier = pltpu.get_barrier_semaphore()
    for offset in range(1, count):
        peer = lax.rem(me + offset, count)
        pl.semaphore_signal(barrier, inc=1, device_id=device(peer), device_id_type=MESH)
    pl.semaphore_wait(barrier, count - 1)
    for offset in range(1, count):
        copy(offset).start()
    local.wait()
    for offset in range(1, count):
        copy(offset).wait_send()
    for offset in range(1, count):
        landing(offset).wait_recv()


def fused_sum_kernel(x_ref, out_ref, got, coll, part_out, part_in, send_a, recv_a, send_b, recv_b,
                     send_c, recv_c, *, axes, factors, over, add_across):
    coords = {a: lax.axis_index(a) for a in axes}

    def value(f):
        axis, size, stride = factors[f]
        return lax.rem(coords[axis] // stride, size)

    def device(f, v):
        place = dict(coords)
        axis, size, stride = factors[f]
        place[axis] = place[axis] + (v - value(f)) * stride
        return tuple(place[a] for a in axes)

    n = factors[over][1]
    me, half = value(over), value("zh")
    partner = device("zh", 1 - half)
    peer = lambda k: lax.rem(me + k, n)
    sender = lambda k: lax.rem(me + n - k, n)

    def step(src, dst_at, k, to, sems):
        return pltpu.make_async_remote_copy(
            src_ref=src, dst_ref=dst_at, send_sem=sems[0].at[k], recv_sem=sems[1].at[k],
            device_id=to, device_id_type=MESH,
        )

    barrier = pltpu.get_barrier_semaphore()
    for k in range(1, n):
        pl.semaphore_signal(barrier, inc=1, device_id=device(over, peer(k)), device_id_type=MESH)
    pl.semaphore_signal(barrier, inc=1, device_id=partner, device_id_type=MESH)
    pl.semaphore_wait(barrier, n)

    for k in range(1, n):
        step(x_ref.at[peer(k)], got.at[me], k, device(over, peer(k)), (send_a, recv_a)).start()
    for k in range(1, n):
        step(x_ref.at[peer(k)], got.at[me], k, device(over, peer(k)), (send_a, recv_a)).wait_send()
    for k in range(1, n):
        step(x_ref.at[me], got.at[sender(k)], k, device(over, sender(k)), (send_a, recv_a)).wait_recv()
    total = x_ref[me].astype(jnp.float32)
    for k in range(1, n):
        total = total + got[sender(k)].astype(jnp.float32)
    part_out[...] = total.astype(part_out.dtype)

    across = pltpu.make_async_remote_copy(
        src_ref=part_out, dst_ref=part_in, send_sem=send_b, recv_sem=recv_b,
        device_id=partner, device_id_type=MESH,
    )
    across.start()
    across.wait_send()
    across.wait_recv()
    if add_across:
        mine, theirs = part_out[...].astype(jnp.float32), part_in[...].astype(jnp.float32)
        coll[me] = (mine + theirs).astype(coll.dtype)
    else:
        mine, theirs = part_out[...], part_in[...]
        first = jnp.where(half == 0, mine, theirs)
        second = jnp.where(half == 0, theirs, mine)
        coll[me] = jnp.stack([first, second])

    for k in range(1, n):
        step(coll.at[me], coll.at[me], k, device(over, peer(k)), (send_c, recv_c)).start()
    for k in range(1, n):
        step(coll.at[me], coll.at[me], k, device(over, peer(k)), (send_c, recv_c)).wait_send()
    for k in range(1, n):
        step(coll.at[me], coll.at[sender(k)], k, device(over, sender(k)), (send_c, recv_c)).wait_recv()
    out_ref[...] = coll[...]


def modal_sum_kernel(mine_ref, theirs_ref, out_ref, sib_in, pieces, got, coll, part_out, part_in,
                     sib_out, send_s, recv_s, send_a, recv_a, send_b, recv_b, send_c, recv_c,
                     send_d, recv_d, *, axes, factors):
    coords = {a: lax.axis_index(a) for a in axes}

    def value(f):
        axis, size, stride = factors[f]
        return lax.rem(coords[axis] // stride, size)

    def device(f, v):
        place = dict(coords)
        axis, size, stride = factors[f]
        place[axis] = place[axis] + (v - value(f)) * stride
        return tuple(place[a] for a in axes)

    n = factors["pcol"][1]
    me, half, core = value("pcol"), value("zh"), value("core")
    partner, sibling = device("zh", 1 - half), device("core", 1 - core)
    peer = lambda k: lax.rem(me + k, n)
    sender = lambda k: lax.rem(me + n - k, n)

    def step(src, dst_at, k, to, sems):
        return pltpu.make_async_remote_copy(
            src_ref=src, dst_ref=dst_at, send_sem=sems[0].at[k], recv_sem=sems[1].at[k],
            device_id=to, device_id_type=MESH,
        )

    def one(src, dst, to, send_sem, recv_sem):
        return pltpu.make_async_remote_copy(
            src_ref=src, dst_ref=dst, send_sem=send_sem, recv_sem=recv_sem,
            device_id=to, device_id_type=MESH,
        )

    pending = []
    barrier = pltpu.get_barrier_semaphore()
    for k in range(1, n):
        pl.semaphore_signal(barrier, inc=1, device_id=device("pcol", peer(k)), device_id_type=MESH)
    pl.semaphore_signal(barrier, inc=1, device_id=partner, device_id_type=MESH)
    pl.semaphore_signal(barrier, inc=1, device_id=sibling, device_id_type=MESH)
    pl.semaphore_wait(barrier, n + 1)

    chip = one(theirs_ref, sib_in, sibling, send_s, recv_s)
    chip.start()
    pending.append(chip)
    chip.wait_recv()
    summed = mine_ref[...] + sib_in[...].astype(jnp.float32)
    pieces[...] = summed.astype(pieces.dtype).reshape(pieces.shape)

    for k in range(1, n):
        step(pieces.at[peer(k)], got.at[me], k, device("pcol", peer(k)), (send_a, recv_a)).start()
    for k in range(1, n):
        pending.append(step(pieces.at[peer(k)], got.at[me], k, device("pcol", peer(k)), (send_a, recv_a)))
    for k in range(1, n):
        step(pieces.at[me], got.at[sender(k)], k, device("pcol", sender(k)), (send_a, recv_a)).wait_recv()
    total = pieces[me].astype(jnp.float32)
    for k in range(1, n):
        total = total + got[sender(k)].astype(jnp.float32)
    part_out[...] = total.astype(part_out.dtype)

    across = one(part_out, part_in, partner, send_b, recv_b)
    across.start()
    pending.append(across)
    across.wait_recv()
    coll[me] = (part_out[...].astype(jnp.float32) + part_in[...].astype(jnp.float32)).astype(coll.dtype)

    for k in range(1, n):
        step(coll.at[me], coll.at[me], k, device("pcol", peer(k)), (send_c, recv_c)).start()
    for k in range(1, n):
        pending.append(step(coll.at[me], coll.at[me], k, device("pcol", peer(k)), (send_c, recv_c)))
    for k in range(1, n):
        step(coll.at[me], coll.at[sender(k)], k, device("pcol", sender(k)), (send_c, recv_c)).wait_recv()

    join = one(coll, sib_out, sibling, send_d, recv_d)
    join.start()
    pending.append(join)
    join.wait_recv()
    out_ref[core] = coll[...]
    out_ref[1 - core] = sib_out[...]
    for sent in pending:
        sent.wait_send()


def modal_sum(mine, theirs, axes, sizes):
    n = sizes["pcol"]
    rows, width = mine.shape
    block = (n, rows // n, width)
    kernel = functools.partial(modal_sum_kernel, axes=axes, factors=factor_table(sizes))
    return pl.pallas_call(
        kernel,
        out_shape=jax.ShapeDtypeStruct((2,) + block, jnp.bfloat16),
        in_specs=[pl.BlockSpec(memory_space=pltpu.VMEM)] * 2,
        out_specs=pl.BlockSpec(memory_space=pltpu.VMEM),
        scratch_shapes=[
            pltpu.VMEM((rows, width), jnp.bfloat16),
            pltpu.VMEM(block, jnp.bfloat16),
            pltpu.VMEM(block, jnp.bfloat16),
            pltpu.VMEM(block, jnp.bfloat16),
            pltpu.VMEM(block[1:], jnp.bfloat16),
            pltpu.VMEM(block[1:], jnp.bfloat16),
            pltpu.VMEM(block, jnp.bfloat16),
            pltpu.SemaphoreType.DMA(()),
            pltpu.SemaphoreType.DMA(()),
            pltpu.SemaphoreType.DMA((n,)),
            pltpu.SemaphoreType.DMA((n,)),
            pltpu.SemaphoreType.DMA(()),
            pltpu.SemaphoreType.DMA(()),
            pltpu.SemaphoreType.DMA((n,)),
            pltpu.SemaphoreType.DMA((n,)),
            pltpu.SemaphoreType.DMA(()),
            pltpu.SemaphoreType.DMA(()),
        ],
        compiler_params=pltpu.CompilerParams(collective_id=102, has_side_effects=True),
    )(mine, theirs)


def gram_weighted_kernel(x_ref, shapes_ref, out_ref, got, coll, sib_coll, part_out, part_in, wbuf,
                         send_a, recv_a, send_b, recv_b, send_c, recv_c, send_d, recv_d, send_e,
                         recv_e, *, axes, factors):
    coords = {a: lax.axis_index(a) for a in axes}

    def value(f):
        axis, size, stride = factors[f]
        return lax.rem(coords[axis] // stride, size)

    def device(f, v):
        place = dict(coords)
        axis, size, stride = factors[f]
        place[axis] = place[axis] + (v - value(f)) * stride
        return tuple(place[a] for a in axes)

    n, n_col = factors["pl"][1], factors["pcol"][1]
    me, half, core, col = value("pl"), value("zh"), value("core"), value("pcol")
    partner, sibling = device("zh", 1 - half), device("core", 1 - core)

    def step(src, dst_at, k, to, sems):
        return pltpu.make_async_remote_copy(
            src_ref=src, dst_ref=dst_at, send_sem=sems[0].at[k], recv_sem=sems[1].at[k],
            device_id=to, device_id_type=MESH,
        )

    def one(src, dst, to, send_sem, recv_sem):
        return pltpu.make_async_remote_copy(
            src_ref=src, dst_ref=dst, send_sem=send_sem, recv_sem=recv_sem,
            device_id=to, device_id_type=MESH,
        )

    pending = []
    barrier = pltpu.get_barrier_semaphore()
    for k in range(1, n):
        pl.semaphore_signal(barrier, inc=1, device_id=device("pl", lax.rem(me + k, n)), device_id_type=MESH)
    for k in range(1, n_col):
        pl.semaphore_signal(
            barrier, inc=1, device_id=device("pcol", lax.rem(col + k, n_col)), device_id_type=MESH
        )
    pl.semaphore_signal(barrier, inc=1, device_id=partner, device_id_type=MESH)
    pl.semaphore_signal(barrier, inc=1, device_id=sibling, device_id_type=MESH)
    pl.semaphore_wait(barrier, n + n_col)

    peer = lambda k: lax.rem(me + k, n)
    sender = lambda k: lax.rem(me + n - k, n)
    for k in range(1, n):
        step(x_ref.at[peer(k)], got.at[me], k, device("pl", peer(k)), (send_a, recv_a)).start()
    for k in range(1, n):
        pending.append(step(x_ref.at[peer(k)], got.at[me], k, device("pl", peer(k)), (send_a, recv_a)))
    for k in range(1, n):
        step(x_ref.at[me], got.at[sender(k)], k, device("pl", sender(k)), (send_a, recv_a)).wait_recv()
    total = x_ref[me].astype(jnp.float32)
    for k in range(1, n):
        total = total + got[sender(k)].astype(jnp.float32)
    part_out[...] = total.astype(part_out.dtype)

    across = one(part_out, part_in, partner, send_b, recv_b)
    across.start()
    pending.append(across)
    across.wait_recv()
    mine, theirs = part_out[...], part_in[...]
    coll[me] = jnp.stack([jnp.where(half == 0, mine, theirs), jnp.where(half == 0, theirs, mine)])

    for k in range(1, n):
        step(coll.at[me], coll.at[me], k, device("pl", peer(k)), (send_c, recv_c)).start()
    for k in range(1, n):
        pending.append(step(coll.at[me], coll.at[me], k, device("pl", peer(k)), (send_c, recv_c)))
    for k in range(1, n):
        step(coll.at[me], coll.at[sender(k)], k, device("pl", sender(k)), (send_c, recv_c)).wait_recv()

    chunk = coll.shape[-1]

    def weighted_block(blocks, h):
        acc = jnp.zeros((shapes_ref.shape[0], blocks.shape[2]), jnp.float32)
        for l in range(n):
            acc = acc + lax.dot_general(
                shapes_ref[:, l * chunk:(l + 1) * chunk], blocks[l, h],
                (((1,), (1,)), ((), ())), preferred_element_type=jnp.float32,
            )
        return acc

    join = one(coll, sib_coll, sibling, send_d, recv_d)
    join.start()
    own = [weighted_block(coll, h) for h in range(2)]
    pending.append(join)
    join.wait_recv()
    other = [weighted_block(sib_coll, h) for h in range(2)]
    parts = []
    for h in range(2):
        parts += [jnp.where(core == 0, own[h], other[h]), jnp.where(core == 0, other[h], own[h])]
    wbuf[col] = jnp.concatenate(parts, axis=1).astype(wbuf.dtype)

    wpeer = lambda k: lax.rem(col + k, n_col)
    wsender = lambda k: lax.rem(col + n_col - k, n_col)
    for k in range(1, n_col):
        step(wbuf.at[col], wbuf.at[col], k, device("pcol", wpeer(k)), (send_e, recv_e)).start()
    for k in range(1, n_col):
        pending.append(step(wbuf.at[col], wbuf.at[col], k, device("pcol", wpeer(k)), (send_e, recv_e)))
    for k in range(1, n_col):
        step(wbuf.at[col], wbuf.at[wsender(k)], k, device("pcol", wsender(k)), (send_e, recv_e)).wait_recv()
    width_w = wbuf.shape[2]
    for c in range(n_col):
        out_ref[:, c * width_w:(c + 1) * width_w] = wbuf[c]
    for sent in pending:
        sent.wait_send()


def gram_weighted(x, mode_shapes, axes, sizes):
    n, rows, width = x.shape
    n_col = sizes["pcol"]
    wshape = (n_col, mode_shapes.shape[0], 4 * rows)
    kernel = functools.partial(gram_weighted_kernel, axes=axes, factors=factor_table(sizes))
    return pl.pallas_call(
        kernel,
        out_shape=jax.ShapeDtypeStruct((wshape[1], n_col * wshape[2]), jnp.bfloat16),
        in_specs=[pl.BlockSpec(memory_space=pltpu.VMEM)] * 2,
        out_specs=pl.BlockSpec(memory_space=pltpu.VMEM),
        scratch_shapes=[
            pltpu.VMEM(x.shape, x.dtype),
            pltpu.VMEM((n, 2, rows, width), x.dtype),
            pltpu.VMEM((n, 2, rows, width), x.dtype),
            pltpu.VMEM((rows, width), x.dtype),
            pltpu.VMEM((rows, width), x.dtype),
            pltpu.VMEM(wshape, jnp.bfloat16),
            pltpu.SemaphoreType.DMA((n,)),
            pltpu.SemaphoreType.DMA((n,)),
            pltpu.SemaphoreType.DMA(()),
            pltpu.SemaphoreType.DMA(()),
            pltpu.SemaphoreType.DMA((n,)),
            pltpu.SemaphoreType.DMA((n,)),
            pltpu.SemaphoreType.DMA(()),
            pltpu.SemaphoreType.DMA(()),
            pltpu.SemaphoreType.DMA((n_col,)),
            pltpu.SemaphoreType.DMA((n_col,)),
        ],
        compiler_params=pltpu.CompilerParams(collective_id=103, has_side_effects=True),
    )(x, mode_shapes)


def fused_sum(x, axes, sizes, over, add_across, kernel_id):
    n, rows, width = x.shape
    block = (rows, width) if add_across else (2, rows, width)
    kernel = functools.partial(
        fused_sum_kernel, axes=axes, factors=factor_table(sizes), over=over, add_across=add_across
    )
    return pl.pallas_call(
        kernel,
        out_shape=jax.ShapeDtypeStruct((n,) + block, x.dtype),
        in_specs=[pl.BlockSpec(memory_space=pltpu.VMEM)],
        out_specs=pl.BlockSpec(memory_space=pltpu.VMEM),
        scratch_shapes=[
            pltpu.VMEM(x.shape, x.dtype),
            pltpu.VMEM((n,) + block, x.dtype),
            pltpu.VMEM((rows, width), x.dtype),
            pltpu.VMEM((rows, width), x.dtype),
            pltpu.SemaphoreType.DMA((n,)),
            pltpu.SemaphoreType.DMA((n,)),
            pltpu.SemaphoreType.DMA(()),
            pltpu.SemaphoreType.DMA(()),
            pltpu.SemaphoreType.DMA((n,)),
            pltpu.SemaphoreType.DMA((n,)),
        ],
        compiler_params=pltpu.CompilerParams(collective_id=kernel_id, has_side_effects=True),
    )(x)


class Exchanger:
    def __init__(self, axes, sizes):
        self.axes, self.factors, self.calls = axes, factor_table(sizes), 0

    def __call__(self, x, group, same):
        count = math.prod(self.factors[f][1] for f in group)
        block = x.shape if same else x.shape[1:]
        if count == 1:
            return x[None] if same else x
        kernel = functools.partial(
            exchange_kernel, axes=self.axes, factors=self.factors, group=group, same=same
        )
        self.calls += 1
        return pl.pallas_call(
            kernel,
            out_shape=jax.ShapeDtypeStruct((count,) + tuple(block), x.dtype),
            in_specs=[pl.BlockSpec(memory_space=pl.ANY)],
            out_specs=pl.BlockSpec(memory_space=pl.ANY),
            scratch_shapes=[
                pltpu.SemaphoreType.DMA((count,)),
                pltpu.SemaphoreType.DMA((count,)),
                pltpu.SemaphoreType.DMA(()),
            ],
            compiler_params=pltpu.CompilerParams(collective_id=self.calls, has_side_effects=True),
        )(x)


def make_body(axes, sizes):
    n_row, n_col, n_pl = sizes["prow"], sizes["pcol"], sizes["pl"]
    swap = [(c * n_col + r, r * n_col + c) for r in range(n_row) for c in range(n_col)]
    sibling = [(r, r ^ 1) for r in range(n_row)]
    n_zh = n_row // 2

    def beside_sibling(part, core):
        other = lax.ppermute(part, "prow", sibling)
        first, second = jnp.where(core == 0, part, other), jnp.where(core == 0, other, part)
        return jnp.concatenate([first, second], axis=0)

    def body(factor_cols, modal_at_loads, mode_shapes, natural_freq, damping):
        ex = Exchanger(axes, sizes)
        in_phase, quadrature = transfer_pair(natural_freq, damping)
        modes = modal_at_loads.shape[0]
        block = modes // (n_row * n_col)
        row, col = lax.axis_index("prow"), lax.axis_index("pcol")
        width = factor_cols.shape[1]
        core = row % 2
        own_modes = lax.dynamic_slice_in_dim(modal_at_loads, core * (modes // 2), modes // 2, 0)
        sib_modes = lax.dynamic_slice_in_dim(modal_at_loads, (1 - core) * (modes // 2), modes // 2, 0)
        mine = jnp.dot(own_modes, factor_cols, preferred_element_type=jnp.float32)
        theirs = jnp.dot(sib_modes, factor_cols, preferred_element_type=jnp.float32)
        modal_load = modal_sum(mine, theirs.astype(jnp.bfloat16), axes, sizes).reshape(modes, width)
        modal_wide = modal_load.astype(jnp.float32)
        pseudo = jnp.concatenate(
            [
                (in_phase[:, None] * modal_wide).astype(jnp.bfloat16),
                (quadrature[:, None] * modal_wide).astype(jnp.bfloat16),
            ],
            axis=1,
        )
        first_row = (col * n_row + row) * block
        own_pseudo = lax.dynamic_slice_in_dim(pseudo, first_row, block, 0)
        partial_gram = outer_rows(own_pseudo, pseudo).astype(jnp.bfloat16)
        chunk = modes // n_pl
        by_chunk = partial_gram.reshape(block, n_pl, chunk).transpose(1, 0, 2)
        half = modes // 2
        send_half = lax.dynamic_slice_in_dim(mode_shapes, (col % 2) * half, half, 1)
        panel_piece = lax.ppermute(send_half, ("prow", "pcol"), swap)
        panel_mine = lax.all_gather(panel_piece, "pl", axis=0, tiled=True)
        weighted = gram_weighted(by_chunk, mode_shapes, axes, sizes)
        panel_mine, weighted = lax.optimization_barrier((panel_mine, weighted))
        panel_other = lax.ppermute(panel_mine, "prow", sibling)
        weighted_mine = lax.dynamic_slice_in_dim(weighted, core * half, half, 1)
        weighted_other = lax.dynamic_slice_in_dim(weighted, (1 - core) * half, half, 1)
        return outer_rows(weighted_other, panel_other) + outer_rows(weighted_mine, panel_mine)

    return body


def solution(mesh):
    in_specs = (
        P(("prow", "pcol"), "pl"),
        P(None, ("prow", "pcol")),
        P(("prow", "pl"), None),
        P(),
        P(),
    )
    out_specs = P(("prow", "pl"), "pcol")
    axes = tuple(mesh.axis_names)
    body = make_body(axes, dict(mesh.shape))
    return jax.shard_map(body, mesh=mesh, in_specs=in_specs, out_specs=out_specs, check_vma=False)
```

```python
import functools
import math

import jax
import jax.numpy as jnp
from jax import lax
from jax.experimental import pallas as pl
from jax.experimental.pallas import tpu as pltpu
from jax.sharding import PartitionSpec as P

MESH = pl.DeviceIdType.MESH


def transfer_pair(natural_freq, damping):
    detuning = natural_freq * natural_freq - 1.0
    damper = 2.0 * damping * natural_freq
    modulus = detuning * detuning + damper * damper
    return (detuning / modulus, -damper / modulus)


def outer_rows(left_rows, right_rows):
    return lax.dot_general(
        left_rows, right_rows, (((1,), (1,)), ((), ())), preferred_element_type=jnp.float32
    )


def factor_table(sizes):
    return {
        "zh": ("prow", sizes["prow"] // 2, 2),
        "core": ("prow", 2, 1),
        "pcol": ("pcol", sizes["pcol"], 1),
        "pl": ("pl", sizes["pl"], 1),
    }


def exchange_kernel(x_ref, out_ref, send_sem, recv_sem, local_sem, *, axes, factors, group, same):
    coords = {a: lax.axis_index(a) for a in axes}

    def value(f):
        axis, size, stride = factors[f]
        return lax.rem(coords[axis] // stride, size)

    count = math.prod(factors[f][1] for f in group)
    me = 0
    for f in group:
        me = me * factors[f][1] + value(f)

    def device(member):
        place = dict(coords)
        for f in reversed(group):
            axis, size, stride = factors[f]
            place[axis] = place[axis] + (lax.rem(member, size) - value(f)) * stride
            member = member // size
        return tuple(place[a] for a in axes)

    def source(member):
        return x_ref if same else x_ref.at[member]

    def copy(offset):
        peer = lax.rem(me + offset, count)
        return pltpu.make_async_remote_copy(
            src_ref=source(peer),
            dst_ref=out_ref.at[me],
            send_sem=send_sem.at[offset],
            recv_sem=recv_sem.at[offset],
            device_id=device(peer),
            device_id_type=MESH,
        )

    def landing(offset):
        sender = lax.rem(me + count - offset, count)
        return pltpu.make_async_remote_copy(
            src_ref=source(me),
            dst_ref=out_ref.at[sender],
            send_sem=send_sem.at[offset],
            recv_sem=recv_sem.at[offset],
            device_id=device(sender),
            device_id_type=MESH,
        )

    local = pltpu.make_async_copy(source(me), out_ref.at[me], local_sem)
    local.start()
    barrier = pltpu.get_barrier_semaphore()
    for offset in range(1, count):
        peer = lax.rem(me + offset, count)
        pl.semaphore_signal(barrier, inc=1, device_id=device(peer), device_id_type=MESH)
    pl.semaphore_wait(barrier, count - 1)
    for offset in range(1, count):
        copy(offset).start()
    local.wait()
    for offset in range(1, count):
        copy(offset).wait_send()
    for offset in range(1, count):
        landing(offset).wait_recv()


def fused_sum_kernel(x_ref, out_ref, got, coll, part_out, part_in, send_a, recv_a, send_b, recv_b,
                     send_c, recv_c, *, axes, factors, over, add_across):
    coords = {a: lax.axis_index(a) for a in axes}

    def value(f):
        axis, size, stride = factors[f]
        return lax.rem(coords[axis] // stride, size)

    def device(f, v):
        place = dict(coords)
        axis, size, stride = factors[f]
        place[axis] = place[axis] + (v - value(f)) * stride
        return tuple(place[a] for a in axes)

    n = factors[over][1]
    me, half = value(over), value("zh")
    partner = device("zh", 1 - half)
    peer = lambda k: lax.rem(me + k, n)
    sender = lambda k: lax.rem(me + n - k, n)

    def step(src, dst_at, k, to, sems):
        return pltpu.make_async_remote_copy(
            src_ref=src, dst_ref=dst_at, send_sem=sems[0].at[k], recv_sem=sems[1].at[k],
            device_id=to, device_id_type=MESH,
        )

    barrier = pltpu.get_barrier_semaphore()
    for k in range(1, n):
        pl.semaphore_signal(barrier, inc=1, device_id=device(over, peer(k)), device_id_type=MESH)
    pl.semaphore_signal(barrier, inc=1, device_id=partner, device_id_type=MESH)
    pl.semaphore_wait(barrier, n)

    for k in range(1, n):
        step(x_ref.at[peer(k)], got.at[me], k, device(over, peer(k)), (send_a, recv_a)).start()
    for k in range(1, n):
        step(x_ref.at[peer(k)], got.at[me], k, device(over, peer(k)), (send_a, recv_a)).wait_send()
    for k in range(1, n):
        step(x_ref.at[me], got.at[sender(k)], k, device(over, sender(k)), (send_a, recv_a)).wait_recv()
    total = x_ref[me].astype(jnp.float32)
    for k in range(1, n):
        total = total + got[sender(k)].astype(jnp.float32)
    part_out[...] = total.astype(part_out.dtype)

    across = pltpu.make_async_remote_copy(
        src_ref=part_out, dst_ref=part_in, send_sem=send_b, recv_sem=recv_b,
        device_id=partner, device_id_type=MESH,
    )
    across.start()
    across.wait_send()
    across.wait_recv()
    if add_across:
        mine, theirs = part_out[...].astype(jnp.float32), part_in[...].astype(jnp.float32)
        coll[me] = (mine + theirs).astype(coll.dtype)
    else:
        mine, theirs = part_out[...], part_in[...]
        first = jnp.where(half == 0, mine, theirs)
        second = jnp.where(half == 0, theirs, mine)
        coll[me] = jnp.stack([first, second])

    for k in range(1, n):
        step(coll.at[me], coll.at[me], k, device(over, peer(k)), (send_c, recv_c)).start()
    for k in range(1, n):
        step(coll.at[me], coll.at[me], k, device(over, peer(k)), (send_c, recv_c)).wait_send()
    for k in range(1, n):
        step(coll.at[me], coll.at[sender(k)], k, device(over, sender(k)), (send_c, recv_c)).wait_recv()
    out_ref[...] = coll[...]


def modal_sum_kernel(mine_ref, theirs_ref, out_ref, sib_in, pieces, got, coll, part_out, part_in,
                     sib_out, send_s, recv_s, send_a, recv_a, send_b, recv_b, send_c, recv_c,
                     send_d, recv_d, *, axes, factors):
    coords = {a: lax.axis_index(a) for a in axes}

    def value(f):
        axis, size, stride = factors[f]
        return lax.rem(coords[axis] // stride, size)

    def device(f, v):
        place = dict(coords)
        axis, size, stride = factors[f]
        place[axis] = place[axis] + (v - value(f)) * stride
        return tuple(place[a] for a in axes)

    n = factors["pcol"][1]
    me, half, core = value("pcol"), value("zh"), value("core")
    partner, sibling = device("zh", 1 - half), device("core", 1 - core)
    peer = lambda k: lax.rem(me + k, n)
    sender = lambda k: lax.rem(me + n - k, n)

    def step(src, dst_at, k, to, sems):
        return pltpu.make_async_remote_copy(
            src_ref=src, dst_ref=dst_at, send_sem=sems[0].at[k], recv_sem=sems[1].at[k],
            device_id=to, device_id_type=MESH,
        )

    def one(src, dst, to, send_sem, recv_sem):
        return pltpu.make_async_remote_copy(
            src_ref=src, dst_ref=dst, send_sem=send_sem, recv_sem=recv_sem,
            device_id=to, device_id_type=MESH,
        )

    pending = []
    barrier = pltpu.get_barrier_semaphore()
    for k in range(1, n):
        pl.semaphore_signal(barrier, inc=1, device_id=device("pcol", peer(k)), device_id_type=MESH)
    pl.semaphore_signal(barrier, inc=1, device_id=partner, device_id_type=MESH)
    pl.semaphore_signal(barrier, inc=1, device_id=sibling, device_id_type=MESH)
    pl.semaphore_wait(barrier, n + 1)

    chip = one(theirs_ref, sib_in, sibling, send_s, recv_s)
    chip.start()
    pending.append(chip)
    chip.wait_recv()
    summed = mine_ref[...] + sib_in[...].astype(jnp.float32)
    pieces[...] = summed.astype(pieces.dtype).reshape(pieces.shape)

    for k in range(1, n):
        step(pieces.at[peer(k)], got.at[me], k, device("pcol", peer(k)), (send_a, recv_a)).start()
    for k in range(1, n):
        pending.append(step(pieces.at[peer(k)], got.at[me], k, device("pcol", peer(k)), (send_a, recv_a)))
    for k in range(1, n):
        step(pieces.at[me], got.at[sender(k)], k, device("pcol", sender(k)), (send_a, recv_a)).wait_recv()
    total = pieces[me].astype(jnp.float32)
    for k in range(1, n):
        total = total + got[sender(k)].astype(jnp.float32)
    part_out[...] = total.astype(part_out.dtype)

    across = one(part_out, part_in, partner, send_b, recv_b)
    across.start()
    pending.append(across)
    across.wait_recv()
    coll[me] = (part_out[...].astype(jnp.float32) + part_in[...].astype(jnp.float32)).astype(coll.dtype)

    for k in range(1, n):
        step(coll.at[me], coll.at[me], k, device("pcol", peer(k)), (send_c, recv_c)).start()
    for k in range(1, n):
        pending.append(step(coll.at[me], coll.at[me], k, device("pcol", peer(k)), (send_c, recv_c)))
    for k in range(1, n):
        step(coll.at[me], coll.at[sender(k)], k, device("pcol", sender(k)), (send_c, recv_c)).wait_recv()

    join = one(coll, sib_out, sibling, send_d, recv_d)
    join.start()
    pending.append(join)
    join.wait_recv()
    out_ref[core] = coll[...]
    out_ref[1 - core] = sib_out[...]
    for sent in pending:
        sent.wait_send()


def modal_sum(mine, theirs, axes, sizes):
    n = sizes["pcol"]
    rows, width = mine.shape
    block = (n, rows // n, width)
    kernel = functools.partial(modal_sum_kernel, axes=axes, factors=factor_table(sizes))
    return pl.pallas_call(
        kernel,
        out_shape=jax.ShapeDtypeStruct((2,) + block, jnp.bfloat16),
        in_specs=[pl.BlockSpec(memory_space=pltpu.VMEM)] * 2,
        out_specs=pl.BlockSpec(memory_space=pltpu.VMEM),
        scratch_shapes=[
            pltpu.VMEM((rows, width), jnp.bfloat16),
            pltpu.VMEM(block, jnp.bfloat16),
            pltpu.VMEM(block, jnp.bfloat16),
            pltpu.VMEM(block, jnp.bfloat16),
            pltpu.VMEM(block[1:], jnp.bfloat16),
            pltpu.VMEM(block[1:], jnp.bfloat16),
            pltpu.VMEM(block, jnp.bfloat16),
            pltpu.SemaphoreType.DMA(()),
            pltpu.SemaphoreType.DMA(()),
            pltpu.SemaphoreType.DMA((n,)),
            pltpu.SemaphoreType.DMA((n,)),
            pltpu.SemaphoreType.DMA(()),
            pltpu.SemaphoreType.DMA(()),
            pltpu.SemaphoreType.DMA((n,)),
            pltpu.SemaphoreType.DMA((n,)),
            pltpu.SemaphoreType.DMA(()),
            pltpu.SemaphoreType.DMA(()),
        ],
        compiler_params=pltpu.CompilerParams(collective_id=102, has_side_effects=True),
    )(mine, theirs)


def gram_weighted_kernel(x_ref, shapes_ref, out_ref, got, coll, sib_coll, part_out, part_in, wbuf,
                         send_a, recv_a, send_b, recv_b, send_c, recv_c, send_d, recv_d, send_e,
                         recv_e, *, axes, factors):
    coords = {a: lax.axis_index(a) for a in axes}

    def value(f):
        axis, size, stride = factors[f]
        return lax.rem(coords[axis] // stride, size)

    def device(f, v):
        place = dict(coords)
        axis, size, stride = factors[f]
        place[axis] = place[axis] + (v - value(f)) * stride
        return tuple(place[a] for a in axes)

    n, n_col = factors["pl"][1], factors["pcol"][1]
    me, half, core, col = value("pl"), value("zh"), value("core"), value("pcol")
    partner, sibling = device("zh", 1 - half), device("core", 1 - core)

    def step(src, dst_at, k, to, sems):
        return pltpu.make_async_remote_copy(
            src_ref=src, dst_ref=dst_at, send_sem=sems[0].at[k], recv_sem=sems[1].at[k],
            device_id=to, device_id_type=MESH,
        )

    def one(src, dst, to, send_sem, recv_sem):
        return pltpu.make_async_remote_copy(
            src_ref=src, dst_ref=dst, send_sem=send_sem, recv_sem=recv_sem,
            device_id=to, device_id_type=MESH,
        )

    pending = []
    barrier = pltpu.get_barrier_semaphore()
    for k in range(1, n):
        pl.semaphore_signal(barrier, inc=1, device_id=device("pl", lax.rem(me + k, n)), device_id_type=MESH)
    for k in range(1, n_col):
        pl.semaphore_signal(
            barrier, inc=1, device_id=device("pcol", lax.rem(col + k, n_col)), device_id_type=MESH
        )
    pl.semaphore_signal(barrier, inc=1, device_id=partner, device_id_type=MESH)
    pl.semaphore_signal(barrier, inc=1, device_id=sibling, device_id_type=MESH)
    pl.semaphore_wait(barrier, n + n_col)

    peer = lambda k: lax.rem(me + k, n)
    sender = lambda k: lax.rem(me + n - k, n)
    for k in range(1, n):
        step(x_ref.at[peer(k)], got.at[me], k, device("pl", peer(k)), (send_a, recv_a)).start()
    for k in range(1, n):
        pending.append(step(x_ref.at[peer(k)], got.at[me], k, device("pl", peer(k)), (send_a, recv_a)))
    for k in range(1, n):
        step(x_ref.at[me], got.at[sender(k)], k, device("pl", sender(k)), (send_a, recv_a)).wait_recv()
    total = x_ref[me].astype(jnp.float32)
    for k in range(1, n):
        total = total + got[sender(k)].astype(jnp.float32)
    part_out[...] = total.astype(part_out.dtype)

    across = one(part_out, part_in, partner, send_b, recv_b)
    across.start()
    pending.append(across)
    across.wait_recv()
    mine, theirs = part_out[...], part_in[...]
    coll[me] = jnp.stack([jnp.where(half == 0, mine, theirs), jnp.where(half == 0, theirs, mine)])

    for k in range(1, n):
        step(coll.at[me], coll.at[me], k, device("pl", peer(k)), (send_c, recv_c)).start()
    for k in range(1, n):
        pending.append(step(coll.at[me], coll.at[me], k, device("pl", peer(k)), (send_c, recv_c)))

    def to_sibling(chunk_at):
        return pltpu.make_async_remote_copy(
            src_ref=coll.at[chunk_at], dst_ref=sib_coll.at[chunk_at], send_sem=send_d.at[chunk_at],
            recv_sem=recv_d.at[chunk_at], device_id=sibling, device_id_type=MESH,
        )

    to_sibling(me).start()
    pending.append(to_sibling(me))
    for k in range(1, n):
        step(coll.at[me], coll.at[sender(k)], k, device("pl", sender(k)), (send_c, recv_c)).wait_recv()
        to_sibling(sender(k)).start()
        pending.append(to_sibling(sender(k)))

    chunk = coll.shape[-1]

    def weighted_block(blocks, h):
        acc = jnp.zeros((shapes_ref.shape[0], blocks.shape[2]), jnp.float32)
        for l in range(n):
            acc = acc + lax.dot_general(
                shapes_ref[:, l * chunk:(l + 1) * chunk], blocks[l, h],
                (((1,), (1,)), ((), ())), preferred_element_type=jnp.float32,
            )
        return acc

    own = [weighted_block(coll, h) for h in range(2)]
    for l in range(n):
        to_sibling(l).wait_recv()
    other = [weighted_block(sib_coll, h) for h in range(2)]
    parts = []
    for h in range(2):
        parts += [jnp.where(core == 0, own[h], other[h]), jnp.where(core == 0, other[h], own[h])]
    wbuf[col] = jnp.concatenate(parts, axis=1).astype(wbuf.dtype)

    wpeer = lambda k: lax.rem(col + k, n_col)
    wsender = lambda k: lax.rem(col + n_col - k, n_col)
    for k in range(1, n_col):
        step(wbuf.at[col], wbuf.at[col], k, device("pcol", wpeer(k)), (send_e, recv_e)).start()
    for k in range(1, n_col):
        pending.append(step(wbuf.at[col], wbuf.at[col], k, device("pcol", wpeer(k)), (send_e, recv_e)))
    for k in range(1, n_col):
        step(wbuf.at[col], wbuf.at[wsender(k)], k, device("pcol", wsender(k)), (send_e, recv_e)).wait_recv()
    width_w = wbuf.shape[2]
    for c in range(n_col):
        out_ref[:, c * width_w:(c + 1) * width_w] = wbuf[c]
    for sent in pending:
        sent.wait_send()


def gram_weighted(x, mode_shapes, axes, sizes):
    n, rows, width = x.shape
    n_col = sizes["pcol"]
    wshape = (n_col, mode_shapes.shape[0], 4 * rows)
    kernel = functools.partial(gram_weighted_kernel, axes=axes, factors=factor_table(sizes))
    return pl.pallas_call(
        kernel,
        out_shape=jax.ShapeDtypeStruct((wshape[1], n_col * wshape[2]), jnp.bfloat16),
        in_specs=[pl.BlockSpec(memory_space=pltpu.VMEM)] * 2,
        out_specs=pl.BlockSpec(memory_space=pltpu.VMEM),
        scratch_shapes=[
            pltpu.VMEM(x.shape, x.dtype),
            pltpu.VMEM((n, 2, rows, width), x.dtype),
            pltpu.VMEM((n, 2, rows, width), x.dtype),
            pltpu.VMEM((rows, width), x.dtype),
            pltpu.VMEM((rows, width), x.dtype),
            pltpu.VMEM(wshape, jnp.bfloat16),
            pltpu.SemaphoreType.DMA((n,)),
            pltpu.SemaphoreType.DMA((n,)),
            pltpu.SemaphoreType.DMA(()),
            pltpu.SemaphoreType.DMA(()),
            pltpu.SemaphoreType.DMA((n,)),
            pltpu.SemaphoreType.DMA((n,)),
            pltpu.SemaphoreType.DMA((n,)),
            pltpu.SemaphoreType.DMA((n,)),
            pltpu.SemaphoreType.DMA((n_col,)),
            pltpu.SemaphoreType.DMA((n_col,)),
        ],
        compiler_params=pltpu.CompilerParams(collective_id=103, has_side_effects=True),
    )(x, mode_shapes)


def fused_sum(x, axes, sizes, over, add_across, kernel_id):
    n, rows, width = x.shape
    block = (rows, width) if add_across else (2, rows, width)
    kernel = functools.partial(
        fused_sum_kernel, axes=axes, factors=factor_table(sizes), over=over, add_across=add_across
    )
    return pl.pallas_call(
        kernel,
        out_shape=jax.ShapeDtypeStruct((n,) + block, x.dtype),
        in_specs=[pl.BlockSpec(memory_space=pltpu.VMEM)],
        out_specs=pl.BlockSpec(memory_space=pltpu.VMEM),
        scratch_shapes=[
            pltpu.VMEM(x.shape, x.dtype),
            pltpu.VMEM((n,) + block, x.dtype),
            pltpu.VMEM((rows, width), x.dtype),
            pltpu.VMEM((rows, width), x.dtype),
            pltpu.SemaphoreType.DMA((n,)),
            pltpu.SemaphoreType.DMA((n,)),
            pltpu.SemaphoreType.DMA(()),
            pltpu.SemaphoreType.DMA(()),
            pltpu.SemaphoreType.DMA((n,)),
            pltpu.SemaphoreType.DMA((n,)),
        ],
        compiler_params=pltpu.CompilerParams(collective_id=kernel_id, has_side_effects=True),
    )(x)


class Exchanger:
    def __init__(self, axes, sizes):
        self.axes, self.factors, self.calls = axes, factor_table(sizes), 0

    def __call__(self, x, group, same):
        count = math.prod(self.factors[f][1] for f in group)
        block = x.shape if same else x.shape[1:]
        if count == 1:
            return x[None] if same else x
        kernel = functools.partial(
            exchange_kernel, axes=self.axes, factors=self.factors, group=group, same=same
        )
        self.calls += 1
        return pl.pallas_call(
            kernel,
            out_shape=jax.ShapeDtypeStruct((count,) + tuple(block), x.dtype),
            in_specs=[pl.BlockSpec(memory_space=pl.ANY)],
            out_specs=pl.BlockSpec(memory_space=pl.ANY),
            scratch_shapes=[
                pltpu.SemaphoreType.DMA((count,)),
                pltpu.SemaphoreType.DMA((count,)),
                pltpu.SemaphoreType.DMA(()),
            ],
            compiler_params=pltpu.CompilerParams(collective_id=self.calls, has_side_effects=True),
        )(x)


def make_body(axes, sizes):
    n_row, n_col, n_pl = sizes["prow"], sizes["pcol"], sizes["pl"]
    swap = [(c * n_col + r, r * n_col + c) for r in range(n_row) for c in range(n_col)]
    sibling = [(r, r ^ 1) for r in range(n_row)]
    n_zh = n_row // 2

    def beside_sibling(part, core):
        other = lax.ppermute(part, "prow", sibling)
        first, second = jnp.where(core == 0, part, other), jnp.where(core == 0, other, part)
        return jnp.concatenate([first, second], axis=0)

    def body(factor_cols, modal_at_loads, mode_shapes, natural_freq, damping):
        ex = Exchanger(axes, sizes)
        in_phase, quadrature = transfer_pair(natural_freq, damping)
        modes = modal_at_loads.shape[0]
        block = modes // (n_row * n_col)
        row, col = lax.axis_index("prow"), lax.axis_index("pcol")
        width = factor_cols.shape[1]
        core = row % 2
        own_modes = lax.dynamic_slice_in_dim(modal_at_loads, core * (modes // 2), modes // 2, 0)
        sib_modes = lax.dynamic_slice_in_dim(modal_at_loads, (1 - core) * (modes // 2), modes // 2, 0)
        mine = jnp.dot(own_modes, factor_cols, preferred_element_type=jnp.float32)
        theirs = jnp.dot(sib_modes, factor_cols, preferred_element_type=jnp.float32)
        modal_load = modal_sum(mine, theirs.astype(jnp.bfloat16), axes, sizes).reshape(modes, width)
        modal_wide = modal_load.astype(jnp.float32)
        pseudo = jnp.concatenate(
            [
                (in_phase[:, None] * modal_wide).astype(jnp.bfloat16),
                (quadrature[:, None] * modal_wide).astype(jnp.bfloat16),
            ],
            axis=1,
        )
        first_row = (col * n_row + row) * block
        own_pseudo = lax.dynamic_slice_in_dim(pseudo, first_row, block, 0)
        partial_gram = outer_rows(own_pseudo, pseudo).astype(jnp.bfloat16)
        chunk = modes // n_pl
        by_chunk = partial_gram.reshape(block, n_pl, chunk).transpose(1, 0, 2)
        half = modes // 2
        send_half = lax.dynamic_slice_in_dim(mode_shapes, (col % 2) * half, half, 1)
        panel_piece = lax.ppermute(send_half, ("prow", "pcol"), swap)
        panel_mine = lax.all_gather(panel_piece, "pl", axis=0, tiled=True)
        weighted = gram_weighted(by_chunk, mode_shapes, axes, sizes)
        panel_mine, weighted = lax.optimization_barrier((panel_mine, weighted))
        panel_other = lax.ppermute(panel_mine, "prow", sibling)
        weighted_mine = lax.dynamic_slice_in_dim(weighted, core * half, half, 1)
        weighted_other = lax.dynamic_slice_in_dim(weighted, (1 - core) * half, half, 1)
        return outer_rows(weighted_other, panel_other) + outer_rows(weighted_mine, panel_mine)

    return body


def solution(mesh):
    in_specs = (
        P(("prow", "pcol"), "pl"),
        P(None, ("prow", "pcol")),
        P(("prow", "pl"), None),
        P(),
        P(),
    )
    out_specs = P(("prow", "pl"), "pcol")
    axes = tuple(mesh.axis_names)
    body = make_body(axes, dict(mesh.shape))
    return jax.shard_map(body, mesh=mesh, in_specs=in_specs, out_specs=out_specs, check_vma=False)
```

```python
import functools
import math

import jax
import jax.numpy as jnp
from jax import lax
from jax.experimental import pallas as pl
from jax.experimental.pallas import tpu as pltpu
from jax.sharding import PartitionSpec as P

MESH = pl.DeviceIdType.MESH


def transfer_pair(natural_freq, damping):
    detuning = natural_freq * natural_freq - 1.0
    damper = 2.0 * damping * natural_freq
    modulus = detuning * detuning + damper * damper
    return (detuning / modulus, -damper / modulus)


def outer_rows(left_rows, right_rows):
    return lax.dot_general(
        left_rows, right_rows, (((1,), (1,)), ((), ())), preferred_element_type=jnp.float32
    )


def factor_table(sizes):
    return {
        "zh": ("prow", sizes["prow"] // 2, 2),
        "core": ("prow", 2, 1),
        "pcol": ("pcol", sizes["pcol"], 1),
        "pl": ("pl", sizes["pl"], 1),
    }


def exchange_kernel(x_ref, out_ref, send_sem, recv_sem, local_sem, *, axes, factors, group, same):
    coords = {a: lax.axis_index(a) for a in axes}

    def value(f):
        axis, size, stride = factors[f]
        return lax.rem(coords[axis] // stride, size)

    count = math.prod(factors[f][1] for f in group)
    me = 0
    for f in group:
        me = me * factors[f][1] + value(f)

    def device(member):
        place = dict(coords)
        for f in reversed(group):
            axis, size, stride = factors[f]
            place[axis] = place[axis] + (lax.rem(member, size) - value(f)) * stride
            member = member // size
        return tuple(place[a] for a in axes)

    def source(member):
        return x_ref if same else x_ref.at[member]

    def copy(offset):
        peer = lax.rem(me + offset, count)
        return pltpu.make_async_remote_copy(
            src_ref=source(peer),
            dst_ref=out_ref.at[me],
            send_sem=send_sem.at[offset],
            recv_sem=recv_sem.at[offset],
            device_id=device(peer),
            device_id_type=MESH,
        )

    def landing(offset):
        sender = lax.rem(me + count - offset, count)
        return pltpu.make_async_remote_copy(
            src_ref=source(me),
            dst_ref=out_ref.at[sender],
            send_sem=send_sem.at[offset],
            recv_sem=recv_sem.at[offset],
            device_id=device(sender),
            device_id_type=MESH,
        )

    local = pltpu.make_async_copy(source(me), out_ref.at[me], local_sem)
    local.start()
    barrier = pltpu.get_barrier_semaphore()
    for offset in range(1, count):
        peer = lax.rem(me + offset, count)
        pl.semaphore_signal(barrier, inc=1, device_id=device(peer), device_id_type=MESH)
    pl.semaphore_wait(barrier, count - 1)
    for offset in range(1, count):
        copy(offset).start()
    local.wait()
    for offset in range(1, count):
        copy(offset).wait_send()
    for offset in range(1, count):
        landing(offset).wait_recv()


def fused_sum_kernel(x_ref, out_ref, got, coll, part_out, part_in, send_a, recv_a, send_b, recv_b,
                     send_c, recv_c, *, axes, factors, over, add_across):
    coords = {a: lax.axis_index(a) for a in axes}

    def value(f):
        axis, size, stride = factors[f]
        return lax.rem(coords[axis] // stride, size)

    def device(f, v):
        place = dict(coords)
        axis, size, stride = factors[f]
        place[axis] = place[axis] + (v - value(f)) * stride
        return tuple(place[a] for a in axes)

    n = factors[over][1]
    me, half = value(over), value("zh")
    partner = device("zh", 1 - half)
    peer = lambda k: lax.rem(me + k, n)
    sender = lambda k: lax.rem(me + n - k, n)

    def step(src, dst_at, k, to, sems):
        return pltpu.make_async_remote_copy(
            src_ref=src, dst_ref=dst_at, send_sem=sems[0].at[k], recv_sem=sems[1].at[k],
            device_id=to, device_id_type=MESH,
        )

    barrier = pltpu.get_barrier_semaphore()
    for k in range(1, n):
        pl.semaphore_signal(barrier, inc=1, device_id=device(over, peer(k)), device_id_type=MESH)
    pl.semaphore_signal(barrier, inc=1, device_id=partner, device_id_type=MESH)
    pl.semaphore_wait(barrier, n)

    for k in range(1, n):
        step(x_ref.at[peer(k)], got.at[me], k, device(over, peer(k)), (send_a, recv_a)).start()
    for k in range(1, n):
        step(x_ref.at[peer(k)], got.at[me], k, device(over, peer(k)), (send_a, recv_a)).wait_send()
    for k in range(1, n):
        step(x_ref.at[me], got.at[sender(k)], k, device(over, sender(k)), (send_a, recv_a)).wait_recv()
    total = x_ref[me].astype(jnp.float32)
    for k in range(1, n):
        total = total + got[sender(k)].astype(jnp.float32)
    part_out[...] = total.astype(part_out.dtype)

    across = pltpu.make_async_remote_copy(
        src_ref=part_out, dst_ref=part_in, send_sem=send_b, recv_sem=recv_b,
        device_id=partner, device_id_type=MESH,
    )
    across.start()
    across.wait_send()
    across.wait_recv()
    if add_across:
        mine, theirs = part_out[...].astype(jnp.float32), part_in[...].astype(jnp.float32)
        coll[me] = (mine + theirs).astype(coll.dtype)
    else:
        mine, theirs = part_out[...], part_in[...]
        first = jnp.where(half == 0, mine, theirs)
        second = jnp.where(half == 0, theirs, mine)
        coll[me] = jnp.stack([first, second])

    for k in range(1, n):
        step(coll.at[me], coll.at[me], k, device(over, peer(k)), (send_c, recv_c)).start()
    for k in range(1, n):
        step(coll.at[me], coll.at[me], k, device(over, peer(k)), (send_c, recv_c)).wait_send()
    for k in range(1, n):
        step(coll.at[me], coll.at[sender(k)], k, device(over, sender(k)), (send_c, recv_c)).wait_recv()
    out_ref[...] = coll[...]


def modal_sum_kernel(mine_ref, theirs_ref, out_ref, sib_in, pieces, got, coll, part_out, part_in,
                     sib_out, send_s, recv_s, send_a, recv_a, send_b, recv_b, send_c, recv_c,
                     send_d, recv_d, *, axes, factors):
    coords = {a: lax.axis_index(a) for a in axes}

    def value(f):
        axis, size, stride = factors[f]
        return lax.rem(coords[axis] // stride, size)

    def device(f, v):
        place = dict(coords)
        axis, size, stride = factors[f]
        place[axis] = place[axis] + (v - value(f)) * stride
        return tuple(place[a] for a in axes)

    n = factors["pcol"][1]
    me, half, core = value("pcol"), value("zh"), value("core")
    partner, sibling = device("zh", 1 - half), device("core", 1 - core)
    peer = lambda k: lax.rem(me + k, n)
    sender = lambda k: lax.rem(me + n - k, n)

    def step(src, dst_at, k, to, sems):
        return pltpu.make_async_remote_copy(
            src_ref=src, dst_ref=dst_at, send_sem=sems[0].at[k], recv_sem=sems[1].at[k],
            device_id=to, device_id_type=MESH,
        )

    def one(src, dst, to, send_sem, recv_sem):
        return pltpu.make_async_remote_copy(
            src_ref=src, dst_ref=dst, send_sem=send_sem, recv_sem=recv_sem,
            device_id=to, device_id_type=MESH,
        )

    pending = []
    barrier = pltpu.get_barrier_semaphore()
    for k in range(1, n):
        pl.semaphore_signal(barrier, inc=1, device_id=device("pcol", peer(k)), device_id_type=MESH)
    pl.semaphore_signal(barrier, inc=1, device_id=partner, device_id_type=MESH)
    pl.semaphore_signal(barrier, inc=1, device_id=sibling, device_id_type=MESH)
    pl.semaphore_wait(barrier, n + 1)

    chip = one(theirs_ref, sib_in, sibling, send_s, recv_s)
    chip.start()
    pending.append(chip)
    chip.wait_recv()
    summed = mine_ref[...] + sib_in[...].astype(jnp.float32)
    pieces[...] = summed.astype(pieces.dtype).reshape(pieces.shape)

    for k in range(1, n):
        step(pieces.at[peer(k)], got.at[me], k, device("pcol", peer(k)), (send_a, recv_a)).start()
    for k in range(1, n):
        pending.append(step(pieces.at[peer(k)], got.at[me], k, device("pcol", peer(k)), (send_a, recv_a)))
    for k in range(1, n):
        step(pieces.at[me], got.at[sender(k)], k, device("pcol", sender(k)), (send_a, recv_a)).wait_recv()
    total = pieces[me].astype(jnp.float32)
    for k in range(1, n):
        total = total + got[sender(k)].astype(jnp.float32)
    part_out[...] = total.astype(part_out.dtype)

    across = one(part_out, part_in, partner, send_b, recv_b)
    across.start()
    pending.append(across)
    across.wait_recv()
    coll[me] = (part_out[...].astype(jnp.float32) + part_in[...].astype(jnp.float32)).astype(coll.dtype)

    for k in range(1, n):
        step(coll.at[me], coll.at[me], k, device("pcol", peer(k)), (send_c, recv_c)).start()
    for k in range(1, n):
        pending.append(step(coll.at[me], coll.at[me], k, device("pcol", peer(k)), (send_c, recv_c)))

    def to_sibling(piece):
        return pltpu.make_async_remote_copy(
            src_ref=coll.at[piece], dst_ref=sib_out.at[piece], send_sem=send_d.at[piece],
            recv_sem=recv_d.at[piece], device_id=sibling, device_id_type=MESH,
        )

    to_sibling(me).start()
    pending.append(to_sibling(me))
    for k in range(1, n):
        step(coll.at[me], coll.at[sender(k)], k, device("pcol", sender(k)), (send_c, recv_c)).wait_recv()
        to_sibling(sender(k)).start()
        pending.append(to_sibling(sender(k)))
    for piece in range(n):
        to_sibling(piece).wait_recv()
    out_ref[core] = coll[...]
    out_ref[1 - core] = sib_out[...]
    for sent in pending:
        sent.wait_send()


def modal_sum(mine, theirs, axes, sizes):
    n = sizes["pcol"]
    rows, width = mine.shape
    block = (n, rows // n, width)
    kernel = functools.partial(modal_sum_kernel, axes=axes, factors=factor_table(sizes))
    return pl.pallas_call(
        kernel,
        out_shape=jax.ShapeDtypeStruct((2,) + block, jnp.bfloat16),
        in_specs=[pl.BlockSpec(memory_space=pltpu.VMEM)] * 2,
        out_specs=pl.BlockSpec(memory_space=pltpu.VMEM),
        scratch_shapes=[
            pltpu.VMEM((rows, width), jnp.bfloat16),
            pltpu.VMEM(block, jnp.bfloat16),
            pltpu.VMEM(block, jnp.bfloat16),
            pltpu.VMEM(block, jnp.bfloat16),
            pltpu.VMEM(block[1:], jnp.bfloat16),
            pltpu.VMEM(block[1:], jnp.bfloat16),
            pltpu.VMEM(block, jnp.bfloat16),
            pltpu.SemaphoreType.DMA(()),
            pltpu.SemaphoreType.DMA(()),
            pltpu.SemaphoreType.DMA((n,)),
            pltpu.SemaphoreType.DMA((n,)),
            pltpu.SemaphoreType.DMA(()),
            pltpu.SemaphoreType.DMA(()),
            pltpu.SemaphoreType.DMA((n,)),
            pltpu.SemaphoreType.DMA((n,)),
            pltpu.SemaphoreType.DMA((n,)),
            pltpu.SemaphoreType.DMA((n,)),
        ],
        compiler_params=pltpu.CompilerParams(collective_id=102, has_side_effects=True),
    )(mine, theirs)


def gram_weighted_kernel(x_ref, shapes_ref, out_ref, got, coll, sib_coll, part_out, part_in, wbuf,
                         send_a, recv_a, send_b, recv_b, send_c, recv_c, send_d, recv_d, send_e,
                         recv_e, *, axes, factors):
    coords = {a: lax.axis_index(a) for a in axes}

    def value(f):
        axis, size, stride = factors[f]
        return lax.rem(coords[axis] // stride, size)

    def device(f, v):
        place = dict(coords)
        axis, size, stride = factors[f]
        place[axis] = place[axis] + (v - value(f)) * stride
        return tuple(place[a] for a in axes)

    n, n_col = factors["pl"][1], factors["pcol"][1]
    me, half, core, col = value("pl"), value("zh"), value("core"), value("pcol")
    partner, sibling = device("zh", 1 - half), device("core", 1 - core)

    def step(src, dst_at, k, to, sems):
        return pltpu.make_async_remote_copy(
            src_ref=src, dst_ref=dst_at, send_sem=sems[0].at[k], recv_sem=sems[1].at[k],
            device_id=to, device_id_type=MESH,
        )

    def one(src, dst, to, send_sem, recv_sem):
        return pltpu.make_async_remote_copy(
            src_ref=src, dst_ref=dst, send_sem=send_sem, recv_sem=recv_sem,
            device_id=to, device_id_type=MESH,
        )

    pending = []
    barrier = pltpu.get_barrier_semaphore()
    for k in range(1, n):
        pl.semaphore_signal(barrier, inc=1, device_id=device("pl", lax.rem(me + k, n)), device_id_type=MESH)
    for k in range(1, n_col):
        pl.semaphore_signal(
            barrier, inc=1, device_id=device("pcol", lax.rem(col + k, n_col)), device_id_type=MESH
        )
    pl.semaphore_signal(barrier, inc=1, device_id=partner, device_id_type=MESH)
    pl.semaphore_signal(barrier, inc=1, device_id=sibling, device_id_type=MESH)
    pl.semaphore_wait(barrier, n + n_col)

    peer = lambda k: lax.rem(me + k, n)
    sender = lambda k: lax.rem(me + n - k, n)
    for k in range(1, n):
        step(x_ref.at[peer(k)], got.at[me], k, device("pl", peer(k)), (send_a, recv_a)).start()
    for k in range(1, n):
        pending.append(step(x_ref.at[peer(k)], got.at[me], k, device("pl", peer(k)), (send_a, recv_a)))
    for k in range(1, n):
        step(x_ref.at[me], got.at[sender(k)], k, device("pl", sender(k)), (send_a, recv_a)).wait_recv()
    total = x_ref[me].astype(jnp.float32)
    for k in range(1, n):
        total = total + got[sender(k)].astype(jnp.float32)
    part_out[...] = total.astype(part_out.dtype)

    across = one(part_out, part_in, partner, send_b, recv_b)
    across.start()
    pending.append(across)
    across.wait_recv()
    mine, theirs = part_out[...], part_in[...]
    coll[me] = jnp.stack([jnp.where(half == 0, mine, theirs), jnp.where(half == 0, theirs, mine)])

    for k in range(1, n):
        step(coll.at[me], coll.at[me], k, device("pl", peer(k)), (send_c, recv_c)).start()
    for k in range(1, n):
        pending.append(step(coll.at[me], coll.at[me], k, device("pl", peer(k)), (send_c, recv_c)))

    def to_sibling(chunk_at):
        return pltpu.make_async_remote_copy(
            src_ref=coll.at[chunk_at], dst_ref=sib_coll.at[chunk_at], send_sem=send_d.at[chunk_at],
            recv_sem=recv_d.at[chunk_at], device_id=sibling, device_id_type=MESH,
        )

    to_sibling(me).start()
    pending.append(to_sibling(me))
    for k in range(1, n):
        step(coll.at[me], coll.at[sender(k)], k, device("pl", sender(k)), (send_c, recv_c)).wait_recv()
        to_sibling(sender(k)).start()
        pending.append(to_sibling(sender(k)))

    chunk = coll.shape[-1]

    def weighted_block(blocks, h):
        acc = jnp.zeros((shapes_ref.shape[0], blocks.shape[2]), jnp.float32)
        for l in range(n):
            acc = acc + lax.dot_general(
                shapes_ref[:, l * chunk:(l + 1) * chunk], blocks[l, h],
                (((1,), (1,)), ((), ())), preferred_element_type=jnp.float32,
            )
        return acc

    own = [weighted_block(coll, h) for h in range(2)]
    for l in range(n):
        to_sibling(l).wait_recv()
    other = [weighted_block(sib_coll, h) for h in range(2)]
    parts = []
    for h in range(2):
        parts += [jnp.where(core == 0, own[h], other[h]), jnp.where(core == 0, other[h], own[h])]
    wbuf[col] = jnp.concatenate(parts, axis=1).astype(wbuf.dtype)

    wpeer = lambda k: lax.rem(col + k, n_col)
    wsender = lambda k: lax.rem(col + n_col - k, n_col)
    for k in range(1, n_col):
        step(wbuf.at[col], wbuf.at[col], k, device("pcol", wpeer(k)), (send_e, recv_e)).start()
    for k in range(1, n_col):
        pending.append(step(wbuf.at[col], wbuf.at[col], k, device("pcol", wpeer(k)), (send_e, recv_e)))
    for k in range(1, n_col):
        step(wbuf.at[col], wbuf.at[wsender(k)], k, device("pcol", wsender(k)), (send_e, recv_e)).wait_recv()
    width_w = wbuf.shape[2]
    for c in range(n_col):
        out_ref[:, c * width_w:(c + 1) * width_w] = wbuf[c]
    for sent in pending:
        sent.wait_send()


def gram_weighted(x, mode_shapes, axes, sizes):
    n, rows, width = x.shape
    n_col = sizes["pcol"]
    wshape = (n_col, mode_shapes.shape[0], 4 * rows)
    kernel = functools.partial(gram_weighted_kernel, axes=axes, factors=factor_table(sizes))
    return pl.pallas_call(
        kernel,
        out_shape=jax.ShapeDtypeStruct((wshape[1], n_col * wshape[2]), jnp.bfloat16),
        in_specs=[pl.BlockSpec(memory_space=pltpu.VMEM)] * 2,
        out_specs=pl.BlockSpec(memory_space=pltpu.VMEM),
        scratch_shapes=[
            pltpu.VMEM(x.shape, x.dtype),
            pltpu.VMEM((n, 2, rows, width), x.dtype),
            pltpu.VMEM((n, 2, rows, width), x.dtype),
            pltpu.VMEM((rows, width), x.dtype),
            pltpu.VMEM((rows, width), x.dtype),
            pltpu.VMEM(wshape, jnp.bfloat16),
            pltpu.SemaphoreType.DMA((n,)),
            pltpu.SemaphoreType.DMA((n,)),
            pltpu.SemaphoreType.DMA(()),
            pltpu.SemaphoreType.DMA(()),
            pltpu.SemaphoreType.DMA((n,)),
            pltpu.SemaphoreType.DMA((n,)),
            pltpu.SemaphoreType.DMA((n,)),
            pltpu.SemaphoreType.DMA((n,)),
            pltpu.SemaphoreType.DMA((n_col,)),
            pltpu.SemaphoreType.DMA((n_col,)),
        ],
        compiler_params=pltpu.CompilerParams(collective_id=103, has_side_effects=True),
    )(x, mode_shapes)


def fused_sum(x, axes, sizes, over, add_across, kernel_id):
    n, rows, width = x.shape
    block = (rows, width) if add_across else (2, rows, width)
    kernel = functools.partial(
        fused_sum_kernel, axes=axes, factors=factor_table(sizes), over=over, add_across=add_across
    )
    return pl.pallas_call(
        kernel,
        out_shape=jax.ShapeDtypeStruct((n,) + block, x.dtype),
        in_specs=[pl.BlockSpec(memory_space=pltpu.VMEM)],
        out_specs=pl.BlockSpec(memory_space=pltpu.VMEM),
        scratch_shapes=[
            pltpu.VMEM(x.shape, x.dtype),
            pltpu.VMEM((n,) + block, x.dtype),
            pltpu.VMEM((rows, width), x.dtype),
            pltpu.VMEM((rows, width), x.dtype),
            pltpu.SemaphoreType.DMA((n,)),
            pltpu.SemaphoreType.DMA((n,)),
            pltpu.SemaphoreType.DMA(()),
            pltpu.SemaphoreType.DMA(()),
            pltpu.SemaphoreType.DMA((n,)),
            pltpu.SemaphoreType.DMA((n,)),
        ],
        compiler_params=pltpu.CompilerParams(collective_id=kernel_id, has_side_effects=True),
    )(x)


class Exchanger:
    def __init__(self, axes, sizes):
        self.axes, self.factors, self.calls = axes, factor_table(sizes), 0

    def __call__(self, x, group, same):
        count = math.prod(self.factors[f][1] for f in group)
        block = x.shape if same else x.shape[1:]
        if count == 1:
            return x[None] if same else x
        kernel = functools.partial(
            exchange_kernel, axes=self.axes, factors=self.factors, group=group, same=same
        )
        self.calls += 1
        return pl.pallas_call(
            kernel,
            out_shape=jax.ShapeDtypeStruct((count,) + tuple(block), x.dtype),
            in_specs=[pl.BlockSpec(memory_space=pl.ANY)],
            out_specs=pl.BlockSpec(memory_space=pl.ANY),
            scratch_shapes=[
                pltpu.SemaphoreType.DMA((count,)),
                pltpu.SemaphoreType.DMA((count,)),
                pltpu.SemaphoreType.DMA(()),
            ],
            compiler_params=pltpu.CompilerParams(collective_id=self.calls, has_side_effects=True),
        )(x)


def make_body(axes, sizes):
    n_row, n_col, n_pl = sizes["prow"], sizes["pcol"], sizes["pl"]
    swap = [(c * n_col + r, r * n_col + c) for r in range(n_row) for c in range(n_col)]
    sibling = [(r, r ^ 1) for r in range(n_row)]
    n_zh = n_row // 2

    def beside_sibling(part, core):
        other = lax.ppermute(part, "prow", sibling)
        first, second = jnp.where(core == 0, part, other), jnp.where(core == 0, other, part)
        return jnp.concatenate([first, second], axis=0)

    def body(factor_cols, modal_at_loads, mode_shapes, natural_freq, damping):
        ex = Exchanger(axes, sizes)
        in_phase, quadrature = transfer_pair(natural_freq, damping)
        modes = modal_at_loads.shape[0]
        block = modes // (n_row * n_col)
        row, col = lax.axis_index("prow"), lax.axis_index("pcol")
        width = factor_cols.shape[1]
        core = row % 2
        own_modes = lax.dynamic_slice_in_dim(modal_at_loads, core * (modes // 2), modes // 2, 0)
        sib_modes = lax.dynamic_slice_in_dim(modal_at_loads, (1 - core) * (modes // 2), modes // 2, 0)
        mine = jnp.dot(own_modes, factor_cols, preferred_element_type=jnp.float32)
        theirs = jnp.dot(sib_modes, factor_cols, preferred_element_type=jnp.float32)
        modal_load = modal_sum(mine, theirs.astype(jnp.bfloat16), axes, sizes).reshape(modes, width)
        modal_wide = modal_load.astype(jnp.float32)
        pseudo = jnp.concatenate(
            [
                (in_phase[:, None] * modal_wide).astype(jnp.bfloat16),
                (quadrature[:, None] * modal_wide).astype(jnp.bfloat16),
            ],
            axis=1,
        )
        first_row = (col * n_row + row) * block
        own_pseudo = lax.dynamic_slice_in_dim(pseudo, first_row, block, 0)
        partial_gram = outer_rows(own_pseudo, pseudo).astype(jnp.bfloat16)
        chunk = modes // n_pl
        by_chunk = partial_gram.reshape(block, n_pl, chunk).transpose(1, 0, 2)
        half = modes // 2
        send_half = lax.dynamic_slice_in_dim(mode_shapes, (col % 2) * half, half, 1)
        panel_piece = lax.ppermute(send_half, ("prow", "pcol"), swap)
        panel_mine = lax.all_gather(panel_piece, "pl", axis=0, tiled=True)
        weighted = gram_weighted(by_chunk, mode_shapes, axes, sizes)
        panel_mine, weighted = lax.optimization_barrier((panel_mine, weighted))
        panel_other = lax.ppermute(panel_mine, "prow", sibling)
        weighted_mine = lax.dynamic_slice_in_dim(weighted, core * half, half, 1)
        weighted_other = lax.dynamic_slice_in_dim(weighted, (1 - core) * half, half, 1)
        return outer_rows(weighted_other, panel_other) + outer_rows(weighted_mine, panel_mine)

    return body


def solution(mesh):
    in_specs = (
        P(("prow", "pcol"), "pl"),
        P(None, ("prow", "pcol")),
        P(("prow", "pl"), None),
        P(),
        P(),
    )
    out_specs = P(("prow", "pl"), "pcol")
    axes = tuple(mesh.axis_names)
    body = make_body(axes, dict(mesh.shape))
    return jax.shard_map(body, mesh=mesh, in_specs=in_specs, out_specs=out_specs, check_vma=False)
```

```python
import functools
import math

import jax
import jax.numpy as jnp
from jax import lax
from jax.experimental import pallas as pl
from jax.experimental.pallas import tpu as pltpu
from jax.sharding import PartitionSpec as P

MESH = pl.DeviceIdType.MESH


def transfer_pair(natural_freq, damping):
    detuning = natural_freq * natural_freq - 1.0
    damper = 2.0 * damping * natural_freq
    modulus = detuning * detuning + damper * damper
    return (detuning / modulus, -damper / modulus)


def outer_rows(left_rows, right_rows):
    return lax.dot_general(
        left_rows, right_rows, (((1,), (1,)), ((), ())), preferred_element_type=jnp.float32
    )


def factor_table(sizes):
    return {
        "zh": ("prow", sizes["prow"] // 2, 2),
        "core": ("prow", 2, 1),
        "pcol": ("pcol", sizes["pcol"], 1),
        "pl": ("pl", sizes["pl"], 1),
    }


def exchange_kernel(x_ref, out_ref, send_sem, recv_sem, local_sem, *, axes, factors, group, same):
    coords = {a: lax.axis_index(a) for a in axes}

    def value(f):
        axis, size, stride = factors[f]
        return lax.rem(coords[axis] // stride, size)

    count = math.prod(factors[f][1] for f in group)
    me = 0
    for f in group:
        me = me * factors[f][1] + value(f)

    def device(member):
        place = dict(coords)
        for f in reversed(group):
            axis, size, stride = factors[f]
            place[axis] = place[axis] + (lax.rem(member, size) - value(f)) * stride
            member = member // size
        return tuple(place[a] for a in axes)

    def source(member):
        return x_ref if same else x_ref.at[member]

    def copy(offset):
        peer = lax.rem(me + offset, count)
        return pltpu.make_async_remote_copy(
            src_ref=source(peer),
            dst_ref=out_ref.at[me],
            send_sem=send_sem.at[offset],
            recv_sem=recv_sem.at[offset],
            device_id=device(peer),
            device_id_type=MESH,
        )

    def landing(offset):
        sender = lax.rem(me + count - offset, count)
        return pltpu.make_async_remote_copy(
            src_ref=source(me),
            dst_ref=out_ref.at[sender],
            send_sem=send_sem.at[offset],
            recv_sem=recv_sem.at[offset],
            device_id=device(sender),
            device_id_type=MESH,
        )

    local = pltpu.make_async_copy(source(me), out_ref.at[me], local_sem)
    local.start()
    barrier = pltpu.get_barrier_semaphore()
    for offset in range(1, count):
        peer = lax.rem(me + offset, count)
        pl.semaphore_signal(barrier, inc=1, device_id=device(peer), device_id_type=MESH)
    pl.semaphore_wait(barrier, count - 1)
    for offset in range(1, count):
        copy(offset).start()
    local.wait()
    for offset in range(1, count):
        copy(offset).wait_send()
    for offset in range(1, count):
        landing(offset).wait_recv()


def fused_sum_kernel(x_ref, out_ref, got, coll, part_out, part_in, send_a, recv_a, send_b, recv_b,
                     send_c, recv_c, *, axes, factors, over, add_across):
    coords = {a: lax.axis_index(a) for a in axes}

    def value(f):
        axis, size, stride = factors[f]
        return lax.rem(coords[axis] // stride, size)

    def device(f, v):
        place = dict(coords)
        axis, size, stride = factors[f]
        place[axis] = place[axis] + (v - value(f)) * stride
        return tuple(place[a] for a in axes)

    n = factors[over][1]
    me, half = value(over), value("zh")
    partner = device("zh", 1 - half)
    peer = lambda k: lax.rem(me + k, n)
    sender = lambda k: lax.rem(me + n - k, n)

    def step(src, dst_at, k, to, sems):
        return pltpu.make_async_remote_copy(
            src_ref=src, dst_ref=dst_at, send_sem=sems[0].at[k], recv_sem=sems[1].at[k],
            device_id=to, device_id_type=MESH,
        )

    barrier = pltpu.get_barrier_semaphore()
    for k in range(1, n):
        pl.semaphore_signal(barrier, inc=1, device_id=device(over, peer(k)), device_id_type=MESH)
    pl.semaphore_signal(barrier, inc=1, device_id=partner, device_id_type=MESH)
    pl.semaphore_wait(barrier, n)

    for k in range(1, n):
        step(x_ref.at[peer(k)], got.at[me], k, device(over, peer(k)), (send_a, recv_a)).start()
    for k in range(1, n):
        step(x_ref.at[peer(k)], got.at[me], k, device(over, peer(k)), (send_a, recv_a)).wait_send()
    for k in range(1, n):
        step(x_ref.at[me], got.at[sender(k)], k, device(over, sender(k)), (send_a, recv_a)).wait_recv()
    total = x_ref[me].astype(jnp.float32)
    for k in range(1, n):
        total = total + got[sender(k)].astype(jnp.float32)
    part_out[...] = total.astype(part_out.dtype)

    across = pltpu.make_async_remote_copy(
        src_ref=part_out, dst_ref=part_in, send_sem=send_b, recv_sem=recv_b,
        device_id=partner, device_id_type=MESH,
    )
    across.start()
    across.wait_send()
    across.wait_recv()
    if add_across:
        mine, theirs = part_out[...].astype(jnp.float32), part_in[...].astype(jnp.float32)
        coll[me] = (mine + theirs).astype(coll.dtype)
    else:
        mine, theirs = part_out[...], part_in[...]
        first = jnp.where(half == 0, mine, theirs)
        second = jnp.where(half == 0, theirs, mine)
        coll[me] = jnp.stack([first, second])

    for k in range(1, n):
        step(coll.at[me], coll.at[me], k, device(over, peer(k)), (send_c, recv_c)).start()
    for k in range(1, n):
        step(coll.at[me], coll.at[me], k, device(over, peer(k)), (send_c, recv_c)).wait_send()
    for k in range(1, n):
        step(coll.at[me], coll.at[sender(k)], k, device(over, sender(k)), (send_c, recv_c)).wait_recv()
    out_ref[...] = coll[...]


def modal_sum_kernel(mine_ref, theirs_ref, out_ref, sib_in, pieces, got, coll, part_out, part_in,
                     sib_out, send_s, recv_s, send_a, recv_a, send_b, recv_b, send_c, recv_c,
                     send_d, recv_d, *, axes, factors):
    coords = {a: lax.axis_index(a) for a in axes}

    def value(f):
        axis, size, stride = factors[f]
        return lax.rem(coords[axis] // stride, size)

    def device(f, v):
        place = dict(coords)
        axis, size, stride = factors[f]
        place[axis] = place[axis] + (v - value(f)) * stride
        return tuple(place[a] for a in axes)

    n = factors["pcol"][1]
    me, half, core = value("pcol"), value("zh"), value("core")
    partner, sibling = device("zh", 1 - half), device("core", 1 - core)
    peer = lambda k: lax.rem(me + k, n)
    sender = lambda k: lax.rem(me + n - k, n)

    def step(src, dst_at, k, to, sems):
        return pltpu.make_async_remote_copy(
            src_ref=src, dst_ref=dst_at, send_sem=sems[0].at[k], recv_sem=sems[1].at[k],
            device_id=to, device_id_type=MESH,
        )

    def one(src, dst, to, send_sem, recv_sem):
        return pltpu.make_async_remote_copy(
            src_ref=src, dst_ref=dst, send_sem=send_sem, recv_sem=recv_sem,
            device_id=to, device_id_type=MESH,
        )

    pending = []
    barrier = pltpu.get_barrier_semaphore()
    for k in range(1, n):
        pl.semaphore_signal(barrier, inc=1, device_id=device("pcol", peer(k)), device_id_type=MESH)
    pl.semaphore_signal(barrier, inc=1, device_id=partner, device_id_type=MESH)
    pl.semaphore_signal(barrier, inc=1, device_id=sibling, device_id_type=MESH)
    pl.semaphore_wait(barrier, n + 1)

    chip = one(theirs_ref, sib_in, sibling, send_s, recv_s)
    chip.start()
    pending.append(chip)
    chip.wait_recv()
    summed = mine_ref[...] + sib_in[...].astype(jnp.float32)
    pieces[...] = summed.astype(pieces.dtype).reshape(pieces.shape)

    for k in range(1, n):
        step(pieces.at[peer(k)], got.at[me], k, device("pcol", peer(k)), (send_a, recv_a)).start()
    for k in range(1, n):
        pending.append(step(pieces.at[peer(k)], got.at[me], k, device("pcol", peer(k)), (send_a, recv_a)))
    for k in range(1, n):
        step(pieces.at[me], got.at[sender(k)], k, device("pcol", sender(k)), (send_a, recv_a)).wait_recv()
    total = pieces[me].astype(jnp.float32)
    for k in range(1, n):
        total = total + got[sender(k)].astype(jnp.float32)
    part_out[...] = total.astype(part_out.dtype)

    across = one(part_out, part_in, partner, send_b, recv_b)
    across.start()
    pending.append(across)
    across.wait_recv()
    coll[me] = (part_out[...].astype(jnp.float32) + part_in[...].astype(jnp.float32)).astype(coll.dtype)

    for k in range(1, n):
        step(coll.at[me], coll.at[me], k, device("pcol", peer(k)), (send_c, recv_c)).start()
    for k in range(1, n):
        pending.append(step(coll.at[me], coll.at[me], k, device("pcol", peer(k)), (send_c, recv_c)))
    for k in range(1, n):
        step(coll.at[me], coll.at[sender(k)], k, device("pcol", sender(k)), (send_c, recv_c)).wait_recv()

    join = one(coll, sib_out, sibling, send_d, recv_d)
    join.start()
    pending.append(join)
    join.wait_recv()
    out_ref[core] = coll[...]
    out_ref[1 - core] = sib_out[...]
    for sent in pending:
        sent.wait_send()


def modal_sum(mine, theirs, axes, sizes):
    n = sizes["pcol"]
    rows, width = mine.shape
    block = (n, rows // n, width)
    kernel = functools.partial(modal_sum_kernel, axes=axes, factors=factor_table(sizes))
    return pl.pallas_call(
        kernel,
        out_shape=jax.ShapeDtypeStruct((2,) + block, jnp.bfloat16),
        in_specs=[pl.BlockSpec(memory_space=pltpu.VMEM)] * 2,
        out_specs=pl.BlockSpec(memory_space=pltpu.VMEM),
        scratch_shapes=[
            pltpu.VMEM((rows, width), jnp.bfloat16),
            pltpu.VMEM(block, jnp.bfloat16),
            pltpu.VMEM(block, jnp.bfloat16),
            pltpu.VMEM(block, jnp.bfloat16),
            pltpu.VMEM(block[1:], jnp.bfloat16),
            pltpu.VMEM(block[1:], jnp.bfloat16),
            pltpu.VMEM(block, jnp.bfloat16),
            pltpu.SemaphoreType.DMA(()),
            pltpu.SemaphoreType.DMA(()),
            pltpu.SemaphoreType.DMA((n,)),
            pltpu.SemaphoreType.DMA((n,)),
            pltpu.SemaphoreType.DMA(()),
            pltpu.SemaphoreType.DMA(()),
            pltpu.SemaphoreType.DMA((n,)),
            pltpu.SemaphoreType.DMA((n,)),
            pltpu.SemaphoreType.DMA(()),
            pltpu.SemaphoreType.DMA(()),
        ],
        compiler_params=pltpu.CompilerParams(collective_id=102, has_side_effects=True),
    )(mine, theirs)


def gram_weighted_kernel(x_ref, shapes_ref, out_ref, got, coll, sib_coll, part_out, part_in, wbuf,
                         send_a, recv_a, send_b, recv_b, send_c, recv_c, send_d, recv_d, send_e,
                         recv_e, *, axes, factors):
    coords = {a: lax.axis_index(a) for a in axes}

    def value(f):
        axis, size, stride = factors[f]
        return lax.rem(coords[axis] // stride, size)

    def device(f, v):
        place = dict(coords)
        axis, size, stride = factors[f]
        place[axis] = place[axis] + (v - value(f)) * stride
        return tuple(place[a] for a in axes)

    n, n_col = factors["pl"][1], factors["pcol"][1]
    me, half, core, col = value("pl"), value("zh"), value("core"), value("pcol")
    partner, sibling = device("zh", 1 - half), device("core", 1 - core)

    def step(src, dst_at, k, to, sems):
        return pltpu.make_async_remote_copy(
            src_ref=src, dst_ref=dst_at, send_sem=sems[0].at[k], recv_sem=sems[1].at[k],
            device_id=to, device_id_type=MESH,
        )

    def one(src, dst, to, send_sem, recv_sem):
        return pltpu.make_async_remote_copy(
            src_ref=src, dst_ref=dst, send_sem=send_sem, recv_sem=recv_sem,
            device_id=to, device_id_type=MESH,
        )

    pending = []
    barrier = pltpu.get_barrier_semaphore()
    for k in range(1, n):
        pl.semaphore_signal(barrier, inc=1, device_id=device("pl", lax.rem(me + k, n)), device_id_type=MESH)
    for k in range(1, n_col):
        pl.semaphore_signal(
            barrier, inc=1, device_id=device("pcol", lax.rem(col + k, n_col)), device_id_type=MESH
        )
    pl.semaphore_signal(barrier, inc=1, device_id=partner, device_id_type=MESH)
    pl.semaphore_signal(barrier, inc=1, device_id=sibling, device_id_type=MESH)
    pl.semaphore_wait(barrier, n + n_col)

    peer = lambda k: lax.rem(me + k, n)
    sender = lambda k: lax.rem(me + n - k, n)
    for k in range(1, n):
        step(x_ref.at[peer(k)], got.at[me], k, device("pl", peer(k)), (send_a, recv_a)).start()
    for k in range(1, n):
        pending.append(step(x_ref.at[peer(k)], got.at[me], k, device("pl", peer(k)), (send_a, recv_a)))
    for k in range(1, n):
        step(x_ref.at[me], got.at[sender(k)], k, device("pl", sender(k)), (send_a, recv_a)).wait_recv()
    total = x_ref[me].astype(jnp.float32)
    for k in range(1, n):
        total = total + got[sender(k)].astype(jnp.float32)
    part_out[...] = total.astype(part_out.dtype)

    across = one(part_out, part_in, partner, send_b, recv_b)
    across.start()
    pending.append(across)
    across.wait_recv()
    mine, theirs = part_out[...], part_in[...]
    coll[me] = jnp.stack([jnp.where(half == 0, mine, theirs), jnp.where(half == 0, theirs, mine)])

    for k in range(1, n):
        step(coll.at[me], coll.at[me], k, device("pl", peer(k)), (send_c, recv_c)).start()
    for k in range(1, n):
        pending.append(step(coll.at[me], coll.at[me], k, device("pl", peer(k)), (send_c, recv_c)))

    def to_sibling(chunk_at):
        return pltpu.make_async_remote_copy(
            src_ref=coll.at[chunk_at], dst_ref=sib_coll.at[chunk_at], send_sem=send_d.at[chunk_at],
            recv_sem=recv_d.at[chunk_at], device_id=sibling, device_id_type=MESH,
        )

    chunk = coll.shape[-1]

    def chunk_dot(blocks, at, h):
        columns = shapes_ref[:, pl.ds(pl.multiple_of(at * chunk, chunk), chunk)]
        return lax.dot_general(
            columns, blocks[at, h], (((1,), (1,)), ((), ())), preferred_element_type=jnp.float32
        )

    to_sibling(me).start()
    pending.append(to_sibling(me))
    own = [chunk_dot(coll, me, h) for h in range(2)]
    for k in range(1, n):
        step(coll.at[me], coll.at[sender(k)], k, device("pl", sender(k)), (send_c, recv_c)).wait_recv()
        to_sibling(sender(k)).start()
        pending.append(to_sibling(sender(k)))
        own = [own[h] + chunk_dot(coll, sender(k), h) for h in range(2)]

    def weighted_block(blocks, h):
        acc = jnp.zeros((shapes_ref.shape[0], blocks.shape[2]), jnp.float32)
        for l in range(n):
            acc = acc + lax.dot_general(
                shapes_ref[:, l * chunk:(l + 1) * chunk], blocks[l, h],
                (((1,), (1,)), ((), ())), preferred_element_type=jnp.float32,
            )
        return acc

    for l in range(n):
        to_sibling(l).wait_recv()
    other = [weighted_block(sib_coll, h) for h in range(2)]
    parts = []
    for h in range(2):
        parts += [jnp.where(core == 0, own[h], other[h]), jnp.where(core == 0, other[h], own[h])]
    wbuf[col] = jnp.concatenate(parts, axis=1).astype(wbuf.dtype)

    wpeer = lambda k: lax.rem(col + k, n_col)
    wsender = lambda k: lax.rem(col + n_col - k, n_col)
    for k in range(1, n_col):
        step(wbuf.at[col], wbuf.at[col], k, device("pcol", wpeer(k)), (send_e, recv_e)).start()
    for k in range(1, n_col):
        pending.append(step(wbuf.at[col], wbuf.at[col], k, device("pcol", wpeer(k)), (send_e, recv_e)))
    for k in range(1, n_col):
        step(wbuf.at[col], wbuf.at[wsender(k)], k, device("pcol", wsender(k)), (send_e, recv_e)).wait_recv()
    width_w = wbuf.shape[2]
    for c in range(n_col):
        out_ref[:, c * width_w:(c + 1) * width_w] = wbuf[c]
    for sent in pending:
        sent.wait_send()


def gram_weighted(x, mode_shapes, axes, sizes):
    n, rows, width = x.shape
    n_col = sizes["pcol"]
    wshape = (n_col, mode_shapes.shape[0], 4 * rows)
    kernel = functools.partial(gram_weighted_kernel, axes=axes, factors=factor_table(sizes))
    return pl.pallas_call(
        kernel,
        out_shape=jax.ShapeDtypeStruct((wshape[1], n_col * wshape[2]), jnp.bfloat16),
        in_specs=[pl.BlockSpec(memory_space=pltpu.VMEM)] * 2,
        out_specs=pl.BlockSpec(memory_space=pltpu.VMEM),
        scratch_shapes=[
            pltpu.VMEM(x.shape, x.dtype),
            pltpu.VMEM((n, 2, rows, width), x.dtype),
            pltpu.VMEM((n, 2, rows, width), x.dtype),
            pltpu.VMEM((rows, width), x.dtype),
            pltpu.VMEM((rows, width), x.dtype),
            pltpu.VMEM(wshape, jnp.bfloat16),
            pltpu.SemaphoreType.DMA((n,)),
            pltpu.SemaphoreType.DMA((n,)),
            pltpu.SemaphoreType.DMA(()),
            pltpu.SemaphoreType.DMA(()),
            pltpu.SemaphoreType.DMA((n,)),
            pltpu.SemaphoreType.DMA((n,)),
            pltpu.SemaphoreType.DMA((n,)),
            pltpu.SemaphoreType.DMA((n,)),
            pltpu.SemaphoreType.DMA((n_col,)),
            pltpu.SemaphoreType.DMA((n_col,)),
        ],
        compiler_params=pltpu.CompilerParams(collective_id=103, has_side_effects=True),
    )(x, mode_shapes)


def fused_sum(x, axes, sizes, over, add_across, kernel_id):
    n, rows, width = x.shape
    block = (rows, width) if add_across else (2, rows, width)
    kernel = functools.partial(
        fused_sum_kernel, axes=axes, factors=factor_table(sizes), over=over, add_across=add_across
    )
    return pl.pallas_call(
        kernel,
        out_shape=jax.ShapeDtypeStruct((n,) + block, x.dtype),
        in_specs=[pl.BlockSpec(memory_space=pltpu.VMEM)],
        out_specs=pl.BlockSpec(memory_space=pltpu.VMEM),
        scratch_shapes=[
            pltpu.VMEM(x.shape, x.dtype),
            pltpu.VMEM((n,) + block, x.dtype),
            pltpu.VMEM((rows, width), x.dtype),
            pltpu.VMEM((rows, width), x.dtype),
            pltpu.SemaphoreType.DMA((n,)),
            pltpu.SemaphoreType.DMA((n,)),
            pltpu.SemaphoreType.DMA(()),
            pltpu.SemaphoreType.DMA(()),
            pltpu.SemaphoreType.DMA((n,)),
            pltpu.SemaphoreType.DMA((n,)),
        ],
        compiler_params=pltpu.CompilerParams(collective_id=kernel_id, has_side_effects=True),
    )(x)


class Exchanger:
    def __init__(self, axes, sizes):
        self.axes, self.factors, self.calls = axes, factor_table(sizes), 0

    def __call__(self, x, group, same):
        count = math.prod(self.factors[f][1] for f in group)
        block = x.shape if same else x.shape[1:]
        if count == 1:
            return x[None] if same else x
        kernel = functools.partial(
            exchange_kernel, axes=self.axes, factors=self.factors, group=group, same=same
        )
        self.calls += 1
        return pl.pallas_call(
            kernel,
            out_shape=jax.ShapeDtypeStruct((count,) + tuple(block), x.dtype),
            in_specs=[pl.BlockSpec(memory_space=pl.ANY)],
            out_specs=pl.BlockSpec(memory_space=pl.ANY),
            scratch_shapes=[
                pltpu.SemaphoreType.DMA((count,)),
                pltpu.SemaphoreType.DMA((count,)),
                pltpu.SemaphoreType.DMA(()),
            ],
            compiler_params=pltpu.CompilerParams(collective_id=self.calls, has_side_effects=True),
        )(x)


def make_body(axes, sizes):
    n_row, n_col, n_pl = sizes["prow"], sizes["pcol"], sizes["pl"]
    swap = [(c * n_col + r, r * n_col + c) for r in range(n_row) for c in range(n_col)]
    sibling = [(r, r ^ 1) for r in range(n_row)]
    n_zh = n_row // 2

    def beside_sibling(part, core):
        other = lax.ppermute(part, "prow", sibling)
        first, second = jnp.where(core == 0, part, other), jnp.where(core == 0, other, part)
        return jnp.concatenate([first, second], axis=0)

    def body(factor_cols, modal_at_loads, mode_shapes, natural_freq, damping):
        ex = Exchanger(axes, sizes)
        in_phase, quadrature = transfer_pair(natural_freq, damping)
        modes = modal_at_loads.shape[0]
        block = modes // (n_row * n_col)
        row, col = lax.axis_index("prow"), lax.axis_index("pcol")
        width = factor_cols.shape[1]
        core = row % 2
        own_modes = lax.dynamic_slice_in_dim(modal_at_loads, core * (modes // 2), modes // 2, 0)
        sib_modes = lax.dynamic_slice_in_dim(modal_at_loads, (1 - core) * (modes // 2), modes // 2, 0)
        mine = jnp.dot(own_modes, factor_cols, preferred_element_type=jnp.float32)
        theirs = jnp.dot(sib_modes, factor_cols, preferred_element_type=jnp.float32)
        modal_load = modal_sum(mine, theirs.astype(jnp.bfloat16), axes, sizes).reshape(modes, width)
        modal_wide = modal_load.astype(jnp.float32)
        pseudo = jnp.concatenate(
            [
                (in_phase[:, None] * modal_wide).astype(jnp.bfloat16),
                (quadrature[:, None] * modal_wide).astype(jnp.bfloat16),
            ],
            axis=1,
        )
        first_row = (col * n_row + row) * block
        own_pseudo = lax.dynamic_slice_in_dim(pseudo, first_row, block, 0)
        partial_gram = outer_rows(own_pseudo, pseudo).astype(jnp.bfloat16)
        chunk = modes // n_pl
        by_chunk = partial_gram.reshape(block, n_pl, chunk).transpose(1, 0, 2)
        half = modes // 2
        send_half = lax.dynamic_slice_in_dim(mode_shapes, (col % 2) * half, half, 1)
        panel_piece = lax.ppermute(send_half, ("prow", "pcol"), swap)
        panel_mine = lax.all_gather(panel_piece, "pl", axis=0, tiled=True)
        weighted = gram_weighted(by_chunk, mode_shapes, axes, sizes)
        panel_mine, weighted = lax.optimization_barrier((panel_mine, weighted))
        panel_other = lax.ppermute(panel_mine, "prow", sibling)
        weighted_mine = lax.dynamic_slice_in_dim(weighted, core * half, half, 1)
        weighted_other = lax.dynamic_slice_in_dim(weighted, (1 - core) * half, half, 1)
        return outer_rows(weighted_other, panel_other) + outer_rows(weighted_mine, panel_mine)

    return body


def solution(mesh):
    in_specs = (
        P(("prow", "pcol"), "pl"),
        P(None, ("prow", "pcol")),
        P(("prow", "pl"), None),
        P(),
        P(),
    )
    out_specs = P(("prow", "pl"), "pcol")
    axes = tuple(mesh.axis_names)
    body = make_body(axes, dict(mesh.shape))
    return jax.shard_map(body, mesh=mesh, in_specs=in_specs, out_specs=out_specs, check_vma=False)
```

```python
import functools
import math

import jax
import jax.numpy as jnp
from jax import lax
from jax.experimental import pallas as pl
from jax.experimental.pallas import tpu as pltpu
from jax.sharding import PartitionSpec as P

MESH = pl.DeviceIdType.MESH


def transfer_pair(natural_freq, damping):
    detuning = natural_freq * natural_freq - 1.0
    damper = 2.0 * damping * natural_freq
    modulus = detuning * detuning + damper * damper
    return (detuning / modulus, -damper / modulus)


def outer_rows(left_rows, right_rows):
    return lax.dot_general(
        left_rows, right_rows, (((1,), (1,)), ((), ())), preferred_element_type=jnp.float32
    )


def factor_table(sizes):
    return {
        "zh": ("prow", sizes["prow"] // 2, 2),
        "core": ("prow", 2, 1),
        "pcol": ("pcol", sizes["pcol"], 1),
        "pl": ("pl", sizes["pl"], 1),
    }


def exchange_kernel(x_ref, out_ref, send_sem, recv_sem, local_sem, *, axes, factors, group, same):
    coords = {a: lax.axis_index(a) for a in axes}

    def value(f):
        axis, size, stride = factors[f]
        return lax.rem(coords[axis] // stride, size)

    count = math.prod(factors[f][1] for f in group)
    me = 0
    for f in group:
        me = me * factors[f][1] + value(f)

    def device(member):
        place = dict(coords)
        for f in reversed(group):
            axis, size, stride = factors[f]
            place[axis] = place[axis] + (lax.rem(member, size) - value(f)) * stride
            member = member // size
        return tuple(place[a] for a in axes)

    def source(member):
        return x_ref if same else x_ref.at[member]

    def copy(offset):
        peer = lax.rem(me + offset, count)
        return pltpu.make_async_remote_copy(
            src_ref=source(peer),
            dst_ref=out_ref.at[me],
            send_sem=send_sem.at[offset],
            recv_sem=recv_sem.at[offset],
            device_id=device(peer),
            device_id_type=MESH,
        )

    def landing(offset):
        sender = lax.rem(me + count - offset, count)
        return pltpu.make_async_remote_copy(
            src_ref=source(me),
            dst_ref=out_ref.at[sender],
            send_sem=send_sem.at[offset],
            recv_sem=recv_sem.at[offset],
            device_id=device(sender),
            device_id_type=MESH,
        )

    local = pltpu.make_async_copy(source(me), out_ref.at[me], local_sem)
    local.start()
    barrier = pltpu.get_barrier_semaphore()
    for offset in range(1, count):
        peer = lax.rem(me + offset, count)
        pl.semaphore_signal(barrier, inc=1, device_id=device(peer), device_id_type=MESH)
    pl.semaphore_wait(barrier, count - 1)
    for offset in range(1, count):
        copy(offset).start()
    local.wait()
    for offset in range(1, count):
        copy(offset).wait_send()
    for offset in range(1, count):
        landing(offset).wait_recv()


def fused_sum_kernel(x_ref, out_ref, got, coll, part_out, part_in, send_a, recv_a, send_b, recv_b,
                     send_c, recv_c, *, axes, factors, over, add_across):
    coords = {a: lax.axis_index(a) for a in axes}

    def value(f):
        axis, size, stride = factors[f]
        return lax.rem(coords[axis] // stride, size)

    def device(f, v):
        place = dict(coords)
        axis, size, stride = factors[f]
        place[axis] = place[axis] + (v - value(f)) * stride
        return tuple(place[a] for a in axes)

    n = factors[over][1]
    me, half = value(over), value("zh")
    partner = device("zh", 1 - half)
    peer = lambda k: lax.rem(me + k, n)
    sender = lambda k: lax.rem(me + n - k, n)

    def step(src, dst_at, k, to, sems):
        return pltpu.make_async_remote_copy(
            src_ref=src, dst_ref=dst_at, send_sem=sems[0].at[k], recv_sem=sems[1].at[k],
            device_id=to, device_id_type=MESH,
        )

    barrier = pltpu.get_barrier_semaphore()
    for k in range(1, n):
        pl.semaphore_signal(barrier, inc=1, device_id=device(over, peer(k)), device_id_type=MESH)
    pl.semaphore_signal(barrier, inc=1, device_id=partner, device_id_type=MESH)
    pl.semaphore_wait(barrier, n)

    for k in range(1, n):
        step(x_ref.at[peer(k)], got.at[me], k, device(over, peer(k)), (send_a, recv_a)).start()
    for k in range(1, n):
        step(x_ref.at[peer(k)], got.at[me], k, device(over, peer(k)), (send_a, recv_a)).wait_send()
    for k in range(1, n):
        step(x_ref.at[me], got.at[sender(k)], k, device(over, sender(k)), (send_a, recv_a)).wait_recv()
    total = x_ref[me].astype(jnp.float32)
    for k in range(1, n):
        total = total + got[sender(k)].astype(jnp.float32)
    part_out[...] = total.astype(part_out.dtype)

    across = pltpu.make_async_remote_copy(
        src_ref=part_out, dst_ref=part_in, send_sem=send_b, recv_sem=recv_b,
        device_id=partner, device_id_type=MESH,
    )
    across.start()
    across.wait_send()
    across.wait_recv()
    if add_across:
        mine, theirs = part_out[...].astype(jnp.float32), part_in[...].astype(jnp.float32)
        coll[me] = (mine + theirs).astype(coll.dtype)
    else:
        mine, theirs = part_out[...], part_in[...]
        first = jnp.where(half == 0, mine, theirs)
        second = jnp.where(half == 0, theirs, mine)
        coll[me] = jnp.stack([first, second])

    for k in range(1, n):
        step(coll.at[me], coll.at[me], k, device(over, peer(k)), (send_c, recv_c)).start()
    for k in range(1, n):
        step(coll.at[me], coll.at[me], k, device(over, peer(k)), (send_c, recv_c)).wait_send()
    for k in range(1, n):
        step(coll.at[me], coll.at[sender(k)], k, device(over, sender(k)), (send_c, recv_c)).wait_recv()
    out_ref[...] = coll[...]


def modal_sum_kernel(mine_ref, theirs_ref, out_ref, sib_in, pieces, got, coll, part_out, part_in,
                     sib_out, send_s, recv_s, send_a, recv_a, send_b, recv_b, send_c, recv_c,
                     send_d, recv_d, *, axes, factors):
    coords = {a: lax.axis_index(a) for a in axes}

    def value(f):
        axis, size, stride = factors[f]
        return lax.rem(coords[axis] // stride, size)

    def device(f, v):
        place = dict(coords)
        axis, size, stride = factors[f]
        place[axis] = place[axis] + (v - value(f)) * stride
        return tuple(place[a] for a in axes)

    n = factors["pcol"][1]
    me, half, core = value("pcol"), value("zh"), value("core")
    partner, sibling = device("zh", 1 - half), device("core", 1 - core)
    peer = lambda k: lax.rem(me + k, n)
    sender = lambda k: lax.rem(me + n - k, n)

    def step(src, dst_at, k, to, sems):
        return pltpu.make_async_remote_copy(
            src_ref=src, dst_ref=dst_at, send_sem=sems[0].at[k], recv_sem=sems[1].at[k],
            device_id=to, device_id_type=MESH,
        )

    def one(src, dst, to, send_sem, recv_sem):
        return pltpu.make_async_remote_copy(
            src_ref=src, dst_ref=dst, send_sem=send_sem, recv_sem=recv_sem,
            device_id=to, device_id_type=MESH,
        )

    pending = []
    barrier = pltpu.get_barrier_semaphore()
    for k in range(1, n):
        pl.semaphore_signal(barrier, inc=1, device_id=device("pcol", peer(k)), device_id_type=MESH)
    pl.semaphore_signal(barrier, inc=1, device_id=partner, device_id_type=MESH)
    pl.semaphore_signal(barrier, inc=1, device_id=sibling, device_id_type=MESH)
    pl.semaphore_wait(barrier, n + 1)

    chip = one(theirs_ref, sib_in, sibling, send_s, recv_s)
    chip.start()
    pending.append(chip)
    chip.wait_recv()
    summed = mine_ref[...].astype(jnp.float32) + sib_in[...].astype(jnp.float32)
    pieces[...] = summed.astype(pieces.dtype).reshape(pieces.shape)

    for k in range(1, n):
        step(pieces.at[peer(k)], got.at[me], k, device("pcol", peer(k)), (send_a, recv_a)).start()
    for k in range(1, n):
        pending.append(step(pieces.at[peer(k)], got.at[me], k, device("pcol", peer(k)), (send_a, recv_a)))
    for k in range(1, n):
        step(pieces.at[me], got.at[sender(k)], k, device("pcol", sender(k)), (send_a, recv_a)).wait_recv()
    total = pieces[me].astype(jnp.float32)
    for k in range(1, n):
        total = total + got[sender(k)].astype(jnp.float32)
    part_out[...] = total.astype(part_out.dtype)

    across = one(part_out, part_in, partner, send_b, recv_b)
    across.start()
    pending.append(across)
    across.wait_recv()
    coll[me] = (part_out[...].astype(jnp.float32) + part_in[...].astype(jnp.float32)).astype(coll.dtype)

    for k in range(1, n):
        step(coll.at[me], coll.at[me], k, device("pcol", peer(k)), (send_c, recv_c)).start()
    for k in range(1, n):
        pending.append(step(coll.at[me], coll.at[me], k, device("pcol", peer(k)), (send_c, recv_c)))
    for k in range(1, n):
        step(coll.at[me], coll.at[sender(k)], k, device("pcol", sender(k)), (send_c, recv_c)).wait_recv()

    join = one(coll, sib_out, sibling, send_d, recv_d)
    join.start()
    pending.append(join)
    join.wait_recv()
    out_ref[core] = coll[...]
    out_ref[1 - core] = sib_out[...]
    for sent in pending:
        sent.wait_send()


def modal_sum(mine, theirs, axes, sizes):
    n = sizes["pcol"]
    rows, width = mine.shape
    block = (n, rows // n, width)
    kernel = functools.partial(modal_sum_kernel, axes=axes, factors=factor_table(sizes))
    return pl.pallas_call(
        kernel,
        out_shape=jax.ShapeDtypeStruct((2,) + block, jnp.bfloat16),
        in_specs=[pl.BlockSpec(memory_space=pltpu.VMEM)] * 2,
        out_specs=pl.BlockSpec(memory_space=pltpu.VMEM),
        scratch_shapes=[
            pltpu.VMEM((rows, width), jnp.bfloat16),
            pltpu.VMEM(block, jnp.bfloat16),
            pltpu.VMEM(block, jnp.bfloat16),
            pltpu.VMEM(block, jnp.bfloat16),
            pltpu.VMEM(block[1:], jnp.bfloat16),
            pltpu.VMEM(block[1:], jnp.bfloat16),
            pltpu.VMEM(block, jnp.bfloat16),
            pltpu.SemaphoreType.DMA(()),
            pltpu.SemaphoreType.DMA(()),
            pltpu.SemaphoreType.DMA((n,)),
            pltpu.SemaphoreType.DMA((n,)),
            pltpu.SemaphoreType.DMA(()),
            pltpu.SemaphoreType.DMA(()),
            pltpu.SemaphoreType.DMA((n,)),
            pltpu.SemaphoreType.DMA((n,)),
            pltpu.SemaphoreType.DMA(()),
            pltpu.SemaphoreType.DMA(()),
        ],
        compiler_params=pltpu.CompilerParams(collective_id=102, has_side_effects=True),
    )(mine, theirs)


def gram_weighted_kernel(x_ref, shapes_ref, out_ref, got, coll, sib_coll, part_out, part_in, wbuf,
                         send_a, recv_a, send_b, recv_b, send_c, recv_c, send_d, recv_d, send_e,
                         recv_e, *, axes, factors):
    coords = {a: lax.axis_index(a) for a in axes}

    def value(f):
        axis, size, stride = factors[f]
        return lax.rem(coords[axis] // stride, size)

    def device(f, v):
        place = dict(coords)
        axis, size, stride = factors[f]
        place[axis] = place[axis] + (v - value(f)) * stride
        return tuple(place[a] for a in axes)

    n, n_col = factors["pl"][1], factors["pcol"][1]
    me, half, core, col = value("pl"), value("zh"), value("core"), value("pcol")
    partner, sibling = device("zh", 1 - half), device("core", 1 - core)

    def step(src, dst_at, k, to, sems):
        return pltpu.make_async_remote_copy(
            src_ref=src, dst_ref=dst_at, send_sem=sems[0].at[k], recv_sem=sems[1].at[k],
            device_id=to, device_id_type=MESH,
        )

    def one(src, dst, to, send_sem, recv_sem):
        return pltpu.make_async_remote_copy(
            src_ref=src, dst_ref=dst, send_sem=send_sem, recv_sem=recv_sem,
            device_id=to, device_id_type=MESH,
        )

    pending = []
    barrier = pltpu.get_barrier_semaphore()
    for k in range(1, n):
        pl.semaphore_signal(barrier, inc=1, device_id=device("pl", lax.rem(me + k, n)), device_id_type=MESH)
    for k in range(1, n_col):
        pl.semaphore_signal(
            barrier, inc=1, device_id=device("pcol", lax.rem(col + k, n_col)), device_id_type=MESH
        )
    pl.semaphore_signal(barrier, inc=1, device_id=partner, device_id_type=MESH)
    pl.semaphore_signal(barrier, inc=1, device_id=sibling, device_id_type=MESH)
    pl.semaphore_wait(barrier, n + n_col)

    peer = lambda k: lax.rem(me + k, n)
    sender = lambda k: lax.rem(me + n - k, n)
    for k in range(1, n):
        step(x_ref.at[peer(k)], got.at[me], k, device("pl", peer(k)), (send_a, recv_a)).start()
    for k in range(1, n):
        pending.append(step(x_ref.at[peer(k)], got.at[me], k, device("pl", peer(k)), (send_a, recv_a)))
    for k in range(1, n):
        step(x_ref.at[me], got.at[sender(k)], k, device("pl", sender(k)), (send_a, recv_a)).wait_recv()
    total = x_ref[me].astype(jnp.float32)
    for k in range(1, n):
        total = total + got[sender(k)].astype(jnp.float32)
    part_out[...] = total.astype(part_out.dtype)

    across = one(part_out, part_in, partner, send_b, recv_b)
    across.start()
    pending.append(across)
    across.wait_recv()
    mine, theirs = part_out[...], part_in[...]
    coll[me] = jnp.stack([jnp.where(half == 0, mine, theirs), jnp.where(half == 0, theirs, mine)])

    for k in range(1, n):
        step(coll.at[me], coll.at[me], k, device("pl", peer(k)), (send_c, recv_c)).start()
    for k in range(1, n):
        pending.append(step(coll.at[me], coll.at[me], k, device("pl", peer(k)), (send_c, recv_c)))

    def to_sibling(chunk_at):
        return pltpu.make_async_remote_copy(
            src_ref=coll.at[chunk_at], dst_ref=sib_coll.at[chunk_at], send_sem=send_d.at[chunk_at],
            recv_sem=recv_d.at[chunk_at], device_id=sibling, device_id_type=MESH,
        )

    to_sibling(me).start()
    pending.append(to_sibling(me))
    for k in range(1, n):
        step(coll.at[me], coll.at[sender(k)], k, device("pl", sender(k)), (send_c, recv_c)).wait_recv()
        to_sibling(sender(k)).start()
        pending.append(to_sibling(sender(k)))

    chunk = coll.shape[-1]

    def weighted_block(blocks, h):
        acc = jnp.zeros((shapes_ref.shape[0], blocks.shape[2]), jnp.float32)
        for l in range(n):
            acc = acc + lax.dot_general(
                shapes_ref[:, l * chunk:(l + 1) * chunk], blocks[l, h],
                (((1,), (1,)), ((), ())), preferred_element_type=jnp.float32,
            )
        return acc

    own = [weighted_block(coll, h) for h in range(2)]
    for l in range(n):
        to_sibling(l).wait_recv()
    other = [weighted_block(sib_coll, h) for h in range(2)]
    parts = []
    for h in range(2):
        parts += [jnp.where(core == 0, own[h], other[h]), jnp.where(core == 0, other[h], own[h])]
    wbuf[col] = jnp.concatenate(parts, axis=1).astype(wbuf.dtype)

    wpeer = lambda k: lax.rem(col + k, n_col)
    wsender = lambda k: lax.rem(col + n_col - k, n_col)
    for k in range(1, n_col):
        step(wbuf.at[col], wbuf.at[col], k, device("pcol", wpeer(k)), (send_e, recv_e)).start()
    for k in range(1, n_col):
        pending.append(step(wbuf.at[col], wbuf.at[col], k, device("pcol", wpeer(k)), (send_e, recv_e)))
    for k in range(1, n_col):
        step(wbuf.at[col], wbuf.at[wsender(k)], k, device("pcol", wsender(k)), (send_e, recv_e)).wait_recv()
    width_w = wbuf.shape[2]
    for c in range(n_col):
        out_ref[:, c * width_w:(c + 1) * width_w] = wbuf[c]
    for sent in pending:
        sent.wait_send()


def gram_weighted(x, mode_shapes, axes, sizes):
    n, rows, width = x.shape
    n_col = sizes["pcol"]
    wshape = (n_col, mode_shapes.shape[0], 4 * rows)
    kernel = functools.partial(gram_weighted_kernel, axes=axes, factors=factor_table(sizes))
    return pl.pallas_call(
        kernel,
        out_shape=jax.ShapeDtypeStruct((wshape[1], n_col * wshape[2]), jnp.bfloat16),
        in_specs=[pl.BlockSpec(memory_space=pltpu.VMEM)] * 2,
        out_specs=pl.BlockSpec(memory_space=pltpu.VMEM),
        scratch_shapes=[
            pltpu.VMEM(x.shape, x.dtype),
            pltpu.VMEM((n, 2, rows, width), x.dtype),
            pltpu.VMEM((n, 2, rows, width), x.dtype),
            pltpu.VMEM((rows, width), x.dtype),
            pltpu.VMEM((rows, width), x.dtype),
            pltpu.VMEM(wshape, jnp.bfloat16),
            pltpu.SemaphoreType.DMA((n,)),
            pltpu.SemaphoreType.DMA((n,)),
            pltpu.SemaphoreType.DMA(()),
            pltpu.SemaphoreType.DMA(()),
            pltpu.SemaphoreType.DMA((n,)),
            pltpu.SemaphoreType.DMA((n,)),
            pltpu.SemaphoreType.DMA((n,)),
            pltpu.SemaphoreType.DMA((n,)),
            pltpu.SemaphoreType.DMA((n_col,)),
            pltpu.SemaphoreType.DMA((n_col,)),
        ],
        compiler_params=pltpu.CompilerParams(collective_id=103, has_side_effects=True),
    )(x, mode_shapes)


def fused_sum(x, axes, sizes, over, add_across, kernel_id):
    n, rows, width = x.shape
    block = (rows, width) if add_across else (2, rows, width)
    kernel = functools.partial(
        fused_sum_kernel, axes=axes, factors=factor_table(sizes), over=over, add_across=add_across
    )
    return pl.pallas_call(
        kernel,
        out_shape=jax.ShapeDtypeStruct((n,) + block, x.dtype),
        in_specs=[pl.BlockSpec(memory_space=pltpu.VMEM)],
        out_specs=pl.BlockSpec(memory_space=pltpu.VMEM),
        scratch_shapes=[
            pltpu.VMEM(x.shape, x.dtype),
            pltpu.VMEM((n,) + block, x.dtype),
            pltpu.VMEM((rows, width), x.dtype),
            pltpu.VMEM((rows, width), x.dtype),
            pltpu.SemaphoreType.DMA((n,)),
            pltpu.SemaphoreType.DMA((n,)),
            pltpu.SemaphoreType.DMA(()),
            pltpu.SemaphoreType.DMA(()),
            pltpu.SemaphoreType.DMA((n,)),
            pltpu.SemaphoreType.DMA((n,)),
        ],
        compiler_params=pltpu.CompilerParams(collective_id=kernel_id, has_side_effects=True),
    )(x)


class Exchanger:
    def __init__(self, axes, sizes):
        self.axes, self.factors, self.calls = axes, factor_table(sizes), 0

    def __call__(self, x, group, same):
        count = math.prod(self.factors[f][1] for f in group)
        block = x.shape if same else x.shape[1:]
        if count == 1:
            return x[None] if same else x
        kernel = functools.partial(
            exchange_kernel, axes=self.axes, factors=self.factors, group=group, same=same
        )
        self.calls += 1
        return pl.pallas_call(
            kernel,
            out_shape=jax.ShapeDtypeStruct((count,) + tuple(block), x.dtype),
            in_specs=[pl.BlockSpec(memory_space=pl.ANY)],
            out_specs=pl.BlockSpec(memory_space=pl.ANY),
            scratch_shapes=[
                pltpu.SemaphoreType.DMA((count,)),
                pltpu.SemaphoreType.DMA((count,)),
                pltpu.SemaphoreType.DMA(()),
            ],
            compiler_params=pltpu.CompilerParams(collective_id=self.calls, has_side_effects=True),
        )(x)


def make_body(axes, sizes):
    n_row, n_col, n_pl = sizes["prow"], sizes["pcol"], sizes["pl"]
    swap = [(c * n_col + r, r * n_col + c) for r in range(n_row) for c in range(n_col)]
    sibling = [(r, r ^ 1) for r in range(n_row)]
    n_zh = n_row // 2

    def beside_sibling(part, core):
        other = lax.ppermute(part, "prow", sibling)
        first, second = jnp.where(core == 0, part, other), jnp.where(core == 0, other, part)
        return jnp.concatenate([first, second], axis=0)

    def body(factor_cols, modal_at_loads, mode_shapes, natural_freq, damping):
        ex = Exchanger(axes, sizes)
        in_phase, quadrature = transfer_pair(natural_freq, damping)
        modes = modal_at_loads.shape[0]
        block = modes // (n_row * n_col)
        row, col = lax.axis_index("prow"), lax.axis_index("pcol")
        width = factor_cols.shape[1]
        core = row % 2
        own_modes = lax.dynamic_slice_in_dim(modal_at_loads, core * (modes // 2), modes // 2, 0)
        sib_modes = lax.dynamic_slice_in_dim(modal_at_loads, (1 - core) * (modes // 2), modes // 2, 0)
        mine = jnp.dot(own_modes, factor_cols, preferred_element_type=jnp.float32)
        theirs = jnp.dot(sib_modes, factor_cols, preferred_element_type=jnp.float32)
        bf16 = jnp.bfloat16
        modal_load = modal_sum(mine.astype(bf16), theirs.astype(bf16), axes, sizes).reshape(modes, width)
        modal_wide = modal_load.astype(jnp.float32)
        pseudo = jnp.concatenate(
            [
                (in_phase[:, None] * modal_wide).astype(jnp.bfloat16),
                (quadrature[:, None] * modal_wide).astype(jnp.bfloat16),
            ],
            axis=1,
        )
        first_row = (col * n_row + row) * block
        own_pseudo = lax.dynamic_slice_in_dim(pseudo, first_row, block, 0)
        partial_gram = outer_rows(own_pseudo, pseudo).astype(jnp.bfloat16)
        chunk = modes // n_pl
        by_chunk = partial_gram.reshape(block, n_pl, chunk).transpose(1, 0, 2)
        half = modes // 2
        send_half = lax.dynamic_slice_in_dim(mode_shapes, (col % 2) * half, half, 1)
        panel_piece = lax.ppermute(send_half, ("prow", "pcol"), swap)
        panel_mine = lax.all_gather(panel_piece, "pl", axis=0, tiled=True)
        weighted = gram_weighted(by_chunk, mode_shapes, axes, sizes)
        panel_mine, weighted = lax.optimization_barrier((panel_mine, weighted))
        panel_other = lax.ppermute(panel_mine, "prow", sibling)
        weighted_mine = lax.dynamic_slice_in_dim(weighted, core * half, half, 1)
        weighted_other = lax.dynamic_slice_in_dim(weighted, (1 - core) * half, half, 1)
        return outer_rows(weighted_other, panel_other) + outer_rows(weighted_mine, panel_mine)

    return body


def solution(mesh):
    in_specs = (
        P(("prow", "pcol"), "pl"),
        P(None, ("prow", "pcol")),
        P(("prow", "pl"), None),
        P(),
        P(),
    )
    out_specs = P(("prow", "pl"), "pcol")
    axes = tuple(mesh.axis_names)
    body = make_body(axes, dict(mesh.shape))
    return jax.shard_map(body, mesh=mesh, in_specs=in_specs, out_specs=out_specs, check_vma=False)
```

```python
import functools
import math

import jax
import jax.numpy as jnp
from jax import lax
from jax.experimental import pallas as pl
from jax.experimental.pallas import tpu as pltpu
from jax.sharding import PartitionSpec as P

MESH = pl.DeviceIdType.MESH


def transfer_pair(natural_freq, damping):
    detuning = natural_freq * natural_freq - 1.0
    damper = 2.0 * damping * natural_freq
    modulus = detuning * detuning + damper * damper
    return (detuning / modulus, -damper / modulus)


def outer_rows(left_rows, right_rows):
    return lax.dot_general(
        left_rows, right_rows, (((1,), (1,)), ((), ())), preferred_element_type=jnp.float32
    )


def factor_table(sizes):
    return {
        "zh": ("prow", sizes["prow"] // 2, 2),
        "core": ("prow", 2, 1),
        "pcol": ("pcol", sizes["pcol"], 1),
        "pl": ("pl", sizes["pl"], 1),
    }


def exchange_kernel(x_ref, out_ref, send_sem, recv_sem, local_sem, *, axes, factors, group, same):
    coords = {a: lax.axis_index(a) for a in axes}

    def value(f):
        axis, size, stride = factors[f]
        return lax.rem(coords[axis] // stride, size)

    count = math.prod(factors[f][1] for f in group)
    me = 0
    for f in group:
        me = me * factors[f][1] + value(f)

    def device(member):
        place = dict(coords)
        for f in reversed(group):
            axis, size, stride = factors[f]
            place[axis] = place[axis] + (lax.rem(member, size) - value(f)) * stride
            member = member // size
        return tuple(place[a] for a in axes)

    def source(member):
        return x_ref if same else x_ref.at[member]

    def copy(offset):
        peer = lax.rem(me + offset, count)
        return pltpu.make_async_remote_copy(
            src_ref=source(peer),
            dst_ref=out_ref.at[me],
            send_sem=send_sem.at[offset],
            recv_sem=recv_sem.at[offset],
            device_id=device(peer),
            device_id_type=MESH,
        )

    def landing(offset):
        sender = lax.rem(me + count - offset, count)
        return pltpu.make_async_remote_copy(
            src_ref=source(me),
            dst_ref=out_ref.at[sender],
            send_sem=send_sem.at[offset],
            recv_sem=recv_sem.at[offset],
            device_id=device(sender),
            device_id_type=MESH,
        )

    local = pltpu.make_async_copy(source(me), out_ref.at[me], local_sem)
    local.start()
    barrier = pltpu.get_barrier_semaphore()
    for offset in range(1, count):
        peer = lax.rem(me + offset, count)
        pl.semaphore_signal(barrier, inc=1, device_id=device(peer), device_id_type=MESH)
    pl.semaphore_wait(barrier, count - 1)
    for offset in range(1, count):
        copy(offset).start()
    local.wait()
    for offset in range(1, count):
        copy(offset).wait_send()
    for offset in range(1, count):
        landing(offset).wait_recv()


def fused_sum_kernel(x_ref, out_ref, got, coll, part_out, part_in, send_a, recv_a, send_b, recv_b,
                     send_c, recv_c, *, axes, factors, over, add_across):
    coords = {a: lax.axis_index(a) for a in axes}

    def value(f):
        axis, size, stride = factors[f]
        return lax.rem(coords[axis] // stride, size)

    def device(f, v):
        place = dict(coords)
        axis, size, stride = factors[f]
        place[axis] = place[axis] + (v - value(f)) * stride
        return tuple(place[a] for a in axes)

    n = factors[over][1]
    me, half = value(over), value("zh")
    partner = device("zh", 1 - half)
    peer = lambda k: lax.rem(me + k, n)
    sender = lambda k: lax.rem(me + n - k, n)

    def step(src, dst_at, k, to, sems):
        return pltpu.make_async_remote_copy(
            src_ref=src, dst_ref=dst_at, send_sem=sems[0].at[k], recv_sem=sems[1].at[k],
            device_id=to, device_id_type=MESH,
        )

    barrier = pltpu.get_barrier_semaphore()
    for k in range(1, n):
        pl.semaphore_signal(barrier, inc=1, device_id=device(over, peer(k)), device_id_type=MESH)
    pl.semaphore_signal(barrier, inc=1, device_id=partner, device_id_type=MESH)
    pl.semaphore_wait(barrier, n)

    for k in range(1, n):
        step(x_ref.at[peer(k)], got.at[me], k, device(over, peer(k)), (send_a, recv_a)).start()
    for k in range(1, n):
        step(x_ref.at[peer(k)], got.at[me], k, device(over, peer(k)), (send_a, recv_a)).wait_send()
    for k in range(1, n):
        step(x_ref.at[me], got.at[sender(k)], k, device(over, sender(k)), (send_a, recv_a)).wait_recv()
    total = x_ref[me].astype(jnp.float32)
    for k in range(1, n):
        total = total + got[sender(k)].astype(jnp.float32)
    part_out[...] = total.astype(part_out.dtype)

    across = pltpu.make_async_remote_copy(
        src_ref=part_out, dst_ref=part_in, send_sem=send_b, recv_sem=recv_b,
        device_id=partner, device_id_type=MESH,
    )
    across.start()
    across.wait_send()
    across.wait_recv()
    if add_across:
        mine, theirs = part_out[...].astype(jnp.float32), part_in[...].astype(jnp.float32)
        coll[me] = (mine + theirs).astype(coll.dtype)
    else:
        mine, theirs = part_out[...], part_in[...]
        first = jnp.where(half == 0, mine, theirs)
        second = jnp.where(half == 0, theirs, mine)
        coll[me] = jnp.stack([first, second])

    for k in range(1, n):
        step(coll.at[me], coll.at[me], k, device(over, peer(k)), (send_c, recv_c)).start()
    for k in range(1, n):
        step(coll.at[me], coll.at[me], k, device(over, peer(k)), (send_c, recv_c)).wait_send()
    for k in range(1, n):
        step(coll.at[me], coll.at[sender(k)], k, device(over, sender(k)), (send_c, recv_c)).wait_recv()
    out_ref[...] = coll[...]


def modal_sum_kernel(mine_ref, theirs_ref, out_ref, sib_in, pieces, got, coll, part_out, part_in,
                     sib_out, send_s, recv_s, send_a, recv_a, send_b, recv_b, send_c, recv_c,
                     send_d, recv_d, *, axes, factors):
    coords = {a: lax.axis_index(a) for a in axes}

    def value(f):
        axis, size, stride = factors[f]
        return lax.rem(coords[axis] // stride, size)

    def device(f, v):
        place = dict(coords)
        axis, size, stride = factors[f]
        place[axis] = place[axis] + (v - value(f)) * stride
        return tuple(place[a] for a in axes)

    n = factors["pcol"][1]
    me, half, core = value("pcol"), value("zh"), value("core")
    partner, sibling = device("zh", 1 - half), device("core", 1 - core)
    peer = lambda k: lax.rem(me + k, n)
    sender = lambda k: lax.rem(me + n - k, n)

    def step(src, dst_at, k, to, sems):
        return pltpu.make_async_remote_copy(
            src_ref=src, dst_ref=dst_at, send_sem=sems[0].at[k], recv_sem=sems[1].at[k],
            device_id=to, device_id_type=MESH,
        )

    def one(src, dst, to, send_sem, recv_sem):
        return pltpu.make_async_remote_copy(
            src_ref=src, dst_ref=dst, send_sem=send_sem, recv_sem=recv_sem,
            device_id=to, device_id_type=MESH,
        )

    pending = []
    barrier = pltpu.get_barrier_semaphore()
    for k in range(1, n):
        pl.semaphore_signal(barrier, inc=1, device_id=device("pcol", peer(k)), device_id_type=MESH)
    pl.semaphore_signal(barrier, inc=1, device_id=partner, device_id_type=MESH)
    pl.semaphore_signal(barrier, inc=1, device_id=sibling, device_id_type=MESH)
    pl.semaphore_wait(barrier, n + 1)

    chip = one(theirs_ref, sib_in, sibling, send_s, recv_s)
    chip.start()
    pending.append(chip)
    chip.wait_recv()
    summed = mine_ref[...] + sib_in[...].astype(jnp.float32)
    pieces[...] = summed.astype(pieces.dtype).reshape(pieces.shape)

    for k in range(1, n):
        step(pieces.at[peer(k)], got.at[me], k, device("pcol", peer(k)), (send_a, recv_a)).start()
    for k in range(1, n):
        pending.append(step(pieces.at[peer(k)], got.at[me], k, device("pcol", peer(k)), (send_a, recv_a)))
    total = pieces[me].astype(jnp.float32)
    for k in range(1, n):
        step(pieces.at[me], got.at[sender(k)], k, device("pcol", sender(k)), (send_a, recv_a)).wait_recv()
        total = total + got[sender(k)].astype(jnp.float32)
    part_out[...] = total.astype(part_out.dtype)

    across = one(part_out, part_in, partner, send_b, recv_b)
    across.start()
    pending.append(across)
    across.wait_recv()
    coll[me] = (part_out[...].astype(jnp.float32) + part_in[...].astype(jnp.float32)).astype(coll.dtype)

    for k in range(1, n):
        step(coll.at[me], coll.at[me], k, device("pcol", peer(k)), (send_c, recv_c)).start()
    for k in range(1, n):
        pending.append(step(coll.at[me], coll.at[me], k, device("pcol", peer(k)), (send_c, recv_c)))
    for k in range(1, n):
        step(coll.at[me], coll.at[sender(k)], k, device("pcol", sender(k)), (send_c, recv_c)).wait_recv()

    join = one(coll, sib_out, sibling, send_d, recv_d)
    join.start()
    pending.append(join)
    join.wait_recv()
    out_ref[core] = coll[...]
    out_ref[1 - core] = sib_out[...]
    for sent in pending:
        sent.wait_send()


def modal_sum(mine, theirs, axes, sizes):
    n = sizes["pcol"]
    rows, width = mine.shape
    block = (n, rows // n, width)
    kernel = functools.partial(modal_sum_kernel, axes=axes, factors=factor_table(sizes))
    return pl.pallas_call(
        kernel,
        out_shape=jax.ShapeDtypeStruct((2,) + block, jnp.bfloat16),
        in_specs=[pl.BlockSpec(memory_space=pltpu.VMEM)] * 2,
        out_specs=pl.BlockSpec(memory_space=pltpu.VMEM),
        scratch_shapes=[
            pltpu.VMEM((rows, width), jnp.bfloat16),
            pltpu.VMEM(block, jnp.bfloat16),
            pltpu.VMEM(block, jnp.bfloat16),
            pltpu.VMEM(block, jnp.bfloat16),
            pltpu.VMEM(block[1:], jnp.bfloat16),
            pltpu.VMEM(block[1:], jnp.bfloat16),
            pltpu.VMEM(block, jnp.bfloat16),
            pltpu.SemaphoreType.DMA(()),
            pltpu.SemaphoreType.DMA(()),
            pltpu.SemaphoreType.DMA((n,)),
            pltpu.SemaphoreType.DMA((n,)),
            pltpu.SemaphoreType.DMA(()),
            pltpu.SemaphoreType.DMA(()),
            pltpu.SemaphoreType.DMA((n,)),
            pltpu.SemaphoreType.DMA((n,)),
            pltpu.SemaphoreType.DMA(()),
            pltpu.SemaphoreType.DMA(()),
        ],
        compiler_params=pltpu.CompilerParams(collective_id=102, has_side_effects=True),
    )(mine, theirs)


def gram_weighted_kernel(x_ref, shapes_ref, out_ref, got, coll, sib_coll, part_out, part_in, wbuf,
                         send_a, recv_a, send_b, recv_b, send_c, recv_c, send_d, recv_d, send_e,
                         recv_e, *, axes, factors):
    coords = {a: lax.axis_index(a) for a in axes}

    def value(f):
        axis, size, stride = factors[f]
        return lax.rem(coords[axis] // stride, size)

    def device(f, v):
        place = dict(coords)
        axis, size, stride = factors[f]
        place[axis] = place[axis] + (v - value(f)) * stride
        return tuple(place[a] for a in axes)

    n, n_col = factors["pl"][1], factors["pcol"][1]
    me, half, core, col = value("pl"), value("zh"), value("core"), value("pcol")
    partner, sibling = device("zh", 1 - half), device("core", 1 - core)

    def step(src, dst_at, k, to, sems):
        return pltpu.make_async_remote_copy(
            src_ref=src, dst_ref=dst_at, send_sem=sems[0].at[k], recv_sem=sems[1].at[k],
            device_id=to, device_id_type=MESH,
        )

    def one(src, dst, to, send_sem, recv_sem):
        return pltpu.make_async_remote_copy(
            src_ref=src, dst_ref=dst, send_sem=send_sem, recv_sem=recv_sem,
            device_id=to, device_id_type=MESH,
        )

    pending = []
    barrier = pltpu.get_barrier_semaphore()
    for k in range(1, n):
        pl.semaphore_signal(barrier, inc=1, device_id=device("pl", lax.rem(me + k, n)), device_id_type=MESH)
    for k in range(1, n_col):
        pl.semaphore_signal(
            barrier, inc=1, device_id=device("pcol", lax.rem(col + k, n_col)), device_id_type=MESH
        )
    pl.semaphore_signal(barrier, inc=1, device_id=partner, device_id_type=MESH)
    pl.semaphore_signal(barrier, inc=1, device_id=sibling, device_id_type=MESH)
    pl.semaphore_wait(barrier, n + n_col)

    peer = lambda k: lax.rem(me + k, n)
    sender = lambda k: lax.rem(me + n - k, n)
    for k in range(1, n):
        step(x_ref.at[peer(k)], got.at[me], k, device("pl", peer(k)), (send_a, recv_a)).start()
    for k in range(1, n):
        pending.append(step(x_ref.at[peer(k)], got.at[me], k, device("pl", peer(k)), (send_a, recv_a)))
    total = x_ref[me].astype(jnp.float32)
    for k in range(1, n):
        step(x_ref.at[me], got.at[sender(k)], k, device("pl", sender(k)), (send_a, recv_a)).wait_recv()
        total = total + got[sender(k)].astype(jnp.float32)
    part_out[...] = total.astype(part_out.dtype)

    across = one(part_out, part_in, partner, send_b, recv_b)
    across.start()
    pending.append(across)
    across.wait_recv()
    mine, theirs = part_out[...], part_in[...]
    coll[me] = jnp.stack([jnp.where(half == 0, mine, theirs), jnp.where(half == 0, theirs, mine)])

    for k in range(1, n):
        step(coll.at[me], coll.at[me], k, device("pl", peer(k)), (send_c, recv_c)).start()
    for k in range(1, n):
        pending.append(step(coll.at[me], coll.at[me], k, device("pl", peer(k)), (send_c, recv_c)))

    def to_sibling(chunk_at):
        return pltpu.make_async_remote_copy(
            src_ref=coll.at[chunk_at], dst_ref=sib_coll.at[chunk_at], send_sem=send_d.at[chunk_at],
            recv_sem=recv_d.at[chunk_at], device_id=sibling, device_id_type=MESH,
        )

    to_sibling(me).start()
    pending.append(to_sibling(me))
    for k in range(1, n):
        step(coll.at[me], coll.at[sender(k)], k, device("pl", sender(k)), (send_c, recv_c)).wait_recv()
        to_sibling(sender(k)).start()
        pending.append(to_sibling(sender(k)))

    chunk = coll.shape[-1]

    def weighted_block(blocks, h):
        acc = jnp.zeros((shapes_ref.shape[0], blocks.shape[2]), jnp.float32)
        for l in range(n):
            acc = acc + lax.dot_general(
                shapes_ref[:, l * chunk:(l + 1) * chunk], blocks[l, h],
                (((1,), (1,)), ((), ())), preferred_element_type=jnp.float32,
            )
        return acc

    own = [weighted_block(coll, h) for h in range(2)]
    for l in range(n):
        to_sibling(l).wait_recv()
    other = [weighted_block(sib_coll, h) for h in range(2)]
    parts = []
    for h in range(2):
        parts += [jnp.where(core == 0, own[h], other[h]), jnp.where(core == 0, other[h], own[h])]
    wbuf[col] = jnp.concatenate(parts, axis=1).astype(wbuf.dtype)

    wpeer = lambda k: lax.rem(col + k, n_col)
    wsender = lambda k: lax.rem(col + n_col - k, n_col)
    for k in range(1, n_col):
        step(wbuf.at[col], wbuf.at[col], k, device("pcol", wpeer(k)), (send_e, recv_e)).start()
    for k in range(1, n_col):
        pending.append(step(wbuf.at[col], wbuf.at[col], k, device("pcol", wpeer(k)), (send_e, recv_e)))
    for k in range(1, n_col):
        step(wbuf.at[col], wbuf.at[wsender(k)], k, device("pcol", wsender(k)), (send_e, recv_e)).wait_recv()
    width_w = wbuf.shape[2]
    for c in range(n_col):
        out_ref[:, c * width_w:(c + 1) * width_w] = wbuf[c]
    for sent in pending:
        sent.wait_send()


def gram_weighted(x, mode_shapes, axes, sizes):
    n, rows, width = x.shape
    n_col = sizes["pcol"]
    wshape = (n_col, mode_shapes.shape[0], 4 * rows)
    kernel = functools.partial(gram_weighted_kernel, axes=axes, factors=factor_table(sizes))
    return pl.pallas_call(
        kernel,
        out_shape=jax.ShapeDtypeStruct((wshape[1], n_col * wshape[2]), jnp.bfloat16),
        in_specs=[pl.BlockSpec(memory_space=pltpu.VMEM)] * 2,
        out_specs=pl.BlockSpec(memory_space=pltpu.VMEM),
        scratch_shapes=[
            pltpu.VMEM(x.shape, x.dtype),
            pltpu.VMEM((n, 2, rows, width), x.dtype),
            pltpu.VMEM((n, 2, rows, width), x.dtype),
            pltpu.VMEM((rows, width), x.dtype),
            pltpu.VMEM((rows, width), x.dtype),
            pltpu.VMEM(wshape, jnp.bfloat16),
            pltpu.SemaphoreType.DMA((n,)),
            pltpu.SemaphoreType.DMA((n,)),
            pltpu.SemaphoreType.DMA(()),
            pltpu.SemaphoreType.DMA(()),
            pltpu.SemaphoreType.DMA((n,)),
            pltpu.SemaphoreType.DMA((n,)),
            pltpu.SemaphoreType.DMA((n,)),
            pltpu.SemaphoreType.DMA((n,)),
            pltpu.SemaphoreType.DMA((n_col,)),
            pltpu.SemaphoreType.DMA((n_col,)),
        ],
        compiler_params=pltpu.CompilerParams(collective_id=103, has_side_effects=True),
    )(x, mode_shapes)


def fused_sum(x, axes, sizes, over, add_across, kernel_id):
    n, rows, width = x.shape
    block = (rows, width) if add_across else (2, rows, width)
    kernel = functools.partial(
        fused_sum_kernel, axes=axes, factors=factor_table(sizes), over=over, add_across=add_across
    )
    return pl.pallas_call(
        kernel,
        out_shape=jax.ShapeDtypeStruct((n,) + block, x.dtype),
        in_specs=[pl.BlockSpec(memory_space=pltpu.VMEM)],
        out_specs=pl.BlockSpec(memory_space=pltpu.VMEM),
        scratch_shapes=[
            pltpu.VMEM(x.shape, x.dtype),
            pltpu.VMEM((n,) + block, x.dtype),
            pltpu.VMEM((rows, width), x.dtype),
            pltpu.VMEM((rows, width), x.dtype),
            pltpu.SemaphoreType.DMA((n,)),
            pltpu.SemaphoreType.DMA((n,)),
            pltpu.SemaphoreType.DMA(()),
            pltpu.SemaphoreType.DMA(()),
            pltpu.SemaphoreType.DMA((n,)),
            pltpu.SemaphoreType.DMA((n,)),
        ],
        compiler_params=pltpu.CompilerParams(collective_id=kernel_id, has_side_effects=True),
    )(x)


class Exchanger:
    def __init__(self, axes, sizes):
        self.axes, self.factors, self.calls = axes, factor_table(sizes), 0

    def __call__(self, x, group, same):
        count = math.prod(self.factors[f][1] for f in group)
        block = x.shape if same else x.shape[1:]
        if count == 1:
            return x[None] if same else x
        kernel = functools.partial(
            exchange_kernel, axes=self.axes, factors=self.factors, group=group, same=same
        )
        self.calls += 1
        return pl.pallas_call(
            kernel,
            out_shape=jax.ShapeDtypeStruct((count,) + tuple(block), x.dtype),
            in_specs=[pl.BlockSpec(memory_space=pl.ANY)],
            out_specs=pl.BlockSpec(memory_space=pl.ANY),
            scratch_shapes=[
                pltpu.SemaphoreType.DMA((count,)),
                pltpu.SemaphoreType.DMA((count,)),
                pltpu.SemaphoreType.DMA(()),
            ],
            compiler_params=pltpu.CompilerParams(collective_id=self.calls, has_side_effects=True),
        )(x)


def make_body(axes, sizes):
    n_row, n_col, n_pl = sizes["prow"], sizes["pcol"], sizes["pl"]
    swap = [(c * n_col + r, r * n_col + c) for r in range(n_row) for c in range(n_col)]
    sibling = [(r, r ^ 1) for r in range(n_row)]
    n_zh = n_row // 2

    def beside_sibling(part, core):
        other = lax.ppermute(part, "prow", sibling)
        first, second = jnp.where(core == 0, part, other), jnp.where(core == 0, other, part)
        return jnp.concatenate([first, second], axis=0)

    def body(factor_cols, modal_at_loads, mode_shapes, natural_freq, damping):
        ex = Exchanger(axes, sizes)
        in_phase, quadrature = transfer_pair(natural_freq, damping)
        modes = modal_at_loads.shape[0]
        block = modes // (n_row * n_col)
        row, col = lax.axis_index("prow"), lax.axis_index("pcol")
        width = factor_cols.shape[1]
        core = row % 2
        own_modes = lax.dynamic_slice_in_dim(modal_at_loads, core * (modes // 2), modes // 2, 0)
        sib_modes = lax.dynamic_slice_in_dim(modal_at_loads, (1 - core) * (modes // 2), modes // 2, 0)
        mine = jnp.dot(own_modes, factor_cols, preferred_element_type=jnp.float32)
        theirs = jnp.dot(sib_modes, factor_cols, preferred_element_type=jnp.float32)
        modal_load = modal_sum(mine, theirs.astype(jnp.bfloat16), axes, sizes).reshape(modes, width)
        modal_wide = modal_load.astype(jnp.float32)
        pseudo = jnp.concatenate(
            [
                (in_phase[:, None] * modal_wide).astype(jnp.bfloat16),
                (quadrature[:, None] * modal_wide).astype(jnp.bfloat16),
            ],
            axis=1,
        )
        first_row = (col * n_row + row) * block
        own_pseudo = lax.dynamic_slice_in_dim(pseudo, first_row, block, 0)
        partial_gram = outer_rows(own_pseudo, pseudo).astype(jnp.bfloat16)
        chunk = modes // n_pl
        by_chunk = partial_gram.reshape(block, n_pl, chunk).transpose(1, 0, 2)
        half = modes // 2
        send_half = lax.dynamic_slice_in_dim(mode_shapes, (col % 2) * half, half, 1)
        panel_piece = lax.ppermute(send_half, ("prow", "pcol"), swap)
        panel_mine = lax.all_gather(panel_piece, "pl", axis=0, tiled=True)
        weighted = gram_weighted(by_chunk, mode_shapes, axes, sizes)
        panel_mine, weighted = lax.optimization_barrier((panel_mine, weighted))
        panel_other = lax.ppermute(panel_mine, "prow", sibling)
        weighted_mine = lax.dynamic_slice_in_dim(weighted, core * half, half, 1)
        weighted_other = lax.dynamic_slice_in_dim(weighted, (1 - core) * half, half, 1)
        return outer_rows(weighted_other, panel_other) + outer_rows(weighted_mine, panel_mine)

    return body


def solution(mesh):
    in_specs = (
        P(("prow", "pcol"), "pl"),
        P(None, ("prow", "pcol")),
        P(("prow", "pl"), None),
        P(),
        P(),
    )
    out_specs = P(("prow", "pl"), "pcol")
    axes = tuple(mesh.axis_names)
    body = make_body(axes, dict(mesh.shape))
    return jax.shard_map(body, mesh=mesh, in_specs=in_specs, out_specs=out_specs, check_vma=False)
```

```python
import functools
import math

import jax
import jax.numpy as jnp
from jax import lax
from jax.experimental import pallas as pl
from jax.experimental.pallas import tpu as pltpu
from jax.sharding import PartitionSpec as P

MESH = pl.DeviceIdType.MESH


def transfer_pair(natural_freq, damping):
    detuning = natural_freq * natural_freq - 1.0
    damper = 2.0 * damping * natural_freq
    modulus = detuning * detuning + damper * damper
    return (detuning / modulus, -damper / modulus)


def outer_rows(left_rows, right_rows):
    return lax.dot_general(
        left_rows, right_rows, (((1,), (1,)), ((), ())), preferred_element_type=jnp.float32
    )


def factor_table(sizes):
    return {
        "zh": ("prow", sizes["prow"] // 2, 2),
        "core": ("prow", 2, 1),
        "pcol": ("pcol", sizes["pcol"], 1),
        "pl": ("pl", sizes["pl"], 1),
    }


def exchange_kernel(x_ref, out_ref, send_sem, recv_sem, local_sem, *, axes, factors, group, same):
    coords = {a: lax.axis_index(a) for a in axes}

    def value(f):
        axis, size, stride = factors[f]
        return lax.rem(coords[axis] // stride, size)

    count = math.prod(factors[f][1] for f in group)
    me = 0
    for f in group:
        me = me * factors[f][1] + value(f)

    def device(member):
        place = dict(coords)
        for f in reversed(group):
            axis, size, stride = factors[f]
            place[axis] = place[axis] + (lax.rem(member, size) - value(f)) * stride
            member = member // size
        return tuple(place[a] for a in axes)

    def source(member):
        return x_ref if same else x_ref.at[member]

    def copy(offset):
        peer = lax.rem(me + offset, count)
        return pltpu.make_async_remote_copy(
            src_ref=source(peer),
            dst_ref=out_ref.at[me],
            send_sem=send_sem.at[offset],
            recv_sem=recv_sem.at[offset],
            device_id=device(peer),
            device_id_type=MESH,
        )

    def landing(offset):
        sender = lax.rem(me + count - offset, count)
        return pltpu.make_async_remote_copy(
            src_ref=source(me),
            dst_ref=out_ref.at[sender],
            send_sem=send_sem.at[offset],
            recv_sem=recv_sem.at[offset],
            device_id=device(sender),
            device_id_type=MESH,
        )

    local = pltpu.make_async_copy(source(me), out_ref.at[me], local_sem)
    local.start()
    barrier = pltpu.get_barrier_semaphore()
    for offset in range(1, count):
        peer = lax.rem(me + offset, count)
        pl.semaphore_signal(barrier, inc=1, device_id=device(peer), device_id_type=MESH)
    pl.semaphore_wait(barrier, count - 1)
    for offset in range(1, count):
        copy(offset).start()
    local.wait()
    for offset in range(1, count):
        copy(offset).wait_send()
    for offset in range(1, count):
        landing(offset).wait_recv()


def fused_sum_kernel(x_ref, out_ref, got, coll, part_out, part_in, send_a, recv_a, send_b, recv_b,
                     send_c, recv_c, *, axes, factors, over, add_across):
    coords = {a: lax.axis_index(a) for a in axes}

    def value(f):
        axis, size, stride = factors[f]
        return lax.rem(coords[axis] // stride, size)

    def device(f, v):
        place = dict(coords)
        axis, size, stride = factors[f]
        place[axis] = place[axis] + (v - value(f)) * stride
        return tuple(place[a] for a in axes)

    n = factors[over][1]
    me, half = value(over), value("zh")
    partner = device("zh", 1 - half)
    peer = lambda k: lax.rem(me + k, n)
    sender = lambda k: lax.rem(me + n - k, n)

    def step(src, dst_at, k, to, sems):
        return pltpu.make_async_remote_copy(
            src_ref=src, dst_ref=dst_at, send_sem=sems[0].at[k], recv_sem=sems[1].at[k],
            device_id=to, device_id_type=MESH,
        )

    barrier = pltpu.get_barrier_semaphore()
    for k in range(1, n):
        pl.semaphore_signal(barrier, inc=1, device_id=device(over, peer(k)), device_id_type=MESH)
    pl.semaphore_signal(barrier, inc=1, device_id=partner, device_id_type=MESH)
    pl.semaphore_wait(barrier, n)

    for k in range(1, n):
        step(x_ref.at[peer(k)], got.at[me], k, device(over, peer(k)), (send_a, recv_a)).start()
    for k in range(1, n):
        step(x_ref.at[peer(k)], got.at[me], k, device(over, peer(k)), (send_a, recv_a)).wait_send()
    for k in range(1, n):
        step(x_ref.at[me], got.at[sender(k)], k, device(over, sender(k)), (send_a, recv_a)).wait_recv()
    total = x_ref[me].astype(jnp.float32)
    for k in range(1, n):
        total = total + got[sender(k)].astype(jnp.float32)
    part_out[...] = total.astype(part_out.dtype)

    across = pltpu.make_async_remote_copy(
        src_ref=part_out, dst_ref=part_in, send_sem=send_b, recv_sem=recv_b,
        device_id=partner, device_id_type=MESH,
    )
    across.start()
    across.wait_send()
    across.wait_recv()
    if add_across:
        mine, theirs = part_out[...].astype(jnp.float32), part_in[...].astype(jnp.float32)
        coll[me] = (mine + theirs).astype(coll.dtype)
    else:
        mine, theirs = part_out[...], part_in[...]
        first = jnp.where(half == 0, mine, theirs)
        second = jnp.where(half == 0, theirs, mine)
        coll[me] = jnp.stack([first, second])

    for k in range(1, n):
        step(coll.at[me], coll.at[me], k, device(over, peer(k)), (send_c, recv_c)).start()
    for k in range(1, n):
        step(coll.at[me], coll.at[me], k, device(over, peer(k)), (send_c, recv_c)).wait_send()
    for k in range(1, n):
        step(coll.at[me], coll.at[sender(k)], k, device(over, sender(k)), (send_c, recv_c)).wait_recv()
    out_ref[...] = coll[...]


def modal_sum_kernel(mine_ref, theirs_ref, out_ref, sib_in, pieces, got, coll, part_out, part_in,
                     sib_out, send_s, recv_s, send_a, recv_a, send_b, recv_b, send_c, recv_c,
                     send_d, recv_d, *, axes, factors):
    coords = {a: lax.axis_index(a) for a in axes}

    def value(f):
        axis, size, stride = factors[f]
        return lax.rem(coords[axis] // stride, size)

    def device(f, v):
        place = dict(coords)
        axis, size, stride = factors[f]
        place[axis] = place[axis] + (v - value(f)) * stride
        return tuple(place[a] for a in axes)

    n = factors["pcol"][1]
    me, half, core = value("pcol"), value("zh"), value("core")
    partner, sibling = device("zh", 1 - half), device("core", 1 - core)
    peer = lambda k: lax.rem(me + k, n)
    sender = lambda k: lax.rem(me + n - k, n)

    def step(src, dst_at, k, to, sems):
        return pltpu.make_async_remote_copy(
            src_ref=src, dst_ref=dst_at, send_sem=sems[0].at[k], recv_sem=sems[1].at[k],
            device_id=to, device_id_type=MESH,
        )

    def one(src, dst, to, send_sem, recv_sem):
        return pltpu.make_async_remote_copy(
            src_ref=src, dst_ref=dst, send_sem=send_sem, recv_sem=recv_sem,
            device_id=to, device_id_type=MESH,
        )

    pending = []
    barrier = pltpu.get_barrier_semaphore()
    for k in range(1, n):
        pl.semaphore_signal(barrier, inc=1, device_id=device("pcol", peer(k)), device_id_type=MESH)
    pl.semaphore_signal(barrier, inc=1, device_id=partner, device_id_type=MESH)
    pl.semaphore_signal(barrier, inc=1, device_id=sibling, device_id_type=MESH)
    pl.semaphore_wait(barrier, n + 1)

    chip = one(theirs_ref, sib_in, sibling, send_s, recv_s)
    chip.start()
    pending.append(chip)
    chip.wait_recv()
    summed = mine_ref[...] + sib_in[...].astype(jnp.float32)
    pieces[...] = summed.astype(pieces.dtype).reshape(pieces.shape)

    for k in range(1, n):
        step(pieces.at[peer(k)], got.at[me], k, device("pcol", peer(k)), (send_a, recv_a)).start()
    for k in range(1, n):
        pending.append(step(pieces.at[peer(k)], got.at[me], k, device("pcol", peer(k)), (send_a, recv_a)))
    for k in range(1, n):
        step(pieces.at[me], got.at[sender(k)], k, device("pcol", sender(k)), (send_a, recv_a)).wait_recv()
    total = pieces[me].astype(jnp.float32)
    for k in range(1, n):
        total = total + got[sender(k)].astype(jnp.float32)
    part_out[...] = total.astype(part_out.dtype)

    across = one(part_out, part_in, partner, send_b, recv_b)
    across.start()
    pending.append(across)
    across.wait_recv()
    coll[me] = (part_out[...].astype(jnp.float32) + part_in[...].astype(jnp.float32)).astype(coll.dtype)

    for k in range(1, n):
        step(coll.at[me], coll.at[me], k, device("pcol", peer(k)), (send_c, recv_c)).start()
    for k in range(1, n):
        pending.append(step(coll.at[me], coll.at[me], k, device("pcol", peer(k)), (send_c, recv_c)))
    for k in range(1, n):
        step(coll.at[me], coll.at[sender(k)], k, device("pcol", sender(k)), (send_c, recv_c)).wait_recv()

    join = one(coll, sib_out, sibling, send_d, recv_d)
    join.start()
    pending.append(join)
    join.wait_recv()
    out_ref[core] = coll[...]
    out_ref[1 - core] = sib_out[...]
    for sent in pending:
        sent.wait_send()


def modal_sum(mine, theirs, axes, sizes):
    n = sizes["pcol"]
    rows, width = mine.shape
    block = (n, rows // n, width)
    kernel = functools.partial(modal_sum_kernel, axes=axes, factors=factor_table(sizes))
    return pl.pallas_call(
        kernel,
        out_shape=jax.ShapeDtypeStruct((2,) + block, jnp.bfloat16),
        in_specs=[pl.BlockSpec(memory_space=pltpu.VMEM)] * 2,
        out_specs=pl.BlockSpec(memory_space=pltpu.VMEM),
        scratch_shapes=[
            pltpu.VMEM((rows, width), jnp.bfloat16),
            pltpu.VMEM(block, jnp.bfloat16),
            pltpu.VMEM(block, jnp.bfloat16),
            pltpu.VMEM(block, jnp.bfloat16),
            pltpu.VMEM(block[1:], jnp.bfloat16),
            pltpu.VMEM(block[1:], jnp.bfloat16),
            pltpu.VMEM(block, jnp.bfloat16),
            pltpu.SemaphoreType.DMA(()),
            pltpu.SemaphoreType.DMA(()),
            pltpu.SemaphoreType.DMA((n,)),
            pltpu.SemaphoreType.DMA((n,)),
            pltpu.SemaphoreType.DMA(()),
            pltpu.SemaphoreType.DMA(()),
            pltpu.SemaphoreType.DMA((n,)),
            pltpu.SemaphoreType.DMA((n,)),
            pltpu.SemaphoreType.DMA(()),
            pltpu.SemaphoreType.DMA(()),
        ],
        compiler_params=pltpu.CompilerParams(collective_id=102, has_side_effects=True),
    )(mine, theirs)


def gram_weighted_kernel(x_ref, shapes_ref, out_ref, got, coll, sib_coll, part_out, part_in, wbuf,
                         send_a, recv_a, send_b, recv_b, send_c, recv_c, send_d, recv_d, send_e,
                         recv_e, *, axes, factors):
    coords = {a: lax.axis_index(a) for a in axes}

    def value(f):
        axis, size, stride = factors[f]
        return lax.rem(coords[axis] // stride, size)

    def device(f, v):
        place = dict(coords)
        axis, size, stride = factors[f]
        place[axis] = place[axis] + (v - value(f)) * stride
        return tuple(place[a] for a in axes)

    n, n_col = factors["pl"][1], factors["pcol"][1]
    me, half, core, col = value("pl"), value("zh"), value("core"), value("pcol")
    partner, sibling = device("zh", 1 - half), device("core", 1 - core)

    def step(src, dst_at, k, to, sems):
        return pltpu.make_async_remote_copy(
            src_ref=src, dst_ref=dst_at, send_sem=sems[0].at[k], recv_sem=sems[1].at[k],
            device_id=to, device_id_type=MESH,
        )

    def one(src, dst, to, send_sem, recv_sem):
        return pltpu.make_async_remote_copy(
            src_ref=src, dst_ref=dst, send_sem=send_sem, recv_sem=recv_sem,
            device_id=to, device_id_type=MESH,
        )

    pending = []
    barrier = pltpu.get_barrier_semaphore()
    for k in range(1, n):
        pl.semaphore_signal(barrier, inc=1, device_id=device("pl", lax.rem(me + k, n)), device_id_type=MESH)
    for k in range(1, n_col):
        pl.semaphore_signal(
            barrier, inc=1, device_id=device("pcol", lax.rem(col + k, n_col)), device_id_type=MESH
        )
    pl.semaphore_signal(barrier, inc=1, device_id=partner, device_id_type=MESH)
    pl.semaphore_signal(barrier, inc=1, device_id=sibling, device_id_type=MESH)
    pl.semaphore_wait(barrier, n + n_col)

    peer = lambda k: lax.rem(me + k, n)
    sender = lambda k: lax.rem(me + n - k, n)
    for k in range(1, n):
        step(x_ref.at[peer(k)], got.at[me], k, device("pl", peer(k)), (send_a, recv_a)).start()
    for k in range(1, n):
        pending.append(step(x_ref.at[peer(k)], got.at[me], k, device("pl", peer(k)), (send_a, recv_a)))
    for k in range(1, n):
        step(x_ref.at[me], got.at[sender(k)], k, device("pl", sender(k)), (send_a, recv_a)).wait_recv()
    total = x_ref[me].astype(jnp.float32)
    for k in range(1, n):
        total = total + got[sender(k)].astype(jnp.float32)
    part_out[...] = total.astype(part_out.dtype)

    across = one(part_out, part_in, partner, send_b, recv_b)
    across.start()
    pending.append(across)
    across.wait_recv()
    mine, theirs = part_out[...], part_in[...]
    coll[me] = jnp.stack([jnp.where(half == 0, mine, theirs), jnp.where(half == 0, theirs, mine)])

    for k in range(1, n):
        step(coll.at[me], coll.at[me], k, device("pl", peer(k)), (send_c, recv_c)).start()
    for k in range(1, n):
        pending.append(step(coll.at[me], coll.at[me], k, device("pl", peer(k)), (send_c, recv_c)))

    def to_sibling(chunk_at):
        return pltpu.make_async_remote_copy(
            src_ref=coll.at[chunk_at], dst_ref=sib_coll.at[chunk_at], send_sem=send_d.at[chunk_at],
            recv_sem=recv_d.at[chunk_at], device_id=sibling, device_id_type=MESH,
        )

    to_sibling(me).start()
    pending.append(to_sibling(me))
    for k in range(1, n):
        step(coll.at[me], coll.at[sender(k)], k, device("pl", sender(k)), (send_c, recv_c)).wait_recv()
        to_sibling(sender(k)).start()
        pending.append(to_sibling(sender(k)))

    chunk = coll.shape[-1]

    def weighted_block(blocks, h):
        acc = jnp.zeros((shapes_ref.shape[0], blocks.shape[2]), jnp.float32)
        for l in range(n):
            acc = acc + lax.dot_general(
                shapes_ref[:, l * chunk:(l + 1) * chunk], blocks[l, h],
                (((1,), (1,)), ((), ())), preferred_element_type=jnp.float32,
            )
        return acc

    own = [weighted_block(coll, h) for h in range(2)]
    wpeer = lambda k: lax.rem(col + k, n_col)
    wsender = lambda k: lax.rem(col + n_col - k, n_col)
    blocks_w = wbuf.shape[1]

    def w_copy(k, r, to_col, at_col):
        return pltpu.make_async_remote_copy(
            src_ref=wbuf.at[col, r], dst_ref=wbuf.at[at_col, r], send_sem=send_e.at[k * blocks_w + r],
            recv_sem=recv_e.at[k * blocks_w + r], device_id=device("pcol", to_col), device_id_type=MESH,
        )

    def send_blocks(values, first):
        for h in range(2):
            r = 2 * h + first
            wbuf[col, r] = values[h].astype(wbuf.dtype)
            for k in range(1, n_col):
                w_copy(k, r, wpeer(k), col).start()
                pending.append(w_copy(k, r, wpeer(k), col))

    send_blocks(own, core)
    for l in range(n):
        to_sibling(l).wait_recv()
    send_blocks([weighted_block(sib_coll, h) for h in range(2)], 1 - core)
    for k in range(1, n_col):
        for r in range(blocks_w):
            w_copy(k, r, wsender(k), wsender(k)).wait_recv()
    width_w = wbuf.shape[3]
    for c in range(n_col):
        for r in range(blocks_w):
            out_ref[:, (c * blocks_w + r) * width_w:(c * blocks_w + r + 1) * width_w] = wbuf[c, r]
    for sent in pending:
        sent.wait_send()


def gram_weighted(x, mode_shapes, axes, sizes):
    n, rows, width = x.shape
    n_col = sizes["pcol"]
    wshape = (n_col, 4, mode_shapes.shape[0], rows)
    kernel = functools.partial(gram_weighted_kernel, axes=axes, factors=factor_table(sizes))
    return pl.pallas_call(
        kernel,
        out_shape=jax.ShapeDtypeStruct((wshape[2], n_col * 4 * rows), jnp.bfloat16),
        in_specs=[pl.BlockSpec(memory_space=pltpu.VMEM)] * 2,
        out_specs=pl.BlockSpec(memory_space=pltpu.VMEM),
        scratch_shapes=[
            pltpu.VMEM(x.shape, x.dtype),
            pltpu.VMEM((n, 2, rows, width), x.dtype),
            pltpu.VMEM((n, 2, rows, width), x.dtype),
            pltpu.VMEM((rows, width), x.dtype),
            pltpu.VMEM((rows, width), x.dtype),
            pltpu.VMEM(wshape, jnp.bfloat16),
            pltpu.SemaphoreType.DMA((n,)),
            pltpu.SemaphoreType.DMA((n,)),
            pltpu.SemaphoreType.DMA(()),
            pltpu.SemaphoreType.DMA(()),
            pltpu.SemaphoreType.DMA((n,)),
            pltpu.SemaphoreType.DMA((n,)),
            pltpu.SemaphoreType.DMA((n,)),
            pltpu.SemaphoreType.DMA((n,)),
            pltpu.SemaphoreType.DMA((4 * n_col,)),
            pltpu.SemaphoreType.DMA((4 * n_col,)),
        ],
        compiler_params=pltpu.CompilerParams(collective_id=103, has_side_effects=True),
    )(x, mode_shapes)


def fused_sum(x, axes, sizes, over, add_across, kernel_id):
    n, rows, width = x.shape
    block = (rows, width) if add_across else (2, rows, width)
    kernel = functools.partial(
        fused_sum_kernel, axes=axes, factors=factor_table(sizes), over=over, add_across=add_across
    )
    return pl.pallas_call(
        kernel,
        out_shape=jax.ShapeDtypeStruct((n,) + block, x.dtype),
        in_specs=[pl.BlockSpec(memory_space=pltpu.VMEM)],
        out_specs=pl.BlockSpec(memory_space=pltpu.VMEM),
        scratch_shapes=[
            pltpu.VMEM(x.shape, x.dtype),
            pltpu.VMEM((n,) + block, x.dtype),
            pltpu.VMEM((rows, width), x.dtype),
            pltpu.VMEM((rows, width), x.dtype),
            pltpu.SemaphoreType.DMA((n,)),
            pltpu.SemaphoreType.DMA((n,)),
            pltpu.SemaphoreType.DMA(()),
            pltpu.SemaphoreType.DMA(()),
            pltpu.SemaphoreType.DMA((n,)),
            pltpu.SemaphoreType.DMA((n,)),
        ],
        compiler_params=pltpu.CompilerParams(collective_id=kernel_id, has_side_effects=True),
    )(x)


class Exchanger:
    def __init__(self, axes, sizes):
        self.axes, self.factors, self.calls = axes, factor_table(sizes), 0

    def __call__(self, x, group, same):
        count = math.prod(self.factors[f][1] for f in group)
        block = x.shape if same else x.shape[1:]
        if count == 1:
            return x[None] if same else x
        kernel = functools.partial(
            exchange_kernel, axes=self.axes, factors=self.factors, group=group, same=same
        )
        self.calls += 1
        return pl.pallas_call(
            kernel,
            out_shape=jax.ShapeDtypeStruct((count,) + tuple(block), x.dtype),
            in_specs=[pl.BlockSpec(memory_space=pl.ANY)],
            out_specs=pl.BlockSpec(memory_space=pl.ANY),
            scratch_shapes=[
                pltpu.SemaphoreType.DMA((count,)),
                pltpu.SemaphoreType.DMA((count,)),
                pltpu.SemaphoreType.DMA(()),
            ],
            compiler_params=pltpu.CompilerParams(collective_id=self.calls, has_side_effects=True),
        )(x)


def make_body(axes, sizes):
    n_row, n_col, n_pl = sizes["prow"], sizes["pcol"], sizes["pl"]
    swap = [(c * n_col + r, r * n_col + c) for r in range(n_row) for c in range(n_col)]
    sibling = [(r, r ^ 1) for r in range(n_row)]
    n_zh = n_row // 2

    def beside_sibling(part, core):
        other = lax.ppermute(part, "prow", sibling)
        first, second = jnp.where(core == 0, part, other), jnp.where(core == 0, other, part)
        return jnp.concatenate([first, second], axis=0)

    def body(factor_cols, modal_at_loads, mode_shapes, natural_freq, damping):
        ex = Exchanger(axes, sizes)
        in_phase, quadrature = transfer_pair(natural_freq, damping)
        modes = modal_at_loads.shape[0]
        block = modes // (n_row * n_col)
        row, col = lax.axis_index("prow"), lax.axis_index("pcol")
        width = factor_cols.shape[1]
        core = row % 2
        own_modes = lax.dynamic_slice_in_dim(modal_at_loads, core * (modes // 2), modes // 2, 0)
        sib_modes = lax.dynamic_slice_in_dim(modal_at_loads, (1 - core) * (modes // 2), modes // 2, 0)
        mine = jnp.dot(own_modes, factor_cols, preferred_element_type=jnp.float32)
        theirs = jnp.dot(sib_modes, factor_cols, preferred_element_type=jnp.float32)
        modal_load = modal_sum(mine, theirs.astype(jnp.bfloat16), axes, sizes).reshape(modes, width)
        modal_wide = modal_load.astype(jnp.float32)
        pseudo = jnp.concatenate(
            [
                (in_phase[:, None] * modal_wide).astype(jnp.bfloat16),
                (quadrature[:, None] * modal_wide).astype(jnp.bfloat16),
            ],
            axis=1,
        )
        first_row = (col * n_row + row) * block
        own_pseudo = lax.dynamic_slice_in_dim(pseudo, first_row, block, 0)
        partial_gram = outer_rows(own_pseudo, pseudo).astype(jnp.bfloat16)
        chunk = modes // n_pl
        by_chunk = partial_gram.reshape(block, n_pl, chunk).transpose(1, 0, 2)
        half = modes // 2
        send_half = lax.dynamic_slice_in_dim(mode_shapes, (col % 2) * half, half, 1)
        panel_piece = lax.ppermute(send_half, ("prow", "pcol"), swap)
        panel_mine = lax.all_gather(panel_piece, "pl", axis=0, tiled=True)
        weighted = gram_weighted(by_chunk, mode_shapes, axes, sizes)
        panel_mine, weighted = lax.optimization_barrier((panel_mine, weighted))
        panel_other = lax.ppermute(panel_mine, "prow", sibling)
        weighted_mine = lax.dynamic_slice_in_dim(weighted, core * half, half, 1)
        weighted_other = lax.dynamic_slice_in_dim(weighted, (1 - core) * half, half, 1)
        return outer_rows(weighted_other, panel_other) + outer_rows(weighted_mine, panel_mine)

    return body


def solution(mesh):
    in_specs = (
        P(("prow", "pcol"), "pl"),
        P(None, ("prow", "pcol")),
        P(("prow", "pl"), None),
        P(),
        P(),
    )
    out_specs = P(("prow", "pl"), "pcol")
    axes = tuple(mesh.axis_names)
    body = make_body(axes, dict(mesh.shape))
    return jax.shard_map(body, mesh=mesh, in_specs=in_specs, out_specs=out_specs, check_vma=False)
```

```python
import functools
import math

import jax
import jax.numpy as jnp
from jax import lax
from jax.experimental import pallas as pl
from jax.experimental.pallas import tpu as pltpu
from jax.sharding import PartitionSpec as P

MESH = pl.DeviceIdType.MESH


def transfer_pair(natural_freq, damping):
    detuning = natural_freq * natural_freq - 1.0
    damper = 2.0 * damping * natural_freq
    modulus = detuning * detuning + damper * damper
    return (detuning / modulus, -damper / modulus)


def outer_rows(left_rows, right_rows):
    return lax.dot_general(
        left_rows, right_rows, (((1,), (1,)), ((), ())), preferred_element_type=jnp.float32
    )


def factor_table(sizes):
    return {
        "zh": ("prow", sizes["prow"] // 2, 2),
        "core": ("prow", 2, 1),
        "pcol": ("pcol", sizes["pcol"], 1),
        "pl": ("pl", sizes["pl"], 1),
    }


def exchange_kernel(x_ref, out_ref, send_sem, recv_sem, local_sem, *, axes, factors, group, same):
    coords = {a: lax.axis_index(a) for a in axes}

    def value(f):
        axis, size, stride = factors[f]
        return lax.rem(coords[axis] // stride, size)

    count = math.prod(factors[f][1] for f in group)
    me = 0
    for f in group:
        me = me * factors[f][1] + value(f)

    def device(member):
        place = dict(coords)
        for f in reversed(group):
            axis, size, stride = factors[f]
            place[axis] = place[axis] + (lax.rem(member, size) - value(f)) * stride
            member = member // size
        return tuple(place[a] for a in axes)

    def source(member):
        return x_ref if same else x_ref.at[member]

    def copy(offset):
        peer = lax.rem(me + offset, count)
        return pltpu.make_async_remote_copy(
            src_ref=source(peer),
            dst_ref=out_ref.at[me],
            send_sem=send_sem.at[offset],
            recv_sem=recv_sem.at[offset],
            device_id=device(peer),
            device_id_type=MESH,
        )

    def landing(offset):
        sender = lax.rem(me + count - offset, count)
        return pltpu.make_async_remote_copy(
            src_ref=source(me),
            dst_ref=out_ref.at[sender],
            send_sem=send_sem.at[offset],
            recv_sem=recv_sem.at[offset],
            device_id=device(sender),
            device_id_type=MESH,
        )

    local = pltpu.make_async_copy(source(me), out_ref.at[me], local_sem)
    local.start()
    barrier = pltpu.get_barrier_semaphore()
    for offset in range(1, count):
        peer = lax.rem(me + offset, count)
        pl.semaphore_signal(barrier, inc=1, device_id=device(peer), device_id_type=MESH)
    pl.semaphore_wait(barrier, count - 1)
    for offset in range(1, count):
        copy(offset).start()
    local.wait()
    for offset in range(1, count):
        copy(offset).wait_send()
    for offset in range(1, count):
        landing(offset).wait_recv()


def fused_sum_kernel(x_ref, out_ref, got, coll, part_out, part_in, send_a, recv_a, send_b, recv_b,
                     send_c, recv_c, *, axes, factors, over, add_across):
    coords = {a: lax.axis_index(a) for a in axes}

    def value(f):
        axis, size, stride = factors[f]
        return lax.rem(coords[axis] // stride, size)

    def device(f, v):
        place = dict(coords)
        axis, size, stride = factors[f]
        place[axis] = place[axis] + (v - value(f)) * stride
        return tuple(place[a] for a in axes)

    n = factors[over][1]
    me, half = value(over), value("zh")
    partner = device("zh", 1 - half)
    peer = lambda k: lax.rem(me + k, n)
    sender = lambda k: lax.rem(me + n - k, n)

    def step(src, dst_at, k, to, sems):
        return pltpu.make_async_remote_copy(
            src_ref=src, dst_ref=dst_at, send_sem=sems[0].at[k], recv_sem=sems[1].at[k],
            device_id=to, device_id_type=MESH,
        )

    barrier = pltpu.get_barrier_semaphore()
    for k in range(1, n):
        pl.semaphore_signal(barrier, inc=1, device_id=device(over, peer(k)), device_id_type=MESH)
    pl.semaphore_signal(barrier, inc=1, device_id=partner, device_id_type=MESH)
    pl.semaphore_wait(barrier, n)

    for k in range(1, n):
        step(x_ref.at[peer(k)], got.at[me], k, device(over, peer(k)), (send_a, recv_a)).start()
    for k in range(1, n):
        step(x_ref.at[peer(k)], got.at[me], k, device(over, peer(k)), (send_a, recv_a)).wait_send()
    for k in range(1, n):
        step(x_ref.at[me], got.at[sender(k)], k, device(over, sender(k)), (send_a, recv_a)).wait_recv()
    total = x_ref[me].astype(jnp.float32)
    for k in range(1, n):
        total = total + got[sender(k)].astype(jnp.float32)
    part_out[...] = total.astype(part_out.dtype)

    across = pltpu.make_async_remote_copy(
        src_ref=part_out, dst_ref=part_in, send_sem=send_b, recv_sem=recv_b,
        device_id=partner, device_id_type=MESH,
    )
    across.start()
    across.wait_send()
    across.wait_recv()
    if add_across:
        mine, theirs = part_out[...].astype(jnp.float32), part_in[...].astype(jnp.float32)
        coll[me] = (mine + theirs).astype(coll.dtype)
    else:
        mine, theirs = part_out[...], part_in[...]
        first = jnp.where(half == 0, mine, theirs)
        second = jnp.where(half == 0, theirs, mine)
        coll[me] = jnp.stack([first, second])

    for k in range(1, n):
        step(coll.at[me], coll.at[me], k, device(over, peer(k)), (send_c, recv_c)).start()
    for k in range(1, n):
        step(coll.at[me], coll.at[me], k, device(over, peer(k)), (send_c, recv_c)).wait_send()
    for k in range(1, n):
        step(coll.at[me], coll.at[sender(k)], k, device(over, sender(k)), (send_c, recv_c)).wait_recv()
    out_ref[...] = coll[...]


def modal_sum_kernel(mine_ref, theirs_ref, out_ref, sib_in, pieces, got, coll, part_out, part_in,
                     sib_out, send_s, recv_s, send_a, recv_a, send_b, recv_b, send_c, recv_c,
                     send_d, recv_d, *, axes, factors):
    coords = {a: lax.axis_index(a) for a in axes}

    def value(f):
        axis, size, stride = factors[f]
        return lax.rem(coords[axis] // stride, size)

    def device(f, v):
        place = dict(coords)
        axis, size, stride = factors[f]
        place[axis] = place[axis] + (v - value(f)) * stride
        return tuple(place[a] for a in axes)

    n = factors["pcol"][1]
    me, half, core = value("pcol"), value("zh"), value("core")
    partner, sibling = device("zh", 1 - half), device("core", 1 - core)
    peer = lambda k: lax.rem(me + k, n)
    sender = lambda k: lax.rem(me + n - k, n)

    def step(src, dst_at, k, to, sems):
        return pltpu.make_async_remote_copy(
            src_ref=src, dst_ref=dst_at, send_sem=sems[0].at[k], recv_sem=sems[1].at[k],
            device_id=to, device_id_type=MESH,
        )

    def one(src, dst, to, send_sem, recv_sem):
        return pltpu.make_async_remote_copy(
            src_ref=src, dst_ref=dst, send_sem=send_sem, recv_sem=recv_sem,
            device_id=to, device_id_type=MESH,
        )

    pending = []
    barrier = pltpu.get_barrier_semaphore()
    for k in range(1, n):
        pl.semaphore_signal(barrier, inc=1, device_id=device("pcol", peer(k)), device_id_type=MESH)
    pl.semaphore_signal(barrier, inc=1, device_id=partner, device_id_type=MESH)
    pl.semaphore_signal(barrier, inc=1, device_id=sibling, device_id_type=MESH)
    pl.semaphore_wait(barrier, n + 1)

    chip = one(theirs_ref, sib_in, sibling, send_s, recv_s)
    chip.start()
    pending.append(chip)
    chip.wait_recv()
    summed = mine_ref[...] + sib_in[...].astype(jnp.float32)
    pieces[...] = summed.astype(pieces.dtype).reshape(pieces.shape)

    for k in range(1, n):
        step(pieces.at[peer(k)], got.at[me], k, device("pcol", peer(k)), (send_a, recv_a)).start()
    for k in range(1, n):
        pending.append(step(pieces.at[peer(k)], got.at[me], k, device("pcol", peer(k)), (send_a, recv_a)))
    for k in range(1, n):
        step(pieces.at[me], got.at[sender(k)], k, device("pcol", sender(k)), (send_a, recv_a)).wait_recv()
    total = pieces[me].astype(jnp.float32)
    for k in range(1, n):
        total = total + got[sender(k)].astype(jnp.float32)
    part_out[...] = total.astype(part_out.dtype)

    across = one(part_out, part_in, partner, send_b, recv_b)
    across.start()
    pending.append(across)
    across.wait_recv()
    coll[me] = (part_out[...].astype(jnp.float32) + part_in[...].astype(jnp.float32)).astype(coll.dtype)

    for k in range(1, n):
        step(coll.at[me], coll.at[me], k, device("pcol", peer(k)), (send_c, recv_c)).start()
    for k in range(1, n):
        pending.append(step(coll.at[me], coll.at[me], k, device("pcol", peer(k)), (send_c, recv_c)))
    for k in range(1, n):
        step(coll.at[me], coll.at[sender(k)], k, device("pcol", sender(k)), (send_c, recv_c)).wait_recv()

    join = one(coll, sib_out, sibling, send_d, recv_d)
    join.start()
    pending.append(join)
    join.wait_recv()
    out_ref[core] = coll[...]
    out_ref[1 - core] = sib_out[...]
    for sent in pending:
        sent.wait_send()


def modal_sum(mine, theirs, axes, sizes):
    n = sizes["pcol"]
    rows, width = mine.shape
    block = (n, rows // n, width)
    kernel = functools.partial(modal_sum_kernel, axes=axes, factors=factor_table(sizes))
    return pl.pallas_call(
        kernel,
        out_shape=jax.ShapeDtypeStruct((2,) + block, jnp.bfloat16),
        in_specs=[pl.BlockSpec(memory_space=pltpu.VMEM)] * 2,
        out_specs=pl.BlockSpec(memory_space=pltpu.VMEM),
        scratch_shapes=[
            pltpu.VMEM((rows, width), jnp.bfloat16),
            pltpu.VMEM(block, jnp.bfloat16),
            pltpu.VMEM(block, jnp.bfloat16),
            pltpu.VMEM(block, jnp.bfloat16),
            pltpu.VMEM(block[1:], jnp.bfloat16),
            pltpu.VMEM(block[1:], jnp.bfloat16),
            pltpu.VMEM(block, jnp.bfloat16),
            pltpu.SemaphoreType.DMA(()),
            pltpu.SemaphoreType.DMA(()),
            pltpu.SemaphoreType.DMA((n,)),
            pltpu.SemaphoreType.DMA((n,)),
            pltpu.SemaphoreType.DMA(()),
            pltpu.SemaphoreType.DMA(()),
            pltpu.SemaphoreType.DMA((n,)),
            pltpu.SemaphoreType.DMA((n,)),
            pltpu.SemaphoreType.DMA(()),
            pltpu.SemaphoreType.DMA(()),
        ],
        compiler_params=pltpu.CompilerParams(collective_id=102, has_side_effects=True),
    )(mine, theirs)


def gram_weighted_kernel(x_ref, shapes_ref, out_ref, got, coll, sib_coll, part_out, part_in, wbuf,
                         send_a, recv_a, send_b, recv_b, send_c, recv_c, send_d, recv_d, send_e,
                         recv_e, *, axes, factors):
    coords = {a: lax.axis_index(a) for a in axes}

    def value(f):
        axis, size, stride = factors[f]
        return lax.rem(coords[axis] // stride, size)

    def device(f, v):
        place = dict(coords)
        axis, size, stride = factors[f]
        place[axis] = place[axis] + (v - value(f)) * stride
        return tuple(place[a] for a in axes)

    n, n_col = factors["pl"][1], factors["pcol"][1]
    me, half, core, col = value("pl"), value("zh"), value("core"), value("pcol")
    partner, sibling = device("zh", 1 - half), device("core", 1 - core)

    def step(src, dst_at, k, to, sems):
        return pltpu.make_async_remote_copy(
            src_ref=src, dst_ref=dst_at, send_sem=sems[0].at[k], recv_sem=sems[1].at[k],
            device_id=to, device_id_type=MESH,
        )

    def one(src, dst, to, send_sem, recv_sem):
        return pltpu.make_async_remote_copy(
            src_ref=src, dst_ref=dst, send_sem=send_sem, recv_sem=recv_sem,
            device_id=to, device_id_type=MESH,
        )

    pending = []
    barrier = pltpu.get_barrier_semaphore()
    for k in range(1, n):
        pl.semaphore_signal(barrier, inc=1, device_id=device("pl", lax.rem(me + k, n)), device_id_type=MESH)
    for k in range(1, n_col):
        pl.semaphore_signal(
            barrier, inc=1, device_id=device("pcol", lax.rem(col + k, n_col)), device_id_type=MESH
        )
    pl.semaphore_signal(barrier, inc=1, device_id=partner, device_id_type=MESH)
    pl.semaphore_signal(barrier, inc=1, device_id=sibling, device_id_type=MESH)
    pl.semaphore_wait(barrier, n + n_col)

    peer = lambda k: lax.rem(me + k, n)
    sender = lambda k: lax.rem(me + n - k, n)
    for k in range(1, n):
        step(x_ref.at[peer(k)], got.at[me], k, device("pl", peer(k)), (send_a, recv_a)).start()
    for k in range(1, n):
        pending.append(step(x_ref.at[peer(k)], got.at[me], k, device("pl", peer(k)), (send_a, recv_a)))
    for k in range(1, n):
        step(x_ref.at[me], got.at[sender(k)], k, device("pl", sender(k)), (send_a, recv_a)).wait_recv()
    total = x_ref[me].astype(jnp.float32)
    for k in range(1, n):
        total = total + got[sender(k)].astype(jnp.float32)
    part_out[...] = total.astype(part_out.dtype)

    across = one(part_out, part_in, partner, send_b, recv_b)
    across.start()
    pending.append(across)
    across.wait_recv()
    mine, theirs = part_out[...], part_in[...]
    coll[me] = jnp.stack([jnp.where(half == 0, mine, theirs), jnp.where(half == 0, theirs, mine)])

    for k in range(1, n):
        step(coll.at[me], coll.at[me], k, device("pl", peer(k)), (send_c, recv_c)).start()
    for k in range(1, n):
        pending.append(step(coll.at[me], coll.at[me], k, device("pl", peer(k)), (send_c, recv_c)))

    def to_sibling(chunk_at):
        return pltpu.make_async_remote_copy(
            src_ref=coll.at[chunk_at], dst_ref=sib_coll.at[chunk_at], send_sem=send_d.at[chunk_at],
            recv_sem=recv_d.at[chunk_at], device_id=sibling, device_id_type=MESH,
        )

    to_sibling(me).start()
    pending.append(to_sibling(me))
    for k in range(1, n):
        step(coll.at[me], coll.at[sender(k)], k, device("pl", sender(k)), (send_c, recv_c)).wait_recv()
        to_sibling(sender(k)).start()
        pending.append(to_sibling(sender(k)))

    chunk = coll.shape[-1]

    def weighted_block(blocks, h):
        acc = jnp.zeros((shapes_ref.shape[0], blocks.shape[2]), jnp.float32)
        for l in range(n):
            acc = acc + lax.dot_general(
                shapes_ref[:, l * chunk:(l + 1) * chunk], blocks[l, h],
                (((1,), (1,)), ((), ())), preferred_element_type=jnp.float32,
            )
        return acc

    own = [weighted_block(coll, h) for h in range(2)]
    wpeer = lambda k: lax.rem(col + k, n_col)
    wsender = lambda k: lax.rem(col + n_col - k, n_col)
    blocks_w = wbuf.shape[1]

    def w_copy(k, r, to_col, at_col):
        return pltpu.make_async_remote_copy(
            src_ref=wbuf.at[col, r], dst_ref=wbuf.at[at_col, r], send_sem=send_e.at[k * blocks_w + r],
            recv_sem=recv_e.at[k * blocks_w + r], device_id=device("pcol", to_col), device_id_type=MESH,
        )

    def send_blocks(values, first):
        for h in range(2):
            r = 2 * h + first
            wbuf[col, r] = values[h].astype(wbuf.dtype)
            for k in range(1, n_col):
                w_copy(k, r, wpeer(k), col).start()
                pending.append(w_copy(k, r, wpeer(k), col))

    send_blocks(own, core)
    other = [jnp.zeros((shapes_ref.shape[0], sib_coll.shape[2]), jnp.float32) for h in range(2)]
    for l in range(n):
        to_sibling(l).wait_recv()
        columns = shapes_ref[:, l * chunk:(l + 1) * chunk]
        other = [
            other[h] + lax.dot_general(
                columns, sib_coll[l, h], (((1,), (1,)), ((), ())), preferred_element_type=jnp.float32
            )
            for h in range(2)
        ]
    send_blocks(other, 1 - core)
    for k in range(1, n_col):
        for r in range(blocks_w):
            w_copy(k, r, wsender(k), wsender(k)).wait_recv()
    width_w = wbuf.shape[3]
    for c in range(n_col):
        for r in range(blocks_w):
            out_ref[:, (c * blocks_w + r) * width_w:(c * blocks_w + r + 1) * width_w] = wbuf[c, r]
    for sent in pending:
        sent.wait_send()


def gram_weighted(x, mode_shapes, axes, sizes):
    n, rows, width = x.shape
    n_col = sizes["pcol"]
    wshape = (n_col, 4, mode_shapes.shape[0], rows)
    kernel = functools.partial(gram_weighted_kernel, axes=axes, factors=factor_table(sizes))
    return pl.pallas_call(
        kernel,
        out_shape=jax.ShapeDtypeStruct((wshape[2], n_col * 4 * rows), jnp.bfloat16),
        in_specs=[pl.BlockSpec(memory_space=pltpu.VMEM)] * 2,
        out_specs=pl.BlockSpec(memory_space=pltpu.VMEM),
        scratch_shapes=[
            pltpu.VMEM(x.shape, x.dtype),
            pltpu.VMEM((n, 2, rows, width), x.dtype),
            pltpu.VMEM((n, 2, rows, width), x.dtype),
            pltpu.VMEM((rows, width), x.dtype),
            pltpu.VMEM((rows, width), x.dtype),
            pltpu.VMEM(wshape, jnp.bfloat16),
            pltpu.SemaphoreType.DMA((n,)),
            pltpu.SemaphoreType.DMA((n,)),
            pltpu.SemaphoreType.DMA(()),
            pltpu.SemaphoreType.DMA(()),
            pltpu.SemaphoreType.DMA((n,)),
            pltpu.SemaphoreType.DMA((n,)),
            pltpu.SemaphoreType.DMA((n,)),
            pltpu.SemaphoreType.DMA((n,)),
            pltpu.SemaphoreType.DMA((4 * n_col,)),
            pltpu.SemaphoreType.DMA((4 * n_col,)),
        ],
        compiler_params=pltpu.CompilerParams(collective_id=103, has_side_effects=True),
    )(x, mode_shapes)


def fused_sum(x, axes, sizes, over, add_across, kernel_id):
    n, rows, width = x.shape
    block = (rows, width) if add_across else (2, rows, width)
    kernel = functools.partial(
        fused_sum_kernel, axes=axes, factors=factor_table(sizes), over=over, add_across=add_across
    )
    return pl.pallas_call(
        kernel,
        out_shape=jax.ShapeDtypeStruct((n,) + block, x.dtype),
        in_specs=[pl.BlockSpec(memory_space=pltpu.VMEM)],
        out_specs=pl.BlockSpec(memory_space=pltpu.VMEM),
        scratch_shapes=[
            pltpu.VMEM(x.shape, x.dtype),
            pltpu.VMEM((n,) + block, x.dtype),
            pltpu.VMEM((rows, width), x.dtype),
            pltpu.VMEM((rows, width), x.dtype),
            pltpu.SemaphoreType.DMA((n,)),
            pltpu.SemaphoreType.DMA((n,)),
            pltpu.SemaphoreType.DMA(()),
            pltpu.SemaphoreType.DMA(()),
            pltpu.SemaphoreType.DMA((n,)),
            pltpu.SemaphoreType.DMA((n,)),
        ],
        compiler_params=pltpu.CompilerParams(collective_id=kernel_id, has_side_effects=True),
    )(x)


class Exchanger:
    def __init__(self, axes, sizes):
        self.axes, self.factors, self.calls = axes, factor_table(sizes), 0

    def __call__(self, x, group, same):
        count = math.prod(self.factors[f][1] for f in group)
        block = x.shape if same else x.shape[1:]
        if count == 1:
            return x[None] if same else x
        kernel = functools.partial(
            exchange_kernel, axes=self.axes, factors=self.factors, group=group, same=same
        )
        self.calls += 1
        return pl.pallas_call(
            kernel,
            out_shape=jax.ShapeDtypeStruct((count,) + tuple(block), x.dtype),
            in_specs=[pl.BlockSpec(memory_space=pl.ANY)],
            out_specs=pl.BlockSpec(memory_space=pl.ANY),
            scratch_shapes=[
                pltpu.SemaphoreType.DMA((count,)),
                pltpu.SemaphoreType.DMA((count,)),
                pltpu.SemaphoreType.DMA(()),
            ],
            compiler_params=pltpu.CompilerParams(collective_id=self.calls, has_side_effects=True),
        )(x)


def make_body(axes, sizes):
    n_row, n_col, n_pl = sizes["prow"], sizes["pcol"], sizes["pl"]
    swap = [(c * n_col + r, r * n_col + c) for r in range(n_row) for c in range(n_col)]
    sibling = [(r, r ^ 1) for r in range(n_row)]
    n_zh = n_row // 2

    def beside_sibling(part, core):
        other = lax.ppermute(part, "prow", sibling)
        first, second = jnp.where(core == 0, part, other), jnp.where(core == 0, other, part)
        return jnp.concatenate([first, second], axis=0)

    def body(factor_cols, modal_at_loads, mode_shapes, natural_freq, damping):
        ex = Exchanger(axes, sizes)
        in_phase, quadrature = transfer_pair(natural_freq, damping)
        modes = modal_at_loads.shape[0]
        block = modes // (n_row * n_col)
        row, col = lax.axis_index("prow"), lax.axis_index("pcol")
        width = factor_cols.shape[1]
        core = row % 2
        own_modes = lax.dynamic_slice_in_dim(modal_at_loads, core * (modes // 2), modes // 2, 0)
        sib_modes = lax.dynamic_slice_in_dim(modal_at_loads, (1 - core) * (modes // 2), modes // 2, 0)
        mine = jnp.dot(own_modes, factor_cols, preferred_element_type=jnp.float32)
        theirs = jnp.dot(sib_modes, factor_cols, preferred_element_type=jnp.float32)
        modal_load = modal_sum(mine, theirs.astype(jnp.bfloat16), axes, sizes).reshape(modes, width)
        modal_wide = modal_load.astype(jnp.float32)
        pseudo = jnp.concatenate(
            [
                (in_phase[:, None] * modal_wide).astype(jnp.bfloat16),
                (quadrature[:, None] * modal_wide).astype(jnp.bfloat16),
            ],
            axis=1,
        )
        first_row = (col * n_row + row) * block
        own_pseudo = lax.dynamic_slice_in_dim(pseudo, first_row, block, 0)
        partial_gram = outer_rows(own_pseudo, pseudo).astype(jnp.bfloat16)
        chunk = modes // n_pl
        by_chunk = partial_gram.reshape(block, n_pl, chunk).transpose(1, 0, 2)
        half = modes // 2
        send_half = lax.dynamic_slice_in_dim(mode_shapes, (col % 2) * half, half, 1)
        panel_piece = lax.ppermute(send_half, ("prow", "pcol"), swap)
        panel_mine = lax.all_gather(panel_piece, "pl", axis=0, tiled=True)
        weighted = gram_weighted(by_chunk, mode_shapes, axes, sizes)
        panel_mine, weighted = lax.optimization_barrier((panel_mine, weighted))
        panel_other = lax.ppermute(panel_mine, "prow", sibling)
        weighted_mine = lax.dynamic_slice_in_dim(weighted, core * half, half, 1)
        weighted_other = lax.dynamic_slice_in_dim(weighted, (1 - core) * half, half, 1)
        return outer_rows(weighted_other, panel_other) + outer_rows(weighted_mine, panel_mine)

    return body


def solution(mesh):
    in_specs = (
        P(("prow", "pcol"), "pl"),
        P(None, ("prow", "pcol")),
        P(("prow", "pl"), None),
        P(),
        P(),
    )
    out_specs = P(("prow", "pl"), "pcol")
    axes = tuple(mesh.axis_names)
    body = make_body(axes, dict(mesh.shape))
    return jax.shard_map(body, mesh=mesh, in_specs=in_specs, out_specs=out_specs, check_vma=False)
```

```python
import functools
import math

import jax
import jax.numpy as jnp
from jax import lax
from jax.experimental import pallas as pl
from jax.experimental.pallas import tpu as pltpu
from jax.sharding import PartitionSpec as P

MESH = pl.DeviceIdType.MESH


def transfer_pair(natural_freq, damping):
    detuning = natural_freq * natural_freq - 1.0
    damper = 2.0 * damping * natural_freq
    modulus = detuning * detuning + damper * damper
    return (detuning / modulus, -damper / modulus)


def outer_rows(left_rows, right_rows):
    return lax.dot_general(
        left_rows, right_rows, (((1,), (1,)), ((), ())), preferred_element_type=jnp.float32
    )


def factor_table(sizes):
    return {
        "zh": ("prow", sizes["prow"] // 2, 2),
        "core": ("prow", 2, 1),
        "pcol": ("pcol", sizes["pcol"], 1),
        "pl": ("pl", sizes["pl"], 1),
    }


def exchange_kernel(x_ref, out_ref, send_sem, recv_sem, local_sem, *, axes, factors, group, same):
    coords = {a: lax.axis_index(a) for a in axes}

    def value(f):
        axis, size, stride = factors[f]
        return lax.rem(coords[axis] // stride, size)

    count = math.prod(factors[f][1] for f in group)
    me = 0
    for f in group:
        me = me * factors[f][1] + value(f)

    def device(member):
        place = dict(coords)
        for f in reversed(group):
            axis, size, stride = factors[f]
            place[axis] = place[axis] + (lax.rem(member, size) - value(f)) * stride
            member = member // size
        return tuple(place[a] for a in axes)

    def source(member):
        return x_ref if same else x_ref.at[member]

    def copy(offset):
        peer = lax.rem(me + offset, count)
        return pltpu.make_async_remote_copy(
            src_ref=source(peer),
            dst_ref=out_ref.at[me],
            send_sem=send_sem.at[offset],
            recv_sem=recv_sem.at[offset],
            device_id=device(peer),
            device_id_type=MESH,
        )

    def landing(offset):
        sender = lax.rem(me + count - offset, count)
        return pltpu.make_async_remote_copy(
            src_ref=source(me),
            dst_ref=out_ref.at[sender],
            send_sem=send_sem.at[offset],
            recv_sem=recv_sem.at[offset],
            device_id=device(sender),
            device_id_type=MESH,
        )

    local = pltpu.make_async_copy(source(me), out_ref.at[me], local_sem)
    local.start()
    barrier = pltpu.get_barrier_semaphore()
    for offset in range(1, count):
        peer = lax.rem(me + offset, count)
        pl.semaphore_signal(barrier, inc=1, device_id=device(peer), device_id_type=MESH)
    pl.semaphore_wait(barrier, count - 1)
    for offset in range(1, count):
        copy(offset).start()
    local.wait()
    for offset in range(1, count):
        copy(offset).wait_send()
    for offset in range(1, count):
        landing(offset).wait_recv()


def fused_sum_kernel(x_ref, out_ref, got, coll, part_out, part_in, send_a, recv_a, send_b, recv_b,
                     send_c, recv_c, *, axes, factors, over, add_across):
    coords = {a: lax.axis_index(a) for a in axes}

    def value(f):
        axis, size, stride = factors[f]
        return lax.rem(coords[axis] // stride, size)

    def device(f, v):
        place = dict(coords)
        axis, size, stride = factors[f]
        place[axis] = place[axis] + (v - value(f)) * stride
        return tuple(place[a] for a in axes)

    n = factors[over][1]
    me, half = value(over), value("zh")
    partner = device("zh", 1 - half)
    peer = lambda k: lax.rem(me + k, n)
    sender = lambda k: lax.rem(me + n - k, n)

    def step(src, dst_at, k, to, sems):
        return pltpu.make_async_remote_copy(
            src_ref=src, dst_ref=dst_at, send_sem=sems[0].at[k], recv_sem=sems[1].at[k],
            device_id=to, device_id_type=MESH,
        )

    barrier = pltpu.get_barrier_semaphore()
    for k in range(1, n):
        pl.semaphore_signal(barrier, inc=1, device_id=device(over, peer(k)), device_id_type=MESH)
    pl.semaphore_signal(barrier, inc=1, device_id=partner, device_id_type=MESH)
    pl.semaphore_wait(barrier, n)

    for k in range(1, n):
        step(x_ref.at[peer(k)], got.at[me], k, device(over, peer(k)), (send_a, recv_a)).start()
    for k in range(1, n):
        step(x_ref.at[peer(k)], got.at[me], k, device(over, peer(k)), (send_a, recv_a)).wait_send()
    for k in range(1, n):
        step(x_ref.at[me], got.at[sender(k)], k, device(over, sender(k)), (send_a, recv_a)).wait_recv()
    total = x_ref[me].astype(jnp.float32)
    for k in range(1, n):
        total = total + got[sender(k)].astype(jnp.float32)
    part_out[...] = total.astype(part_out.dtype)

    across = pltpu.make_async_remote_copy(
        src_ref=part_out, dst_ref=part_in, send_sem=send_b, recv_sem=recv_b,
        device_id=partner, device_id_type=MESH,
    )
    across.start()
    across.wait_send()
    across.wait_recv()
    if add_across:
        mine, theirs = part_out[...].astype(jnp.float32), part_in[...].astype(jnp.float32)
        coll[me] = (mine + theirs).astype(coll.dtype)
    else:
        mine, theirs = part_out[...], part_in[...]
        first = jnp.where(half == 0, mine, theirs)
        second = jnp.where(half == 0, theirs, mine)
        coll[me] = jnp.stack([first, second])

    for k in range(1, n):
        step(coll.at[me], coll.at[me], k, device(over, peer(k)), (send_c, recv_c)).start()
    for k in range(1, n):
        step(coll.at[me], coll.at[me], k, device(over, peer(k)), (send_c, recv_c)).wait_send()
    for k in range(1, n):
        step(coll.at[me], coll.at[sender(k)], k, device(over, sender(k)), (send_c, recv_c)).wait_recv()
    out_ref[...] = coll[...]


def modal_sum_kernel(mine_ref, theirs_ref, out_ref, sib_in, pieces, got, coll, part_out, part_in,
                     sib_out, send_s, recv_s, send_a, recv_a, send_b, recv_b, send_c, recv_c,
                     send_d, recv_d, *, axes, factors):
    coords = {a: lax.axis_index(a) for a in axes}

    def value(f):
        axis, size, stride = factors[f]
        return lax.rem(coords[axis] // stride, size)

    def device(f, v):
        place = dict(coords)
        axis, size, stride = factors[f]
        place[axis] = place[axis] + (v - value(f)) * stride
        return tuple(place[a] for a in axes)

    n = factors["pcol"][1]
    me, half, core = value("pcol"), value("zh"), value("core")
    partner, sibling = device("zh", 1 - half), device("core", 1 - core)
    peer = lambda k: lax.rem(me + k, n)
    sender = lambda k: lax.rem(me + n - k, n)

    def step(src, dst_at, k, to, sems):
        return pltpu.make_async_remote_copy(
            src_ref=src, dst_ref=dst_at, send_sem=sems[0].at[k], recv_sem=sems[1].at[k],
            device_id=to, device_id_type=MESH,
        )

    def one(src, dst, to, send_sem, recv_sem):
        return pltpu.make_async_remote_copy(
            src_ref=src, dst_ref=dst, send_sem=send_sem, recv_sem=recv_sem,
            device_id=to, device_id_type=MESH,
        )

    pending = []
    barrier = pltpu.get_barrier_semaphore()
    for k in range(1, n):
        pl.semaphore_signal(barrier, inc=1, device_id=device("pcol", peer(k)), device_id_type=MESH)
    pl.semaphore_signal(barrier, inc=1, device_id=partner, device_id_type=MESH)
    pl.semaphore_signal(barrier, inc=1, device_id=sibling, device_id_type=MESH)
    pl.semaphore_wait(barrier, n + 1)

    chip = one(theirs_ref, sib_in, sibling, send_s, recv_s)
    chip.start()
    pending.append(chip)
    chip.wait_recv()
    summed = mine_ref[...] + sib_in[...].astype(jnp.float32)
    pieces[...] = summed.astype(pieces.dtype).reshape(pieces.shape)

    for k in range(1, n):
        step(pieces.at[peer(k)], got.at[me], k, device("pcol", peer(k)), (send_a, recv_a)).start()
    for k in range(1, n):
        pending.append(step(pieces.at[peer(k)], got.at[me], k, device("pcol", peer(k)), (send_a, recv_a)))
    for k in range(1, n):
        step(pieces.at[me], got.at[sender(k)], k, device("pcol", sender(k)), (send_a, recv_a)).wait_recv()
    total = pieces[me].astype(jnp.float32)
    for k in range(1, n):
        total = total + got[sender(k)].astype(jnp.float32)
    part_out[...] = total.astype(part_out.dtype)

    across = one(part_out, part_in, partner, send_b, recv_b)
    across.start()
    pending.append(across)
    across.wait_recv()
    coll[me] = (part_out[...].astype(jnp.float32) + part_in[...].astype(jnp.float32)).astype(coll.dtype)

    for k in range(1, n):
        step(coll.at[me], coll.at[me], k, device("pcol", peer(k)), (send_c, recv_c)).start()
    for k in range(1, n):
        pending.append(step(coll.at[me], coll.at[me], k, device("pcol", peer(k)), (send_c, recv_c)))
    for k in range(1, n):
        step(coll.at[me], coll.at[sender(k)], k, device("pcol", sender(k)), (send_c, recv_c)).wait_recv()

    join = one(coll, sib_out, sibling, send_d, recv_d)
    join.start()
    pending.append(join)
    join.wait_recv()
    out_ref[core] = coll[...]
    out_ref[1 - core] = sib_out[...]
    for sent in pending:
        sent.wait_send()


def modal_sum(mine, theirs, axes, sizes):
    n = sizes["pcol"]
    rows, width = mine.shape
    block = (n, rows // n, width)
    kernel = functools.partial(modal_sum_kernel, axes=axes, factors=factor_table(sizes))
    return pl.pallas_call(
        kernel,
        out_shape=jax.ShapeDtypeStruct((2,) + block, jnp.bfloat16),
        in_specs=[pl.BlockSpec(memory_space=pltpu.VMEM)] * 2,
        out_specs=pl.BlockSpec(memory_space=pltpu.VMEM),
        scratch_shapes=[
            pltpu.VMEM((rows, width), jnp.bfloat16),
            pltpu.VMEM(block, jnp.bfloat16),
            pltpu.VMEM(block, jnp.bfloat16),
            pltpu.VMEM(block, jnp.bfloat16),
            pltpu.VMEM(block[1:], jnp.bfloat16),
            pltpu.VMEM(block[1:], jnp.bfloat16),
            pltpu.VMEM(block, jnp.bfloat16),
            pltpu.SemaphoreType.DMA(()),
            pltpu.SemaphoreType.DMA(()),
            pltpu.SemaphoreType.DMA((n,)),
            pltpu.SemaphoreType.DMA((n,)),
            pltpu.SemaphoreType.DMA(()),
            pltpu.SemaphoreType.DMA(()),
            pltpu.SemaphoreType.DMA((n,)),
            pltpu.SemaphoreType.DMA((n,)),
            pltpu.SemaphoreType.DMA(()),
            pltpu.SemaphoreType.DMA(()),
        ],
        compiler_params=pltpu.CompilerParams(collective_id=102, has_side_effects=True),
    )(mine, theirs)


def gram_weighted_kernel(x_ref, shapes_ref, out_ref, got, coll, sib_coll, part_out, part_in, wbuf,
                         send_a, recv_a, send_b, recv_b, send_c, recv_c, send_d, recv_d, send_e,
                         recv_e, *, axes, factors):
    coords = {a: lax.axis_index(a) for a in axes}

    def value(f):
        axis, size, stride = factors[f]
        return lax.rem(coords[axis] // stride, size)

    def device(f, v):
        place = dict(coords)
        axis, size, stride = factors[f]
        place[axis] = place[axis] + (v - value(f)) * stride
        return tuple(place[a] for a in axes)

    n, n_col = factors["pl"][1], factors["pcol"][1]
    me, half, core, col = value("pl"), value("zh"), value("core"), value("pcol")
    partner, sibling = device("zh", 1 - half), device("core", 1 - core)

    def step(src, dst_at, k, to, sems):
        return pltpu.make_async_remote_copy(
            src_ref=src, dst_ref=dst_at, send_sem=sems[0].at[k], recv_sem=sems[1].at[k],
            device_id=to, device_id_type=MESH,
        )

    def one(src, dst, to, send_sem, recv_sem):
        return pltpu.make_async_remote_copy(
            src_ref=src, dst_ref=dst, send_sem=send_sem, recv_sem=recv_sem,
            device_id=to, device_id_type=MESH,
        )

    pending = []
    barrier = pltpu.get_barrier_semaphore()
    for k in range(1, n):
        pl.semaphore_signal(barrier, inc=1, device_id=device("pl", lax.rem(me + k, n)), device_id_type=MESH)
    for k in range(1, n_col):
        pl.semaphore_signal(
            barrier, inc=1, device_id=device("pcol", lax.rem(col + k, n_col)), device_id_type=MESH
        )
    pl.semaphore_signal(barrier, inc=1, device_id=partner, device_id_type=MESH)
    pl.semaphore_signal(barrier, inc=1, device_id=sibling, device_id_type=MESH)
    pl.semaphore_wait(barrier, n + n_col)

    peer = lambda k: lax.rem(me + k, n)
    sender = lambda k: lax.rem(me + n - k, n)
    for k in range(1, n):
        step(x_ref.at[peer(k)], got.at[me], k, device("pl", peer(k)), (send_a, recv_a)).start()
    for k in range(1, n):
        pending.append(step(x_ref.at[peer(k)], got.at[me], k, device("pl", peer(k)), (send_a, recv_a)))
    for k in range(1, n):
        step(x_ref.at[me], got.at[sender(k)], k, device("pl", sender(k)), (send_a, recv_a)).wait_recv()
    total = x_ref[me].astype(jnp.float32)
    for k in range(1, n):
        total = total + got[sender(k)].astype(jnp.float32)
    part_out[...] = total.astype(part_out.dtype)

    across = one(part_out, part_in, partner, send_b, recv_b)
    across.start()
    pending.append(across)
    across.wait_recv()
    mine, theirs = part_out[...], part_in[...]
    coll[me] = jnp.stack([jnp.where(half == 0, mine, theirs), jnp.where(half == 0, theirs, mine)])


    def to_sibling(chunk_at):
        return pltpu.make_async_remote_copy(
            src_ref=coll.at[chunk_at], dst_ref=sib_coll.at[chunk_at], send_sem=send_d.at[chunk_at],
            recv_sem=recv_d.at[chunk_at], device_id=sibling, device_id_type=MESH,
        )

    to_sibling(me).start()
    pending.append(to_sibling(me))
    for k in range(1, n):
        step(coll.at[me], coll.at[me], k, device("pl", peer(k)), (send_c, recv_c)).start()
    for k in range(1, n):
        pending.append(step(coll.at[me], coll.at[me], k, device("pl", peer(k)), (send_c, recv_c)))
    for k in range(1, n):
        step(coll.at[me], coll.at[sender(k)], k, device("pl", sender(k)), (send_c, recv_c)).wait_recv()
        to_sibling(sender(k)).start()
        pending.append(to_sibling(sender(k)))

    chunk = coll.shape[-1]

    def weighted_block(blocks, h):
        acc = jnp.zeros((shapes_ref.shape[0], blocks.shape[2]), jnp.float32)
        for l in range(n):
            acc = acc + lax.dot_general(
                shapes_ref[:, l * chunk:(l + 1) * chunk], blocks[l, h],
                (((1,), (1,)), ((), ())), preferred_element_type=jnp.float32,
            )
        return acc

    own = [weighted_block(coll, h) for h in range(2)]
    wpeer = lambda k: lax.rem(col + k, n_col)
    wsender = lambda k: lax.rem(col + n_col - k, n_col)
    blocks_w = wbuf.shape[1]

    def w_copy(k, r, to_col, at_col):
        return pltpu.make_async_remote_copy(
            src_ref=wbuf.at[col, r], dst_ref=wbuf.at[at_col, r], send_sem=send_e.at[k * blocks_w + r],
            recv_sem=recv_e.at[k * blocks_w + r], device_id=device("pcol", to_col), device_id_type=MESH,
        )

    def send_blocks(values, first):
        for h in range(2):
            r = 2 * h + first
            wbuf[col, r] = values[h].astype(wbuf.dtype)
            for k in range(1, n_col):
                w_copy(k, r, wpeer(k), col).start()
                pending.append(w_copy(k, r, wpeer(k), col))

    send_blocks(own, core)
    for l in range(n):
        to_sibling(l).wait_recv()
    send_blocks([weighted_block(sib_coll, h) for h in range(2)], 1 - core)
    for k in range(1, n_col):
        for r in range(blocks_w):
            w_copy(k, r, wsender(k), wsender(k)).wait_recv()
    width_w = wbuf.shape[3]
    for c in range(n_col):
        for r in range(blocks_w):
            out_ref[:, (c * blocks_w + r) * width_w:(c * blocks_w + r + 1) * width_w] = wbuf[c, r]
    for sent in pending:
        sent.wait_send()


def gram_weighted(x, mode_shapes, axes, sizes):
    n, rows, width = x.shape
    n_col = sizes["pcol"]
    wshape = (n_col, 4, mode_shapes.shape[0], rows)
    kernel = functools.partial(gram_weighted_kernel, axes=axes, factors=factor_table(sizes))
    return pl.pallas_call(
        kernel,
        out_shape=jax.ShapeDtypeStruct((wshape[2], n_col * 4 * rows), jnp.bfloat16),
        in_specs=[pl.BlockSpec(memory_space=pltpu.VMEM)] * 2,
        out_specs=pl.BlockSpec(memory_space=pltpu.VMEM),
        scratch_shapes=[
            pltpu.VMEM(x.shape, x.dtype),
            pltpu.VMEM((n, 2, rows, width), x.dtype),
            pltpu.VMEM((n, 2, rows, width), x.dtype),
            pltpu.VMEM((rows, width), x.dtype),
            pltpu.VMEM((rows, width), x.dtype),
            pltpu.VMEM(wshape, jnp.bfloat16),
            pltpu.SemaphoreType.DMA((n,)),
            pltpu.SemaphoreType.DMA((n,)),
            pltpu.SemaphoreType.DMA(()),
            pltpu.SemaphoreType.DMA(()),
            pltpu.SemaphoreType.DMA((n,)),
            pltpu.SemaphoreType.DMA((n,)),
            pltpu.SemaphoreType.DMA((n,)),
            pltpu.SemaphoreType.DMA((n,)),
            pltpu.SemaphoreType.DMA((4 * n_col,)),
            pltpu.SemaphoreType.DMA((4 * n_col,)),
        ],
        compiler_params=pltpu.CompilerParams(collective_id=103, has_side_effects=True),
    )(x, mode_shapes)


def fused_sum(x, axes, sizes, over, add_across, kernel_id):
    n, rows, width = x.shape
    block = (rows, width) if add_across else (2, rows, width)
    kernel = functools.partial(
        fused_sum_kernel, axes=axes, factors=factor_table(sizes), over=over, add_across=add_across
    )
    return pl.pallas_call(
        kernel,
        out_shape=jax.ShapeDtypeStruct((n,) + block, x.dtype),
        in_specs=[pl.BlockSpec(memory_space=pltpu.VMEM)],
        out_specs=pl.BlockSpec(memory_space=pltpu.VMEM),
        scratch_shapes=[
            pltpu.VMEM(x.shape, x.dtype),
            pltpu.VMEM((n,) + block, x.dtype),
            pltpu.VMEM((rows, width), x.dtype),
            pltpu.VMEM((rows, width), x.dtype),
            pltpu.SemaphoreType.DMA((n,)),
            pltpu.SemaphoreType.DMA((n,)),
            pltpu.SemaphoreType.DMA(()),
            pltpu.SemaphoreType.DMA(()),
            pltpu.SemaphoreType.DMA((n,)),
            pltpu.SemaphoreType.DMA((n,)),
        ],
        compiler_params=pltpu.CompilerParams(collective_id=kernel_id, has_side_effects=True),
    )(x)


class Exchanger:
    def __init__(self, axes, sizes):
        self.axes, self.factors, self.calls = axes, factor_table(sizes), 0

    def __call__(self, x, group, same):
        count = math.prod(self.factors[f][1] for f in group)
        block = x.shape if same else x.shape[1:]
        if count == 1:
            return x[None] if same else x
        kernel = functools.partial(
            exchange_kernel, axes=self.axes, factors=self.factors, group=group, same=same
        )
        self.calls += 1
        return pl.pallas_call(
            kernel,
            out_shape=jax.ShapeDtypeStruct((count,) + tuple(block), x.dtype),
            in_specs=[pl.BlockSpec(memory_space=pl.ANY)],
            out_specs=pl.BlockSpec(memory_space=pl.ANY),
            scratch_shapes=[
                pltpu.SemaphoreType.DMA((count,)),
                pltpu.SemaphoreType.DMA((count,)),
                pltpu.SemaphoreType.DMA(()),
            ],
            compiler_params=pltpu.CompilerParams(collective_id=self.calls, has_side_effects=True),
        )(x)


def make_body(axes, sizes):
    n_row, n_col, n_pl = sizes["prow"], sizes["pcol"], sizes["pl"]
    swap = [(c * n_col + r, r * n_col + c) for r in range(n_row) for c in range(n_col)]
    sibling = [(r, r ^ 1) for r in range(n_row)]
    n_zh = n_row // 2

    def beside_sibling(part, core):
        other = lax.ppermute(part, "prow", sibling)
        first, second = jnp.where(core == 0, part, other), jnp.where(core == 0, other, part)
        return jnp.concatenate([first, second], axis=0)

    def body(factor_cols, modal_at_loads, mode_shapes, natural_freq, damping):
        ex = Exchanger(axes, sizes)
        in_phase, quadrature = transfer_pair(natural_freq, damping)
        modes = modal_at_loads.shape[0]
        block = modes // (n_row * n_col)
        row, col = lax.axis_index("prow"), lax.axis_index("pcol")
        width = factor_cols.shape[1]
        core = row % 2
        own_modes = lax.dynamic_slice_in_dim(modal_at_loads, core * (modes // 2), modes // 2, 0)
        sib_modes = lax.dynamic_slice_in_dim(modal_at_loads, (1 - core) * (modes // 2), modes // 2, 0)
        mine = jnp.dot(own_modes, factor_cols, preferred_element_type=jnp.float32)
        theirs = jnp.dot(sib_modes, factor_cols, preferred_element_type=jnp.float32)
        modal_load = modal_sum(mine, theirs.astype(jnp.bfloat16), axes, sizes).reshape(modes, width)
        modal_wide = modal_load.astype(jnp.float32)
        pseudo = jnp.concatenate(
            [
                (in_phase[:, None] * modal_wide).astype(jnp.bfloat16),
                (quadrature[:, None] * modal_wide).astype(jnp.bfloat16),
            ],
            axis=1,
        )
        first_row = (col * n_row + row) * block
        own_pseudo = lax.dynamic_slice_in_dim(pseudo, first_row, block, 0)
        partial_gram = outer_rows(own_pseudo, pseudo).astype(jnp.bfloat16)
        chunk = modes // n_pl
        by_chunk = partial_gram.reshape(block, n_pl, chunk).transpose(1, 0, 2)
        half = modes // 2
        send_half = lax.dynamic_slice_in_dim(mode_shapes, (col % 2) * half, half, 1)
        panel_piece = lax.ppermute(send_half, ("prow", "pcol"), swap)
        panel_mine = lax.all_gather(panel_piece, "pl", axis=0, tiled=True)
        weighted = gram_weighted(by_chunk, mode_shapes, axes, sizes)
        panel_mine, weighted = lax.optimization_barrier((panel_mine, weighted))
        panel_other = lax.ppermute(panel_mine, "prow", sibling)
        weighted_mine = lax.dynamic_slice_in_dim(weighted, core * half, half, 1)
        weighted_other = lax.dynamic_slice_in_dim(weighted, (1 - core) * half, half, 1)
        return outer_rows(weighted_other, panel_other) + outer_rows(weighted_mine, panel_mine)

    return body


def solution(mesh):
    in_specs = (
        P(("prow", "pcol"), "pl"),
        P(None, ("prow", "pcol")),
        P(("prow", "pl"), None),
        P(),
        P(),
    )
    out_specs = P(("prow", "pl"), "pcol")
    axes = tuple(mesh.axis_names)
    body = make_body(axes, dict(mesh.shape))
    return jax.shard_map(body, mesh=mesh, in_specs=in_specs, out_specs=out_specs, check_vma=False)
```

```python
import functools
import math

import jax
import jax.numpy as jnp
from jax import lax
from jax.experimental import pallas as pl
from jax.experimental.pallas import tpu as pltpu
from jax.sharding import PartitionSpec as P

MESH = pl.DeviceIdType.MESH


def transfer_pair(natural_freq, damping):
    detuning = natural_freq * natural_freq - 1.0
    damper = 2.0 * damping * natural_freq
    modulus = detuning * detuning + damper * damper
    return (detuning / modulus, -damper / modulus)


def outer_rows(left_rows, right_rows):
    return lax.dot_general(
        left_rows, right_rows, (((1,), (1,)), ((), ())), preferred_element_type=jnp.float32
    )


def factor_table(sizes):
    return {
        "zh": ("prow", sizes["prow"] // 2, 2),
        "core": ("prow", 2, 1),
        "pcol": ("pcol", sizes["pcol"], 1),
        "pl": ("pl", sizes["pl"], 1),
    }


def exchange_kernel(x_ref, out_ref, send_sem, recv_sem, local_sem, *, axes, factors, group, same):
    coords = {a: lax.axis_index(a) for a in axes}

    def value(f):
        axis, size, stride = factors[f]
        return lax.rem(coords[axis] // stride, size)

    count = math.prod(factors[f][1] for f in group)
    me = 0
    for f in group:
        me = me * factors[f][1] + value(f)

    def device(member):
        place = dict(coords)
        for f in reversed(group):
            axis, size, stride = factors[f]
            place[axis] = place[axis] + (lax.rem(member, size) - value(f)) * stride
            member = member // size
        return tuple(place[a] for a in axes)

    def source(member):
        return x_ref if same else x_ref.at[member]

    def copy(offset):
        peer = lax.rem(me + offset, count)
        return pltpu.make_async_remote_copy(
            src_ref=source(peer),
            dst_ref=out_ref.at[me],
            send_sem=send_sem.at[offset],
            recv_sem=recv_sem.at[offset],
            device_id=device(peer),
            device_id_type=MESH,
        )

    def landing(offset):
        sender = lax.rem(me + count - offset, count)
        return pltpu.make_async_remote_copy(
            src_ref=source(me),
            dst_ref=out_ref.at[sender],
            send_sem=send_sem.at[offset],
            recv_sem=recv_sem.at[offset],
            device_id=device(sender),
            device_id_type=MESH,
        )

    local = pltpu.make_async_copy(source(me), out_ref.at[me], local_sem)
    local.start()
    barrier = pltpu.get_barrier_semaphore()
    for offset in range(1, count):
        peer = lax.rem(me + offset, count)
        pl.semaphore_signal(barrier, inc=1, device_id=device(peer), device_id_type=MESH)
    pl.semaphore_wait(barrier, count - 1)
    for offset in range(1, count):
        copy(offset).start()
    local.wait()
    for offset in range(1, count):
        copy(offset).wait_send()
    for offset in range(1, count):
        landing(offset).wait_recv()


def fused_sum_kernel(x_ref, out_ref, got, coll, part_out, part_in, send_a, recv_a, send_b, recv_b,
                     send_c, recv_c, *, axes, factors, over, add_across):
    coords = {a: lax.axis_index(a) for a in axes}

    def value(f):
        axis, size, stride = factors[f]
        return lax.rem(coords[axis] // stride, size)

    def device(f, v):
        place = dict(coords)
        axis, size, stride = factors[f]
        place[axis] = place[axis] + (v - value(f)) * stride
        return tuple(place[a] for a in axes)

    n = factors[over][1]
    me, half = value(over), value("zh")
    partner = device("zh", 1 - half)
    peer = lambda k: lax.rem(me + k, n)
    sender = lambda k: lax.rem(me + n - k, n)

    def step(src, dst_at, k, to, sems):
        return pltpu.make_async_remote_copy(
            src_ref=src, dst_ref=dst_at, send_sem=sems[0].at[k], recv_sem=sems[1].at[k],
            device_id=to, device_id_type=MESH,
        )

    barrier = pltpu.get_barrier_semaphore()
    for k in range(1, n):
        pl.semaphore_signal(barrier, inc=1, device_id=device(over, peer(k)), device_id_type=MESH)
    pl.semaphore_signal(barrier, inc=1, device_id=partner, device_id_type=MESH)
    pl.semaphore_wait(barrier, n)

    for k in range(1, n):
        step(x_ref.at[peer(k)], got.at[me], k, device(over, peer(k)), (send_a, recv_a)).start()
    for k in range(1, n):
        step(x_ref.at[peer(k)], got.at[me], k, device(over, peer(k)), (send_a, recv_a)).wait_send()
    for k in range(1, n):
        step(x_ref.at[me], got.at[sender(k)], k, device(over, sender(k)), (send_a, recv_a)).wait_recv()
    total = x_ref[me].astype(jnp.float32)
    for k in range(1, n):
        total = total + got[sender(k)].astype(jnp.float32)
    part_out[...] = total.astype(part_out.dtype)

    across = pltpu.make_async_remote_copy(
        src_ref=part_out, dst_ref=part_in, send_sem=send_b, recv_sem=recv_b,
        device_id=partner, device_id_type=MESH,
    )
    across.start()
    across.wait_send()
    across.wait_recv()
    if add_across:
        mine, theirs = part_out[...].astype(jnp.float32), part_in[...].astype(jnp.float32)
        coll[me] = (mine + theirs).astype(coll.dtype)
    else:
        mine, theirs = part_out[...], part_in[...]
        first = jnp.where(half == 0, mine, theirs)
        second = jnp.where(half == 0, theirs, mine)
        coll[me] = jnp.stack([first, second])

    for k in range(1, n):
        step(coll.at[me], coll.at[me], k, device(over, peer(k)), (send_c, recv_c)).start()
    for k in range(1, n):
        step(coll.at[me], coll.at[me], k, device(over, peer(k)), (send_c, recv_c)).wait_send()
    for k in range(1, n):
        step(coll.at[me], coll.at[sender(k)], k, device(over, sender(k)), (send_c, recv_c)).wait_recv()
    out_ref[...] = coll[...]


def modal_sum_kernel(mine_ref, theirs_ref, out_ref, sib_in, pieces, got, coll, part_out, part_in,
                     sib_out, send_s, recv_s, send_a, recv_a, send_b, recv_b, send_c, recv_c,
                     send_d, recv_d, *, axes, factors):
    coords = {a: lax.axis_index(a) for a in axes}

    def value(f):
        axis, size, stride = factors[f]
        return lax.rem(coords[axis] // stride, size)

    def device(f, v):
        place = dict(coords)
        axis, size, stride = factors[f]
        place[axis] = place[axis] + (v - value(f)) * stride
        return tuple(place[a] for a in axes)

    n = factors["pcol"][1]
    me, half, core = value("pcol"), value("zh"), value("core")
    partner, sibling = device("zh", 1 - half), device("core", 1 - core)
    peer = lambda k: lax.rem(me + k, n)
    sender = lambda k: lax.rem(me + n - k, n)

    def step(src, dst_at, k, to, sems):
        return pltpu.make_async_remote_copy(
            src_ref=src, dst_ref=dst_at, send_sem=sems[0].at[k], recv_sem=sems[1].at[k],
            device_id=to, device_id_type=MESH,
        )

    def one(src, dst, to, send_sem, recv_sem):
        return pltpu.make_async_remote_copy(
            src_ref=src, dst_ref=dst, send_sem=send_sem, recv_sem=recv_sem,
            device_id=to, device_id_type=MESH,
        )

    pending = []
    barrier = pltpu.get_barrier_semaphore()
    for k in range(1, n):
        pl.semaphore_signal(barrier, inc=1, device_id=device("pcol", peer(k)), device_id_type=MESH)
    pl.semaphore_signal(barrier, inc=1, device_id=partner, device_id_type=MESH)
    pl.semaphore_signal(barrier, inc=1, device_id=sibling, device_id_type=MESH)
    pl.semaphore_wait(barrier, n + 1)

    chip = one(theirs_ref, sib_in, sibling, send_s, recv_s)
    chip.start()
    pending.append(chip)
    chip.wait_recv()
    summed = mine_ref[...] + sib_in[...].astype(jnp.float32)
    pieces[...] = summed.astype(pieces.dtype).reshape(pieces.shape)

    for k in range(1, n):
        step(pieces.at[peer(k)], got.at[me], k, device("pcol", peer(k)), (send_a, recv_a)).start()
    for k in range(1, n):
        pending.append(step(pieces.at[peer(k)], got.at[me], k, device("pcol", peer(k)), (send_a, recv_a)))
    for k in range(1, n):
        step(pieces.at[me], got.at[sender(k)], k, device("pcol", sender(k)), (send_a, recv_a)).wait_recv()
    total = pieces[me].astype(jnp.float32)
    for k in range(1, n):
        total = total + got[sender(k)].astype(jnp.float32)
    part_out[...] = total.astype(part_out.dtype)

    across = one(part_out, part_in, partner, send_b, recv_b)
    across.start()
    pending.append(across)
    across.wait_recv()
    coll[me] = (part_out[...].astype(jnp.float32) + part_in[...].astype(jnp.float32)).astype(coll.dtype)

    for k in range(1, n):
        step(coll.at[me], coll.at[me], k, device("pcol", peer(k)), (send_c, recv_c)).start()
    for k in range(1, n):
        pending.append(step(coll.at[me], coll.at[me], k, device("pcol", peer(k)), (send_c, recv_c)))
    for k in range(1, n):
        step(coll.at[me], coll.at[sender(k)], k, device("pcol", sender(k)), (send_c, recv_c)).wait_recv()

    join = one(coll, sib_out, sibling, send_d, recv_d)
    join.start()
    pending.append(join)
    join.wait_recv()
    out_ref[core] = coll[...]
    out_ref[1 - core] = sib_out[...]
    for sent in pending:
        sent.wait_send()


def modal_sum(mine, theirs, axes, sizes):
    n = sizes["pcol"]
    rows, width = mine.shape
    block = (n, rows // n, width)
    kernel = functools.partial(modal_sum_kernel, axes=axes, factors=factor_table(sizes))
    return pl.pallas_call(
        kernel,
        out_shape=jax.ShapeDtypeStruct((2,) + block, jnp.bfloat16),
        in_specs=[pl.BlockSpec(memory_space=pltpu.VMEM)] * 2,
        out_specs=pl.BlockSpec(memory_space=pltpu.VMEM),
        scratch_shapes=[
            pltpu.VMEM((rows, width), jnp.bfloat16),
            pltpu.VMEM(block, jnp.bfloat16),
            pltpu.VMEM(block, jnp.bfloat16),
            pltpu.VMEM(block, jnp.bfloat16),
            pltpu.VMEM(block[1:], jnp.bfloat16),
            pltpu.VMEM(block[1:], jnp.bfloat16),
            pltpu.VMEM(block, jnp.bfloat16),
            pltpu.SemaphoreType.DMA(()),
            pltpu.SemaphoreType.DMA(()),
            pltpu.SemaphoreType.DMA((n,)),
            pltpu.SemaphoreType.DMA((n,)),
            pltpu.SemaphoreType.DMA(()),
            pltpu.SemaphoreType.DMA(()),
            pltpu.SemaphoreType.DMA((n,)),
            pltpu.SemaphoreType.DMA((n,)),
            pltpu.SemaphoreType.DMA(()),
            pltpu.SemaphoreType.DMA(()),
        ],
        compiler_params=pltpu.CompilerParams(collective_id=102, has_side_effects=True),
    )(mine, theirs)


def gram_weighted_kernel(x_ref, shapes_ref, out_ref, got, coll, sib_coll, part_out, part_in, wbuf,
                         send_a, recv_a, send_b, recv_b, send_c, recv_c, send_d, recv_d, send_e,
                         recv_e, *, axes, factors):
    coords = {a: lax.axis_index(a) for a in axes}

    def value(f):
        axis, size, stride = factors[f]
        return lax.rem(coords[axis] // stride, size)

    def device(f, v):
        place = dict(coords)
        axis, size, stride = factors[f]
        place[axis] = place[axis] + (v - value(f)) * stride
        return tuple(place[a] for a in axes)

    n, n_col = factors["pl"][1], factors["pcol"][1]
    me, half, core, col = value("pl"), value("zh"), value("core"), value("pcol")
    partner, sibling = device("zh", 1 - half), device("core", 1 - core)

    def step(src, dst_at, k, to, sems):
        return pltpu.make_async_remote_copy(
            src_ref=src, dst_ref=dst_at, send_sem=sems[0].at[k], recv_sem=sems[1].at[k],
            device_id=to, device_id_type=MESH,
        )

    def one(src, dst, to, send_sem, recv_sem):
        return pltpu.make_async_remote_copy(
            src_ref=src, dst_ref=dst, send_sem=send_sem, recv_sem=recv_sem,
            device_id=to, device_id_type=MESH,
        )

    pending = []
    barrier = pltpu.get_barrier_semaphore()
    pl.semaphore_signal(barrier, inc=1, device_id=partner, device_id_type=MESH)
    pl.semaphore_signal(barrier, inc=1, device_id=sibling, device_id_type=MESH)
    for k in range(1, n):
        pl.semaphore_signal(barrier, inc=1, device_id=device("pl", lax.rem(me + k, n)), device_id_type=MESH)
    for k in range(1, n_col):
        pl.semaphore_signal(
            barrier, inc=1, device_id=device("pcol", lax.rem(col + k, n_col)), device_id_type=MESH
        )
    pl.semaphore_wait(barrier, n + n_col)

    peer = lambda k: lax.rem(me + k, n)
    sender = lambda k: lax.rem(me + n - k, n)
    for k in range(1, n):
        step(x_ref.at[peer(k)], got.at[me], k, device("pl", peer(k)), (send_a, recv_a)).start()
    for k in range(1, n):
        pending.append(step(x_ref.at[peer(k)], got.at[me], k, device("pl", peer(k)), (send_a, recv_a)))
    for k in range(1, n):
        step(x_ref.at[me], got.at[sender(k)], k, device("pl", sender(k)), (send_a, recv_a)).wait_recv()
    total = x_ref[me].astype(jnp.float32)
    for k in range(1, n):
        total = total + got[sender(k)].astype(jnp.float32)
    part_out[...] = total.astype(part_out.dtype)

    across = one(part_out, part_in, partner, send_b, recv_b)
    across.start()
    pending.append(across)
    across.wait_recv()
    mine, theirs = part_out[...], part_in[...]
    coll[me] = jnp.stack([jnp.where(half == 0, mine, theirs), jnp.where(half == 0, theirs, mine)])

    for k in range(1, n):
        step(coll.at[me], coll.at[me], k, device("pl", peer(k)), (send_c, recv_c)).start()
    for k in range(1, n):
        pending.append(step(coll.at[me], coll.at[me], k, device("pl", peer(k)), (send_c, recv_c)))

    def to_sibling(chunk_at):
        return pltpu.make_async_remote_copy(
            src_ref=coll.at[chunk_at], dst_ref=sib_coll.at[chunk_at], send_sem=send_d.at[chunk_at],
            recv_sem=recv_d.at[chunk_at], device_id=sibling, device_id_type=MESH,
        )

    to_sibling(me).start()
    pending.append(to_sibling(me))
    for k in range(1, n):
        step(coll.at[me], coll.at[sender(k)], k, device("pl", sender(k)), (send_c, recv_c)).wait_recv()
        to_sibling(sender(k)).start()
        pending.append(to_sibling(sender(k)))

    chunk = coll.shape[-1]

    def weighted_block(blocks, h):
        acc = jnp.zeros((shapes_ref.shape[0], blocks.shape[2]), jnp.float32)
        for l in range(n):
            acc = acc + lax.dot_general(
                shapes_ref[:, l * chunk:(l + 1) * chunk], blocks[l, h],
                (((1,), (1,)), ((), ())), preferred_element_type=jnp.float32,
            )
        return acc

    own = [weighted_block(coll, h) for h in range(2)]
    wpeer = lambda k: lax.rem(col + k, n_col)
    wsender = lambda k: lax.rem(col + n_col - k, n_col)
    blocks_w = wbuf.shape[1]

    def w_copy(k, r, to_col, at_col):
        return pltpu.make_async_remote_copy(
            src_ref=wbuf.at[col, r], dst_ref=wbuf.at[at_col, r], send_sem=send_e.at[k * blocks_w + r],
            recv_sem=recv_e.at[k * blocks_w + r], device_id=device("pcol", to_col), device_id_type=MESH,
        )

    def send_blocks(values, first):
        for h in range(2):
            r = 2 * h + first
            wbuf[col, r] = values[h].astype(wbuf.dtype)
            for k in range(1, n_col):
                w_copy(k, r, wpeer(k), col).start()
                pending.append(w_copy(k, r, wpeer(k), col))

    send_blocks(own, core)
    for l in range(n):
        to_sibling(l).wait_recv()
    send_blocks([weighted_block(sib_coll, h) for h in range(2)], 1 - core)
    for k in range(1, n_col):
        for r in range(blocks_w):
            w_copy(k, r, wsender(k), wsender(k)).wait_recv()
    width_w = wbuf.shape[3]
    for c in range(n_col):
        for r in range(blocks_w):
            out_ref[:, (c * blocks_w + r) * width_w:(c * blocks_w + r + 1) * width_w] = wbuf[c, r]
    for sent in pending:
        sent.wait_send()


def gram_weighted(x, mode_shapes, axes, sizes):
    n, rows, width = x.shape
    n_col = sizes["pcol"]
    wshape = (n_col, 4, mode_shapes.shape[0], rows)
    kernel = functools.partial(gram_weighted_kernel, axes=axes, factors=factor_table(sizes))
    return pl.pallas_call(
        kernel,
        out_shape=jax.ShapeDtypeStruct((wshape[2], n_col * 4 * rows), jnp.bfloat16),
        in_specs=[pl.BlockSpec(memory_space=pltpu.VMEM)] * 2,
        out_specs=pl.BlockSpec(memory_space=pltpu.VMEM),
        scratch_shapes=[
            pltpu.VMEM(x.shape, x.dtype),
            pltpu.VMEM((n, 2, rows, width), x.dtype),
            pltpu.VMEM((n, 2, rows, width), x.dtype),
            pltpu.VMEM((rows, width), x.dtype),
            pltpu.VMEM((rows, width), x.dtype),
            pltpu.VMEM(wshape, jnp.bfloat16),
            pltpu.SemaphoreType.DMA((n,)),
            pltpu.SemaphoreType.DMA((n,)),
            pltpu.SemaphoreType.DMA(()),
            pltpu.SemaphoreType.DMA(()),
            pltpu.SemaphoreType.DMA((n,)),
            pltpu.SemaphoreType.DMA((n,)),
            pltpu.SemaphoreType.DMA((n,)),
            pltpu.SemaphoreType.DMA((n,)),
            pltpu.SemaphoreType.DMA((4 * n_col,)),
            pltpu.SemaphoreType.DMA((4 * n_col,)),
        ],
        compiler_params=pltpu.CompilerParams(collective_id=103, has_side_effects=True),
    )(x, mode_shapes)


def fused_sum(x, axes, sizes, over, add_across, kernel_id):
    n, rows, width = x.shape
    block = (rows, width) if add_across else (2, rows, width)
    kernel = functools.partial(
        fused_sum_kernel, axes=axes, factors=factor_table(sizes), over=over, add_across=add_across
    )
    return pl.pallas_call(
        kernel,
        out_shape=jax.ShapeDtypeStruct((n,) + block, x.dtype),
        in_specs=[pl.BlockSpec(memory_space=pltpu.VMEM)],
        out_specs=pl.BlockSpec(memory_space=pltpu.VMEM),
        scratch_shapes=[
            pltpu.VMEM(x.shape, x.dtype),
            pltpu.VMEM((n,) + block, x.dtype),
            pltpu.VMEM((rows, width), x.dtype),
            pltpu.VMEM((rows, width), x.dtype),
            pltpu.SemaphoreType.DMA((n,)),
            pltpu.SemaphoreType.DMA((n,)),
            pltpu.SemaphoreType.DMA(()),
            pltpu.SemaphoreType.DMA(()),
            pltpu.SemaphoreType.DMA((n,)),
            pltpu.SemaphoreType.DMA((n,)),
        ],
        compiler_params=pltpu.CompilerParams(collective_id=kernel_id, has_side_effects=True),
    )(x)


class Exchanger:
    def __init__(self, axes, sizes):
        self.axes, self.factors, self.calls = axes, factor_table(sizes), 0

    def __call__(self, x, group, same):
        count = math.prod(self.factors[f][1] for f in group)
        block = x.shape if same else x.shape[1:]
        if count == 1:
            return x[None] if same else x
        kernel = functools.partial(
            exchange_kernel, axes=self.axes, factors=self.factors, group=group, same=same
        )
        self.calls += 1
        return pl.pallas_call(
            kernel,
            out_shape=jax.ShapeDtypeStruct((count,) + tuple(block), x.dtype),
            in_specs=[pl.BlockSpec(memory_space=pl.ANY)],
            out_specs=pl.BlockSpec(memory_space=pl.ANY),
            scratch_shapes=[
                pltpu.SemaphoreType.DMA((count,)),
                pltpu.SemaphoreType.DMA((count,)),
                pltpu.SemaphoreType.DMA(()),
            ],
            compiler_params=pltpu.CompilerParams(collective_id=self.calls, has_side_effects=True),
        )(x)


def make_body(axes, sizes):
    n_row, n_col, n_pl = sizes["prow"], sizes["pcol"], sizes["pl"]
    swap = [(c * n_col + r, r * n_col + c) for r in range(n_row) for c in range(n_col)]
    sibling = [(r, r ^ 1) for r in range(n_row)]
    n_zh = n_row // 2

    def beside_sibling(part, core):
        other = lax.ppermute(part, "prow", sibling)
        first, second = jnp.where(core == 0, part, other), jnp.where(core == 0, other, part)
        return jnp.concatenate([first, second], axis=0)

    def body(factor_cols, modal_at_loads, mode_shapes, natural_freq, damping):
        ex = Exchanger(axes, sizes)
        in_phase, quadrature = transfer_pair(natural_freq, damping)
        modes = modal_at_loads.shape[0]
        block = modes // (n_row * n_col)
        row, col = lax.axis_index("prow"), lax.axis_index("pcol")
        width = factor_cols.shape[1]
        core = row % 2
        own_modes = lax.dynamic_slice_in_dim(modal_at_loads, core * (modes // 2), modes // 2, 0)
        sib_modes = lax.dynamic_slice_in_dim(modal_at_loads, (1 - core) * (modes // 2), modes // 2, 0)
        mine = jnp.dot(own_modes, factor_cols, preferred_element_type=jnp.float32)
        theirs = jnp.dot(sib_modes, factor_cols, preferred_element_type=jnp.float32)
        modal_load = modal_sum(mine, theirs.astype(jnp.bfloat16), axes, sizes).reshape(modes, width)
        modal_wide = modal_load.astype(jnp.float32)
        pseudo = jnp.concatenate(
            [
                (in_phase[:, None] * modal_wide).astype(jnp.bfloat16),
                (quadrature[:, None] * modal_wide).astype(jnp.bfloat16),
            ],
            axis=1,
        )
        first_row = (col * n_row + row) * block
        own_pseudo = lax.dynamic_slice_in_dim(pseudo, first_row, block, 0)
        partial_gram = outer_rows(own_pseudo, pseudo).astype(jnp.bfloat16)
        chunk = modes // n_pl
        by_chunk = partial_gram.reshape(block, n_pl, chunk).transpose(1, 0, 2)
        half = modes // 2
        send_half = lax.dynamic_slice_in_dim(mode_shapes, (col % 2) * half, half, 1)
        panel_piece = lax.ppermute(send_half, ("prow", "pcol"), swap)
        panel_mine = lax.all_gather(panel_piece, "pl", axis=0, tiled=True)
        weighted = gram_weighted(by_chunk, mode_shapes, axes, sizes)
        panel_mine, weighted = lax.optimization_barrier((panel_mine, weighted))
        panel_other = lax.ppermute(panel_mine, "prow", sibling)
        weighted_mine = lax.dynamic_slice_in_dim(weighted, core * half, half, 1)
        weighted_other = lax.dynamic_slice_in_dim(weighted, (1 - core) * half, half, 1)
        return outer_rows(weighted_other, panel_other) + outer_rows(weighted_mine, panel_mine)

    return body


def solution(mesh):
    in_specs = (
        P(("prow", "pcol"), "pl"),
        P(None, ("prow", "pcol")),
        P(("prow", "pl"), None),
        P(),
        P(),
    )
    out_specs = P(("prow", "pl"), "pcol")
    axes = tuple(mesh.axis_names)
    body = make_body(axes, dict(mesh.shape))
    return jax.shard_map(body, mesh=mesh, in_specs=in_specs, out_specs=out_specs, check_vma=False)
```
